32 devices in a mesh: tm: 4 (over y, x), rows: 8 (over z, core).
Axes of the slice: x: 2, y: 2, z: 4, core: 2. Of those that a mesh axis runs over, the one named last changes fastest.
Arguments:
- features: bfloat16 [48, 1280, 512], P('rows', 'tm'), may hold values from -6 to 6
- cotangent: bfloat16 [48, 1280, 512], P('rows', 'tm'), may hold values from -6 to 6
- state_bank: float32 [48, 512, 32], P('rows', 'tm'), may hold values from -6 to 6
- state_source: int32 [48], P('rows'), may hold values from 0 to 5, as said below
- master: float32 [88, 256, 256], P('tm', 'rows'), may hold values from -0.13258252 to 0.13258252
- left_stats: float32 [88, 256, 256], P('tm', 'rows'), may hold values from -7.68 to 64
- right_stats: float32 [88, 256, 256], P('tm', 'rows'), may hold values from -7.68 to 64
- left_root: float32 [88, 256, 256], P('tm', 'rows'), may hold values from -0.2 to 1.6
- right_root: float32 [88, 256, 256], P('tm'), may hold values from -0.2 to 1.6
- small_params: float32 [20, 512], replicated, may hold values from -1 to 1.5
- decay_logs: float32 [8, 32], P('tm'), may hold values from -7 to -1.5
- state_mix: float32 [2, 512, 32], P(None, 'tm'), may hold values from -0.6 to 0.6
Outputs:
- layer_out: bfloat16 [48, 1280, 512], P('rows', 'tm')
- grad_features: float32 [48, 1280, 512], P('rows', 'tm')
- grad_state: float32 [48, 512, 32], P('rows', 'tm')
- grad_blocks: float32 [88, 256, 256], P('tm', 'rows')
- new_left: float32 [88, 256, 256], P('tm', 'rows')
- new_right: float32 [88, 256, 256], P('tm', 'rows')
- new_master: float32 [88, 256, 256], P('tm', 'rows')
- new_copy: bfloat16 [88, 256, 256], P('tm', 'rows')
- grad_small: float32 [20, 512], P(None, 'tm')
- new_small: float32 [20, 512], P(None, 'tm')
- grad_decay: float32 [8, 32], P('tm')
- grad_mix: float32 [2, 512, 32], P(None, 'tm')
- new_decay: float32 [8, 32], P('tm')
- new_mix: float32 [2, 512, 32], P(None, 'tm')
The draws below stay inside these ranges and needn't reach their ends.
Inputs may be any that keep to these rules, and one draw needn't show every extreme that they name: `state_source`: within each aligned block of 6 rows the values are a permutation of 0 to 5.
All inputs are finite; a program needn't handle non-finite values.
Results may differ from the reference program's by a relative error of at most 0.018.
Values may be sent and summed in bfloat16 or wider, within the bound.
A program may use at most 320 MiB of HBM per device.

```python
import jax
import jax.numpy as jnp
from jax import lax

D = 512
FF = 2048
HEADS = 8
NST = 32
KW = 15
BS = 256
FRAMES = 1280
ROWS_DEV = 6
ROWS = 48
TOKENS = 61440
NB = 88
NSMALL = 20


def draw_state_source(key, part):
    block_keys = jax.random.split(jax.random.fold_in(key, 31), ROWS // ROWS_DEV)

    def shuffle_block(block_key):
        return jax.random.permutation(block_key, ROWS_DEV)
    return jax.vmap(shuffle_block)(block_keys).reshape(ROWS).astype(jnp.int32)


def base_noise(noise_key, shape):
    return jnp.clip(jax.random.normal(noise_key, shape, jnp.float32), -3.0, 3.0)


def draw_master(key, part):
    raw = base_noise(jax.random.fold_in(key, 21), (NB, BS, BS))
    ffn_count = D // BS * (FF // BS)
    index = jnp.arange(NB)[:, None, None]
    wide_in = (index >= ffn_count) & (index < 2 * ffn_count) | (index >= 3 * ffn_count) & (index < 4 * ffn_count)
    scale_by = jnp.where(wide_in, FF ** (-0.5), D ** (-0.5)).astype(jnp.float32)
    return raw * scale_by


def statistic(key, salt_value, low_end, high_end):
    base_key, noise_key = jax.random.split(jax.random.fold_in(key, salt_value))
    base_value = jnp.exp(jax.random.uniform(base_key, (NB, 1, 1), jnp.float32, jnp.log(low_end), jnp.log(high_end)))
    noise = base_noise(noise_key, (NB, BS, BS))
    noise = 0.5 * (noise + jnp.swapaxes(noise, 1, 2))
    counter = jnp.arange(BS)
    identity = (counter[:, None] == counter[None, :]).astype(jnp.float32)
    return base_value * (identity + noise / 60.0)


def draw_left_stats(key, part):
    return statistic(key, 11, 0.05 * BS, 0.2 * BS)


def draw_right_stats(key, part):
    return statistic(key, 12, 0.05 * BS, 0.2 * BS)


def draw_left_root(key, part):
    return statistic(key, 13, 0.7, 1.4)


def draw_right_root(key, part):
    return statistic(key, 14, 0.7, 1.4)


def draw_small_params(key, part):
    gain_key, kernel_key = jax.random.split(jax.random.fold_in(key, 41))
    gains = 1.0 + 0.1 * jnp.clip(jax.random.normal(gain_key, (NSMALL, D), jnp.float32), -5.0, 5.0)
    kernel = jnp.clip(jax.random.normal(kernel_key, (NSMALL, D), jnp.float32), -3.0, 3.0) * KW ** (-0.5)
    row_index = jnp.arange(NSMALL)[:, None]
    return jnp.where(row_index < 5, gains, kernel)


def block_levels(key, shape, cuts, least, largest):
    def one(position, parts):
        draws = jax.random.uniform(jax.random.fold_in(jax.random.fold_in(key, 6), position), (parts,), jnp.float32, least / len(cuts), largest / len(cuts))
        return jnp.repeat(jnp.exp(draws), shape[position] // parts).reshape((-1,) + (1,) * (len(shape) - position - 1))

    level = one(*cuts[0])
    for cut in cuts[1:]:
        level = level * one(*cut)
    return level


def normal_values(own_key, shape, scale, bound, pieces=(), kind=jnp.bfloat16):
    level = block_levels(own_key, shape, pieces, -0.22, 0.18) if pieces else 1.0
    values = jax.random.normal(own_key, shape, jnp.float32) * scale * level
    return jnp.minimum(jnp.maximum(values, -bound), bound).astype(kind)


def setup_inputs(seed: int = 0) -> dict:
    splits = jax.random.split(jax.random.key(seed), 13)
    return {
        "features": normal_values(splits[0], (ROWS, FRAMES, D), 1.0, 6.0, ((0, 8), (1, 4))),
        "cotangent": normal_values(splits[1], (ROWS, FRAMES, D), 1.0, 6.0, ((0, 8), (1, 4))),
        "state_bank": normal_values(splits[2], (ROWS, D, NST), 1.0, 6.0, ((0, 8), (1, 4)), jnp.float32),
        "state_source": draw_state_source(jax.random.fold_in(splits[12], 71), 0),
        "master": draw_master(jax.random.fold_in(splits[12], 71), 0),
        "left_stats": draw_left_stats(jax.random.fold_in(splits[12], 71), 0),
        "right_stats": draw_right_stats(jax.random.fold_in(splits[12], 71), 0),
        "left_root": draw_left_root(jax.random.fold_in(splits[12], 71), 0),
        "right_root": draw_right_root(jax.random.fold_in(splits[12], 71), 0),
        "small_params": draw_small_params(jax.random.fold_in(splits[12], 71), 0),
        "decay_logs": jnp.clip(-7.0 + 5.5 * jax.random.uniform(splits[10], (HEADS, NST), jnp.float32) ** block_levels(splits[10], (HEADS, NST), ((0, 4),), -0.2, 0.2), -7.0, -1.5),
        "state_mix": normal_values(splits[11], (2, D, NST), 0.1, 0.6, ((1, 4),), jnp.float32),
    }


@jax.custom_vjp
def low(v):
    return lax.optimization_barrier(v.astype(jnp.bfloat16)).astype(jnp.float32)

@jax.custom_vjp
def low_back(v):
    return v

def low_keep(v):
    return (low(v), None)

def low_pass(kept, grad):
    return (grad,)

def back_keep(v):
    return (v, None)

def back_low(kept, grad):
    return (low(grad),)
low.defvjp(low_keep, low_pass)
low_back.defvjp(back_keep, back_low)
precise = lax.Precision.HIGHEST
rate_blocks = 0.1
rate_small = 0.5

def layer_norm(values, scales):
    center = values - lax.optimization_barrier(jnp.mean(values, axis=-1, keepdims=True))
    spread = lax.optimization_barrier(jnp.mean(center * center, axis=-1, keepdims=True))
    return center * lax.rsqrt(spread + 1e-05) * scales

def product(first, second):
    return jnp.dot(first, second, precision=precise)

def gating(values):
    half_width = values.shape[-1] // 2
    return values[..., :half_width] * jax.nn.sigmoid(values[..., half_width:])

def to_matrix(block_stack, first, rows_count, cols_count):
    blocks_down = rows_count // BS
    blocks_across = cols_count // BS
    picked = block_stack[first:first + blocks_down * blocks_across]
    picked = picked.reshape(blocks_down, blocks_across, BS, BS).transpose(0, 2, 1, 3)
    return picked.reshape(rows_count, cols_count)

def matrices(block_stack):
    ffn_count = D // BS * (FF // BS)
    mix_count = (D // BS) ** 2
    base_index = 4 * ffn_count
    return (to_matrix(block_stack, 0, D, FF), to_matrix(block_stack, ffn_count, FF, D), to_matrix(block_stack, 2 * ffn_count, D, FF), to_matrix(block_stack, 3 * ffn_count, FF, D), to_matrix(block_stack, base_index, D, D), to_matrix(block_stack, base_index + mix_count, D, 2 * D), to_matrix(block_stack, base_index + 3 * mix_count, D, 2 * D), to_matrix(block_stack, base_index + 5 * mix_count, D, D))

def half_ffn(values, scales, weight_in, weight_out):
    normed = layer_norm(values, scales)
    inner = low_back(product(low(normed), weight_in))
    outer = low_back(product(low(jax.nn.silu(inner)), weight_out))
    return 0.5 * outer

def layer_row(weights, small_terms, kernel_hat, decay_next, out_coeff, features_row, start_state):
    ffa_in, ffa_out, ffb_in, ffb_out, mixer_in, mixer_out, conv_in, conv_out = weights
    margin = (KW - 1) // 2
    period = 2 * FRAMES - 1
    stream_one = features_row + half_ffn(features_row, small_terms[0], ffa_in, ffa_out)
    normed = layer_norm(stream_one, small_terms[1])
    inputs = low_back(low(product(low(normed), mixer_in)))
    spectrum = jnp.fft.rfft(inputs, n=period, axis=0)
    mixed = jnp.fft.irfft(spectrum * kernel_hat, n=period, axis=0)[:FRAMES]
    carried = (out_coeff * start_state).reshape(HEADS, D // HEADS, NST)
    mixed = mixed + jnp.einsum('hdn,hnt->thd', carried, decay_next, precision=precise).reshape(FRAMES, D)
    mixed = low_back(low(mixed))
    gated = low_back(product(mixed, mixer_out))
    stream_two = stream_one + gating(gated)
    normed = layer_norm(stream_two, small_terms[2])
    pointwise = low_back(product(low(normed), conv_in))
    gated_units = low(gating(pointwise))
    padded = jnp.pad(gated_units, ((margin, margin), (0, 0)))
    depthwise = small_terms[5] * padded[0:FRAMES]
    for offset in range(1, KW):
        depthwise = depthwise + small_terms[5 + offset] * padded[offset:offset + FRAMES]
    depthwise = low_back(depthwise)
    conv_branch = low_back(product(low(jax.nn.silu(depthwise)), conv_out))
    stream_three = stream_two + conv_branch
    stream_four = stream_three + half_ffn(stream_three, small_terms[3], ffb_in, ffb_out)
    return layer_norm(stream_four, small_terms[4])

def reference(features, cotangent, state_bank, state_source, master, left_stats, right_stats, left_root, right_root, small_params, decay_logs, state_mix):
    rounded = master.astype(jnp.bfloat16).astype(jnp.float32)
    inputs_full = features.astype(jnp.float32)
    first_rows = jnp.arange(ROWS, dtype=jnp.int32) // ROWS_DEV * ROWS_DEV
    state_rows = (first_rows + state_source).astype(jnp.int32)

    def forward(block_stack, small_terms, log_rates, mix_terms, inputs, bank_rows):
        weights = matrices(block_stack)
        decay_rates = jnp.exp(log_rates)
        positions = jnp.arange(FRAMES, dtype=jnp.float32)
        decay_now = jnp.exp(-decay_rates[:, :, None] * positions)
        decay_next = jnp.exp(-decay_rates[:, :, None] * (positions + 1.0))
        coupling = (mix_terms[0] * mix_terms[1]).reshape(HEADS, D // HEADS, NST)
        kernel = jnp.einsum('hdn,hnt->thd', coupling, decay_now, precision=precise).reshape(FRAMES, D)
        kernel_hat = jnp.fft.rfft(kernel, n=2 * FRAMES - 1, axis=0)
        starts = bank_rows[state_rows]

        def one_row(row_pair):
            return layer_row(weights, small_terms, kernel_hat, decay_next, mix_terms[1], row_pair[0], row_pair[1])
        return lax.map(jax.checkpoint(one_row), (inputs, starts))
    result, pull_back = jax.vjp(forward, rounded, small_params, decay_logs, state_mix, inputs_full, state_bank)
    grad_stack, grad_small, grad_decay, grad_mix, grad_features, grad_state = pull_back(cotangent.astype(jnp.float32))
    scaling = 1.0 / jnp.sqrt(jnp.float32(TOKENS))
    grad_stack = grad_stack * scaling
    grad_small = grad_small * scaling
    grad_decay = grad_decay * scaling
    grad_mix = grad_mix * scaling
    new_left = 0.5 * left_stats + 0.5 * jnp.einsum('bik,bjk->bij', grad_stack, grad_stack, precision=precise)
    new_right = 0.5 * right_stats + 0.5 * jnp.einsum('bki,bkj->bij', grad_stack, grad_stack, precision=precise)
    left_side = jnp.einsum('bij,bjk->bik', left_root, grad_stack, precision=precise)
    step_value = jnp.einsum('bik,bkl->bil', left_side, right_root, precision=precise)
    new_master = master - rate_blocks * step_value
    new_small = small_params - rate_small * grad_small
    new_decay = decay_logs - rate_small * grad_decay
    new_mix = state_mix - rate_small * grad_mix
    return (result.astype(jnp.bfloat16), grad_features, grad_state, grad_stack, new_left, new_right, new_master, new_master.astype(jnp.bfloat16), grad_small, new_small, grad_decay, grad_mix, new_decay, new_mix)
```

```python
from functools import partial
import math

import jax
import jax.numpy as jnp
from jax import lax
from jax.experimental import pallas as pl
from jax.experimental.pallas import tpu as pltpu
from jax.sharding import PartitionSpec as P

D = 512
FF = 2048
NST = 32
KW = 15
BS = 256
HEADS = 8
HALF = 64
LANES = 128
SUB = 16
PAD = 8
VMEM_BYTES = 60 * 1024 * 1024

rate_blocks = 0.1
rate_small = 0.5
bf16 = jnp.bfloat16
f32 = jnp.float32


def shape(dims, dtype=f32):
    return jax.ShapeDtypeStruct(dims, dtype)


def mm(a, b):
    return jnp.dot(a, b, preferred_element_type=f32)


def mm_nt(a, b):
    return lax.dot_general(a, b, (((1,), (1,)), ((), ())), preferred_element_type=f32)


def mm_tn(a, b):
    return lax.dot_general(a, b, (((0,), (0,)), ((), ())), preferred_element_type=f32)


def sigmoid(v):
    return 0.5 * jnp.tanh(0.5 * v) + 0.5


def norm(v):
    center = v - jnp.mean(v, axis=-1, keepdims=True)
    spread = jnp.mean(center * center, axis=-1, keepdims=True)
    inv = lax.rsqrt(spread + 1e-05)
    return center * inv, inv


def norm_back(hat, inv, scale, incoming):
    scaled = incoming * scale
    mean_one = jnp.mean(scaled, axis=-1, keepdims=True)
    mean_two = jnp.mean(scaled * hat, axis=-1, keepdims=True)
    return inv * (scaled - mean_one - hat * mean_two)


def fold8(v):
    return jnp.sum(v.reshape(-1, 8, v.shape[-1]), axis=0)


def load_matrices(stack, plan, sem):
    copies = []
    for first, dst in plan:
        down, across = dst.shape[0] // BS, dst.shape[1] // BS
        for i in range(down):
            for j in range(across):
                copies.append(
                    pltpu.make_async_copy(
                        stack.at[first + i * across + j],
                        dst.at[pl.ds(i * BS, BS), pl.ds(j * BS, BS)],
                        sem,
                    )
                )
    for copy in copies:
        copy.start()
    for copy in copies:
        copy.wait()


def store_blocks(acc, out, scaling, transposed=False):
    rows, cols = acc.shape
    if transposed:
        for i in range(cols // BS):
            for j in range(rows // BS):
                part = acc[pl.ds(j * BS, BS), pl.ds(i * BS, BS)] * scaling
                out[i * (rows // BS) + j] = part.T.astype(bf16)
    else:
        for i in range(rows // BS):
            for j in range(cols // BS):
                part = acc[pl.ds(i * BS, BS), pl.ds(j * BS, BS)] * scaling
                out[i * (cols // BS) + j] = part.astype(bf16)


def head_mask():
    row = lax.broadcasted_iota(jnp.int32, (HEADS * NST, D), 0) // NST
    col = lax.broadcasted_iota(jnp.int32, (HEADS * NST, D), 1) // HALF
    return (row == col).astype(f32)


def spread_heads(v, mask):
    return (jnp.concatenate([v] * HEADS, axis=0) * mask).astype(bf16)


def local_states(table, v, out):
    first = lax.broadcasted_iota(jnp.int32, (NST, LANES), 1) < HALF
    for g in range(D // LANES):
        both = mm(table[pl.ds(2 * NST * g, 2 * NST), :], v[:, g * LANES : (g + 1) * LANES])
        out[0, :, pl.ds(g * LANES, LANES)] = jnp.where(first, both[:NST], both[NST:])


def ffa_forward_kernel(feat, small, stack, mfin, x1_o, inner_o, act_o, u_o, f_o, wi, wo, wu, sem):
    @pl.when(pl.program_id(0) == 0)
    def _():
        ffn, mix = D // BS * (FF // BS), (D // BS) ** 2
        load_matrices(stack, ((0, wi), (ffn, wo), (4 * ffn, wu)), sem)

    x0 = feat[0].astype(f32)
    hat, unused = norm(x0)
    inner = mm((hat * small[0:1]).astype(bf16), wi[...])
    act = (inner * sigmoid(inner)).astype(bf16)
    inner_o[0] = inner.astype(bf16)
    act_o[0] = act
    x1 = x0 + 0.5 * mm(act, wo[...])
    x1_o[0] = x1
    hat, unused = norm(x1)
    u = mm((hat * small[1:2]).astype(bf16), wu[...]).astype(bf16)
    u_o[0] = u
    local_states(mfin, u, f_o)


def pack_heads(ref, rows):
    first = lax.broadcasted_iota(jnp.int32, (ref.shape[1], LANES), 1) < HALF
    low, high = [], []
    for p in range(rows // 2):
        a, b = ref[2 * p].astype(f32), ref[2 * p + 1].astype(f32)
        low.append(jnp.where(first, a, pltpu.roll(b, HALF, 1)).astype(bf16))
        high.append(jnp.where(first, pltpu.roll(a, HALF, 1), b).astype(bf16))
    return jnp.concatenate(low, axis=1), jnp.concatenate(high, axis=1)


def pack_params(v, rows):
    first = lax.broadcasted_iota(jnp.int32, v.shape, 1) < HALF
    rolled = pltpu.roll(v, HALF, 1)
    low = jnp.where(first, v, rolled)
    high = jnp.where(first, rolled, v)
    return (
        jnp.concatenate([low] * (rows // 2), axis=1),
        jnp.concatenate([high] * (rows // 2), axis=1),
    )


def unpack_pair(low, high, p):
    low = low[:, p * LANES : (p + 1) * LANES]
    high = high[:, p * LANES : (p + 1) * LANES]
    first = lax.broadcasted_iota(jnp.int32, low.shape, 1) < HALF
    return (
        jnp.where(first, low, pltpu.roll(high, HALF, 1)),
        jnp.where(first, pltpu.roll(low, HALF, 1), high),
    )


def conv_forward_kernel(u, m_tab, p_tab, coup, taps, y_o, pad):
    rows, frames = u.shape[0], u.shape[1]
    sub = frames // SUB
    coup_both = pack_params(coup[...], rows)
    packed = pack_heads(u, rows)
    results = []
    for h in range(2):
        states = mm(m_tab[h], packed[h])
        scaled = (states.reshape(sub, NST, -1) * coup_both[h][None]).reshape(states.shape)
        results.append(mm(p_tab[h], scaled.astype(bf16)))
    for p in range(rows // 2):
        one, two = unpack_pair(results[0], results[1], p)
        y_o[2 * p] = one
        y_o[2 * p + 1] = two
    pad[0:SUB] = jnp.zeros((SUB, LANES), f32)
    chunk = frames // 5
    for i in range(rows):
        pad[pl.ds(SUB, frames)] = u[i].astype(f32)
        for r in range(0, frames, chunk):
            acc = y_o[i, pl.ds(r, chunk)].reshape(-1, SUB, LANES)
            for d in range(SUB):
                piece = pad[pl.ds(SUB + r - d, chunk)].reshape(-1, SUB, LANES)
                acc = acc + piece * taps[d][None]
            y_o[i, pl.ds(r, chunk)] = acc.reshape(chunk, LANES)


def mixer_out_kernel(
    y, zin, x1, small, stack, pfull, ys_o, gated_o, x2_o, pw_o, g_o, wo, wp, mask, sem
):
    @pl.when(pl.program_id(0) == 0)
    def _():
        ffn, mix = D // BS * (FF // BS), (D // BS) ** 2
        load_matrices(stack, ((4 * ffn + mix, wo), (4 * ffn + 3 * mix, wp)), sem)
        mask[...] = head_mask()

    ys = (y[0] + mm(pfull[...], spread_heads(zin[0], mask[...]))).astype(bf16)
    ys_o[0] = ys
    gated = mm(ys, wo[...])
    gated_o[0] = gated.astype(bf16)
    x2 = x1[0] + gated[:, :D] * sigmoid(gated[:, D:])
    x2_o[0] = x2
    hat, unused = norm(x2)
    pw = mm((hat * small[2:3]).astype(bf16), wp[...])
    pw_o[0] = pw.astype(bf16)
    g_o[0] = (pw[:, :D] * sigmoid(pw[:, D:])).astype(bf16)


def fill_pad(pad, low, body, high):
    frames = body.shape[0]
    for g in range(D // LANES):
        lanes = slice(g * LANES, (g + 1) * LANES)
        pad[g, 0:PAD] = low[:, lanes].astype(f32)
        pad[g, pl.ds(PAD, frames)] = body[:, lanes].astype(f32)
        pad[g, pl.ds(PAD + frames, PAD)] = high[:, lanes].astype(f32)


def ffb_kernel(
    g, low, high, x2, cot, small, stack, scale,
    out_o, dx3_o, dq_o, gin_o, gout_o, gq_o, gain_o,
    wi, wo, wq, acc_in, acc_out, acc_q, pad, q_s, sem,
):
    step = pl.program_id(0)
    frames = g.shape[1]

    @pl.when(step == 0)
    def _():
        ffn, mix = D // BS * (FF // BS), (D // BS) ** 2
        load_matrices(stack, ((2 * ffn, wi), (3 * ffn, wo), (4 * ffn + 5 * mix, wq)), sem)
        acc_in[...] = jnp.zeros_like(acc_in)
        acc_out[...] = jnp.zeros_like(acc_out)
        acc_q[...] = jnp.zeros_like(acc_q)
        gain_o[...] = jnp.zeros_like(gain_o)

    fill_pad(pad, low[0], g[0], high[0])
    chunk = frames // 5
    for c in range(D // LANES):
        lanes = slice(c * LANES, (c + 1) * LANES)
        for r in range(0, frames, chunk):
            acc = small[5:6, lanes] * pad[c, pl.ds(r + PAD - 7, chunk)]
            for j in range(1, KW):
                acc = acc + small[5 + j : 6 + j, lanes] * pad[c, pl.ds(r + j + PAD - 7, chunk)]
            q_s[pl.ds(r, chunk), lanes] = acc
    q = q_s[...]
    sig_q = sigmoid(q)
    act_q = q * sig_q
    a3 = act_q.astype(bf16)
    x3 = x2[0] + mm(a3, wq[...])
    hat3, inv3 = norm(x3)
    n3 = (hat3 * small[3:4]).astype(bf16)
    inner = mm(n3, wi[...])
    sig = sigmoid(inner)
    act = inner * sig
    b4 = act.astype(bf16)
    x4 = x3 + 0.5 * mm(b4, wo[...])
    hat4, inv4 = norm(x4)
    out_o[0] = (hat4 * small[4:5]).astype(bf16)
    c4 = cot[0].astype(f32)
    gain_o[1] += fold8(c4 * hat4)
    dx4 = norm_back(hat4, inv4, small[4:5], c4)
    dp = (0.5 * dx4).astype(bf16)
    acc_out[...] += mm_tn(dp, b4)
    dact = mm_nt(dp, wo[...])
    dinner = ((sig + act * (1.0 - sig)) * dact).astype(bf16)
    acc_in[...] += mm_tn(n3, dinner)
    dn3 = mm_nt(dinner, wi[...])
    gain_o[0] += fold8(dn3 * hat3)
    dx3 = dx4 + norm_back(hat3, inv3, small[3:4], dn3)
    dx3_o[0] = dx3
    dpq = dx3.astype(bf16)
    acc_q[...] += mm_tn(a3, dpq)
    da3 = mm_nt(dpq, wq[...])
    dq_o[0] = ((sig_q + act_q * (1.0 - sig_q)) * da3).astype(bf16)

    @pl.when(step == pl.num_programs(0) - 1)
    def _():
        store_blocks(acc_in, gin_o, scale)
        store_blocks(acc_out, gout_o, scale, transposed=True)
        store_blocks(acc_q, gq_o, scale)


def mixer_back_kernel(
    dq, dlow, dhigh, g, glow, ghigh, pw, x2, gated, ys, dx3, small, stack, pfull_t, scale,
    dx2_o, dy_o, gst_o, gp_o, go_o, gain_o, dk_o,
    wo, wp, acc_p, acc_o, dpad, gpad, dg_s, dk_s, sem,
):
    step = pl.program_id(0)
    frames = dq.shape[1]

    @pl.when(step == 0)
    def _():
        ffn, mix = D // BS * (FF // BS), (D // BS) ** 2
        load_matrices(stack, ((4 * ffn + mix, wo), (4 * ffn + 3 * mix, wp)), sem)
        acc_p[...] = jnp.zeros_like(acc_p)
        acc_o[...] = jnp.zeros_like(acc_o)
        gain_o[...] = jnp.zeros_like(gain_o)
        dk_s[...] = jnp.zeros_like(dk_s)

    fill_pad(dpad, dlow[0], dq[0], dhigh[0])
    fill_pad(gpad, glow[0], g[0], ghigh[0])
    chunk = frames // 5
    for c in range(D // LANES):
        lanes = slice(c * LANES, (c + 1) * LANES)
        for r in range(0, frames, chunk):
            here = dpad[c, pl.ds(r + PAD, chunk)]
            acc = small[5:6, lanes] * dpad[c, pl.ds(r + PAD + 7, chunk)]
            for j in range(1, KW):
                acc = acc + small[5 + j : 6 + j, lanes] * dpad[c, pl.ds(r - j + PAD + 7, chunk)]
            dg_s[pl.ds(r, chunk), lanes] = acc
            for j in range(KW):
                dk_s[j, :, lanes] += fold8(here * gpad[c, pl.ds(r + j + PAD - 7, chunk)])
    dg = dg_s[...]
    value = pw[0, :, :D].astype(f32)
    gate = sigmoid(pw[0, :, D:].astype(f32))
    dvalue = (dg * gate).astype(bf16)
    dgate = (dg * value * gate * (1.0 - gate)).astype(bf16)
    dpw = jnp.concatenate([dvalue, dgate], axis=1)
    hat2, inv2 = norm(x2[0])
    n2 = (hat2 * small[2:3]).astype(bf16)
    acc_p[...] += mm_tn(n2, dpw)
    dn2 = mm_nt(dpw, wp[...])
    gain_o[...] += fold8(dn2 * hat2)
    dx2 = dx3[0] + norm_back(hat2, inv2, small[2:3], dn2)
    dx2_o[0] = dx2
    value = gated[0, :, :D].astype(f32)
    gate = sigmoid(gated[0, :, D:].astype(f32))
    dvalue = (dx2 * gate).astype(bf16)
    dgate = (dx2 * value * gate * (1.0 - gate)).astype(bf16)
    dgated = jnp.concatenate([dvalue, dgate], axis=1)
    acc_o[...] += mm_tn(ys[0], dgated)
    dy = mm_nt(dgated, wo[...]).astype(bf16)
    dy_o[0] = dy
    local_states(pfull_t, dy, gst_o)

    @pl.when(step == pl.num_programs(0) - 1)
    def _():
        store_blocks(acc_p, gp_o, scale)
        store_blocks(acc_o, go_o, scale)
        for j in range(KW):
            dk_o[j : j + 1] = jnp.sum(dk_s[j], axis=0, keepdims=True)


def conv_back_kernel(
    u, dy, m_tab, mp_tab, pt_tab, ptp_tab, mt_tab, coup, taps,
    du_o, t1_o, t2_o, fp_o, gp_o, dk_o,
    upad, dpad, acc_s,
):
    rows, frames = u.shape[0], u.shape[1]
    sub = frames // SUB
    last = (sub - 1) * NST
    coup_both = pack_params(coup[...], rows)
    u_both = pack_heads(u, rows)
    d_both = pack_heads(dy, rows)
    du, first_sum, second_sum, end_u, end_d = [], [], [], [], []
    for h in range(2):
        states = mm(m_tab[h], u_both[h])
        states_w = mm(mp_tab[h], u_both[h])
        back = mm(pt_tab[h], d_both[h])
        back_w = mm(ptp_tab[h], d_both[h])
        end_u.append(states_w[last:])
        end_d.append(back_w[last:])
        s3 = states[:last].reshape(sub - 1, NST, -1)
        b3 = back[:last].reshape(sub - 1, NST, -1)
        sw3 = states_w[:last].reshape(sub - 1, NST, -1)
        bw3 = back_w[:last].reshape(sub - 1, NST, -1)
        first_sum.append(jnp.sum(s3 * b3, axis=0))
        second_sum.append(jnp.sum(bw3 * s3 + b3 * sw3, axis=0))
        grads = (back.reshape(sub, NST, -1) * coup_both[h][None]).reshape(back.shape)
        du.append(mm(mt_tab[h], grads.astype(bf16)))
    first = lax.broadcasted_iota(jnp.int32, (NST, LANES), 1) < HALF
    for sums, out in ((first_sum, t1_o), (second_sum, t2_o)):
        both = []
        for v in sums:
            total = v[:, :LANES]
            for p in range(1, rows // 2):
                total = total + v[:, p * LANES : (p + 1) * LANES]
            both.append(total + pltpu.roll(total, HALF, 1))
        out[...] = jnp.where(first, both[0], both[1])
    for p in range(rows // 2):
        for pair, out in ((du, du_o), (end_u, fp_o), (end_d, gp_o)):
            one, two = unpack_pair(pair[0], pair[1], p)
            out[2 * p] = one
            out[2 * p + 1] = two
    chunk = frames // 5
    upad[0:SUB] = jnp.zeros((SUB, LANES), f32)
    dpad[pl.ds(frames, SUB)] = jnp.zeros((SUB, LANES), f32)
    acc_s[...] = jnp.zeros_like(acc_s)
    for i in range(rows):
        upad[pl.ds(SUB, frames)] = u[i].astype(f32)
        dpad[pl.ds(0, frames)] = dy[i].astype(f32)
        for r in range(0, frames, chunk):
            acc = du_o[i, pl.ds(r, chunk)].reshape(-1, SUB, LANES)
            here = dpad[pl.ds(r, chunk)]
            for d in range(SUB):
                piece = dpad[pl.ds(r + d, chunk)].reshape(-1, SUB, LANES)
                acc = acc + piece * taps[d][None]
                product = (here * upad[pl.ds(SUB + r - d, chunk)]).reshape(-1, SUB, LANES)
                acc_s[d] += jnp.sum(product, axis=0)
            du_o[i, pl.ds(r, chunk)] = acc.reshape(chunk, LANES)
    place = lax.broadcasted_iota(jnp.int32, (SUB, LANES), 0)
    for d in range(SUB):
        kept = jnp.where(place >= d, acc_s[d], 0.0)
        dk_o[d : d + 1] = jnp.sum(kept, axis=0, keepdims=True)


def ffa_back_kernel(
    du_loc, lam, x1, feat, inner_r, act_r, dx2, small, stack, mfin_t, scale,
    dx0_o, gin_o, gout_o, gu_o, gain_o,
    wi, wo, wu, acc_in, acc_out, acc_u, mask, sem,
):
    step = pl.program_id(0)

    @pl.when(step == 0)
    def _():
        ffn, mix = D // BS * (FF // BS), (D // BS) ** 2
        load_matrices(stack, ((0, wi), (ffn, wo), (4 * ffn, wu)), sem)
        mask[...] = head_mask()
        acc_in[...] = jnp.zeros_like(acc_in)
        acc_out[...] = jnp.zeros_like(acc_out)
        acc_u[...] = jnp.zeros_like(acc_u)
        gain_o[...] = jnp.zeros_like(gain_o)

    du = (du_loc[0] + mm(mfin_t[...], spread_heads(lam[0], mask[...]))).astype(bf16)
    hat1, inv1 = norm(x1[0])
    n1 = (hat1 * small[1:2]).astype(bf16)
    acc_u[...] += mm_tn(n1, du)
    dn1 = mm_nt(du, wu[...])
    gain_o[1] += fold8(dn1 * hat1)
    dx1 = dx2[0] + norm_back(hat1, inv1, small[1:2], dn1)
    dp = (0.5 * dx1).astype(bf16)
    acc_out[...] += mm_tn(dp, act_r[0])
    dact = mm_nt(dp, wo[...])
    inner = inner_r[0].astype(f32)
    sig = sigmoid(inner)
    dinner = ((sig + inner * sig * (1.0 - sig)) * dact).astype(bf16)
    hat0, inv0 = norm(feat[0].astype(f32))
    n0 = (hat0 * small[0:1]).astype(bf16)
    acc_in[...] += mm_tn(n0, dinner)
    dn0 = mm_nt(dinner, wi[...])
    gain_o[0] += fold8(dn0 * hat0)
    dx0_o[0] = dx1 + norm_back(hat0, inv0, small[0:1], dn0)

    @pl.when(step == pl.num_programs(0) - 1)
    def _():
        store_blocks(acc_in, gin_o, scale)
        store_blocks(acc_out, gout_o, scale, transposed=True)
        store_blocks(acc_u, gu_o, scale)


def shampoo_kernel(
    pick, owned, full, left, right, lroot, rroot, master, nl_o, nr_o, nm_o, nc_o, own_o
):
    for i in range(full.shape[0]):
        whole = full[i]
        mine = owned[i]
        own_o[i] = mine.astype(f32)
        nl_o[i] = 0.5 * left[i] + 0.5 * mm_nt(mine, whole)
        columns = mm_nt(pick[...], whole).astype(bf16)
        nr_o[i] = 0.5 * right[i] + 0.5 * mm(columns, whole)
        side = mm(lroot[i].astype(bf16), whole)
        step = mm(side.astype(bf16), rroot[i].astype(bf16))
        new = master[i] - rate_blocks * step
        nm_o[i] = new
        nc_o[i] = new.astype(bf16)


def peers():
    place, row = lax.axis_index("tm"), lax.axis_index("rows")
    return place, row // 2, row % 2


def square(place):
    x, y = place % 2, place // 2
    return 2 * y + 1 - x, 2 * (1 - y) + x, 2 * (1 - y) + 1 - x


def at(place, level, core):
    return {"tm": place, "rows": level * 2 + core}


def remote(src, dst, send, recv, device):
    return pltpu.make_async_remote_copy(
        src_ref=src,
        dst_ref=dst,
        send_sem=send,
        recv_sem=recv,
        device_id=device,
        device_id_type=pl.DeviceIdType.MESH,
    )


def signal(sem, device):
    pl.semaphore_signal(sem, inc=1, device_id=device, device_id_type=pl.DeviceIdType.MESH)


def chunk_ranges(count, chunks):
    edges = [count * c // chunks for c in range(chunks + 1)]
    out = []
    for first, end in zip(edges[:-1], edges[1:]):
        middle = (first + end + 1) // 2
        out.append((first, end, middle))
    return out


def gather_kernel(
    levels, piece, pack, stack, pack_all, own_sem, pk_send, pk_recv,
    z_send, z_recv, x_send, x_recv, y_send, y_recv, c_send, c_recv,
):
    place, level, core = peers()
    count = piece.shape[0]
    xp, yp, dp = others = square(place)
    up, down = level < levels - 1, level > 0
    barrier = pltpu.get_barrier_semaphore()
    for other in (xp, yp, dp):
        signal(barrier, at(other, level, core))
    signal(barrier, at(place, level, 1 - core))

    @pl.when(up)
    def _():
        signal(barrier, at(place, level + 1, core))

    @pl.when(down)
    def _():
        signal(barrier, at(place, level - 1, core))

    below = (level + levels - 1) // levels
    above = (2 * levels - 2 - level) // levels
    pl.semaphore_wait(barrier, 4 + below + above)

    sends = []
    own = pltpu.make_async_copy(piece, stack.at[place, :, level, core], own_sem)
    own.start()
    own_pack = pltpu.make_async_copy(pack, pack_all.at[place], pk_send.at[3])
    own_pack.start()
    ranges = chunk_ranges(count, z_send.shape[0])

    def z_copy(c, side, s):
        first, end, unused = ranges[c]
        step = 1 if side == 0 else -1
        origin = level - s * step
        spot = stack.at[place, pl.ds(first, end - first), origin, core]
        src = piece.at[pl.ds(first, end - first)] if s == 0 else spot
        return remote(
            src, spot, z_send.at[c, side, s], z_recv.at[c, side, s], at(place, (level + step + levels) % levels, core)
        )

    def z_ok(side, s):
        if side == 0:
            return jnp.logical_and(level - s >= 0, level + 1 < levels)
        return jnp.logical_and(level + s < levels, level - 1 >= 0)

    def z_in(side, s):
        if side == 0:
            return level - s - 1 >= 0
        return level + s + 1 < levels

    for c in range(len(ranges)):
        for side in range(2):
            pl.when(z_ok(side, 0))(lambda c=c, side=side: z_copy(c, side, 0).start())
        if c == 0:
            for d in range(1, 4):
                copy = remote(
                    pack,
                    pack_all.at[place],
                    pk_send.at[d - 1],
                    pk_recv.at[d - 1],
                    at(others[d - 1], level, core),
                )
                copy.start()
                sends.append(copy)
    own.wait()
    own_pack.wait()

    def part(owner, first, end):
        return stack.at[owner, pl.ds(first, end - first), :, core]

    def to_x(c, i, owner, first, end):
        return remote(
            part(owner, first, end), part(owner, first, end),
            x_send.at[c, i], x_recv.at[c, i], at(xp, level, core),
        )

    def to_y(c, i, owner, first, end):
        return remote(
            part(owner, first, end), part(owner, first, end),
            y_send.at[c, i], y_recv.at[c, i], at(yp, level, core),
        )

    def to_core(c, i, owner, first, end):
        return remote(
            part(owner, first, end), part(owner, first, end),
            c_send.at[c, i], c_recv.at[c, i], at(place, level, 1 - core),
        )

    def go(copy):
        copy.start()
        sends.append(copy)
        return copy

    moved = []

    def z_phase(c):
        for s in range(levels - 1):
            for side in range(2):

                def step(c=c, side=side, s=s):
                    z_copy(c, side, s).wait_recv()
                    if s + 1 < levels - 1:
                        pl.when(z_ok(side, s + 1))(lambda: z_copy(c, side, s + 1).start())

                pl.when(z_in(side, s))(step)

    def spread(c):
        first, end, middle = ranges[c]
        out = (
            go(to_x(c, 0, place, first, middle)),
            go(to_y(c, 0, place, middle, end)),
            go(to_x(c, 1, place, middle, end)),
            go(to_y(c, 1, place, first, middle)),
        )
        moved.append(go(to_core(c, 0, place, first, end)))
        return out

    def forward(c, copies):
        first, end, middle = ranges[c]
        copies[0].wait_recv()
        y_in = go(to_y(c, 2, xp, first, middle))
        copies[1].wait_recv()
        x_in = go(to_x(c, 2, yp, middle, end))
        moved.append(go(to_core(c, 1, xp, first, middle)))
        moved.append(go(to_core(c, 2, yp, middle, end)))
        copies[2].wait_recv()
        moved.append(go(to_core(c, 3, xp, middle, end)))
        copies[3].wait_recv()
        moved.append(go(to_core(c, 4, yp, first, middle)))
        return y_in, x_in

    def finish(c, copies):
        first, end, middle = ranges[c]
        copies[0].wait_recv()
        moved.append(go(to_core(c, 5, dp, first, middle)))
        copies[1].wait_recv()
        moved.append(go(to_core(c, 6, dp, middle, end)))

    out = {}
    for c in range(len(ranges)):
        z_phase(c)
        mine = spread(c)
        if c >= 1:
            out[c - 1] = forward(c - 1, out[c - 1])
        out[c] = mine
        if c >= 2:
            finish(c - 2, out[c - 2])
    last = len(ranges) - 1
    out[last] = forward(last, out[last])
    for c in range(max(last - 1, 0), last + 1):
        finish(c, out[c])
    for copy in moved:
        copy.wait_recv()
    for copy in sends[:3]:
        copy.wait_recv()
    for copy in sends:
        copy.wait_send()
    for c in range(len(ranges)):
        for side in range(2):
            for s in range(levels - 1):
                pl.when(z_ok(side, s))(lambda c=c, side=side, s=s: z_copy(c, side, s).wait_send())


def gather_weights(piece, pack, parts, devices, chunks=2):
    count, slab, cols = piece.shape
    if parts != 4:
        stack = lax.all_gather(lax.all_gather(piece, "rows", axis=1, tiled=True), "tm", axis=0)
        return stack.reshape(-1, BS, BS), lax.all_gather(pack, "tm", axis=0)
    levels = devices // 2
    dma = lambda *dims: pltpu.SemaphoreType.DMA(dims)
    stack, pack_all = pl.pallas_call(
        partial(gather_kernel, levels),
        in_specs=[ANY, ANY],
        out_specs=[ANY, ANY],
        out_shape=[
            shape((parts, count, levels, 2, slab, cols), piece.dtype),
            shape((parts,) + pack.shape, pack.dtype),
        ],
        scratch_shapes=[
            pltpu.SemaphoreType.DMA,
            dma(4), dma(3),
            dma(chunks, 2, levels - 1), dma(chunks, 2, levels - 1),
            dma(chunks, 3), dma(chunks, 3),
            dma(chunks, 3), dma(chunks, 3),
            dma(chunks, 7), dma(chunks, 7),
        ],
        compiler_params=pltpu.CompilerParams(
            collective_id=1, has_side_effects=True, vmem_limit_bytes=VMEM_BYTES
        ),
        name="gather_weights",
    )(piece, pack)
    return stack.reshape(-1, BS, BS), pack_all


def reduce_kernel(
    levels, grads, small, full, owned, small_sum,
    mine, came, from_x, from_y, red, z_in, s_tm, s_core, s_z,
    load_sem, c_send, c_recv, x_send, x_recv, y_send, y_recv,
    z_send, z_recv, a_send, a_recv, f_send, f_recv, s_send, s_recv, put_sem,
):
    place, level, core = peers()
    count = grads.shape[1]
    xp, yp, dp = others = square(place)
    barrier = pltpu.get_barrier_semaphore()
    for other in (xp, yp, dp):
        signal(barrier, at(other, level, core))
    signal(barrier, at(place, level, 1 - core))
    for d in range(1, levels):
        signal(barrier, at(place, (level + d) % levels, core))
    pl.semaphore_wait(barrier, 4 + levels - 1)
    ranges = chunk_ranges(count, c_send.shape[0])
    sends = []

    def go(copy):
        copy.start()
        sends.append(copy)
        return copy

    def over(ref, first, end):
        return ref.at[:, pl.ds(first, end - first)]

    loads, core_in = [], []
    for c, (first, end, unused) in enumerate(ranges):
        core_in.append(
            go(
                remote(
                    over(grads, first, end).at[:, :, :, 1 - core],
                    over(came, first, end),
                    c_send.at[c],
                    c_recv.at[c],
                    at(place, level, 1 - core),
                )
            )
        )
        load = pltpu.make_async_copy(
            over(grads, first, end).at[:, :, :, core], over(mine, first, end), load_sem.at[c]
        )
        load.start()
        loads.append(load)

    small_in = []
    for d in range(1, 4):
        small_in.append(
            go(
                remote(
                    small.at[others[d - 1]], s_tm.at[d - 1], s_send.at[d - 1], s_recv.at[d - 1],
                    at(others[d - 1], level, core),
                )
            )
        )
    for copy in small_in:
        copy.wait_recv()
    s_core[0] = small[place] + (s_tm[0] + s_tm[1]) + s_tm[2]
    swap = go(
        remote(s_core.at[0], s_core.at[1], s_send.at[3], s_recv.at[3], at(place, level, 1 - core))
    )

    def add_core(owner, first, end):
        def one(k, carry):
            total = mine[owner, k].astype(f32) + came[owner, k].astype(f32)
            mine[owner, k] = total.astype(bf16)
            return carry

        lax.fori_loop(first, end, one, 0)

    def add_into(owner, ref, slot, first, end):
        def one(k, carry):
            total = mine[owner, k].astype(f32) + ref[slot, k].astype(f32)
            mine[owner, k] = total.astype(bf16)
            return carry

        lax.fori_loop(first, end, one, 0)

    def to_x(c, i, owner, slot, first, end):
        n = pl.ds(first, end - first)
        return go(
            remote(
                mine.at[owner, n], from_x.at[slot, n], x_send.at[c, i], x_recv.at[c, i],
                at(xp, level, core),
            )
        )

    def to_y(c, i, owner, slot, first, end):
        n = pl.ds(first, end - first)
        return go(
            remote(
                mine.at[owner, n], from_y.at[slot, n], y_send.at[c, i], y_recv.at[c, i],
                at(yp, level, core),
            )
        )

    def begin(c):
        first, end, middle = ranges[c]
        loads[c].wait()
        core_in[c].wait_recv()
        add_core(dp, first, end)
        x_one = to_x(c, 0, dp, 0, first, middle)
        y_one = to_y(c, 0, dp, 0, middle, end)
        add_core(xp, first, end)
        x_two = to_x(c, 1, xp, 1, first, middle)
        add_core(yp, first, end)
        y_two = to_y(c, 1, yp, 1, middle, end)
        add_core(place, first, end)
        return x_one, y_one, x_two, y_two

    def second(c, copies):
        first, end, middle = ranges[c]
        copies[0].wait_recv()
        add_into(yp, from_x, 0, first, middle)
        y_three = to_y(c, 2, yp, 1, first, middle)
        copies[1].wait_recv()
        add_into(xp, from_y, 0, middle, end)
        x_three = to_x(c, 2, xp, 1, middle, end)
        return copies[2], copies[3], x_three, y_three

    def along(c, copies):
        first, end, middle = ranges[c]
        for copy in copies:
            copy.wait_recv()

        def one(k, carry):
            total = mine[place, k].astype(f32) + from_x[1, k].astype(f32)
            red[k] = (total + from_y[1, k].astype(f32)).astype(bf16)
            return carry

        lax.fori_loop(first, end, one, 0)
        out = []
        n = pl.ds(first, end - first)
        for d in range(1, levels):
            target = (level + d) % levels
            out.append(
                go(
                    remote(
                        red.at[n, target], z_in.at[d - 1, n], z_send.at[c, d - 1],
                        z_recv.at[c, d - 1], at(place, target, core),
                    )
                )
            )
        return out

    def settle(c, copies):
        first, end, middle = ranges[c]
        for copy in copies:
            copy.wait_recv()

        def one(k, carry):
            total = red[k, level].astype(f32)
            for d in range(levels - 1):
                total = total + z_in[d, k].astype(f32)
            owned[k] = total.astype(bf16)
            return carry

        lax.fori_loop(first, end, one, 0)
        n = pl.ds(first, end - first)
        out = []
        for d in range(1, levels):
            target = (level + d) % levels
            out.append(
                go(
                    remote(
                        owned.at[n], full.at[n, level, core], a_send.at[c, d - 1],
                        a_recv.at[c, d - 1], at(place, target, core),
                    )
                )
            )
        put = pltpu.make_async_copy(owned.at[n], full.at[n, level, core], put_sem.at[c])
        put.start()
        sibling = go(
            remote(
                owned.at[n], full.at[n, level, core], f_send.at[c, 0], f_recv.at[c, 0],
                at(place, level, 1 - core),
            )
        )
        return out, put, [sibling]

    def share(c, state):
        first, end, middle = ranges[c]
        n = pl.ds(first, end - first)
        copies, put, passed = state
        for d in range(1, levels):
            copies[d - 1].wait_recv()
            source = (level + levels - d) % levels
            passed.append(
                go(
                    remote(
                        full.at[n, source, core], full.at[n, source, core], f_send.at[c, d],
                        f_recv.at[c, d], at(place, level, 1 - core),
                    )
                )
            )
        put.wait()
        return passed

    chunks = len(ranges)
    state = [begin(0)]
    swap.wait_recv()
    s_z[level] = s_core[0] + s_core[1]
    small_z = []
    for d in range(1, levels):
        target = (level + d) % levels
        small_z.append(
            go(
                remote(
                    s_z.at[level], s_z.at[level], s_send.at[3 + d], s_recv.at[3 + d],
                    at(place, target, core),
                )
            )
        )
    for c in range(1, chunks):
        state.append(begin(c))
        state[c - 1] = second(c - 1, state[c - 1])
        if c >= 2:
            state[c - 2] = along(c - 2, state[c - 2])
        if c >= 3:
            state[c - 3] = settle(c - 3, state[c - 3])
    state[chunks - 1] = second(chunks - 1, state[chunks - 1])
    for c in range(max(chunks - 2, 0), chunks):
        state[c] = along(c, state[c])
    for c in range(max(chunks - 3, 0), chunks):
        state[c] = settle(c, state[c])
    passed = []
    for c in range(chunks):
        passed += share(c, state[c])
    for copy in small_z:
        copy.wait_recv()
    total = s_z[0]
    for i in range(1, levels):
        total = total + s_z[i]
    small_sum[...] = total
    for copy in passed:
        copy.wait_recv()
    for copy in sends:
        copy.wait_send()


def reduce_grads(grads, small, parts, devices, slab, chunks=2):
    if parts != 4:
        owned = lax.psum_scatter(grads, "tm", scatter_dimension=0, tiled=True)
        owned = lax.psum_scatter(owned, "rows", scatter_dimension=1, tiled=True)
        full = lax.all_gather(owned, "rows", axis=1, tiled=True)
        small = lax.psum_scatter(small, "tm", scatter_dimension=0, tiled=True)[0]
        return full, owned, lax.psum(small, "rows")
    levels = devices // 2
    count = grads.shape[0] // parts
    grads = grads.reshape(parts, count, levels, 2, slab, BS)
    dma = lambda *dims: pltpu.SemaphoreType.DMA(dims)
    vb = lambda *dims: pltpu.VMEM(dims, bf16)
    vmem = pl.BlockSpec(memory_space=pltpu.VMEM)
    part = small.shape[1:]
    full, owned, small_sum = pl.pallas_call(
        partial(reduce_kernel, levels),
        in_specs=[ANY, vmem],
        out_specs=[ANY, vmem, vmem],
        out_shape=[
            shape((count, levels, 2, slab, BS), bf16),
            shape((count, slab, BS), bf16),
            shape(part),
        ],
        scratch_shapes=[
            vb(parts, count, levels, slab, BS), vb(parts, count, levels, slab, BS),
            vb(2, count, levels, slab, BS), vb(2, count, levels, slab, BS),
            vb(count, levels, slab, BS), vb(levels - 1, count, slab, BS),
            vm(3, *part), vm(2, *part), vm(levels, *part),
            dma(chunks), dma(chunks), dma(chunks),
            dma(chunks, 3), dma(chunks, 3), dma(chunks, 3), dma(chunks, 3),
            dma(chunks, levels - 1), dma(chunks, levels - 1),
            dma(chunks, levels - 1), dma(chunks, levels - 1),
            dma(chunks, levels), dma(chunks, levels),
            dma(3 + levels), dma(3 + levels), dma(chunks),
        ],
        compiler_params=pltpu.CompilerParams(
            collective_id=2, has_side_effects=True, vmem_limit_bytes=VMEM_BYTES
        ),
        name="reduce_grads",
    )(grads, small)
    return full.reshape(count, BS, BS), owned, small_sum


def row_spec(frames, width):
    return pl.BlockSpec((1, frames, width), lambda i: (i, 0, 0))


def whole_spec(*dims):
    return pl.BlockSpec(dims, lambda i: (0,) * len(dims))


ANY = pl.BlockSpec(memory_space=pl.ANY)
PARAMS = pltpu.CompilerParams(
    dimension_semantics=("arbitrary",), vmem_limit_bytes=VMEM_BYTES
)


def cost(flops, moved):
    return pl.CostEstimate(flops=int(flops), bytes_accessed=int(moved), transcendentals=0)


def vm(*dims, dtype=f32):
    return pltpu.VMEM(dims, dtype)


def exchange_edges(v, axis):
    count = lax.axis_size(axis)
    forward = [(i, i + 1) for i in range(count - 1)]
    backward = [(target, source) for source, target in forward]
    low = lax.ppermute(v[:, -PAD:], axis, forward)
    high = lax.ppermute(v[:, :PAD], axis, backward)
    return low, high


def body(
    features,
    cotangent,
    state_bank,
    state_source,
    master,
    left_stats,
    right_stats,
    left_root,
    right_root,
    small_params,
    decay_logs,
    state_mix,
):
    rows, frames, width = features.shape
    tokens = rows * frames
    parts = lax.axis_size("tm")
    place = lax.axis_index("tm")
    scaling = 1.0 / math.sqrt(tokens * parts * lax.axis_size("rows"))
    sub = frames // SUB
    ffn, mix = D // BS * (FF // BS), (D // BS) ** 2

    own_heads, own_channels = decay_logs.shape[0], state_mix.shape[1]
    starts_own = state_bank[state_source]
    flat = jnp.concatenate(
        [decay_logs.reshape(-1), state_mix.reshape(-1), starts_own.reshape(-1)]
    )
    cut_one = own_heads * NST
    cut_two = cut_one + 2 * own_channels * NST
    cut_three = cut_two + rows * own_channels * NST
    flat = jnp.pad(flat, (0, -cut_three % (8 * LANES))).reshape(-1, LANES)
    stack, packed = gather_weights(
        master.astype(bf16), flat, parts, lax.axis_size("rows")
    )
    packed = packed.reshape(parts, -1)
    logs = packed[:, :cut_one].reshape(HEADS, NST)
    mix_all = packed[:, cut_one:cut_two].reshape(parts, 2, own_channels, NST)
    mix_all = mix_all.transpose(1, 3, 0, 2).reshape(2, NST, D)
    starts = packed[:, cut_two:cut_three].reshape(parts, rows, own_channels, NST)
    starts = starts.transpose(1, 3, 0, 2).reshape(rows, NST, D)

    rates = jnp.exp(logs)
    rate_nc = jnp.repeat(rates.T, HALF, axis=1)
    coupling = mix_all[0] * mix_all[1]
    column = jnp.arange(sub * NST, dtype=jnp.int32)
    end_of = (column // NST + 1) * SUB
    rate_col = jnp.tile(rates, (1, sub))
    time = jnp.arange(frames, dtype=jnp.int32)
    age = end_of[:, None] - 1 - time[None, :]
    ok = age >= 0
    age_f = jnp.maximum(age, 0).astype(f32)
    m_f = jnp.where(ok, jnp.exp(-rate_col[:, :, None] * age_f), 0.0)
    m_tab = m_f.astype(bf16)
    mp_tab = (m_f * age_f).astype(bf16)
    age_t = end_of[None, :] - 1 - time[:, None]
    mt_tab = jnp.where(
        age_t >= 0, jnp.exp(-rate_col[:, None, :] * jnp.maximum(age_t, 0).astype(f32)), 0.0
    ).astype(bf16)
    since_t = (time % SUB + 1).astype(f32)
    inside = (time // SUB)[:, None] == (column // NST + 1)[None, :]
    p_tab = jnp.where(
        inside, jnp.exp(-rate_col[:, None, :] * since_t[:, None]), 0.0
    ).astype(bf16)
    inside_t = (time // SUB)[None, :] == (column // NST + 1)[:, None]
    final = (column // NST == sub - 1)[:, None]
    since = jnp.where(final, (time + 1).astype(f32)[None, :], since_t[None, :])
    pt_f = jnp.where(inside_t | final, jnp.exp(-rate_col[:, :, None] * since), 0.0)
    pt_tab = jnp.where(final, 0.0, pt_f).astype(bf16)
    ptp_tab = (pt_f * since).astype(bf16)
    flat = rates.reshape(-1)
    next_t = (time + 1).astype(f32)
    left_t = (frames - 1 - time).astype(f32)
    pfull = jnp.exp(-flat[None, :] * next_t[:, None]).astype(bf16)
    pfull_t = jnp.exp(-flat[:, None] * next_t[None, :]).astype(bf16)
    mfin = jnp.exp(-flat[:, None] * left_t[None, :]).astype(bf16)
    mfin_t = jnp.exp(-flat[None, :] * left_t[:, None]).astype(bf16)
    lag = jnp.arange(SUB, dtype=f32)
    lag_decay = jnp.exp(-rate_nc[None] * lag[:, None, None])
    kernel_lags = jnp.sum(coupling[None] * lag_decay, axis=1)
    slot = jnp.arange(SUB, dtype=jnp.int32)
    taps_f = jnp.where(slot[:, None, None] <= slot[None, :, None], kernel_lags[:, None, :], 0.0)
    taps_b = jnp.where(
        slot[:, None, None] + slot[None, :, None] < SUB, kernel_lags[:, None, :], 0.0
    )

    mat = lambda r, c: vm(r, c, dtype=bf16)
    dma = pltpu.SemaphoreType.DMA
    small_spec = whole_spec(*small_params.shape)
    state_spec = pl.BlockSpec((1, NST, D), lambda i: (i, 0, 0))
    x1, inner_a, act_a, u, ends = pl.pallas_call(
        ffa_forward_kernel,
        grid=(rows,),
        in_specs=[row_spec(frames, D), small_spec, ANY, whole_spec(HEADS * NST, frames)],
        out_specs=[
            row_spec(frames, D),
            row_spec(frames, FF),
            row_spec(frames, FF),
            row_spec(frames, D),
            state_spec,
        ],
        out_shape=[
            shape((rows, frames, D)),
            shape((rows, frames, FF), bf16),
            shape((rows, frames, FF), bf16),
            shape((rows, frames, D), bf16),
            shape((rows, NST, D)),
        ],
        scratch_shapes=[mat(D, FF), mat(FF, D), mat(D, D), dma],
        compiler_params=PARAMS,
        cost_estimate=cost(2 * tokens * D * (2 * FF + D), 30e6),
        name="ffa_forward",
    )(features, small_params, stack, mfin)

    group_spec = pl.BlockSpec((rows, frames, LANES), lambda i: (0, 0, i))
    table_spec = pl.BlockSpec((2, sub * NST, frames), lambda i: (i, 0, 0))
    table_t_spec = pl.BlockSpec((2, frames, sub * NST), lambda i: (i, 0, 0))
    coup_spec = pl.BlockSpec((NST, LANES), lambda i: (0, i))
    taps_spec = pl.BlockSpec((SUB, SUB, LANES), lambda i: (0, 0, i))
    conv_flops = 2 * HEADS * sub * NST * frames * HALF * rows
    y_loc = pl.pallas_call(
        conv_forward_kernel,
        grid=(D // LANES,),
        in_specs=[group_spec, table_spec, table_t_spec, coup_spec, taps_spec],
        out_specs=group_spec,
        out_shape=shape((rows, frames, D)),
        scratch_shapes=[vm(SUB + frames, LANES)],
        compiler_params=PARAMS,
        cost_estimate=cost(2 * conv_flops, 12e6),
        name="conv_forward",
    )(u, m_tab, p_tab, coupling, taps_f)

    span = float(frames)
    ends_all = lax.all_gather(ends.astype(bf16), "tm", axis=0, tiled=False).astype(f32)
    shard = jnp.arange(parts, dtype=jnp.int32)
    behind = place - 1 - shard
    behind_f = jnp.maximum(behind, 0).astype(f32) * span
    behind_w = jnp.where(
        (behind >= 0)[:, None, None],
        jnp.exp(-rate_nc[None] * behind_f[:, None, None]),
        0.0,
    )
    begin = place.astype(f32) * span
    begin_w = jnp.exp(-rate_nc * begin)
    came = jnp.sum(ends_all * behind_w[:, None], axis=0)
    zin = coupling * came + (mix_all[1] * begin_w) * starts

    ys, gated, x2, pw, g = pl.pallas_call(
        mixer_out_kernel,
        grid=(rows,),
        in_specs=[
            row_spec(frames, D),
            state_spec,
            row_spec(frames, D),
            small_spec,
            ANY,
            whole_spec(frames, HEADS * NST),
        ],
        out_specs=[
            row_spec(frames, D),
            row_spec(frames, 2 * D),
            row_spec(frames, D),
            row_spec(frames, 2 * D),
            row_spec(frames, D),
        ],
        out_shape=[
            shape((rows, frames, D), bf16),
            shape((rows, frames, 2 * D), bf16),
            shape((rows, frames, D)),
            shape((rows, frames, 2 * D), bf16),
            shape((rows, frames, D), bf16),
        ],
        scratch_shapes=[mat(D, 2 * D), mat(D, 2 * D), vm(HEADS * NST, D), dma],
        compiler_params=PARAMS,
        cost_estimate=cost(8 * tokens * D * D, 30e6),
        name="mixer_out",
    )(y_loc, zin, x1, small_params, stack, pfull)

    g_low, g_high = exchange_edges(g, "tm")
    edge_spec = pl.BlockSpec((1, PAD, D), lambda i: (i, 0, 0))
    layer_out, dx3, dq, grad_bi, grad_bo, grad_q, gain_b = pl.pallas_call(
        partial(ffb_call, scaling),
        grid=(rows,),
        in_specs=[
            row_spec(frames, D),
            edge_spec,
            edge_spec,
            row_spec(frames, D),
            row_spec(frames, D),
            small_spec,
            ANY,
        ],
        out_specs=[
            row_spec(frames, D),
            row_spec(frames, D),
            row_spec(frames, D),
            whole_spec(ffn, BS, BS),
            whole_spec(ffn, BS, BS),
            whole_spec(mix, BS, BS),
            whole_spec(2, 8, D),
        ],
        out_shape=[
            shape((rows, frames, D), bf16),
            shape((rows, frames, D)),
            shape((rows, frames, D), bf16),
            shape((ffn, BS, BS), bf16),
            shape((ffn, BS, BS), bf16),
            shape((mix, BS, BS), bf16),
            shape((2, 8, D)),
        ],
        scratch_shapes=[
            mat(D, FF),
            mat(FF, D),
            mat(D, D),
            vm(D, FF),
            vm(D, FF),
            vm(D, D),
            vm(D // LANES, frames + 2 * PAD, LANES),
            vm(frames, D),
            dma,
        ],
        compiler_params=PARAMS,
        cost_estimate=cost(6 * tokens * D * (2 * FF + D), 30e6),
        name="ffb",
    )(g, g_low, g_high, x2, cotangent, small_params, stack)

    d_low, d_high = exchange_edges(dq, "tm")
    dx2, dy, back_ends, grad_p, grad_o, gain_c, kernel_grads = pl.pallas_call(
        partial(mixer_back_call, scaling),
        grid=(rows,),
        in_specs=[
            row_spec(frames, D),
            edge_spec,
            edge_spec,
            row_spec(frames, D),
            edge_spec,
            edge_spec,
            row_spec(frames, 2 * D),
            row_spec(frames, D),
            row_spec(frames, 2 * D),
            row_spec(frames, D),
            row_spec(frames, D),
            small_spec,
            ANY,
            whole_spec(HEADS * NST, frames),
        ],
        out_specs=[
            row_spec(frames, D),
            row_spec(frames, D),
            state_spec,
            whole_spec(2 * mix, BS, BS),
            whole_spec(2 * mix, BS, BS),
            whole_spec(8, D),
            whole_spec(16, D),
        ],
        out_shape=[
            shape((rows, frames, D)),
            shape((rows, frames, D), bf16),
            shape((rows, NST, D)),
            shape((2 * mix, BS, BS), bf16),
            shape((2 * mix, BS, BS), bf16),
            shape((8, D)),
            shape((16, D)),
        ],
        scratch_shapes=[
            mat(D, 2 * D),
            mat(D, 2 * D),
            vm(D, 2 * D),
            vm(D, 2 * D),
            vm(D // LANES, frames + 2 * PAD, LANES),
            vm(D // LANES, frames + 2 * PAD, LANES),
            vm(frames, D),
            vm(KW, 8, D),
            dma,
        ],
        compiler_params=PARAMS,
        cost_estimate=cost(16 * tokens * D * D, 30e6),
        name="mixer_back",
    )(dq, d_low, d_high, g, g_low, g_high, pw, x2, gated, ys, dx3, small_params, stack, pfull_t)
    back_all = lax.all_gather(back_ends.astype(bf16), "tm", axis=0, tiled=False).astype(f32)
    nst_spec = pl.BlockSpec((rows, NST, LANES), lambda i: (0, 0, i))
    du_loc, t_one, t_two, ends_w, back_w, lag_grads = pl.pallas_call(
        conv_back_kernel,
        grid=(D // LANES,),
        in_specs=[group_spec, group_spec]
        + [table_spec] * 4
        + [table_t_spec, coup_spec, taps_spec],
        out_specs=[
            group_spec,
            coup_spec,
            coup_spec,
            nst_spec,
            nst_spec,
            pl.BlockSpec((SUB, LANES), lambda i: (0, i)),
        ],
        out_shape=[
            shape((rows, frames, D)),
            shape((NST, D)),
            shape((NST, D)),
            shape((rows, NST, D)),
            shape((rows, NST, D)),
            shape((SUB, D)),
        ],
        scratch_shapes=[
            vm(SUB + frames, LANES),
            vm(SUB + frames, LANES),
            vm(SUB, SUB, LANES),
        ],
        compiler_params=PARAMS,
        cost_estimate=cost(5 * conv_flops, 30e6),
        name="conv_back",
    )(u, dy, m_tab, mp_tab, pt_tab, ptp_tab, mt_tab, coupling, taps_b)

    ahead = shard - place - 1
    ahead_f = jnp.maximum(ahead, 0).astype(f32) * span
    ahead_w = jnp.where(
        (ahead >= 0)[:, None, None],
        jnp.exp(-rate_nc[None] * ahead_f[:, None, None]),
        0.0,
    )
    later = jnp.sum(back_all * ahead_w[:, None], axis=0)
    lam = coupling * later

    grad_zero, grad_ai, grad_ao, grad_u, gain_a = pl.pallas_call(
        partial(ffa_back_call, scaling),
        grid=(rows,),
        in_specs=[
            row_spec(frames, D),
            state_spec,
            row_spec(frames, D),
            row_spec(frames, D),
            row_spec(frames, FF),
            row_spec(frames, FF),
            row_spec(frames, D),
            small_spec,
            ANY,
            whole_spec(frames, HEADS * NST),
        ],
        out_specs=[
            row_spec(frames, D),
            whole_spec(ffn, BS, BS),
            whole_spec(ffn, BS, BS),
            whole_spec(mix, BS, BS),
            whole_spec(2, 8, D),
        ],
        out_shape=[
            shape((rows, frames, D)),
            shape((ffn, BS, BS), bf16),
            shape((ffn, BS, BS), bf16),
            shape((mix, BS, BS), bf16),
            shape((2, 8, D)),
        ],
        scratch_shapes=[
            mat(D, FF),
            mat(FF, D),
            mat(D, D),
            vm(D, FF),
            vm(D, FF),
            vm(D, D),
            vm(HEADS * NST, D),
            dma,
        ],
        compiler_params=PARAMS,
        cost_estimate=cost(4 * tokens * D * (2 * FF + D), 40e6),
        name="ffa_back",
    )(du_loc, lam, x1, features, inner_a, act_a, dx2, small_params, stack, mfin_t)
    grads = jnp.concatenate(
        [grad_ai, grad_ao, grad_bi, grad_bo, grad_u, grad_o, grad_p, grad_q], axis=0
    )

    lag_grad_c = jnp.sum(lag_decay * lag_grads[:, None, :], axis=0)
    lag_grad_r = jnp.sum(lag_decay * (lag[:, None] * lag_grads)[:, None, :], axis=0)
    came_w = jnp.sum(ends_all * (behind_w * behind_f[:, None, None])[:, None], axis=0)
    d_coup = t_one + lag_grad_c + jnp.sum(back_ends * came, axis=0)
    d_first = d_coup * mix_all[1]
    start_back = jnp.sum(starts * back_ends, axis=0) * begin_w
    d_second = d_coup * mix_all[0] + start_back
    d_rate = coupling * (
        t_two
        + lag_grad_r
        + jnp.sum(back_w * came + back_ends * came_w + later * ends_w, axis=0)
    )
    d_rate = d_rate + mix_all[1] * (
        begin * start_back + begin_w * jnp.sum(starts * back_w, axis=0)
    )
    d_logs = -jnp.sum(d_rate.reshape(NST, HEADS, HALF), axis=2).T * rates
    small_grads = jnp.concatenate(
        [
            jnp.sum(gain_a, axis=1),
            jnp.sum(gain_c, axis=0, keepdims=True),
            jnp.sum(gain_b, axis=1),
            kernel_grads[:KW],
        ],
        axis=0,
    )
    own = place * own_channels
    lanes_own = lambda v: lax.dynamic_slice_in_dim(v, own, own_channels, v.ndim - 1)
    stacked = jnp.concatenate([small_grads, d_first, d_second], axis=0) * scaling
    stacked = stacked.reshape(-1, parts, own_channels).transpose(1, 0, 2)
    logs_row = jnp.pad(
        (d_logs * scaling).reshape(parts, 1, own_heads * NST),
        ((0, 0), (0, 0), (0, own_channels - own_heads * NST)),
    )
    stacked = jnp.concatenate([stacked, logs_row], axis=1)
    stacked = jnp.pad(stacked, ((0, 0), (0, -stacked.shape[1] % 8), (0, 0)))
    full_grad, owned, sums = reduce_grads(
        grads, stacked, parts, lax.axis_size("rows"), master.shape[1]
    )
    count_small = small_params.shape[0]
    small_sum = sums[:count_small]
    mix_sum = sums[count_small : count_small + 2 * NST]
    mix_sum = mix_sum.reshape(2, NST, own_channels).transpose(0, 2, 1)
    decay_sum = sums[count_small + 2 * NST, : own_heads * NST].reshape(own_heads, NST)
    new_small = lanes_own(small_params) - rate_small * small_sum
    new_decay = decay_logs - rate_small * decay_sum
    new_mix = state_mix - rate_small * mix_sum

    shard_w = jnp.exp(-lanes_own(rate_nc)[None] * (shard.astype(f32) * span)[:, None, None])
    start_grad = jnp.sum(lanes_own(back_all) * shard_w[:, None], axis=0) * lanes_own(mix_all[1])
    start_grad = start_grad.transpose(0, 2, 1)
    chosen = (state_source[None, :] == jnp.arange(rows, dtype=jnp.int32)[:, None]).astype(f32)
    grad_state = jnp.sum(chosen[:, :, None, None] * start_grad[None], axis=1)

    count, slice_rows = owned.shape[0], owned.shape[1]
    mine = lax.axis_index("rows") * slice_rows
    pick = (
        jnp.arange(slice_rows, dtype=jnp.int32)[:, None] + mine
        == jnp.arange(BS, dtype=jnp.int32)[None, :]
    ).astype(bf16)
    group = 11 if count % 11 == 0 else 1
    part_spec = pl.BlockSpec((group, slice_rows, BS), lambda i: (i, 0, 0))
    full_spec = pl.BlockSpec((group, BS, BS), lambda i: (i, 0, 0))
    new_left, new_right, new_master, new_copy, grad_blocks = pl.pallas_call(
        shampoo_kernel,
        grid=(count // group,),
        in_specs=[
            whole_spec(slice_rows, BS),
            part_spec,
            full_spec,
            part_spec,
            part_spec,
            part_spec,
            full_spec,
            part_spec,
        ],
        out_specs=[part_spec] * 5,
        out_shape=[
            shape(owned.shape),
            shape(owned.shape),
            shape(owned.shape),
            shape(owned.shape, bf16),
            shape(owned.shape),
        ],
        compiler_params=PARAMS,
        name="shampoo",
    )(pick, owned, full_grad, left_stats, right_stats, left_root, right_root, master)
    return (
        layer_out,
        grad_zero,
        grad_state,
        grad_blocks,
        new_left,
        new_right,
        new_master,
        new_copy,
        small_sum,
        new_small,
        decay_sum,
        mix_sum,
        new_decay,
        new_mix,
    )


def ffb_call(scaling, *refs):
    ffb_kernel(*refs[:7], scaling, *refs[7:])


def mixer_back_call(scaling, *refs):
    mixer_back_kernel(*refs[:14], scaling, *refs[14:])


def ffa_back_call(scaling, *refs):
    ffa_back_kernel(*refs[:10], scaling, *refs[10:])


def solution(mesh):
    return jax.shard_map(
        body,
        mesh=mesh,
        in_specs=(
            P("rows", "tm", None),
            P("rows", "tm", None),
            P("rows", "tm", None),
            P("rows"),
            P("tm", "rows", None),
            P("tm", "rows", None),
            P("tm", "rows", None),
            P("tm", "rows", None),
            P("tm", None, None),
            P(),
            P("tm", None),
            P(None, "tm", None),
        ),
        out_specs=(
            P("rows", "tm", None),
            P("rows", "tm", None),
            P("rows", "tm", None),
            P("tm", "rows", None),
            P("tm", "rows", None),
            P("tm", "rows", None),
            P("tm", "rows", None),
            P("tm", "rows", None),
            P(None, "tm"),
            P(None, "tm"),
            P("tm", None),
            P(None, "tm", None),
            P("tm", None),
            P(None, "tm", None),
        ),
        check_vma=False,
    )
```

```python
from functools import partial
import math

import jax
import jax.numpy as jnp
from jax import lax
from jax.experimental import pallas as pl
from jax.experimental.pallas import tpu as pltpu
from jax.sharding import PartitionSpec as P

D = 512
FF = 2048
NST = 32
KW = 15
BS = 256
HEADS = 8
HALF = 64
LANES = 128
SUB = 16
GROUP = 5
PAD = 8
VMEM_BYTES = 60 * 1024 * 1024

rate_blocks = 0.1
rate_small = 0.5
bf16 = jnp.bfloat16
f32 = jnp.float32


def shape(dims, dtype=f32):
    return jax.ShapeDtypeStruct(dims, dtype)


def mm(a, b):
    return jnp.dot(a, b, preferred_element_type=f32)


def mm_nt(a, b):
    return lax.dot_general(a, b, (((1,), (1,)), ((), ())), preferred_element_type=f32)


def mm_tn(a, b):
    return lax.dot_general(a, b, (((0,), (0,)), ((), ())), preferred_element_type=f32)


def sigmoid(v):
    return 0.5 * jnp.tanh(0.5 * v) + 0.5


def norm(v):
    center = v - jnp.mean(v, axis=-1, keepdims=True)
    spread = jnp.mean(center * center, axis=-1, keepdims=True)
    inv = lax.rsqrt(spread + 1e-05)
    return center * inv, inv


def norm_back(hat, inv, scale, incoming):
    scaled = incoming * scale
    mean_one = jnp.mean(scaled, axis=-1, keepdims=True)
    mean_two = jnp.mean(scaled * hat, axis=-1, keepdims=True)
    return inv * (scaled - mean_one - hat * mean_two)


def fold8(v):
    return jnp.sum(v.reshape(-1, 8, v.shape[-1]), axis=0)


def load_matrices(stack, plan, sem):
    copies = []
    for first, dst in plan:
        down, across = dst.shape[0] // BS, dst.shape[1] // BS
        for i in range(down):
            for j in range(across):
                copies.append(
                    pltpu.make_async_copy(
                        stack.at[first + i * across + j],
                        dst.at[pl.ds(i * BS, BS), pl.ds(j * BS, BS)],
                        sem,
                    )
                )
    for copy in copies:
        copy.start()
    for copy in copies:
        copy.wait()


def store_blocks(plan, scaling, grads, stage, sem):
    copies = []
    for acc, first, transposed in plan:
        rows, cols = acc.shape
        down, across = (cols, rows) if transposed else (rows, cols)
        for i in range(down // BS):
            for j in range(across // BS):
                slot = len(copies)
                if transposed:
                    part = (acc[pl.ds(j * BS, BS), pl.ds(i * BS, BS)] * scaling).T
                else:
                    part = acc[pl.ds(i * BS, BS), pl.ds(j * BS, BS)] * scaling
                stage[slot] = part.astype(bf16)
                copy = pltpu.make_async_copy(
                    stage.at[slot], grads.at[first + i * (across // BS) + j], sem
                )
                copy.start()
                copies.append(copy)
    for copy in copies:
        copy.wait()


def head_mask():
    row = lax.broadcasted_iota(jnp.int32, (HEADS * NST, D), 0) // NST
    col = lax.broadcasted_iota(jnp.int32, (HEADS * NST, D), 1) // HALF
    return (row == col).astype(f32)


def spread_heads(v, mask):
    return (jnp.concatenate([v] * HEADS, axis=0) * mask).astype(bf16)


def local_states(table, v, out):
    first = lax.broadcasted_iota(jnp.int32, (NST, LANES), 1) < HALF
    for g in range(D // LANES):
        both = mm(table[pl.ds(2 * NST * g, 2 * NST), :], v[:, g * LANES : (g + 1) * LANES])
        picked = jnp.where(first, both[:NST], both[NST:])
        out[0, :, pl.ds(g * LANES, LANES)] = picked.astype(out.dtype)


def ffa_forward_kernel(feat, small, stack, mfin, x1_o, inner_o, act_o, u_o, f_o, wi, wo, wu, sem):
    @pl.when(pl.program_id(0) == 0)
    def _():
        ffn, mix = D // BS * (FF // BS), (D // BS) ** 2
        load_matrices(stack, ((0, wi), (ffn, wo), (4 * ffn, wu)), sem)

    x0 = feat[0].astype(f32)
    hat, unused = norm(x0)
    inner = mm((hat * small[0:1]).astype(bf16), wi[...])
    act = (inner * sigmoid(inner)).astype(bf16)
    inner_o[0] = inner.astype(bf16)
    act_o[0] = act
    x1 = x0 + 0.5 * mm(act, wo[...])
    x1_o[0] = x1
    hat, unused = norm(x1)
    u = mm((hat * small[1:2]).astype(bf16), wu[...]).astype(bf16)
    u_o[0] = u
    local_states(mfin, u, f_o)


def pack_heads(ref, rows):
    first = lax.broadcasted_iota(jnp.int32, (ref.shape[1], LANES), 1) < HALF
    low, high = [], []
    for p in range(rows // 2):
        a, b = ref[2 * p].astype(f32), ref[2 * p + 1].astype(f32)
        low.append(jnp.where(first, a, pltpu.roll(b, HALF, 1)).astype(bf16))
        high.append(jnp.where(first, pltpu.roll(a, HALF, 1), b).astype(bf16))
    return jnp.concatenate(low, axis=1), jnp.concatenate(high, axis=1)


def pack_params(v, rows):
    first = lax.broadcasted_iota(jnp.int32, v.shape, 1) < HALF
    rolled = pltpu.roll(v, HALF, 1)
    low = jnp.where(first, v, rolled)
    high = jnp.where(first, rolled, v)
    return (
        jnp.concatenate([low] * (rows // 2), axis=1),
        jnp.concatenate([high] * (rows // 2), axis=1),
    )


def unpack_pair(low, high, p):
    low = low[:, p * LANES : (p + 1) * LANES]
    high = high[:, p * LANES : (p + 1) * LANES]
    first = lax.broadcasted_iota(jnp.int32, low.shape, 1) < HALF
    return (
        jnp.where(first, low, pltpu.roll(high, HALF, 1)),
        jnp.where(first, pltpu.roll(low, HALF, 1), high),
    )


def swap_states(mine, whole, first_step, last_step, own_sem, send, recv):
    place, level, core = peers()
    parts = whole.shape[0]
    others = [(place + d) % parts for d in range(1, parts)]

    def copies():
        return [
            remote(mine, whole.at[place], send.at[d], recv.at[d], at(other, level, core))
            for d, other in enumerate(others)
        ]

    own = lambda: pltpu.make_async_copy(mine, whole.at[place], own_sem)

    @pl.when(first_step)
    def _():
        barrier = pltpu.get_barrier_semaphore()
        for other in others:
            signal(barrier, at(other, level, core))
        own().start()

    def end():
        @pl.when(first_step)
        def _():
            pl.semaphore_wait(pltpu.get_barrier_semaphore(), parts - 1)
            for copy in copies():
                copy.start()

        @pl.when(last_step)
        def _():
            own().wait()
            for copy in copies():
                copy.wait()

    return end


def tile_lanes(v, width):
    return jnp.concatenate([v] * (width // LANES), axis=1)


def conv_forward_kernel(
    u, ends, tab_a, tab_b, power, coup, taps, y_o, ends_all, pad, own_sem, send, recv
):
    step = pl.program_id(0)
    end_swap = swap_states(
        ends, ends_all, step == 0, step == pl.num_programs(0) - 1, own_sem, send, recv
    )
    rows, frames = u.shape[0], u.shape[1]
    span = GROUP * SUB
    coup_both = pack_params(coup[...], rows)
    packed = pack_heads(u, rows)
    width = packed[0].shape[1]
    results = []
    for h in range(2):
        scale = [tile_lanes(power[h, i], width) for i in range(GROUP)]
        carry = None
        outs = []
        for g in range(frames // span):
            local = mm(tab_a[h, 0], packed[h][g * span : (g + 1) * span])
            parts = [local[i * NST : (i + 1) * NST] for i in range(GROUP)]
            if carry is None:
                states = [jnp.zeros_like(parts[0])] + parts[:-1]
                carry = parts[-1]
            else:
                states = [carry] + [parts[i] + scale[i] * carry for i in range(GROUP - 1)]
                carry = parts[-1] + scale[-1] * carry
            scaled = jnp.concatenate([v * coup_both[h] for v in states], axis=0)
            outs.append(mm(tab_b[h, 1], scaled.astype(bf16)))
        results.append(jnp.concatenate(outs, axis=0))
    for p in range(rows // 2):
        one, two = unpack_pair(results[0], results[1], p)
        y_o[2 * p] = one
        y_o[2 * p + 1] = two
    pad[0:SUB] = jnp.zeros((SUB, LANES), f32)
    chunk = frames // 5

    def one_row(i, carry):
        pad[pl.ds(SUB, frames)] = u[i].astype(f32)
        for r in range(0, frames, chunk):
            acc = y_o[i, pl.ds(r, chunk)].reshape(-1, SUB, LANES)
            for d in range(SUB):
                piece = pad[pl.ds(SUB + r - d, chunk)].reshape(-1, SUB, LANES)
                acc = acc + piece * taps[d][None]
            y_o[i, pl.ds(r, chunk)] = acc.reshape(chunk, LANES)
        return carry

    lax.fori_loop(0, rows, one_row, 0)
    end_swap()


def edge_sender(edges, low_all, high_all, zeros, send, recv, zero_sem, step, steps):
    place, level, core = peers()
    parts = lax.axis_size("tm")
    not_first, not_last = place > 0, place < parts - 1
    after = (place + 1) % parts
    before = (place + parts - 1) % parts

    def up(i):
        return remote(
            edges.at[i, 1], low_all.at[i], send.at[0, i], recv.at[0, i], at(after, level, core)
        )

    def down(i):
        return remote(
            edges.at[i, 0], high_all.at[i], send.at[1, i], recv.at[1, i], at(before, level, core)
        )

    def blank(ref, i, k):
        return pltpu.make_async_copy(zeros, ref.at[i], zero_sem.at[k])

    @pl.when(step == 0)
    def _():
        barrier = pltpu.get_barrier_semaphore()
        pl.when(not_last)(lambda: signal(barrier, at(after, level, core)))
        pl.when(not_first)(lambda: signal(barrier, at(before, level, core)))
        zeros[...] = jnp.zeros_like(zeros)

        @pl.when(place == 0)
        def _():
            for i in range(steps):
                blank(low_all, i, 0).start()

        @pl.when(place == parts - 1)
        def _():
            for i in range(steps):
                blank(high_all, i, 1).start()

    def put(v):
        @pl.when(step == 0)
        def _():
            below = (place + parts - 1) // parts
            above = (2 * parts - 2 - place) // parts
            pl.semaphore_wait(pltpu.get_barrier_semaphore(), below + above)

        edges[step, 0] = v[:PAD]
        edges[step, 1] = v[-PAD:]
        pl.when(not_last)(lambda: up(step).start())
        pl.when(not_first)(lambda: down(step).start())

        @pl.when(step == steps - 1)
        def _():
            for i in range(steps):
                pl.when(not_last)(lambda i=i: up(i).wait_send())
                pl.when(not_first)(lambda i=i: down(i).wait_send())
                pl.when(not_first)(lambda i=i: up(i).wait_recv())
                pl.when(not_last)(lambda i=i: down(i).wait_recv())

            @pl.when(place == 0)
            def _():
                for i in range(steps):
                    blank(low_all, i, 0).wait()

            @pl.when(place == parts - 1)
            def _():
                for i in range(steps):
                    blank(high_all, i, 1).wait()

    return put


def mixer_out_kernel(
    y, ends_all, starts, weigh, coup, x1, small, stack, pfull,
    ys_o, gated_o, x2_o, pw_o, g_o, low_o, high_o,
    wo, wp, mask, sem, edges, zeros, send, recv, zero_sem,
):
    step = pl.program_id(0)
    put = edge_sender(edges, low_o, high_o, zeros, send, recv, zero_sem, step, edges.shape[0])

    @pl.when(step == 0)
    def _():
        ffn, mix = D // BS * (FF // BS), (D // BS) ** 2
        load_matrices(stack, ((4 * ffn + mix, wo), (4 * ffn + 3 * mix, wp)), sem)
        mask[...] = head_mask()

    came = weigh[0] * ends_all[0, 0].astype(f32)
    for i in range(1, ends_all.shape[0]):
        came = came + weigh[i] * ends_all[i, 0].astype(f32)
    zin = coup[...] * came + weigh[ends_all.shape[0]] * starts[0]
    ys = (y[0] + mm(pfull[...], spread_heads(zin, mask[...]))).astype(bf16)
    ys_o[0] = ys
    gated = mm(ys, wo[...])
    gated_o[0] = gated.astype(bf16)
    x2 = x1[0] + gated[:, :D] * sigmoid(gated[:, D:])
    x2_o[0] = x2
    hat, unused = norm(x2)
    pw = mm((hat * small[2:3]).astype(bf16), wp[...])
    pw_o[0] = pw.astype(bf16)
    g = (pw[:, :D] * sigmoid(pw[:, D:])).astype(bf16)
    g_o[0] = g
    put(g)


def fill_pad(pad, low, body, high):
    frames = body.shape[0]
    for g in range(D // LANES):
        lanes = slice(g * LANES, (g + 1) * LANES)
        pad[g, 0:PAD] = low[:, lanes].astype(f32)
        pad[g, pl.ds(PAD, frames)] = body[:, lanes].astype(f32)
        pad[g, pl.ds(PAD + frames, PAD)] = high[:, lanes].astype(f32)


def ffb_kernel(
    scale, g, low, high, x2, cot, small, stack,
    out_o, dx3_o, dq_o, grads, gain_o, low_o, high_o,
    wi, wo, wq, acc_in, acc_out, acc_q, pad, q_s, stage, k_act, k_din, k_n, k_dp, k_a, k_dpq, sem,
    edges, zeros, send, recv, zero_sem,
):
    step = pl.program_id(0)
    frames = g.shape[1]
    put = edge_sender(edges, low_o, high_o, zeros, send, recv, zero_sem, step, edges.shape[0])

    @pl.when(step == 0)
    def _():
        ffn, mix = D // BS * (FF // BS), (D // BS) ** 2
        load_matrices(stack, ((2 * ffn, wi), (3 * ffn, wo), (4 * ffn + 5 * mix, wq)), sem)
        acc_in[...] = jnp.zeros_like(acc_in)
        acc_out[...] = jnp.zeros_like(acc_out)
        acc_q[...] = jnp.zeros_like(acc_q)
        gain_o[...] = jnp.zeros_like(gain_o)

    fill_pad(pad, low[0], g[0], high[0])
    chunk = frames // 5
    for c in range(D // LANES):
        lanes = slice(c * LANES, (c + 1) * LANES)
        for r in range(0, frames, chunk):
            acc = small[5:6, lanes] * pad[c, pl.ds(r + PAD - 7, chunk)]
            for j in range(1, KW):
                acc = acc + small[5 + j : 6 + j, lanes] * pad[c, pl.ds(r + j + PAD - 7, chunk)]
            q_s[pl.ds(r, chunk), lanes] = acc
    q = q_s[...]
    sig_q = sigmoid(q)
    act_q = q * sig_q
    a3 = act_q.astype(bf16)
    x3 = x2[0] + mm(a3, wq[...])
    hat3, inv3 = norm(x3)
    n3 = (hat3 * small[3:4]).astype(bf16)
    inner = mm(n3, wi[...])
    sig = sigmoid(inner)
    act = inner * sig
    b4 = act.astype(bf16)
    x4 = x3 + 0.5 * mm(b4, wo[...])
    hat4, inv4 = norm(x4)
    out_o[0] = (hat4 * small[4:5]).astype(bf16)
    c4 = cot[0].astype(f32)
    gain_o[1] += fold8(c4 * hat4)
    dx4 = norm_back(hat4, inv4, small[4:5], c4)
    dp = (0.5 * dx4).astype(bf16)
    dact = mm_nt(dp, wo[...])
    dinner = ((sig + act * (1.0 - sig)) * dact).astype(bf16)
    group = k_n.shape[0] // frames
    keep = pl.ds(pl.multiple_of(step % group * frames, frames), frames)
    k_act[keep] = b4
    k_din[keep] = dinner
    k_n[keep] = n3
    k_dp[keep] = dp
    k_a[keep] = a3
    dn3 = mm_nt(dinner, wi[...])
    gain_o[0] += fold8(dn3 * hat3)
    dx3 = dx4 + norm_back(hat3, inv3, small[3:4], dn3)
    dx3_o[0] = dx3
    dpq = dx3.astype(bf16)
    k_dpq[keep] = dpq
    da3 = mm_nt(dpq, wq[...])
    dq = ((sig_q + act_q * (1.0 - sig_q)) * da3).astype(bf16)
    dq_o[0] = dq
    put(dq)

    @pl.when(step % group == group - 1)
    def _():
        acc_out[...] += mm_tn(k_dp[...], k_act[...])
        acc_in[...] += mm_tn(k_n[...], k_din[...])
        acc_q[...] += mm_tn(k_a[...], k_dpq[...])

    @pl.when(step == pl.num_programs(0) - 1)
    def _():
        ffn, mix = D // BS * (FF // BS), (D // BS) ** 2
        plan = (
            (acc_in, 2 * ffn, False),
            (acc_out, 3 * ffn, True),
            (acc_q, 4 * ffn + 5 * mix, False),
        )
        store_blocks(plan, scale, grads, stage, sem)


def mixer_back_kernel(
    scale, dq, dlow, dhigh, g, glow, ghigh, pw, x2, gated, ys, dx3, small, stack, pfull_t, grads_in,
    dx2_o, dy_o, gst_o, grads, gain_o, dk_o,
    wo, wp, acc_p, acc_o, dpad, gpad, dg_s, dk_s, stage, k_n, k_dpw, k_ys, k_dg, sem,
):
    step = pl.program_id(0)
    frames = dq.shape[1]

    @pl.when(step == 0)
    def _():
        ffn, mix = D // BS * (FF // BS), (D // BS) ** 2
        load_matrices(stack, ((4 * ffn + mix, wo), (4 * ffn + 3 * mix, wp)), sem)
        acc_p[...] = jnp.zeros_like(acc_p)
        acc_o[...] = jnp.zeros_like(acc_o)
        gain_o[...] = jnp.zeros_like(gain_o)
        dk_s[...] = jnp.zeros_like(dk_s)

    fill_pad(dpad, dlow[0], dq[0], dhigh[0])
    fill_pad(gpad, glow[0], g[0], ghigh[0])
    chunk = frames // 5
    for c in range(D // LANES):
        lanes = slice(c * LANES, (c + 1) * LANES)
        for r in range(0, frames, chunk):
            here = dpad[c, pl.ds(r + PAD, chunk)]
            acc = small[5:6, lanes] * dpad[c, pl.ds(r + PAD + 7, chunk)]
            for j in range(1, KW):
                acc = acc + small[5 + j : 6 + j, lanes] * dpad[c, pl.ds(r - j + PAD + 7, chunk)]
            dg_s[pl.ds(r, chunk), lanes] = acc
            for j in range(KW):
                dk_s[j, :, lanes] += fold8(here * gpad[c, pl.ds(r + j + PAD - 7, chunk)])
    dg = dg_s[...]
    value = pw[0, :, :D].astype(f32)
    gate = sigmoid(pw[0, :, D:].astype(f32))
    dvalue = (dg * gate).astype(bf16)
    dgate = (dg * value * gate * (1.0 - gate)).astype(bf16)
    dpw = jnp.concatenate([dvalue, dgate], axis=1)
    hat2, inv2 = norm(x2[0])
    n2 = (hat2 * small[2:3]).astype(bf16)
    group = k_n.shape[0] // frames
    keep = pl.ds(pl.multiple_of(step % group * frames, frames), frames)
    k_n[keep] = n2
    k_dpw[keep] = dpw
    k_ys[keep] = ys[0]
    dn2 = mm_nt(dpw, wp[...])
    gain_o[...] += fold8(dn2 * hat2)
    dx2 = dx3[0] + norm_back(hat2, inv2, small[2:3], dn2)
    dx2_o[0] = dx2
    value = gated[0, :, :D].astype(f32)
    gate = sigmoid(gated[0, :, D:].astype(f32))
    dvalue = (dx2 * gate).astype(bf16)
    dgate = (dx2 * value * gate * (1.0 - gate)).astype(bf16)
    dgated = jnp.concatenate([dvalue, dgate], axis=1)
    k_dg[keep] = dgated
    dy = mm_nt(dgated, wo[...]).astype(bf16)
    dy_o[0] = dy
    local_states(pfull_t, dy, gst_o)

    @pl.when(step % group == group - 1)
    def _():
        acc_p[...] += mm_tn(k_n[...], k_dpw[...])
        acc_o[...] += mm_tn(k_ys[...], k_dg[...])

    @pl.when(step == pl.num_programs(0) - 1)
    def _():
        ffn, mix = D // BS * (FF // BS), (D // BS) ** 2
        plan = ((acc_o, 4 * ffn + mix, False), (acc_p, 4 * ffn + 3 * mix, False))
        store_blocks(plan, scale, grads, stage, sem)
        for j in range(KW):
            dk_o[j : j + 1] = jnp.sum(dk_s[j], axis=0, keepdims=True)


def conv_back_kernel(
    u, dy, back_ends, tab_a, tab_b, power, coup, taps,
    du_o, t1_o, t2_o, fp_o, gp_o, dk_o, back_all,
    upad, dpad, acc_s, own_sem, send, recv,
):
    step = pl.program_id(0)
    end_swap = swap_states(
        back_ends, back_all, step == 0, step == pl.num_programs(0) - 1, own_sem, send, recv
    )
    rows, frames = u.shape[0], u.shape[1]
    span = GROUP * SUB
    coup_both = pack_params(coup[...], rows)
    u_both = pack_heads(u, rows)
    d_both = pack_heads(dy, rows)
    width = u_both[0].shape[1]
    du, first_sum, second_sum, end_u, end_d = [], [], [], [], []
    for h in range(2):
        scale = [tile_lanes(power[h, i], width) for i in range(GROUP)]
        aged = [scale[i] * float(SUB * (i + 1)) for i in range(GROUP)]
        zero = jnp.zeros((NST, width), f32)
        carry, carry_w = zero, zero
        states, states_w = [], []
        for g in range(frames // span):
            here = u_both[h][g * span : (g + 1) * span]
            local = mm(tab_a[h, 0], here)
            local_w = mm(tab_a[h, 1], here)
            parts = [local[i * NST : (i + 1) * NST] for i in range(GROUP)]
            parts_w = [local_w[i * NST : (i + 1) * NST] for i in range(GROUP)]
            states.append([carry] + [parts[i] + scale[i] * carry for i in range(GROUP - 1)])
            states_w.append(
                [carry_w]
                + [parts_w[i] + scale[i] * carry_w + aged[i] * carry for i in range(GROUP - 1)]
            )
            carry_w = parts_w[-1] + scale[-1] * carry_w + aged[-1] * carry
            carry = parts[-1] + scale[-1] * carry
        end_u.append(carry_w)
        later, later_w = zero, zero
        one, two = zero, zero
        outs = []
        for g in reversed(range(frames // span)):
            here = d_both[h][g * span : (g + 1) * span]
            back = mm(tab_a[h, 2], here)
            back_w = mm(tab_a[h, 3], here)
            parts = [back[i * NST : (i + 1) * NST] for i in range(GROUP)]
            parts_w = [back_w[i * NST : (i + 1) * NST] for i in range(GROUP)]
            into = jnp.concatenate([v * coup_both[h] for v in parts[1:] + [later]], axis=0)
            outs.append(mm(tab_b[h, 0], into.astype(bf16)))
            for i in range(GROUP):
                one = one + parts[i] * states[g][i]
                two = two + (parts_w[i] * states[g][i] + parts[i] * states_w[g][i])
            new, new_w = parts[0], parts_w[0]
            for i in range(GROUP - 1):
                new = new + scale[i] * parts[i + 1]
                new_w = new_w + (scale[i] * parts_w[i + 1] + aged[i] * parts[i + 1])
            later_w = new_w + scale[-1] * later_w + aged[-1] * later
            later = new + scale[-1] * later
        end_d.append(later_w)
        first_sum.append(one)
        second_sum.append(two)
        du.append(jnp.concatenate(outs[::-1], axis=0))
    first = lax.broadcasted_iota(jnp.int32, (NST, LANES), 1) < HALF
    for sums, out in ((first_sum, t1_o), (second_sum, t2_o)):
        both = []
        for v in sums:
            total = v[:, :LANES]
            for p in range(1, rows // 2):
                total = total + v[:, p * LANES : (p + 1) * LANES]
            both.append(total + pltpu.roll(total, HALF, 1))
        out[...] = jnp.where(first, both[0], both[1])
    for p in range(rows // 2):
        for pair, out in ((du, du_o), (end_u, fp_o), (end_d, gp_o)):
            one, two = unpack_pair(pair[0], pair[1], p)
            out[2 * p] = one
            out[2 * p + 1] = two
    chunk = frames // 5
    upad[0:SUB] = jnp.zeros((SUB, LANES), f32)
    dpad[pl.ds(frames, SUB)] = jnp.zeros((SUB, LANES), f32)
    acc_s[...] = jnp.zeros_like(acc_s)

    def one_row(i, carry):
        upad[pl.ds(SUB, frames)] = u[i].astype(f32)
        dpad[pl.ds(0, frames)] = dy[i].astype(f32)
        for r in range(0, frames, chunk):
            acc = du_o[i, pl.ds(r, chunk)].reshape(-1, SUB, LANES)
            here = dpad[pl.ds(r, chunk)]
            for d in range(SUB):
                piece = dpad[pl.ds(r + d, chunk)].reshape(-1, SUB, LANES)
                acc = acc + piece * taps[d][None]
                product = (here * upad[pl.ds(SUB + r - d, chunk)]).reshape(-1, SUB, LANES)
                acc_s[d] += jnp.sum(product, axis=0)
            du_o[i, pl.ds(r, chunk)] = acc.reshape(chunk, LANES)
        return carry

    lax.fori_loop(0, rows, one_row, 0)
    spot = lax.broadcasted_iota(jnp.int32, (SUB, LANES), 0)
    for d in range(SUB):
        kept = jnp.where(spot >= d, acc_s[d], 0.0)
        dk_o[d : d + 1] = jnp.sum(kept, axis=0, keepdims=True)
    end_swap()


def ffa_back_kernel(
    scale, du_loc, back_all, ends_all, back_ends, ends_w, back_w, starts, weigh, coup,
    x1, feat, inner_r, act_r, dx2, small, stack, mfin_t, grads_in,
    dx0_o, grads, gain_o, sums_o,
    wi, wo, wu, acc_in, acc_out, acc_u, mask, stage, k_act, k_din, k_n, k_dp, k_m, k_du, sem,
):
    step = pl.program_id(0)

    @pl.when(step == 0)
    def _():
        ffn, mix = D // BS * (FF // BS), (D // BS) ** 2
        load_matrices(stack, ((0, wi), (ffn, wo), (4 * ffn, wu)), sem)
        mask[...] = head_mask()
        acc_in[...] = jnp.zeros_like(acc_in)
        acc_out[...] = jnp.zeros_like(acc_out)
        acc_u[...] = jnp.zeros_like(acc_u)
        gain_o[...] = jnp.zeros_like(gain_o)
        sums_o[...] = jnp.zeros_like(sums_o)

    frames = feat.shape[1]
    group = k_n.shape[0] // frames
    keep = pl.ds(pl.multiple_of(step % group * frames, frames), frames)
    parts = ends_all.shape[0]
    came, came_w, later = 0.0, 0.0, 0.0
    for i in range(parts):
        end = ends_all[i, 0].astype(f32)
        came = came + weigh[0, i] * end
        came_w = came_w + weigh[1, i] * end
        later = later + weigh[2, i] * back_all[i, 0].astype(f32)
    mine = back_ends[0].astype(f32)
    sums_o[0] += mine * came
    sums_o[1] += starts[0] * mine
    sums_o[2] += starts[0] * back_w[0]
    sums_o[3] += back_w[0] * came + mine * came_w + later * ends_w[0]
    du = (du_loc[0] + mm(mfin_t[...], spread_heads(coup[...] * later, mask[...]))).astype(bf16)
    hat1, inv1 = norm(x1[0])
    n1 = (hat1 * small[1:2]).astype(bf16)
    k_m[keep] = n1
    k_du[keep] = du
    dn1 = mm_nt(du, wu[...])
    gain_o[1] += fold8(dn1 * hat1)
    dx1 = dx2[0] + norm_back(hat1, inv1, small[1:2], dn1)
    dp = (0.5 * dx1).astype(bf16)
    dact = mm_nt(dp, wo[...])
    inner = inner_r[0].astype(f32)
    sig = sigmoid(inner)
    dinner = ((sig + inner * sig * (1.0 - sig)) * dact).astype(bf16)
    hat0, inv0 = norm(feat[0].astype(f32))
    n0 = (hat0 * small[0:1]).astype(bf16)
    k_act[keep] = act_r[0]
    k_din[keep] = dinner
    k_n[keep] = n0
    k_dp[keep] = dp
    dn0 = mm_nt(dinner, wi[...])
    gain_o[0] += fold8(dn0 * hat0)
    dx0_o[0] = dx1 + norm_back(hat0, inv0, small[0:1], dn0)

    @pl.when(step % group == group - 1)
    def _():
        acc_out[...] += mm_tn(k_dp[...], k_act[...])
        acc_in[...] += mm_tn(k_n[...], k_din[...])
        acc_u[...] += mm_tn(k_m[...], k_du[...])

    @pl.when(step == pl.num_programs(0) - 1)
    def _():
        ffn, mix = D // BS * (FF // BS), (D // BS) ** 2
        plan = ((acc_in, 0, False), (acc_out, ffn, True), (acc_u, 4 * ffn, False))
        store_blocks(plan, scale, grads, stage, sem)


def shampoo_kernel(
    pick, owned, full, left, right, lroot, rroot, master, nl_o, nr_o, nm_o, nc_o, own_o
):
    for i in range(full.shape[0]):
        whole = full[i]
        mine = owned[i]
        own_o[i] = mine.astype(f32)
        nl_o[i] = 0.5 * left[i] + 0.5 * mm_nt(mine, whole)
        columns = mm_nt(pick[...], whole).astype(bf16)
        nr_o[i] = 0.5 * right[i] + 0.5 * mm(columns, whole)
        side = mm(lroot[i].astype(bf16), whole)
        step = mm(side.astype(bf16), rroot[i].astype(bf16))
        new = master[i] - rate_blocks * step
        nm_o[i] = new
        nc_o[i] = new.astype(bf16)


def peers():
    place, row = lax.axis_index("tm"), lax.axis_index("rows")
    return place, row // 2, row % 2


def square(place):
    x, y = place % 2, place // 2
    return 2 * y + 1 - x, 2 * (1 - y) + x, 2 * (1 - y) + 1 - x


def at(place, level, core):
    return {"tm": place, "rows": level * 2 + core}


def remote(src, dst, send, recv, device):
    return pltpu.make_async_remote_copy(
        src_ref=src,
        dst_ref=dst,
        send_sem=send,
        recv_sem=recv,
        device_id=device,
        device_id_type=pl.DeviceIdType.MESH,
    )


def signal(sem, device):
    pl.semaphore_signal(sem, inc=1, device_id=device, device_id_type=pl.DeviceIdType.MESH)


def chunk_ranges(count, chunks):
    edges = [count * c // chunks for c in range(chunks + 1)]
    out = []
    for first, end in zip(edges[:-1], edges[1:]):
        middle = (first + end + 1) // 2
        out.append((first, end, middle))
    return out


def gather_kernel(
    levels, piece, pack, stack, pack_all, own_sem, pk_send, pk_recv,
    z_send, z_recv, x_send, x_recv, y_send, y_recv, c_send, c_recv,
):
    place, level, core = peers()
    count = piece.shape[0]
    xp, yp, dp = others = square(place)
    up, down = level < levels - 1, level > 0
    barrier = pltpu.get_barrier_semaphore()
    for other in (xp, yp, dp):
        signal(barrier, at(other, level, core))
    signal(barrier, at(place, level, 1 - core))

    @pl.when(up)
    def _():
        signal(barrier, at(place, level + 1, core))

    @pl.when(down)
    def _():
        signal(barrier, at(place, level - 1, core))

    below = (level + levels - 1) // levels
    above = (2 * levels - 2 - level) // levels
    pl.semaphore_wait(barrier, 4 + below + above)

    sends = []
    own = pltpu.make_async_copy(piece, stack.at[place, :, level, core], own_sem)
    own.start()
    own_pack = pltpu.make_async_copy(pack, pack_all.at[place], pk_send.at[3])
    own_pack.start()
    ranges = chunk_ranges(count, z_send.shape[0])

    def z_copy(c, side, s):
        first, end, unused = ranges[c]
        step = 1 if side == 0 else -1
        origin = level - s * step
        spot = stack.at[place, pl.ds(first, end - first), origin, core]
        src = piece.at[pl.ds(first, end - first)] if s == 0 else spot
        return remote(
            src, spot, z_send.at[c, side, s], z_recv.at[c, side, s], at(place, (level + step + levels) % levels, core)
        )

    def z_ok(side, s):
        if side == 0:
            return jnp.logical_and(level - s >= 0, level + 1 < levels)
        return jnp.logical_and(level + s < levels, level - 1 >= 0)

    def z_in(side, s):
        if side == 0:
            return level - s - 1 >= 0
        return level + s + 1 < levels

    for c in range(len(ranges)):
        for side in range(2):
            pl.when(z_ok(side, 0))(lambda c=c, side=side: z_copy(c, side, 0).start())
        if c == 0:
            for d in range(1, 4):
                copy = remote(
                    pack,
                    pack_all.at[place],
                    pk_send.at[d - 1],
                    pk_recv.at[d - 1],
                    at(others[d - 1], level, core),
                )
                copy.start()
                sends.append(copy)
    own.wait()
    own_pack.wait()

    def part(owner, first, end):
        return stack.at[owner, pl.ds(first, end - first), :, core]

    def to_x(c, i, owner, first, end):
        return remote(
            part(owner, first, end), part(owner, first, end),
            x_send.at[c, i], x_recv.at[c, i], at(xp, level, core),
        )

    def to_y(c, i, owner, first, end):
        return remote(
            part(owner, first, end), part(owner, first, end),
            y_send.at[c, i], y_recv.at[c, i], at(yp, level, core),
        )

    def to_core(c, i, owner, first, end):
        return remote(
            part(owner, first, end), part(owner, first, end),
            c_send.at[c, i], c_recv.at[c, i], at(place, level, 1 - core),
        )

    def go(copy):
        copy.start()
        sends.append(copy)
        return copy

    moved = []

    def z_phase(c):
        for s in range(levels - 1):
            for side in range(2):

                def step(c=c, side=side, s=s):
                    z_copy(c, side, s).wait_recv()
                    if s + 1 < levels - 1:
                        pl.when(z_ok(side, s + 1))(lambda: z_copy(c, side, s + 1).start())

                pl.when(z_in(side, s))(step)

    def spread(c):
        first, end, middle = ranges[c]
        out = (
            go(to_x(c, 0, place, first, middle)),
            go(to_y(c, 0, place, middle, end)),
            go(to_x(c, 1, place, middle, end)),
            go(to_y(c, 1, place, first, middle)),
        )
        moved.append(go(to_core(c, 0, place, first, end)))
        return out

    def forward(c, copies):
        first, end, middle = ranges[c]
        copies[0].wait_recv()
        y_in = go(to_y(c, 2, xp, first, middle))
        copies[1].wait_recv()
        x_in = go(to_x(c, 2, yp, middle, end))
        moved.append(go(to_core(c, 1, xp, first, middle)))
        moved.append(go(to_core(c, 2, yp, middle, end)))
        copies[2].wait_recv()
        moved.append(go(to_core(c, 3, xp, middle, end)))
        copies[3].wait_recv()
        moved.append(go(to_core(c, 4, yp, first, middle)))
        return y_in, x_in

    def finish(c, copies):
        first, end, middle = ranges[c]
        copies[0].wait_recv()
        moved.append(go(to_core(c, 5, dp, first, middle)))
        copies[1].wait_recv()
        moved.append(go(to_core(c, 6, dp, middle, end)))

    out = {}
    for c in range(len(ranges)):
        z_phase(c)
        mine = spread(c)
        if c >= 1:
            out[c - 1] = forward(c - 1, out[c - 1])
        out[c] = mine
        if c >= 2:
            finish(c - 2, out[c - 2])
    last = len(ranges) - 1
    out[last] = forward(last, out[last])
    for c in range(max(last - 1, 0), last + 1):
        finish(c, out[c])
    for copy in moved:
        copy.wait_recv()
    for copy in sends[:3]:
        copy.wait_recv()
    for copy in sends:
        copy.wait_send()
    for c in range(len(ranges)):
        for side in range(2):
            for s in range(levels - 1):
                pl.when(z_ok(side, s))(lambda c=c, side=side, s=s: z_copy(c, side, s).wait_send())


def gather_weights(piece, pack, parts, devices, chunks=4):
    count, slab, cols = piece.shape
    if parts != 4:
        stack = lax.all_gather(lax.all_gather(piece, "rows", axis=1, tiled=True), "tm", axis=0)
        return stack.reshape(-1, BS, BS), lax.all_gather(pack, "tm", axis=0)
    levels = devices // 2
    dma = lambda *dims: pltpu.SemaphoreType.DMA(dims)
    stack, pack_all = pl.pallas_call(
        partial(gather_kernel, levels),
        in_specs=[ANY, ANY],
        out_specs=[ANY, ANY],
        out_shape=[
            shape((parts, count, levels, 2, slab, cols), piece.dtype),
            shape((parts,) + pack.shape, pack.dtype),
        ],
        scratch_shapes=[
            pltpu.SemaphoreType.DMA,
            dma(4), dma(3),
            dma(chunks, 2, levels - 1), dma(chunks, 2, levels - 1),
            dma(chunks, 3), dma(chunks, 3),
            dma(chunks, 3), dma(chunks, 3),
            dma(chunks, 7), dma(chunks, 7),
        ],
        compiler_params=pltpu.CompilerParams(
            collective_id=1, has_side_effects=True, vmem_limit_bytes=VMEM_BYTES
        ),
        name="gather_weights",
    )(piece, pack)
    return stack.reshape(-1, BS, BS), pack_all


def reduce_kernel(
    levels, grads, small, full, owned, small_sum,
    mine, came, from_x, from_y, red, z_in, s_tm, s_core, s_z,
    load_sem, c_send, c_recv, x_send, x_recv, y_send, y_recv,
    z_send, z_recv, a_send, a_recv, f_send, f_recv, s_send, s_recv, put_sem,
):
    place, level, core = peers()
    count = grads.shape[1]
    xp, yp, dp = others = square(place)
    barrier = pltpu.get_barrier_semaphore()
    for other in (xp, yp, dp):
        signal(barrier, at(other, level, core))
    signal(barrier, at(place, level, 1 - core))
    for d in range(1, levels):
        signal(barrier, at(place, (level + d) % levels, core))
    pl.semaphore_wait(barrier, 4 + levels - 1)
    ranges = chunk_ranges(count, c_send.shape[0])
    sends = []

    def go(copy):
        copy.start()
        sends.append(copy)
        return copy

    def over(ref, first, end):
        return ref.at[:, pl.ds(first, end - first)]

    loads, core_in = [], []
    for c, (first, end, unused) in enumerate(ranges):
        core_in.append(
            go(
                remote(
                    over(grads, first, end).at[:, :, :, 1 - core],
                    over(came, first, end),
                    c_send.at[c],
                    c_recv.at[c],
                    at(place, level, 1 - core),
                )
            )
        )
        load = pltpu.make_async_copy(
            over(grads, first, end).at[:, :, :, core], over(mine, first, end), load_sem.at[c]
        )
        load.start()
        loads.append(load)

    small_in = []
    for d in range(1, 4):
        small_in.append(
            go(
                remote(
                    small.at[others[d - 1]], s_tm.at[d - 1], s_send.at[d - 1], s_recv.at[d - 1],
                    at(others[d - 1], level, core),
                )
            )
        )
    for copy in small_in:
        copy.wait_recv()
    s_core[0] = small[place] + (s_tm[0] + s_tm[1]) + s_tm[2]
    swap = go(
        remote(s_core.at[0], s_core.at[1], s_send.at[3], s_recv.at[3], at(place, level, 1 - core))
    )

    def add_core(owner, first, end):
        def one(k, carry):
            total = mine[owner, k].astype(f32) + came[owner, k].astype(f32)
            mine[owner, k] = total.astype(bf16)
            return carry

        lax.fori_loop(first, end, one, 0)

    def add_into(owner, ref, slot, first, end):
        def one(k, carry):
            total = mine[owner, k].astype(f32) + ref[slot, k].astype(f32)
            mine[owner, k] = total.astype(bf16)
            return carry

        lax.fori_loop(first, end, one, 0)

    def to_x(c, i, owner, slot, first, end):
        n = pl.ds(first, end - first)
        return go(
            remote(
                mine.at[owner, n], from_x.at[slot, n], x_send.at[c, i], x_recv.at[c, i],
                at(xp, level, core),
            )
        )

    def to_y(c, i, owner, slot, first, end):
        n = pl.ds(first, end - first)
        return go(
            remote(
                mine.at[owner, n], from_y.at[slot, n], y_send.at[c, i], y_recv.at[c, i],
                at(yp, level, core),
            )
        )

    def begin(c):
        first, end, middle = ranges[c]
        loads[c].wait()
        core_in[c].wait_recv()
        add_core(dp, first, end)
        x_one = to_x(c, 0, dp, 0, first, middle)
        y_one = to_y(c, 0, dp, 0, middle, end)
        add_core(xp, first, end)
        x_two = to_x(c, 1, xp, 1, first, middle)
        add_core(yp, first, end)
        y_two = to_y(c, 1, yp, 1, middle, end)
        add_core(place, first, end)
        return x_one, y_one, x_two, y_two

    def second(c, copies):
        first, end, middle = ranges[c]
        copies[0].wait_recv()
        add_into(yp, from_x, 0, first, middle)
        y_three = to_y(c, 2, yp, 1, first, middle)
        copies[1].wait_recv()
        add_into(xp, from_y, 0, middle, end)
        x_three = to_x(c, 2, xp, 1, middle, end)
        return copies[2], copies[3], x_three, y_three

    def along(c, copies):
        first, end, middle = ranges[c]
        for copy in copies:
            copy.wait_recv()

        def one(k, carry):
            total = mine[place, k].astype(f32) + from_x[1, k].astype(f32)
            red[k] = (total + from_y[1, k].astype(f32)).astype(bf16)
            return carry

        lax.fori_loop(first, end, one, 0)
        out = []
        n = pl.ds(first, end - first)
        for d in range(1, levels):
            target = (level + d) % levels
            out.append(
                go(
                    remote(
                        red.at[n, target], z_in.at[d - 1, n], z_send.at[c, d - 1],
                        z_recv.at[c, d - 1], at(place, target, core),
                    )
                )
            )
        return out

    def settle(c, copies):
        first, end, middle = ranges[c]
        for copy in copies:
            copy.wait_recv()

        def one(k, carry):
            total = red[k, level].astype(f32)
            for d in range(levels - 1):
                total = total + z_in[d, k].astype(f32)
            owned[k] = total.astype(bf16)
            return carry

        lax.fori_loop(first, end, one, 0)
        n = pl.ds(first, end - first)
        out = []
        for d in range(1, levels):
            target = (level + d) % levels
            out.append(
                go(
                    remote(
                        owned.at[n], full.at[n, level, core], a_send.at[c, d - 1],
                        a_recv.at[c, d - 1], at(place, target, core),
                    )
                )
            )
        put = pltpu.make_async_copy(owned.at[n], full.at[n, level, core], put_sem.at[c])
        put.start()
        sibling = go(
            remote(
                owned.at[n], full.at[n, level, core], f_send.at[c, 0], f_recv.at[c, 0],
                at(place, level, 1 - core),
            )
        )
        return out, put, [sibling]

    def share(c, state):
        first, end, middle = ranges[c]
        n = pl.ds(first, end - first)
        copies, put, passed = state
        for d in range(1, levels):
            copies[d - 1].wait_recv()
            source = (level + levels - d) % levels
            passed.append(
                go(
                    remote(
                        full.at[n, source, core], full.at[n, source, core], f_send.at[c, d],
                        f_recv.at[c, d], at(place, level, 1 - core),
                    )
                )
            )
        put.wait()
        return passed

    chunks = len(ranges)
    state = [begin(0)]
    swap.wait_recv()
    s_z[level] = s_core[0] + s_core[1]
    small_z = []
    for d in range(1, levels):
        target = (level + d) % levels
        small_z.append(
            go(
                remote(
                    s_z.at[level], s_z.at[level], s_send.at[3 + d], s_recv.at[3 + d],
                    at(place, target, core),
                )
            )
        )
    for c in range(1, chunks):
        state.append(begin(c))
        state[c - 1] = second(c - 1, state[c - 1])
        if c >= 2:
            state[c - 2] = along(c - 2, state[c - 2])
        if c >= 3:
            state[c - 3] = settle(c - 3, state[c - 3])
    state[chunks - 1] = second(chunks - 1, state[chunks - 1])
    for c in range(max(chunks - 2, 0), chunks):
        state[c] = along(c, state[c])
    for c in range(max(chunks - 3, 0), chunks):
        state[c] = settle(c, state[c])
    passed = []
    for c in range(chunks):
        passed += share(c, state[c])
    for copy in small_z:
        copy.wait_recv()
    total = s_z[0]
    for i in range(1, levels):
        total = total + s_z[i]
    small_sum[...] = total
    for copy in passed:
        copy.wait_recv()
    for copy in sends:
        copy.wait_send()


def reduce_grads(grads, small, parts, devices, slab, chunks=4):
    if parts != 4:
        owned = lax.psum_scatter(grads, "tm", scatter_dimension=0, tiled=True)
        owned = lax.psum_scatter(owned, "rows", scatter_dimension=1, tiled=True)
        full = lax.all_gather(owned, "rows", axis=1, tiled=True)
        small = lax.psum_scatter(small, "tm", scatter_dimension=0, tiled=True)[0]
        return full, owned, lax.psum(small, "rows")
    levels = devices // 2
    count = grads.shape[0] // parts
    grads = grads.reshape(parts, count, levels, 2, slab, BS)
    dma = lambda *dims: pltpu.SemaphoreType.DMA(dims)
    vb = lambda *dims: pltpu.VMEM(dims, bf16)
    vmem = pl.BlockSpec(memory_space=pltpu.VMEM)
    part = small.shape[1:]
    full, owned, small_sum = pl.pallas_call(
        partial(reduce_kernel, levels),
        in_specs=[ANY, vmem],
        out_specs=[ANY, vmem, vmem],
        out_shape=[
            shape((count, levels, 2, slab, BS), bf16),
            shape((count, slab, BS), bf16),
            shape(part),
        ],
        scratch_shapes=[
            vb(parts, count, levels, slab, BS), vb(parts, count, levels, slab, BS),
            vb(2, count, levels, slab, BS), vb(2, count, levels, slab, BS),
            vb(count, levels, slab, BS), vb(levels - 1, count, slab, BS),
            vm(3, *part), vm(2, *part), vm(levels, *part),
            dma(chunks), dma(chunks), dma(chunks),
            dma(chunks, 3), dma(chunks, 3), dma(chunks, 3), dma(chunks, 3),
            dma(chunks, levels - 1), dma(chunks, levels - 1),
            dma(chunks, levels - 1), dma(chunks, levels - 1),
            dma(chunks, levels), dma(chunks, levels),
            dma(3 + levels), dma(3 + levels), dma(chunks),
        ],
        compiler_params=pltpu.CompilerParams(
            collective_id=2, has_side_effects=True, vmem_limit_bytes=VMEM_BYTES
        ),
        name="reduce_grads",
    )(grads, small)
    return full.reshape(count, BS, BS), owned, small_sum


def row_spec(frames, width):
    return pl.BlockSpec((1, frames, width), lambda i: (i, 0, 0))


def whole_spec(*dims):
    return pl.BlockSpec(dims, lambda i: (0,) * len(dims))


ANY = pl.BlockSpec(memory_space=pl.ANY)
PARAMS = pltpu.CompilerParams(
    dimension_semantics=("arbitrary",), vmem_limit_bytes=VMEM_BYTES
)


def talking(number):
    return pltpu.CompilerParams(
        dimension_semantics=("arbitrary",),
        vmem_limit_bytes=VMEM_BYTES,
        collective_id=number,
        has_side_effects=True,
    )


def vm(*dims, dtype=f32):
    return pltpu.VMEM(dims, dtype)


def body(
    features,
    cotangent,
    state_bank,
    state_source,
    master,
    left_stats,
    right_stats,
    left_root,
    right_root,
    small_params,
    decay_logs,
    state_mix,
):
    rows, frames, width = features.shape
    tokens = rows * frames
    parts = lax.axis_size("tm")
    place = lax.axis_index("tm")
    scaling = 1.0 / math.sqrt(tokens * parts * lax.axis_size("rows"))
    ffn, mix = D // BS * (FF // BS), (D // BS) ** 2

    own_heads, own_channels = decay_logs.shape[0], state_mix.shape[1]
    starts_own = state_bank[state_source]
    flat = jnp.concatenate(
        [decay_logs.reshape(-1), state_mix.reshape(-1), starts_own.reshape(-1)]
    )
    cut_one = own_heads * NST
    cut_two = cut_one + 2 * own_channels * NST
    cut_three = cut_two + rows * own_channels * NST
    flat = jnp.pad(flat, (0, -cut_three % (8 * LANES))).reshape(-1, LANES)
    stack, packed = gather_weights(
        master.astype(bf16), flat, parts, lax.axis_size("rows")
    )
    packed = packed.reshape(parts, -1)
    logs = packed[:, :cut_one].reshape(HEADS, NST)
    mix_all = packed[:, cut_one:cut_two].reshape(parts, 2, own_channels, NST)
    mix_all = mix_all.transpose(1, 3, 0, 2).reshape(2, NST, D)
    starts = packed[:, cut_two:cut_three].reshape(parts, rows, own_channels, NST)
    starts = starts.transpose(1, 3, 0, 2).reshape(rows, NST, D)

    rates = jnp.exp(logs)
    rate_nc = jnp.repeat(rates.T, HALF, axis=1)
    coupling = mix_all[0] * mix_all[1]
    state_row = jnp.arange(GROUP * NST, dtype=jnp.int32)
    part_of = state_row // NST
    rate_row = jnp.tile(rates, (1, GROUP))[:, :, None]
    inner_t = jnp.arange(GROUP * SUB, dtype=jnp.int32)
    age = SUB * (part_of + 1)[:, None] - 1 - inner_t[None, :]
    age_f = jnp.maximum(age, 0).astype(f32)
    tab_in = jnp.where(age >= 0, jnp.exp(-rate_row * age_f), 0.0)
    since = (inner_t % SUB + 1).astype(f32)
    inside = (inner_t // SUB)[None, :] == part_of[:, None]
    tab_out = jnp.where(inside, jnp.exp(-rate_row * since), 0.0)
    tab_a = jnp.stack([tab_in, tab_in * age_f, tab_out, tab_out * since], axis=1).astype(bf16)
    tab_b = jnp.stack([tab_in, tab_out], axis=1).astype(bf16).transpose(0, 1, 3, 2)
    steps_of = SUB * jnp.arange(1, GROUP + 1, dtype=f32)
    power = jnp.exp(-rates[:, None, :, None] * steps_of[None, :, None, None])
    power = jnp.broadcast_to(power, (HEADS, GROUP, NST, LANES))
    time = jnp.arange(frames, dtype=jnp.int32)
    flat_rates = rates.reshape(-1)
    next_t = (time + 1).astype(f32)
    left_t = (frames - 1 - time).astype(f32)
    pfull = jnp.exp(-flat_rates[None, :] * next_t[:, None]).astype(bf16)
    pfull_t = jnp.exp(-flat_rates[:, None] * next_t[None, :]).astype(bf16)
    mfin = jnp.exp(-flat_rates[:, None] * left_t[None, :]).astype(bf16)
    mfin_t = jnp.exp(-flat_rates[None, :] * left_t[:, None]).astype(bf16)
    lag = jnp.arange(SUB, dtype=f32)
    lag_decay = jnp.exp(-rate_nc[None] * lag[:, None, None])
    kernel_lags = jnp.sum(coupling[None] * lag_decay, axis=1)
    slot = jnp.arange(SUB, dtype=jnp.int32)
    taps_f = jnp.where(slot[:, None, None] <= slot[None, :, None], kernel_lags[:, None, :], 0.0)
    taps_b = jnp.where(
        slot[:, None, None] + slot[None, :, None] < SUB, kernel_lags[:, None, :], 0.0
    )

    span = float(frames)
    shard = jnp.arange(parts, dtype=jnp.int32)

    def passing(apart):
        length = jnp.maximum(apart, 0).astype(f32)[:, None, None] * span
        weight = jnp.where(
            (apart >= 0)[:, None, None], jnp.exp(-rate_nc[None] * length), 0.0
        )
        return weight, weight * length

    behind_w, behind_l = passing(place - 1 - shard)
    ahead_w, unused = passing(shard - place - 1)
    begin = place.astype(f32) * span
    begin_w = jnp.exp(-rate_nc * begin)
    weigh_in = jnp.concatenate([behind_w, (mix_all[1] * begin_w)[None]], axis=0)
    weigh_back = jnp.stack([behind_w, behind_l, ahead_w], axis=0)

    mat = lambda r, c: vm(r, c, dtype=bf16)
    dma = pltpu.SemaphoreType.DMA
    group = 3 if rows % 3 == 0 else 1
    small_spec = whole_spec(*small_params.shape)
    state_spec = pl.BlockSpec((1, NST, D), lambda i: (i, 0, 0))
    states_spec = pl.BlockSpec((parts, 1, NST, D), lambda i: (0, i, 0, 0))
    flat_spec = whole_spec(NST, D)
    x1, inner_a, act_a, u, ends = pl.pallas_call(
        ffa_forward_kernel,
        grid=(rows,),
        in_specs=[row_spec(frames, D), small_spec, ANY, whole_spec(HEADS * NST, frames)],
        out_specs=[
            row_spec(frames, D),
            row_spec(frames, FF),
            row_spec(frames, FF),
            row_spec(frames, D),
            state_spec,
        ],
        out_shape=[
            shape((rows, frames, D)),
            shape((rows, frames, FF), bf16),
            shape((rows, frames, FF), bf16),
            shape((rows, frames, D), bf16),
            shape((rows, NST, D), bf16),
        ],
        scratch_shapes=[mat(D, FF), mat(FF, D), mat(D, D), dma],
        compiler_params=PARAMS,
        name="ffa_forward",
    )(features, small_params, stack, mfin)

    group_spec = pl.BlockSpec((rows, frames, LANES), lambda i: (0, 0, i))
    tab_a_spec = pl.BlockSpec((2,) + tab_a.shape[1:], lambda i: (i, 0, 0, 0))
    tab_b_spec = pl.BlockSpec((2,) + tab_b.shape[1:], lambda i: (i, 0, 0, 0))
    power_spec = pl.BlockSpec((2,) + power.shape[1:], lambda i: (i, 0, 0, 0))
    coup_spec = pl.BlockSpec((NST, LANES), lambda i: (0, i))
    taps_spec = pl.BlockSpec((SUB, SUB, LANES), lambda i: (0, 0, i))
    swap_scratch = [dma, dma((parts - 1,)), dma((parts - 1,))]
    all_states = shape((parts, rows, NST, D), bf16)
    y_loc, ends_all = pl.pallas_call(
        conv_forward_kernel,
        grid=(D // LANES,),
        in_specs=[group_spec, ANY, tab_a_spec, tab_b_spec, power_spec, coup_spec, taps_spec],
        out_specs=[group_spec, ANY],
        out_shape=[shape((rows, frames, D)), all_states],
        scratch_shapes=[vm(SUB + frames, LANES)] + swap_scratch,
        compiler_params=talking(3),
        name="conv_forward",
    )(u, ends, tab_a, tab_b, power, coupling, taps_f)

    edge_spec = pl.BlockSpec((1, PAD, D), lambda i: (i, 0, 0))
    edge_scratch = [
        vm(rows, 2, PAD, D, dtype=bf16),
        vm(PAD, D, dtype=bf16),
        dma((2, rows)),
        dma((2, rows)),
        dma((2,)),
    ]
    edge_shapes = [shape((rows, PAD, D), bf16)] * 2
    ys, gated, x2, pw, g, g_low, g_high = pl.pallas_call(
        mixer_out_kernel,
        grid=(rows,),
        in_specs=[
            row_spec(frames, D),
            states_spec,
            state_spec,
            whole_spec(parts + 1, NST, D),
            flat_spec,
            row_spec(frames, D),
            small_spec,
            ANY,
            whole_spec(frames, HEADS * NST),
        ],
        out_specs=[
            row_spec(frames, D),
            row_spec(frames, 2 * D),
            row_spec(frames, D),
            row_spec(frames, 2 * D),
            row_spec(frames, D),
            ANY,
            ANY,
        ],
        out_shape=[
            shape((rows, frames, D), bf16),
            shape((rows, frames, 2 * D), bf16),
            shape((rows, frames, D)),
            shape((rows, frames, 2 * D), bf16),
            shape((rows, frames, D), bf16),
        ]
        + edge_shapes,
        scratch_shapes=[mat(D, 2 * D), mat(D, 2 * D), vm(HEADS * NST, D), dma] + edge_scratch,
        compiler_params=talking(4),
        name="mixer_out",
    )(y_loc, ends_all, starts, weigh_in, coupling, x1, small_params, stack, pfull)

    kept = lambda *widths: [mat(group * frames, w) for w in widths]
    grad_shape = shape(stack.shape, bf16)
    layer_out, dx3, dq, grads, gain_b, d_low, d_high = pl.pallas_call(
        partial(ffb_kernel, scaling),
        grid=(rows,),
        in_specs=[
            row_spec(frames, D),
            edge_spec,
            edge_spec,
            row_spec(frames, D),
            row_spec(frames, D),
            small_spec,
            ANY,
        ],
        out_specs=[
            row_spec(frames, D),
            row_spec(frames, D),
            row_spec(frames, D),
            ANY,
            whole_spec(2, 8, D),
            ANY,
            ANY,
        ],
        out_shape=[
            shape((rows, frames, D), bf16),
            shape((rows, frames, D)),
            shape((rows, frames, D), bf16),
            grad_shape,
            shape((2, 8, D)),
        ]
        + edge_shapes,
        scratch_shapes=[
            mat(D, FF),
            mat(FF, D),
            mat(D, D),
            vm(D, FF),
            vm(D, FF),
            vm(D, D),
            vm(D // LANES, frames + 2 * PAD, LANES),
            vm(frames, D),
            vm(2 * ffn + mix, BS, BS, dtype=bf16),
        ]
        + kept(FF, FF, D, D, D, D)
        + [dma]
        + edge_scratch,
        compiler_params=talking(5),
        name="ffb",
    )(g, g_low, g_high, x2, cotangent, small_params, stack)

    dx2, dy, back_ends, grads, gain_c, kernel_grads = pl.pallas_call(
        partial(mixer_back_kernel, scaling),
        grid=(rows,),
        in_specs=[
            row_spec(frames, D),
            edge_spec,
            edge_spec,
            row_spec(frames, D),
            edge_spec,
            edge_spec,
            row_spec(frames, 2 * D),
            row_spec(frames, D),
            row_spec(frames, 2 * D),
            row_spec(frames, D),
            row_spec(frames, D),
            small_spec,
            ANY,
            whole_spec(HEADS * NST, frames),
            ANY,
        ],
        out_specs=[
            row_spec(frames, D),
            row_spec(frames, D),
            state_spec,
            ANY,
            whole_spec(8, D),
            whole_spec(16, D),
        ],
        out_shape=[
            shape((rows, frames, D)),
            shape((rows, frames, D), bf16),
            shape((rows, NST, D), bf16),
            grad_shape,
            shape((8, D)),
            shape((16, D)),
        ],
        scratch_shapes=[
            mat(D, 2 * D),
            mat(D, 2 * D),
            vm(D, 2 * D),
            vm(D, 2 * D),
            vm(D // LANES, frames + 2 * PAD, LANES),
            vm(D // LANES, frames + 2 * PAD, LANES),
            vm(frames, D),
            vm(KW, 8, D),
            vm(4 * mix, BS, BS, dtype=bf16),
        ]
        + kept(D, 2 * D, D, 2 * D)
        + [dma],
        input_output_aliases={14: 3},
        compiler_params=PARAMS,
        name="mixer_back",
    )(
        dq, d_low, d_high, g, g_low, g_high, pw, x2, gated, ys, dx3, small_params, stack,
        pfull_t, grads,
    )

    nst_spec = pl.BlockSpec((rows, NST, LANES), lambda i: (0, 0, i))
    du_loc, t_one, t_two, ends_w, back_w, lag_grads, back_all = pl.pallas_call(
        conv_back_kernel,
        grid=(D // LANES,),
        in_specs=[
            group_spec, group_spec, ANY, tab_a_spec, tab_b_spec, power_spec, coup_spec, taps_spec
        ],
        out_specs=[
            group_spec,
            coup_spec,
            coup_spec,
            nst_spec,
            nst_spec,
            pl.BlockSpec((SUB, LANES), lambda i: (0, i)),
            ANY,
        ],
        out_shape=[
            shape((rows, frames, D)),
            shape((NST, D)),
            shape((NST, D)),
            shape((rows, NST, D)),
            shape((rows, NST, D)),
            shape((SUB, D)),
            all_states,
        ],
        scratch_shapes=[
            vm(SUB + frames, LANES),
            vm(SUB + frames, LANES),
            vm(SUB, SUB, LANES),
        ]
        + swap_scratch,
        compiler_params=talking(6),
        name="conv_back",
    )(u, dy, back_ends, tab_a, tab_b, power, coupling, taps_b)

    grad_zero, grads, gain_a, sums_c = pl.pallas_call(
        partial(ffa_back_kernel, scaling),
        grid=(rows,),
        in_specs=[
            row_spec(frames, D),
            states_spec,
            states_spec,
            state_spec,
            state_spec,
            state_spec,
            state_spec,
            whole_spec(3, parts, NST, D),
            flat_spec,
            row_spec(frames, D),
            row_spec(frames, D),
            row_spec(frames, FF),
            row_spec(frames, FF),
            row_spec(frames, D),
            small_spec,
            ANY,
            whole_spec(frames, HEADS * NST),
            ANY,
        ],
        out_specs=[row_spec(frames, D), ANY, whole_spec(2, 8, D), whole_spec(4, NST, D)],
        out_shape=[
            shape((rows, frames, D)),
            grad_shape,
            shape((2, 8, D)),
            shape((4, NST, D)),
        ],
        scratch_shapes=[
            mat(D, FF),
            mat(FF, D),
            mat(D, D),
            vm(D, FF),
            vm(D, FF),
            vm(D, D),
            vm(HEADS * NST, D),
            vm(2 * ffn + mix, BS, BS, dtype=bf16),
        ]
        + kept(FF, FF, D, D, D, D)
        + [dma],
        input_output_aliases={17: 1},
        compiler_params=PARAMS,
        name="ffa_back",
    )(
        du_loc, back_all, ends_all, back_ends, ends_w, back_w, starts, weigh_back, coupling,
        x1, features, inner_a, act_a, dx2, small_params, stack, mfin_t, grads,
    )

    lag_grad_c = jnp.sum(lag_decay * lag_grads[:, None, :], axis=0)
    lag_grad_r = jnp.sum(lag_decay * (lag[:, None] * lag_grads)[:, None, :], axis=0)
    d_coup = t_one + lag_grad_c + sums_c[0]
    start_back = sums_c[1] * begin_w
    d_first = d_coup * mix_all[1]
    d_second = d_coup * mix_all[0] + start_back
    d_rate = coupling * (t_two + lag_grad_r + sums_c[3])
    d_rate = d_rate + mix_all[1] * (begin * start_back + begin_w * sums_c[2])
    small_grads = [
        jnp.sum(gain_a, axis=1),
        jnp.sum(gain_c, axis=0, keepdims=True),
        jnp.sum(gain_b, axis=1),
        kernel_grads[:KW],
    ]
    stacked = jnp.concatenate(small_grads + [d_first, d_second, d_rate], axis=0) * scaling
    stacked = jnp.pad(stacked, ((0, -stacked.shape[0] % 8), (0, 0)))
    own = place * own_channels
    lanes_own = lambda v: lax.dynamic_slice_in_dim(v, own, own_channels, v.ndim - 1)
    stacked = stacked.reshape(-1, parts, own_channels).transpose(1, 0, 2)
    full_grad, owned, sums = reduce_grads(
        grads, stacked, parts, lax.axis_size("rows"), master.shape[1]
    )
    count_small = small_params.shape[0]
    small_sum = sums[:count_small]
    mix_sum = sums[count_small : count_small + 2 * NST]
    mix_sum = mix_sum.reshape(2, NST, own_channels).transpose(0, 2, 1)
    rate_sum = sums[count_small + 2 * NST : count_small + 3 * NST]
    rate_sum = jnp.sum(rate_sum.reshape(NST, own_heads, HALF), axis=2)
    decay_sum = -rate_sum.T * jnp.exp(decay_logs)
    new_small = lanes_own(small_params) - rate_small * small_sum
    new_decay = decay_logs - rate_small * decay_sum
    new_mix = state_mix - rate_small * mix_sum

    shard_w = jnp.exp(-lanes_own(rate_nc)[None] * (shard.astype(f32) * span)[:, None, None])
    start_grad = jnp.sum(lanes_own(back_all).astype(f32) * shard_w[:, None], axis=0) * lanes_own(mix_all[1])
    start_grad = start_grad.transpose(0, 2, 1)
    chosen = (state_source[None, :] == jnp.arange(rows, dtype=jnp.int32)[:, None]).astype(f32)
    grad_state = jnp.sum(chosen[:, :, None, None] * start_grad[None], axis=1)

    count, slice_rows = owned.shape[0], owned.shape[1]
    mine = lax.axis_index("rows") * slice_rows
    pick = (
        jnp.arange(slice_rows, dtype=jnp.int32)[:, None] + mine
        == jnp.arange(BS, dtype=jnp.int32)[None, :]
    ).astype(bf16)
    group = 11 if count % 11 == 0 else 1
    part_spec = pl.BlockSpec((group, slice_rows, BS), lambda i: (i, 0, 0))
    full_spec = pl.BlockSpec((group, BS, BS), lambda i: (i, 0, 0))
    new_left, new_right, new_master, new_copy, grad_blocks = pl.pallas_call(
        shampoo_kernel,
        grid=(count // group,),
        in_specs=[
            whole_spec(slice_rows, BS),
            part_spec,
            full_spec,
            part_spec,
            part_spec,
            part_spec,
            full_spec,
            part_spec,
        ],
        out_specs=[part_spec] * 5,
        out_shape=[
            shape(owned.shape),
            shape(owned.shape),
            shape(owned.shape),
            shape(owned.shape, bf16),
            shape(owned.shape),
        ],
        compiler_params=PARAMS,
        name="shampoo",
    )(pick, owned, full_grad, left_stats, right_stats, left_root, right_root, master)
    return (
        layer_out,
        grad_zero,
        grad_state,
        grad_blocks,
        new_left,
        new_right,
        new_master,
        new_copy,
        small_sum,
        new_small,
        decay_sum,
        mix_sum,
        new_decay,
        new_mix,
    )


def solution(mesh):
    return jax.shard_map(
        body,
        mesh=mesh,
        in_specs=(
            P("rows", "tm", None),
            P("rows", "tm", None),
            P("rows", "tm", None),
            P("rows"),
            P("tm", "rows", None),
            P("tm", "rows", None),
            P("tm", "rows", None),
            P("tm", "rows", None),
            P("tm", None, None),
            P(),
            P("tm", None),
            P(None, "tm", None),
        ),
        out_specs=(
            P("rows", "tm", None),
            P("rows", "tm", None),
            P("rows", "tm", None),
            P("tm", "rows", None),
            P("tm", "rows", None),
            P("tm", "rows", None),
            P("tm", "rows", None),
            P("tm", "rows", None),
            P(None, "tm"),
            P(None, "tm"),
            P("tm", None),
            P(None, "tm", None),
            P("tm", None),
            P(None, "tm", None),
        ),
        check_vma=False,
    )
```

```python
from functools import partial
import math

import jax
import jax.numpy as jnp
from jax import lax
from jax.experimental import pallas as pl
from jax.experimental.pallas import tpu as pltpu
from jax.sharding import PartitionSpec as P

D = 512
FF = 2048
NST = 32
KW = 15
BS = 256
HEADS = 8
HALF = 64
LANES = 128
SUB = 16
GROUP = 5
BOTH = 2
PAD = 8
VMEM_BYTES = 60 * 1024 * 1024

rate_blocks = 0.1
rate_small = 0.5
bf16 = jnp.bfloat16
f32 = jnp.float32


def shape(dims, dtype=f32):
    return jax.ShapeDtypeStruct(dims, dtype)


def mm(a, b):
    return jnp.dot(a, b, preferred_element_type=f32)


def mm_nt(a, b):
    return lax.dot_general(a, b, (((1,), (1,)), ((), ())), preferred_element_type=f32)


def mm_tn(a, b):
    return lax.dot_general(a, b, (((0,), (0,)), ((), ())), preferred_element_type=f32)


def sigmoid(v):
    return 0.5 * jnp.tanh(0.5 * v) + 0.5


def norm(v):
    center = v - jnp.mean(v, axis=-1, keepdims=True)
    spread = jnp.mean(center * center, axis=-1, keepdims=True)
    inv = lax.rsqrt(spread + 1e-05)
    return center * inv, inv


def norm_back(hat, inv, scale, incoming):
    scaled = incoming * scale
    mean_one = jnp.mean(scaled, axis=-1, keepdims=True)
    mean_two = jnp.mean(scaled * hat, axis=-1, keepdims=True)
    return inv * (scaled - mean_one - hat * mean_two)


def flat(ref):
    v = ref[...]
    return v.reshape(-1, v.shape[-1])


def put_rows(ref, v):
    ref[...] = v.astype(ref.dtype).reshape(ref.shape)


def fold8(v):
    return jnp.sum(v.reshape(-1, 8, v.shape[-1]), axis=0)


def load_matrices(stack, plan, sem):
    copies = []
    for first, dst in plan:
        down, across = dst.shape[0] // BS, dst.shape[1] // BS
        for i in range(down):
            for j in range(across):
                copies.append(
                    pltpu.make_async_copy(
                        stack.at[first + i * across + j],
                        dst.at[pl.ds(i * BS, BS), pl.ds(j * BS, BS)],
                        sem,
                    )
                )
    for copy in copies:
        copy.start()
    for copy in copies:
        copy.wait()


def store_blocks(plan, scaling, grads, stage, sem):
    copies = []
    for acc, first, transposed in plan:
        rows, cols = acc.shape
        down, across = (cols, rows) if transposed else (rows, cols)
        for i in range(down // BS):
            for j in range(across // BS):
                slot = len(copies)
                if transposed:
                    part = (acc[pl.ds(j * BS, BS), pl.ds(i * BS, BS)] * scaling).T
                else:
                    part = acc[pl.ds(i * BS, BS), pl.ds(j * BS, BS)] * scaling
                stage[slot] = part.astype(bf16)
                copy = pltpu.make_async_copy(
                    stage.at[slot], grads.at[first + i * (across // BS) + j], sem
                )
                copy.start()
                copies.append(copy)
    for copy in copies:
        copy.wait()


def head_mask():
    row = lax.broadcasted_iota(jnp.int32, (HEADS * NST, D), 0) // NST
    col = lax.broadcasted_iota(jnp.int32, (HEADS * NST, D), 1) // HALF
    return (row == col).astype(f32)


def spread_heads(v, mask):
    return (jnp.concatenate([v] * HEADS, axis=0) * mask).astype(bf16)


def local_states(table, v, out):
    frames = table.shape[1]
    first = lax.broadcasted_iota(jnp.int32, (NST, LANES), 1) < HALF
    for b in range(out.shape[0]):
        for g in range(D // LANES):
            here = v[b * frames : (b + 1) * frames, g * LANES : (g + 1) * LANES]
            both = mm(table[pl.ds(2 * NST * g, 2 * NST), :], here)
            picked = jnp.where(first, both[:NST], both[NST:])
            out[b, :, pl.ds(g * LANES, LANES)] = picked.astype(out.dtype)


ANY = pl.BlockSpec(memory_space=pl.ANY)
PARAMS = pltpu.CompilerParams(
    dimension_semantics=("arbitrary",), vmem_limit_bytes=VMEM_BYTES
)


def vm(*dims, dtype=f32):
    return pltpu.VMEM(dims, dtype)


def peers():
    place, row = lax.axis_index("tm"), lax.axis_index("rows")
    return place, row // 2, row % 2


def square(place):
    x, y = place % 2, place // 2
    return 2 * y + 1 - x, 2 * (1 - y) + x, 2 * (1 - y) + 1 - x


def at(place, level, core):
    return {"tm": place, "rows": level * 2 + core}


def remote(src, dst, send, recv, device):
    return pltpu.make_async_remote_copy(
        src_ref=src,
        dst_ref=dst,
        send_sem=send,
        recv_sem=recv,
        device_id=device,
        device_id_type=pl.DeviceIdType.MESH,
    )


def signal(sem, device):
    pl.semaphore_signal(sem, inc=1, device_id=device, device_id_type=pl.DeviceIdType.MESH)


def chunk_ranges(count, chunks):
    edges = [count * c // chunks for c in range(chunks + 1)]
    out = []
    for first, end in zip(edges[:-1], edges[1:]):
        middle = (first + end + 1) // 2
        out.append((first, end, middle))
    return out


class Gather:
    def __init__(self, piece, stack, sems, chunks=1):
        self.piece, self.stack, self.sems = piece, stack, sems
        self.place, self.level, self.core = peers()
        self.xp, self.yp, self.dp = square(self.place)
        self.levels = stack.shape[2]
        self.ranges = chunk_ranges(stack.shape[1], chunks)
        self.all = range(chunks)

    def own(self, c):
        first, end, unused = self.ranges[c]
        n = pl.ds(first, end - first)
        spot = self.stack.at[self.place, n, self.level, self.core]
        return pltpu.make_async_copy(self.piece.at[n], spot, self.sems["own"].at[c])

    def z(self, c, d):
        first, end, unused = self.ranges[c]
        n = pl.ds(first, end - first)
        spot = self.stack.at[self.place, n, self.level, self.core]
        send, recv = self.sems["zs"].at[c, d - 1], self.sems["zr"].at[c, d - 1]
        target = (self.level + d) % self.levels
        return remote(self.piece.at[n], spot, send, recv, at(self.place, target, self.core))

    def z_start(self, c):
        self.own(c).start()
        for d in range(1, self.levels):
            self.z(c, d).start()

    def z_arrive(self, c):
        self.own(c).wait()
        for d in range(1, self.levels):
            self.z(c, d).wait_recv()

    def z_end(self, c):
        for d in range(1, self.levels):
            self.z(c, d).wait_send()

    def part(self, name, c, i, owner, first, end, device):
        spot = self.stack.at[owner, pl.ds(first, end - first), :, self.core]
        send, recv = self.sems[name + "s"].at[c, i], self.sems[name + "r"].at[c, i]
        return remote(spot, spot, send, recv, device)

    def x(self, c, i):
        first, end, mid = self.ranges[c]
        what = ((self.place, first, mid), (self.place, mid, end), (self.yp, mid, end))[i]
        return self.part("x", c, i, *what, at(self.xp, self.level, self.core))

    def y(self, c, i):
        first, end, mid = self.ranges[c]
        what = ((self.place, mid, end), (self.place, first, mid), (self.xp, first, mid))[i]
        return self.part("y", c, i, *what, at(self.yp, self.level, self.core))

    def other(self, c, i):
        first, end, mid = self.ranges[c]
        what = (
            (self.place, first, end),
            (self.xp, first, mid),
            (self.yp, mid, end),
            (self.xp, mid, end),
            (self.yp, first, mid),
            (self.dp, first, mid),
            (self.dp, mid, end),
        )[i]
        return self.part("c", c, i, *what, at(self.place, self.level, 1 - self.core))

    def spread(self, c):
        for copy in (self.x(c, 0), self.y(c, 0), self.x(c, 1), self.y(c, 1), self.other(c, 0)):
            copy.start()

    def forward(self, c):
        self.x(c, 0).wait_recv()
        self.y(c, 2).start()
        self.y(c, 0).wait_recv()
        self.x(c, 2).start()
        self.other(c, 1).start()
        self.other(c, 2).start()
        self.x(c, 1).wait_recv()
        self.other(c, 3).start()
        self.y(c, 1).wait_recv()
        self.other(c, 4).start()

    def finish(self, c):
        self.y(c, 2).wait_recv()
        self.other(c, 5).start()
        self.x(c, 2).wait_recv()
        self.other(c, 6).start()

    def end(self, c):
        for i in range(7):
            self.other(c, i).wait_recv()
        for i in range(7):
            self.other(c, i).wait_send()
        for i in range(3):
            self.x(c, i).wait_send()
            self.y(c, i).wait_send()


Z_SEMS = ("own", "zs", "zr")
XY_SEMS = ("xs", "xr", "ys", "yr", "cs", "cr")


def gather_sems(names, levels, chunks=1):
    width = {"own": (), "z": (levels - 1,), "x": (3,), "y": (3,), "c": (7,)}
    key = lambda name: name if name == "own" else name[0]
    return [pltpu.SemaphoreType.DMA((chunks,) + width[key(name)]) for name in names]


def block_sets():
    ffn, mix = D // BS * (FF // BS), (D // BS) ** 2
    ids = lambda *ranges: [b for first, end in ranges for b in range(first, end)]
    return (
        ids((0, 2 * ffn), (4 * ffn, 4 * ffn + mix)),
        ids((4 * ffn + mix, 4 * ffn + 5 * mix)),
        ids((2 * ffn, 4 * ffn), (4 * ffn + 5 * mix, 4 * ffn + 6 * mix)),
    )


def move_runs(ids, places, count):
    runs, each = [], len(ids) // places
    for index, b in enumerate(ids):
        owner, k, v, j = b // count, b % count, index // each, index % each
        if runs:
            o0, k0, v0, j0, n0 = runs[-1]
            if (o0, v0) == (owner, v) and k0 + n0 == k:
                runs[-1] = (o0, k0, v0, j0, n0 + 1)
                continue
        runs.append((owner, k, v, j, 1))
    return runs


def greet(devices):
    barrier = pltpu.get_barrier_semaphore()
    for device in devices:
        signal(barrier, device)


def met(count):
    pl.semaphore_wait(pltpu.get_barrier_semaphore(), count)


def gather_kernel(
    master, pack, first, pair, rest, pack_all,
    rounded, piece, piece_pair, piece_rest, run_send, run_recv, pk_send, pk_recv, *sems,
):
    place, level, core = peers()
    others = square(place)
    levels = first.shape[2]
    greet([at(other, level, core) for other in others] + [at(place, level, 1 - core)])
    greet([at(place, (level + d) % levels, core) for d in range(1, levels)])
    rounded[...] = master[...].astype(bf16)
    met(3 + levels)
    moves = []
    for ids, target in zip(block_sets(), (piece, piece_pair, piece_rest)):
        for run in move_runs(ids, first.shape[0], master.shape[0]):
            moves.append((len(moves), target) + run)

    def move(index, target, owner, k, v, j, n):
        src, dst = rounded.at[pl.ds(k, n)], target.at[pl.ds(j, n)]
        if owner == v:
            return pltpu.make_async_copy(src, dst, run_send.at[index])
        return remote(src, dst, run_send.at[index], run_recv.at[index], at(v, level, core))

    def arrive(entry):
        index, target, owner, k, v, j, n = entry
        if owner == v:
            pl.when(place == v)(lambda: move(*entry).wait())
        else:
            pl.when(place == v)(lambda: move(*entry).wait_recv())

    for entry in moves:
        pl.when(place == entry[2])(lambda entry=entry: move(*entry).start())
    own_pack = pltpu.make_async_copy(pack, pack_all.at[place], pk_send.at[3])
    own_pack.start()
    packs = [
        remote(pack, pack_all.at[place], pk_send.at[d], pk_recv.at[d], at(other, level, core))
        for d, other in enumerate(others)
    ]
    for copy in packs:
        copy.start()
    for entry in moves:
        if entry[1] is piece:
            arrive(entry)
    names = Z_SEMS + XY_SEMS
    chunks = sems[0].shape[0]
    it = Gather(piece, first, dict(zip(names, sems)), chunks)
    later, sems = [], sems[len(names) :]
    for i, (what, stack) in enumerate(((piece_pair, pair), (piece_rest, rest))):
        later.append(Gather(what, stack, dict(zip(Z_SEMS, sems[3 * i : 3 * i + 3]))))
    it.z_start(0)
    for c in it.all:
        it.z_arrive(c)
        it.spread(c)
        if c == 0:
            for ahead in range(1, chunks):
                it.z_start(ahead)
            for entry in moves:
                if entry[1] is not piece:
                    arrive(entry)
        if c == chunks - 1:
            for other_set in later:
                other_set.z_start(0)
        if c >= 1:
            it.forward(c - 1)
        if c >= 2:
            it.finish(c - 2)
    it.forward(chunks - 1)
    for c in range(max(chunks - 2, 0), chunks):
        it.finish(c)
    for c in it.all:
        it.end(c)
        it.z_end(c)
    for other_set in later:
        other_set.z_arrive(0)
        other_set.z_end(0)
    for entry in moves:
        if entry[2] != entry[4]:
            pl.when(place == entry[2])(lambda entry=entry: move(*entry).wait_send())
    own_pack.wait()
    for copy in packs:
        copy.wait()


def gather_first(master, pack, parts, devices, chunks=3):
    count, slab, cols = master.shape
    levels = devices // 2
    each = [len(ids) // parts for ids in block_sets()]
    runs = sum(len(move_runs(ids, parts, count)) for ids in block_sets())
    dma = lambda *dims: pltpu.SemaphoreType.DMA(dims)
    return pl.pallas_call(
        gather_kernel,
        in_specs=[pl.BlockSpec(memory_space=pltpu.VMEM), ANY],
        out_specs=[ANY] * 4,
        out_shape=[
            shape((parts, each[0], levels, 2, slab, cols), bf16),
            shape((parts, each[1], levels, 2, slab, cols), bf16),
            shape((parts, each[2], levels, 2, slab, cols), bf16),
            shape((parts,) + pack.shape, pack.dtype),
        ],
        scratch_shapes=[
            vm(count, slab, cols, dtype=bf16),
            vm(each[0], slab, cols, dtype=bf16),
            vm(each[1], slab, cols, dtype=bf16),
            vm(each[2], slab, cols, dtype=bf16),
            dma(runs),
            dma(runs),
            dma(4),
            dma(3),
        ]
        + gather_sems(Z_SEMS + XY_SEMS, levels, chunks)
        + gather_sems(Z_SEMS, levels) * 2,
        compiler_params=pltpu.CompilerParams(
            collective_id=1, has_side_effects=True, vmem_limit_bytes=VMEM_BYTES
        ),
        name="gather_first",
    )(master, pack)


def ffa_forward_kernel(feat, small, stack, mfin, *refs):
    step, last = pl.program_id(0), pl.num_programs(0) - 1
    pair = None
    if len(refs) > 9:
        refs, sems = refs[1:7] + refs[7:11], refs[11:]
        pair = Gather(None, refs[5], dict(zip(XY_SEMS, sems)))
        refs = refs[:5] + refs[6:]
    x1_o, inner_o, act_o, u_o, f_o, wi, wo, wu, sem = refs

    @pl.when(step == 0)
    def _():
        if pair is not None:
            place, level, core = peers()
            greet([at(other, level, core) for other in square(place)])
            greet([at(place, level, 1 - core)])
        ffn, mix = D // BS * (FF // BS), (D // BS) ** 2
        load_matrices(stack, ((0, wi), (ffn, wo), (2 * ffn, wu)), sem)
        if pair is not None:
            met(4)
            pair.spread(0)

    x0 = flat(feat).astype(f32)
    hat, unused = norm(x0)
    inner = mm((hat * small[0:1]).astype(bf16), wi[...])
    act = (inner * sigmoid(inner)).astype(bf16)
    put_rows(inner_o, inner)
    put_rows(act_o, act)
    x1 = x0 + 0.5 * mm(act, wo[...])
    put_rows(x1_o, x1)
    hat, unused = norm(x1)
    u = mm((hat * small[1:2]).astype(bf16), wu[...]).astype(bf16)
    put_rows(u_o, u)
    local_states(mfin, u, f_o)
    if pair is not None:
        pl.when(step == last - 1)(lambda: pair.forward(0))

        @pl.when(step == last)
        def _():
            pair.finish(0)
            pair.end(0)


def pack_heads(ref, rows):
    first = lax.broadcasted_iota(jnp.int32, (ref.shape[1], LANES), 1) < HALF
    low, high = [], []
    for p in range(rows // 2):
        a, b = ref[2 * p].astype(f32), ref[2 * p + 1].astype(f32)
        low.append(jnp.where(first, a, pltpu.roll(b, HALF, 1)).astype(bf16))
        high.append(jnp.where(first, pltpu.roll(a, HALF, 1), b).astype(bf16))
    return jnp.concatenate(low, axis=1), jnp.concatenate(high, axis=1)


def pack_params(v, rows):
    first = lax.broadcasted_iota(jnp.int32, v.shape, 1) < HALF
    rolled = pltpu.roll(v, HALF, 1)
    low = jnp.where(first, v, rolled)
    high = jnp.where(first, rolled, v)
    return (
        jnp.concatenate([low] * (rows // 2), axis=1),
        jnp.concatenate([high] * (rows // 2), axis=1),
    )


def unpack_pair(low, high, p):
    low = low[:, p * LANES : (p + 1) * LANES]
    high = high[:, p * LANES : (p + 1) * LANES]
    first = lax.broadcasted_iota(jnp.int32, low.shape, 1) < HALF
    return (
        jnp.where(first, low, pltpu.roll(high, HALF, 1)),
        jnp.where(first, pltpu.roll(low, HALF, 1), high),
    )


def swap_states(mine, whole, first_step, last_step, own_sem, send, recv, pair=None):
    place, level, core = peers()
    parts = whole.shape[0]
    others = [(place + d) % parts for d in range(1, parts)]

    def copies():
        return [
            remote(mine, whole.at[place], send.at[d], recv.at[d], at(other, level, core))
            for d, other in enumerate(others)
        ]

    own = lambda: pltpu.make_async_copy(mine, whole.at[place], own_sem)

    @pl.when(first_step)
    def _():
        barrier = pltpu.get_barrier_semaphore()
        for other in others:
            signal(barrier, at(other, level, core))
        if pair is not None:
            signal(barrier, at(place, level, 1 - core))
        own().start()

    def end():
        @pl.when(first_step)
        def _():
            met(parts - 1 + (pair is not None))
            for copy in copies():
                copy.start()
            if pair is not None:
                pair.spread(0)

        if pair is not None:
            step = pl.program_id(0)

            @pl.when(step == pl.num_programs(0) - 2)
            def _():
                pair.forward(0)

            @pl.when(last_step)
            def _():
                pair.finish(0)
                pair.end(0)

        @pl.when(last_step)
        def _():
            own().wait()
            for copy in copies():
                copy.wait()

    return end


def tile_lanes(v, width):
    return jnp.concatenate([v] * (width // LANES), axis=1)


def conv_forward_kernel(u, ends, tab_a, tab_b, power, coup, taps, *refs):
    step = pl.program_id(0)
    pair = None
    if len(refs) > 6:
        refs, sems = refs[1:7] + refs[7:8], refs[8:]
        pair = Gather(None, refs[2], dict(zip(XY_SEMS, sems)), 2)
        refs = refs[:2] + refs[3:]
    y_o, ends_all, pad, own_sem, send, recv = refs
    end_swap = swap_states(
        ends, ends_all, step == 0, step == pl.num_programs(0) - 1, own_sem, send, recv, pair
    )
    rows, frames = u.shape[0], u.shape[1]
    span = GROUP * SUB
    coup_both = pack_params(coup[...], rows)
    packed = pack_heads(u, rows)
    width = packed[0].shape[1]
    results = []
    for h in range(2):
        scale = [tile_lanes(power[h, i], width) for i in range(GROUP)]
        carry = None
        outs = []
        for g in range(frames // span):
            local = mm(tab_a[h, 0], packed[h][g * span : (g + 1) * span])
            parts = [local[i * NST : (i + 1) * NST] for i in range(GROUP)]
            if carry is None:
                states = [jnp.zeros_like(parts[0])] + parts[:-1]
                carry = parts[-1]
            else:
                states = [carry] + [parts[i] + scale[i] * carry for i in range(GROUP - 1)]
                carry = parts[-1] + scale[-1] * carry
            scaled = jnp.concatenate([v * coup_both[h] for v in states], axis=0)
            outs.append(mm(tab_b[h, 1], scaled.astype(bf16)))
        results.append(jnp.concatenate(outs, axis=0))
    for p in range(rows // 2):
        one, two = unpack_pair(results[0], results[1], p)
        y_o[2 * p] = one
        y_o[2 * p + 1] = two
    pad[0:SUB] = jnp.zeros((SUB, LANES), f32)
    chunk = frames // 5

    def one_row(i, carry):
        pad[pl.ds(SUB, frames)] = u[i].astype(f32)
        for r in range(0, frames, chunk):
            acc = y_o[i, pl.ds(r, chunk)].reshape(-1, SUB, LANES)
            for d in range(SUB):
                piece = pad[pl.ds(SUB + r - d, chunk)].reshape(-1, SUB, LANES)
                acc = acc + piece * taps[d][None]
            y_o[i, pl.ds(r, chunk)] = acc.reshape(chunk, LANES)
        return carry

    lax.fori_loop(0, rows, one_row, 0)
    end_swap()


def edge_sender(edges, low_all, high_all, zeros, send, recv, zero_sem, step, per, rest=None):
    place, level, core = peers()
    parts = lax.axis_size("tm")
    steps = edges.shape[0]
    not_first, not_last = place > 0, place < parts - 1
    after = (place + 1) % parts
    before = (place + parts - 1) % parts

    def up(i):
        return remote(
            edges.at[i, 1], low_all.at[i], send.at[0, i], recv.at[0, i], at(after, level, core)
        )

    def down(i):
        return remote(
            edges.at[i, 0], high_all.at[i], send.at[1, i], recv.at[1, i], at(before, level, core)
        )

    def blank(ref, i, k):
        return pltpu.make_async_copy(zeros, ref.at[i], zero_sem.at[k])

    @pl.when(step == 0)
    def _():
        if rest is None:
            pl.when(not_last)(lambda: greet([at(after, level, core)]))
            pl.when(not_first)(lambda: greet([at(before, level, core)]))
        else:
            greet([at(other, level, core) for other in square(place)])
            greet([at(place, level, 1 - core)])
        zeros[...] = jnp.zeros_like(zeros)

        @pl.when(place == 0)
        def _():
            for i in range(steps):
                blank(low_all, i, 0).start()

        @pl.when(place == parts - 1)
        def _():
            for i in range(steps):
                blank(high_all, i, 1).start()

    def put(v):
        @pl.when(step == 0)
        def _():
            below = (place + parts - 1) // parts
            above = (2 * parts - 2 - place) // parts
            met(below + above if rest is None else parts)
            if rest is not None:
                rest.spread(1)

        if rest is not None:
            pl.when(step == steps // per // 2)(lambda: rest.forward(1))
            pl.when(step == steps // per - 1)(lambda: rest.finish(1))

        frames = v.shape[0] // per
        for b in range(per):
            row = step * per + b
            edges[row, 0] = v[b * frames : b * frames + PAD]
            edges[row, 1] = v[(b + 1) * frames - PAD : (b + 1) * frames]
            pl.when(not_last)(lambda row=row: up(row).start())
            pl.when(not_first)(lambda row=row: down(row).start())

        @pl.when(step == steps // per - 1)
        def _():
            for i in range(steps):
                pl.when(not_last)(lambda i=i: up(i).wait_send())
                pl.when(not_first)(lambda i=i: down(i).wait_send())
                pl.when(not_first)(lambda i=i: up(i).wait_recv())
                pl.when(not_last)(lambda i=i: down(i).wait_recv())

            if rest is not None:
                rest.end(1)

            @pl.when(place == 0)
            def _():
                for i in range(steps):
                    blank(low_all, i, 0).wait()

            @pl.when(place == parts - 1)
            def _():
                for i in range(steps):
                    blank(high_all, i, 1).wait()

    return put


def mixer_out_kernel(
    y, ends_all, starts, weigh, coup, x1, small, stack, pfull, *refs
):
    step = pl.program_id(0)
    rest = None
    if len(refs) > 16:
        refs, sems = refs[1:8] + refs[8:18], refs[18:]
        rest = Gather(None, refs[7], dict(zip(XY_SEMS, sems)), 2)
        refs = refs[:7] + refs[8:]
    ys_o, gated_o, x2_o, pw_o, g_o, low_o, high_o, wo, wp, mask, sem = refs[:11]
    edges, zeros, send, recv, zero_sem = refs[11:]
    put = edge_sender(edges, low_o, high_o, zeros, send, recv, zero_sem, step, 1, rest)

    @pl.when(step == 0)
    def _():
        ffn, mix = D // BS * (FF // BS), (D // BS) ** 2
        load_matrices(stack, ((0, wo), (2 * mix, wp)), sem)
        mask[...] = head_mask()

    came = weigh[0] * ends_all[0, 0].astype(f32)
    for i in range(1, ends_all.shape[0]):
        came = came + weigh[i] * ends_all[i, 0].astype(f32)
    zin = coup[...] * came + weigh[ends_all.shape[0]] * starts[0]
    ys = (y[0] + mm(pfull[...], spread_heads(zin, mask[...]))).astype(bf16)
    ys_o[0] = ys
    gated = mm(ys, wo[...])
    gated_o[0] = gated.astype(bf16)
    x2 = x1[0] + gated[:, :D] * sigmoid(gated[:, D:])
    x2_o[0] = x2
    hat, unused = norm(x2)
    pw = mm((hat * small[2:3]).astype(bf16), wp[...])
    pw_o[0] = pw.astype(bf16)
    g = (pw[:, :D] * sigmoid(pw[:, D:])).astype(bf16)
    g_o[0] = g
    put(g)


def fill_pad(pad, low, body, high):
    frames = body.shape[0]
    for g in range(D // LANES):
        lanes = slice(g * LANES, (g + 1) * LANES)
        pad[g, 0:PAD] = low[:, lanes].astype(f32)
        pad[g, pl.ds(PAD, frames)] = body[:, lanes].astype(f32)
        pad[g, pl.ds(PAD + frames, PAD)] = high[:, lanes].astype(f32)


def ffb_kernel(
    scale, g, low, high, x2, cot, small, stack,
    out_o, dx3_o, dq_o, grads, gain_o, low_o, high_o,
    wi, wo, wq, acc_in, acc_out, acc_q, pad, q_s, stage, k_act, k_din, k_n, k_dp, k_a, k_dpq, sem,
    edges, zeros, send, recv, zero_sem,
):
    step = pl.program_id(0)
    frames = g.shape[1]
    put = edge_sender(edges, low_o, high_o, zeros, send, recv, zero_sem, step, 1)

    @pl.when(step == 0)
    def _():
        ffn, mix = D // BS * (FF // BS), (D // BS) ** 2
        load_matrices(stack, ((0, wi), (ffn, wo), (2 * ffn, wq)), sem)
        acc_in[...] = jnp.zeros_like(acc_in)
        acc_out[...] = jnp.zeros_like(acc_out)
        acc_q[...] = jnp.zeros_like(acc_q)
        gain_o[...] = jnp.zeros_like(gain_o)

    fill_pad(pad, low[0], g[0], high[0])
    chunk = frames // 5
    for c in range(D // LANES):
        lanes = slice(c * LANES, (c + 1) * LANES)
        for r in range(0, frames, chunk):
            acc = small[5:6, lanes] * pad[c, pl.ds(r + PAD - 7, chunk)]
            for j in range(1, KW):
                acc = acc + small[5 + j : 6 + j, lanes] * pad[c, pl.ds(r + j + PAD - 7, chunk)]
            q_s[pl.ds(r, chunk), lanes] = acc
    q = q_s[...]
    sig_q = sigmoid(q)
    act_q = q * sig_q
    a3 = act_q.astype(bf16)
    x3 = x2[0] + mm(a3, wq[...])
    hat3, inv3 = norm(x3)
    n3 = (hat3 * small[3:4]).astype(bf16)
    inner = mm(n3, wi[...])
    sig = sigmoid(inner)
    act = inner * sig
    b4 = act.astype(bf16)
    x4 = x3 + 0.5 * mm(b4, wo[...])
    hat4, inv4 = norm(x4)
    out_o[0] = (hat4 * small[4:5]).astype(bf16)
    c4 = cot[0].astype(f32)
    gain_o[1] += fold8(c4 * hat4)
    dx4 = norm_back(hat4, inv4, small[4:5], c4)
    dp = (0.5 * dx4).astype(bf16)
    dact = mm_nt(dp, wo[...])
    dinner = ((sig + act * (1.0 - sig)) * dact).astype(bf16)
    group = k_n.shape[0] // frames
    keep = pl.ds(pl.multiple_of(step % group * frames, frames), frames)
    k_act[keep] = b4
    k_din[keep] = dinner
    k_n[keep] = n3
    k_dp[keep] = dp
    k_a[keep] = a3
    dn3 = mm_nt(dinner, wi[...])
    gain_o[0] += fold8(dn3 * hat3)
    dx3 = dx4 + norm_back(hat3, inv3, small[3:4], dn3)
    dx3_o[0] = dx3
    dpq = dx3.astype(bf16)
    k_dpq[keep] = dpq
    da3 = mm_nt(dpq, wq[...])
    dq = ((sig_q + act_q * (1.0 - sig_q)) * da3).astype(bf16)
    dq_o[0] = dq
    put(dq)

    @pl.when(step % group == group - 1)
    def _():
        acc_out[...] += mm_tn(k_dp[...], k_act[...])
        acc_in[...] += mm_tn(k_n[...], k_din[...])
        acc_q[...] += mm_tn(k_a[...], k_dpq[...])

    @pl.when(step == pl.num_programs(0) - 1)
    def _():
        ffn, mix = D // BS * (FF // BS), (D // BS) ** 2
        plan = (
            (acc_in, 2 * ffn, False),
            (acc_out, 3 * ffn, True),
            (acc_q, 4 * ffn + 5 * mix, False),
        )
        store_blocks(plan, scale, grads, stage, sem)


def mixer_back_kernel(
    scale, dq, dlow, dhigh, g, glow, ghigh, pw, x2, gated, ys, dx3, small, stack, pfull_t, grads_in,
    dx2_o, dy_o, gst_o, grads, gain_o, dk_o,
    wo, wp, acc_p, acc_o, dpad, gpad, dg_s, dk_s, stage, k_n, k_dpw, k_ys, k_dg, sem,
):
    step = pl.program_id(0)
    frames = dq.shape[1]

    @pl.when(step == 0)
    def _():
        ffn, mix = D // BS * (FF // BS), (D // BS) ** 2
        load_matrices(stack, ((0, wo), (2 * mix, wp)), sem)
        acc_p[...] = jnp.zeros_like(acc_p)
        acc_o[...] = jnp.zeros_like(acc_o)
        gain_o[...] = jnp.zeros_like(gain_o)
        dk_s[...] = jnp.zeros_like(dk_s)

    fill_pad(dpad, dlow[0], dq[0], dhigh[0])
    fill_pad(gpad, glow[0], g[0], ghigh[0])
    chunk = frames // 5
    for c in range(D // LANES):
        lanes = slice(c * LANES, (c + 1) * LANES)
        for r in range(0, frames, chunk):
            here = dpad[c, pl.ds(r + PAD, chunk)]
            acc = small[5:6, lanes] * dpad[c, pl.ds(r + PAD + 7, chunk)]
            for j in range(1, KW):
                acc = acc + small[5 + j : 6 + j, lanes] * dpad[c, pl.ds(r - j + PAD + 7, chunk)]
            dg_s[pl.ds(r, chunk), lanes] = acc
            for j in range(KW):
                dk_s[j, :, lanes] += fold8(here * gpad[c, pl.ds(r + j + PAD - 7, chunk)])
    dg = dg_s[...]
    value = pw[0, :, :D].astype(f32)
    gate = sigmoid(pw[0, :, D:].astype(f32))
    dvalue = (dg * gate).astype(bf16)
    dgate = (dg * value * gate * (1.0 - gate)).astype(bf16)
    dpw = jnp.concatenate([dvalue, dgate], axis=1)
    hat2, inv2 = norm(x2[0])
    n2 = (hat2 * small[2:3]).astype(bf16)
    group = k_n.shape[0] // frames
    keep = pl.ds(pl.multiple_of(step % group * frames, frames), frames)
    k_n[keep] = n2
    k_dpw[keep] = dpw
    k_ys[keep] = ys[0]
    dn2 = mm_nt(dpw, wp[...])
    gain_o[...] += fold8(dn2 * hat2)
    dx2 = dx3[0] + norm_back(hat2, inv2, small[2:3], dn2)
    dx2_o[0] = dx2
    value = gated[0, :, :D].astype(f32)
    gate = sigmoid(gated[0, :, D:].astype(f32))
    dvalue = (dx2 * gate).astype(bf16)
    dgate = (dx2 * value * gate * (1.0 - gate)).astype(bf16)
    dgated = jnp.concatenate([dvalue, dgate], axis=1)
    k_dg[keep] = dgated
    dy = mm_nt(dgated, wo[...]).astype(bf16)
    dy_o[0] = dy
    local_states(pfull_t, dy, gst_o)

    @pl.when(step % group == group - 1)
    def _():
        acc_p[...] += mm_tn(k_n[...], k_dpw[...])
        acc_o[...] += mm_tn(k_ys[...], k_dg[...])

    @pl.when(step == pl.num_programs(0) - 1)
    def _():
        ffn, mix = D // BS * (FF // BS), (D // BS) ** 2
        plan = ((acc_o, 4 * ffn + mix, False), (acc_p, 4 * ffn + 3 * mix, False))
        store_blocks(plan, scale, grads, stage, sem)
        for j in range(KW):
            dk_o[j : j + 1] = jnp.sum(dk_s[j], axis=0, keepdims=True)


def conv_back_kernel(
    u, dy, back_ends, tab_a, tab_b, power, coup, taps,
    du_o, t1_o, t2_o, fp_o, gp_o, dk_o, back_all,
    upad, dpad, acc_s, own_sem, send, recv,
):
    step = pl.program_id(0)
    end_swap = swap_states(
        back_ends, back_all, step == 0, step == pl.num_programs(0) - 1, own_sem, send, recv
    )
    rows, frames = u.shape[0], u.shape[1]
    span = GROUP * SUB
    coup_both = pack_params(coup[...], rows)
    u_both = pack_heads(u, rows)
    d_both = pack_heads(dy, rows)
    width = u_both[0].shape[1]
    du, first_sum, second_sum, end_u, end_d = [], [], [], [], []
    for h in range(2):
        scale = [tile_lanes(power[h, i], width) for i in range(GROUP)]
        aged = [scale[i] * float(SUB * (i + 1)) for i in range(GROUP)]
        zero = jnp.zeros((NST, width), f32)
        carry, carry_w = zero, zero
        states, states_w = [], []
        for g in range(frames // span):
            here = u_both[h][g * span : (g + 1) * span]
            local = mm(tab_a[h, 0], here)
            local_w = mm(tab_a[h, 1], here)
            parts = [local[i * NST : (i + 1) * NST] for i in range(GROUP)]
            parts_w = [local_w[i * NST : (i + 1) * NST] for i in range(GROUP)]
            states.append([carry] + [parts[i] + scale[i] * carry for i in range(GROUP - 1)])
            states_w.append(
                [carry_w]
                + [parts_w[i] + scale[i] * carry_w + aged[i] * carry for i in range(GROUP - 1)]
            )
            carry_w = parts_w[-1] + scale[-1] * carry_w + aged[-1] * carry
            carry = parts[-1] + scale[-1] * carry
        end_u.append(carry_w)
        later, later_w = zero, zero
        one, two = zero, zero
        outs = []
        for g in reversed(range(frames // span)):
            here = d_both[h][g * span : (g + 1) * span]
            back = mm(tab_a[h, 2], here)
            back_w = mm(tab_a[h, 3], here)
            parts = [back[i * NST : (i + 1) * NST] for i in range(GROUP)]
            parts_w = [back_w[i * NST : (i + 1) * NST] for i in range(GROUP)]
            into = jnp.concatenate([v * coup_both[h] for v in parts[1:] + [later]], axis=0)
            outs.append(mm(tab_b[h, 0], into.astype(bf16)))
            for i in range(GROUP):
                one = one + parts[i] * states[g][i]
                two = two + (parts_w[i] * states[g][i] + parts[i] * states_w[g][i])
            new, new_w = parts[0], parts_w[0]
            for i in range(GROUP - 1):
                new = new + scale[i] * parts[i + 1]
                new_w = new_w + (scale[i] * parts_w[i + 1] + aged[i] * parts[i + 1])
            later_w = new_w + scale[-1] * later_w + aged[-1] * later
            later = new + scale[-1] * later
        end_d.append(later_w)
        first_sum.append(one)
        second_sum.append(two)
        du.append(jnp.concatenate(outs[::-1], axis=0))
    first = lax.broadcasted_iota(jnp.int32, (NST, LANES), 1) < HALF
    for sums, out in ((first_sum, t1_o), (second_sum, t2_o)):
        both = []
        for v in sums:
            total = v[:, :LANES]
            for p in range(1, rows // 2):
                total = total + v[:, p * LANES : (p + 1) * LANES]
            both.append(total + pltpu.roll(total, HALF, 1))
        out[...] = jnp.where(first, both[0], both[1])
    for p in range(rows // 2):
        for pair, out in ((du, du_o), (end_u, fp_o), (end_d, gp_o)):
            one, two = unpack_pair(pair[0], pair[1], p)
            out[2 * p] = one
            out[2 * p + 1] = two
    chunk = frames // 5
    upad[0:SUB] = jnp.zeros((SUB, LANES), f32)
    dpad[pl.ds(frames, SUB)] = jnp.zeros((SUB, LANES), f32)
    acc_s[...] = jnp.zeros_like(acc_s)

    def one_row(i, carry):
        upad[pl.ds(SUB, frames)] = u[i].astype(f32)
        dpad[pl.ds(0, frames)] = dy[i].astype(f32)
        for r in range(0, frames, chunk):
            acc = du_o[i, pl.ds(r, chunk)].reshape(-1, SUB, LANES)
            here = dpad[pl.ds(r, chunk)]
            for d in range(SUB):
                piece = dpad[pl.ds(r + d, chunk)].reshape(-1, SUB, LANES)
                acc = acc + piece * taps[d][None]
                product = (here * upad[pl.ds(SUB + r - d, chunk)]).reshape(-1, SUB, LANES)
                acc_s[d] += jnp.sum(product, axis=0)
            du_o[i, pl.ds(r, chunk)] = acc.reshape(chunk, LANES)
        return carry

    lax.fori_loop(0, rows, one_row, 0)
    spot = lax.broadcasted_iota(jnp.int32, (SUB, LANES), 0)
    for d in range(SUB):
        kept = jnp.where(spot >= d, acc_s[d], 0.0)
        dk_o[d : d + 1] = jnp.sum(kept, axis=0, keepdims=True)
    end_swap()


def ffa_back_kernel(
    scale, du_loc, back_all, ends_all, back_ends, ends_w, back_w, starts, weigh, coup,
    x1, feat, inner_r, act_r, dx2, small, stack, mfin_t, grads_in,
    dx0_o, grads, gain_o, sums_o,
    wi, wo, wu, acc_in, acc_out, acc_u, mask, stage, k_act, k_din, k_n, k_dp, k_m, k_du, sem,
):
    step = pl.program_id(0)

    @pl.when(step == 0)
    def _():
        ffn, mix = D // BS * (FF // BS), (D // BS) ** 2
        load_matrices(stack, ((0, wi), (ffn, wo), (2 * ffn, wu)), sem)
        mask[...] = head_mask()
        acc_in[...] = jnp.zeros_like(acc_in)
        acc_out[...] = jnp.zeros_like(acc_out)
        acc_u[...] = jnp.zeros_like(acc_u)
        gain_o[...] = jnp.zeros_like(gain_o)
        sums_o[...] = jnp.zeros_like(sums_o)

    frames = feat.shape[1]
    group = k_n.shape[0] // frames
    keep = pl.ds(pl.multiple_of(step % group * frames, frames), frames)
    parts = ends_all.shape[0]
    came, came_w, later = 0.0, 0.0, 0.0
    for i in range(parts):
        end = ends_all[i, 0].astype(f32)
        came = came + weigh[0, i] * end
        came_w = came_w + weigh[1, i] * end
        later = later + weigh[2, i] * back_all[i, 0].astype(f32)
    mine = back_ends[0].astype(f32)
    sums_o[0] += mine * came
    sums_o[1] += starts[0] * mine
    sums_o[2] += starts[0] * back_w[0]
    sums_o[3] += back_w[0] * came + mine * came_w + later * ends_w[0]
    du = (du_loc[0] + mm(mfin_t[...], spread_heads(coup[...] * later, mask[...]))).astype(bf16)
    hat1, inv1 = norm(x1[0])
    n1 = (hat1 * small[1:2]).astype(bf16)
    k_m[keep] = n1
    k_du[keep] = du
    dn1 = mm_nt(du, wu[...])
    gain_o[1] += fold8(dn1 * hat1)
    dx1 = dx2[0] + norm_back(hat1, inv1, small[1:2], dn1)
    dp = (0.5 * dx1).astype(bf16)
    dact = mm_nt(dp, wo[...])
    inner = inner_r[0].astype(f32)
    sig = sigmoid(inner)
    dinner = ((sig + inner * sig * (1.0 - sig)) * dact).astype(bf16)
    hat0, inv0 = norm(feat[0].astype(f32))
    n0 = (hat0 * small[0:1]).astype(bf16)
    k_act[keep] = act_r[0]
    k_din[keep] = dinner
    k_n[keep] = n0
    k_dp[keep] = dp
    dn0 = mm_nt(dinner, wi[...])
    gain_o[0] += fold8(dn0 * hat0)
    dx0_o[0] = dx1 + norm_back(hat0, inv0, small[0:1], dn0)

    @pl.when(step % group == group - 1)
    def _():
        acc_out[...] += mm_tn(k_dp[...], k_act[...])
        acc_in[...] += mm_tn(k_n[...], k_din[...])
        acc_u[...] += mm_tn(k_m[...], k_du[...])

    @pl.when(step == pl.num_programs(0) - 1)
    def _():
        ffn, mix = D // BS * (FF // BS), (D // BS) ** 2
        plan = ((acc_in, 0, False), (acc_out, ffn, True), (acc_u, 4 * ffn, False))
        store_blocks(plan, scale, grads, stage, sem)


def shampoo_kernel(
    pick, owned, full, left, right, lroot, rroot, master, nl_o, nr_o, nm_o, nc_o, own_o
):
    for i in range(full.shape[0]):
        whole = full[i]
        mine = owned[i]
        own_o[i] = mine.astype(f32)
        nl_o[i] = 0.5 * left[i] + 0.5 * mm_nt(mine, whole)
        columns = mm_nt(pick[...], whole).astype(bf16)
        nr_o[i] = 0.5 * right[i] + 0.5 * mm(columns, whole)
        side = mm(lroot[i].astype(bf16), whole)
        step = mm(side.astype(bf16), rroot[i].astype(bf16))
        new = master[i] - rate_blocks * step
        nm_o[i] = new
        nc_o[i] = new.astype(bf16)


def reduce_kernel(
    sizes, grads, small, full, owned, small_sum,
    mine, came, from_x, from_y, red, near_in, far_in, s_tm, s_core, s_z,
    load_sem, c_send, c_recv, x_send, x_recv, y_send, y_recv,
    z_send, z_recv, f_send, f_recv, s_send, s_recv, put_sem,
):
    place, level, core = peers()
    low, high = level % 2, level // 2
    near, far = level + 1 - 2 * low, level + 2 - 4 * high
    xp, yp, dp = others = square(place)
    greet([at(other, level, core) for other in others])
    greet([at(place, level, 1 - core), at(place, near, core), at(place, far, core)])
    diagonal = 2 * (1 - high) + 1 - low
    greet([at(place, diagonal, core)])
    edges = [sum(sizes[:c]) for c in range(len(sizes) + 1)]
    ranges = [(a, b, (a + b + 1) // 2) for a, b in zip(edges[:-1], edges[1:])]
    sends = []

    def go(copy):
        copy.start()
        sends.append(copy)
        return copy

    loads, core_in = [], []
    for c, (first, end, unused) in enumerate(ranges):
        n = pl.ds(first, end - first)
        load = pltpu.make_async_copy(grads.at[:, n, :, core], mine.at[:, n], load_sem.at[c])
        load.start()
        loads.append(load)
    met(7)
    for c, (first, end, unused) in enumerate(ranges):
        n = pl.ds(first, end - first)
        core_in.append(
            go(
                remote(
                    grads.at[:, n, :, 1 - core], came.at[:, n], c_send.at[c], c_recv.at[c],
                    at(place, level, 1 - core),
                )
            )
        )

    small_in = [
        go(remote(small.at[other], s_tm.at[d], s_send.at[d], s_recv.at[d], at(other, level, core)))
        for d, other in enumerate(others)
    ]

    def add(owner, first, end):
        def one(k, carry):
            mine[owner, k] = mine[owner, k] + came[owner, k]
            return carry

        lax.fori_loop(first, end, one, 0)

    def add_into(owner, ref, first, end):
        def one(k, carry):
            mine[owner, k] = mine[owner, k] + ref[0, k]
            return carry

        lax.fori_loop(first, end, one, 0)

    def to_x(c, i, owner, slot, first, end):
        n = pl.ds(first, end - first)
        send, recv = x_send.at[c, i], x_recv.at[c, i]
        return go(
            remote(mine.at[owner, n], from_x.at[slot, n], send, recv, at(xp, level, core))
        )

    def to_y(c, i, owner, slot, first, end):
        n = pl.ds(first, end - first)
        send, recv = y_send.at[c, i], y_recv.at[c, i]
        return go(
            remote(mine.at[owner, n], from_y.at[slot, n], send, recv, at(yp, level, core))
        )

    def begin(c):
        first, end, middle = ranges[c]
        loads[c].wait()
        core_in[c].wait_recv()
        add(dp, first, end)
        x_one = to_x(c, 0, dp, 0, first, middle)
        y_one = to_y(c, 0, dp, 0, middle, end)
        add(xp, first, end)
        x_two = to_x(c, 1, xp, 1, first, middle)
        add(yp, first, end)
        y_two = to_y(c, 1, yp, 1, middle, end)
        add(place, first, end)
        return x_one, y_one, x_two, y_two

    def second(c, copies):
        first, end, middle = ranges[c]
        copies[0].wait_recv()
        add_into(yp, from_x, first, middle)
        y_three = to_y(c, 2, yp, 1, first, middle)
        copies[1].wait_recv()
        add_into(xp, from_y, middle, end)
        x_three = to_x(c, 2, xp, 1, middle, end)
        return copies[2], copies[3], x_three, y_three

    def along(c, copies):
        first, end, unused = ranges[c]
        for copy in copies:
            copy.wait_recv()

        def one(k, carry):
            total = mine[place, k].astype(f32) + from_x[1, k].astype(f32)
            total = (total + from_y[1, k].astype(f32)).astype(bf16)
            red[k] = total.reshape(red.shape[1:])
            return carry

        lax.fori_loop(first, end, one, 0)
        n = pl.ds(first, end - first)
        return go(
            remote(
                red.at[n, :, 1 - low], near_in.at[n], z_send.at[c, 0], z_recv.at[c, 0],
                at(place, near, core),
            )
        )

    def across(c, copy):
        first, end, unused = ranges[c]
        copy.wait_recv()

        def one(k, carry):
            near_in[k] = red[k, :, low] + near_in[k]
            return carry

        lax.fori_loop(first, end, one, 0)
        n = pl.ds(first, end - first)
        return go(
            remote(
                near_in.at[n, 1 - high], far_in.at[n], z_send.at[c, 1], z_recv.at[c, 1],
                at(place, far, core),
            )
        )

    def to_core(c, i, source):
        first, end, unused = ranges[c]
        spot = full.at[pl.ds(first, end - first), source // 2, source % 2, core]
        src = owned.at[pl.ds(first, end - first)] if i == 0 else spot
        return go(
            remote(src, spot, f_send.at[c, i], f_recv.at[c, i], at(place, level, 1 - core))
        )

    def settle(c, copy):
        first, end, unused = ranges[c]
        copy.wait_recv()

        def one(k, carry):
            owned[k] = near_in[k, high] + far_in[k]
            return carry

        lax.fori_loop(first, end, one, 0)
        n = pl.ds(first, end - first)
        spot = full.at[n, high, low, core]
        put = pltpu.make_async_copy(owned.at[n], spot, put_sem.at[c])
        put.start()
        to_far = go(
            remote(owned.at[n], spot, z_send.at[c, 2], z_recv.at[c, 2], at(place, far, core))
        )
        to_near = go(
            remote(owned.at[n], spot, z_send.at[c, 3], z_recv.at[c, 3], at(place, near, core))
        )
        return put, to_far, to_near, to_core(c, 0, level)

    def pass_on(c, state):
        first, end, unused = ranges[c]
        put, to_far, to_near, own = state
        to_far.wait_recv()
        spot = full.at[pl.ds(first, end - first), 1 - high, low, core]
        more = go(
            remote(spot, spot, z_send.at[c, 4], z_recv.at[c, 4], at(place, near, core))
        )
        passed = [own, to_core(c, 1, far)]
        to_near.wait_recv()
        passed.append(to_core(c, 2, near))
        return put, more, passed

    def last(c, state):
        put, more, passed = state
        more.wait_recv()
        passed.append(to_core(c, 3, diagonal))
        return put, passed

    stages = (
        lambda c, state: begin(c), second, along, across, settle, pass_on, last
    )
    chunks = len(ranges)
    state = [None] * chunks
    for tick in range(chunks + len(stages) - 1):
        for index, stage in enumerate(stages):
            c = tick - index
            if 0 <= c < chunks:
                state[c] = stage(c, state[c])
        if tick == 0:
            for copy in small_in:
                copy.wait_recv()
            s_core[0] = small[place] + (s_tm[0] + s_tm[1]) + s_tm[2]
            swap = go(
                remote(
                    s_core.at[0], s_core.at[1], s_send.at[3], s_recv.at[3],
                    at(place, level, 1 - core),
                )
            )
        if tick == 1:
            swap.wait_recv()
            s_z[level] = s_core[0] + s_core[1]
            spot = s_z.at[level]
            small_z = [
                go(
                    remote(spot, spot, s_send.at[4 + d], s_recv.at[4 + d], at(place, target, core))
                )
                for d, target in enumerate((near, far, diagonal))
            ]
    for copy in small_z:
        copy.wait_recv()
    small_sum[...] = (s_z[0] + s_z[1]) + (s_z[2] + s_z[3])
    for put, passed in state:
        put.wait()
        for copy in passed:
            copy.wait_recv()
    for copy in sends:
        copy.wait_send()


def reduce_grads(grads, small, parts, devices, slab):
    levels = devices // 2
    if parts != 4 or levels != 4:
        owned = lax.psum_scatter(grads, "tm", scatter_dimension=0, tiled=True)
        owned = lax.psum_scatter(owned, "rows", scatter_dimension=1, tiled=True)
        full = lax.all_gather(owned, "rows", axis=1, tiled=True)
        small = lax.psum_scatter(small, "tm", scatter_dimension=0, tiled=True)[0]
        return full, owned, lax.psum(small, "rows")
    count = grads.shape[0] // parts
    sizes = (6, 6, 5, 3, 2)
    grads = grads.reshape(parts, count, levels, 2, slab, BS)
    dma = lambda *dims: pltpu.SemaphoreType.DMA(dims)
    vb = lambda *dims: pltpu.VMEM(dims, bf16)
    vmem = pl.BlockSpec(memory_space=pltpu.VMEM)
    part = small.shape[1:]
    chunks = len(sizes)
    full, owned, small_sum = pl.pallas_call(
        partial(reduce_kernel, sizes),
        in_specs=[ANY, vmem],
        out_specs=[ANY, vmem, vmem],
        out_shape=[
            shape((count, 2, 2, 2, slab, BS), bf16),
            shape((count, slab, BS), bf16),
            shape(part),
        ],
        scratch_shapes=[
            vb(parts, count, levels, slab, BS), vb(parts, count, levels, slab, BS),
            vb(2, count, levels, slab, BS), vb(2, count, levels, slab, BS),
            vb(count, 2, 2, slab, BS), vb(count, 2, slab, BS), vb(count, slab, BS),
            vm(3, *part), vm(2, *part), vm(levels, *part),
            dma(chunks), dma(chunks), dma(chunks),
            dma(chunks, 3), dma(chunks, 3), dma(chunks, 3), dma(chunks, 3),
            dma(chunks, 5), dma(chunks, 5), dma(chunks, 4), dma(chunks, 4),
            dma(7), dma(7), dma(chunks),
        ],
        compiler_params=pltpu.CompilerParams(
            collective_id=2, has_side_effects=True, vmem_limit_bytes=VMEM_BYTES
        ),
        name="reduce_grads",
    )(grads, small)
    return full.reshape(count, BS, BS), owned, small_sum


def row_spec(frames, width, per=1):
    return pl.BlockSpec((per, frames, width), lambda i: (i, 0, 0))


def whole_spec(*dims):
    return pl.BlockSpec(dims, lambda i: (0,) * len(dims))


def talking(number):
    return pltpu.CompilerParams(
        dimension_semantics=("arbitrary",),
        vmem_limit_bytes=VMEM_BYTES,
        collective_id=number,
        has_side_effects=True,
    )


def body(
    features,
    cotangent,
    state_bank,
    state_source,
    master,
    left_stats,
    right_stats,
    left_root,
    right_root,
    small_params,
    decay_logs,
    state_mix,
):
    rows, frames, width = features.shape
    tokens = rows * frames
    parts = lax.axis_size("tm")
    place = lax.axis_index("tm")
    scaling = 1.0 / math.sqrt(tokens * parts * lax.axis_size("rows"))
    ffn, mix = D // BS * (FF // BS), (D // BS) ** 2

    own_heads, own_channels = decay_logs.shape[0], state_mix.shape[1]
    starts_own = state_bank[state_source]
    params = jnp.concatenate(
        [decay_logs.reshape(-1), state_mix.reshape(-1), starts_own.reshape(-1)]
    )
    cut_one = own_heads * NST
    cut_two = cut_one + 2 * own_channels * NST
    cut_three = cut_two + rows * own_channels * NST
    params = jnp.pad(params, (0, -cut_three % (8 * LANES))).reshape(-1, LANES)
    devices = lax.axis_size("rows")
    levels = devices // 2
    spread_out = parts == 4
    if spread_out:
        first, pair, rest, packed = gather_first(master, params, parts, devices)
        first = first.reshape(-1, BS, BS)
        pair_out, rest_out = [shape(pair.shape, bf16)], [shape(rest.shape, bf16)]
        any_one, pair_in, rest_in = [ANY], [pair], [rest]
        pair_sems, rest_sems = gather_sems(XY_SEMS, levels), gather_sems(XY_SEMS, levels, 2)
    else:
        stack = lax.all_gather(master.astype(bf16), "rows", axis=1, tiled=True)
        stack = lax.all_gather(stack, "tm", axis=0, tiled=True)
        packed = lax.all_gather(params, "tm", axis=0)
        first, pair, rest = (stack[jnp.array(ids)] for ids in block_sets())
        pair_out = rest_out = any_one = pair_in = rest_in = pair_sems = rest_sems = []

    packed = packed.reshape(parts, -1)
    logs = packed[:, :cut_one].reshape(HEADS, NST)
    mix_all = packed[:, cut_one:cut_two].reshape(parts, 2, own_channels, NST)
    mix_all = mix_all.transpose(1, 3, 0, 2).reshape(2, NST, D)
    starts = packed[:, cut_two:cut_three].reshape(parts, rows, own_channels, NST)
    starts = starts.transpose(1, 3, 0, 2).reshape(rows, NST, D)

    rates = jnp.exp(logs)
    rate_nc = jnp.repeat(rates.T, HALF, axis=1)
    coupling = mix_all[0] * mix_all[1]
    state_row = jnp.arange(GROUP * NST, dtype=jnp.int32)
    part_of = state_row // NST
    rate_row = jnp.tile(rates, (1, GROUP))[:, :, None]
    inner_t = jnp.arange(GROUP * SUB, dtype=jnp.int32)
    age = SUB * (part_of + 1)[:, None] - 1 - inner_t[None, :]
    age_f = jnp.maximum(age, 0).astype(f32)
    tab_in = jnp.where(age >= 0, jnp.exp(-rate_row * age_f), 0.0)
    since = (inner_t % SUB + 1).astype(f32)
    inside = (inner_t // SUB)[None, :] == part_of[:, None]
    tab_out = jnp.where(inside, jnp.exp(-rate_row * since), 0.0)
    tab_a = jnp.stack([tab_in, tab_in * age_f, tab_out, tab_out * since], axis=1).astype(bf16)
    tab_b = jnp.stack([tab_in, tab_out], axis=1).astype(bf16).transpose(0, 1, 3, 2)
    steps_of = SUB * jnp.arange(1, GROUP + 1, dtype=f32)
    power = jnp.exp(-rates[:, None, :, None] * steps_of[None, :, None, None])
    power = jnp.broadcast_to(power, (HEADS, GROUP, NST, LANES))
    time = jnp.arange(frames, dtype=jnp.int32)
    flat_rates = rates.reshape(-1)
    next_t = (time + 1).astype(f32)
    left_t = (frames - 1 - time).astype(f32)
    pfull = jnp.exp(-flat_rates[None, :] * next_t[:, None]).astype(bf16)
    pfull_t = jnp.exp(-flat_rates[:, None] * next_t[None, :]).astype(bf16)
    mfin = jnp.exp(-flat_rates[:, None] * left_t[None, :]).astype(bf16)
    mfin_t = jnp.exp(-flat_rates[None, :] * left_t[:, None]).astype(bf16)
    lag = jnp.arange(SUB, dtype=f32)
    lag_decay = jnp.exp(-rate_nc[None] * lag[:, None, None])
    kernel_lags = jnp.sum(coupling[None] * lag_decay, axis=1)
    slot = jnp.arange(SUB, dtype=jnp.int32)
    taps_f = jnp.where(slot[:, None, None] <= slot[None, :, None], kernel_lags[:, None, :], 0.0)
    taps_b = jnp.where(
        slot[:, None, None] + slot[None, :, None] < SUB, kernel_lags[:, None, :], 0.0
    )

    span = float(frames)
    shard = jnp.arange(parts, dtype=jnp.int32)

    def passing(apart):
        length = jnp.maximum(apart, 0).astype(f32)[:, None, None] * span
        weight = jnp.where(
            (apart >= 0)[:, None, None], jnp.exp(-rate_nc[None] * length), 0.0
        )
        return weight, weight * length

    behind_w, behind_l = passing(place - 1 - shard)
    ahead_w, unused = passing(shard - place - 1)
    begin = place.astype(f32) * span
    begin_w = jnp.exp(-rate_nc * begin)
    weigh_in = jnp.concatenate([behind_w, (mix_all[1] * begin_w)[None]], axis=0)
    weigh_back = jnp.stack([behind_w, behind_l, ahead_w], axis=0)

    mat = lambda r, c: vm(r, c, dtype=bf16)
    dma = pltpu.SemaphoreType.DMA
    group = 3 if rows % 3 == 0 else 1
    small_spec = whole_spec(*small_params.shape)
    state_spec = pl.BlockSpec((1, NST, D), lambda i: (i, 0, 0))
    states_spec = pl.BlockSpec((parts, 1, NST, D), lambda i: (0, i, 0, 0))
    flat_spec = whole_spec(NST, D)
    x1, inner_a, act_a, u, ends, *done = pl.pallas_call(
        ffa_forward_kernel,
        grid=(rows // BOTH,),
        in_specs=[row_spec(frames, D, BOTH), small_spec, ANY, whole_spec(HEADS * NST, frames)]
        + any_one,
        out_specs=[
            row_spec(frames, D, BOTH),
            row_spec(frames, FF, BOTH),
            row_spec(frames, FF, BOTH),
            row_spec(frames, D, BOTH),
            pl.BlockSpec((BOTH, NST, D), lambda i: (i, 0, 0)),
        ]
        + any_one,
        out_shape=[
            shape((rows, frames, D)),
            shape((rows, frames, FF), bf16),
            shape((rows, frames, FF), bf16),
            shape((rows, frames, D), bf16),
            shape((rows, NST, D), bf16),
        ]
        + pair_out,
        scratch_shapes=[mat(D, FF), mat(FF, D), mat(D, D), dma] + pair_sems,
        input_output_aliases={4: 5} if spread_out else {},
        compiler_params=talking(7) if spread_out else PARAMS,
        name="ffa_forward",
    )(features, small_params, first, mfin, *pair_in)
    if spread_out:
        pair = done[0].reshape(-1, BS, BS)

    group_spec = pl.BlockSpec((rows, frames, LANES), lambda i: (0, 0, i))
    tab_a_spec = pl.BlockSpec((2,) + tab_a.shape[1:], lambda i: (i, 0, 0, 0))
    tab_b_spec = pl.BlockSpec((2,) + tab_b.shape[1:], lambda i: (i, 0, 0, 0))
    power_spec = pl.BlockSpec((2,) + power.shape[1:], lambda i: (i, 0, 0, 0))
    coup_spec = pl.BlockSpec((NST, LANES), lambda i: (0, i))
    taps_spec = pl.BlockSpec((SUB, SUB, LANES), lambda i: (0, 0, i))
    swap_scratch = [dma, dma((parts - 1,)), dma((parts - 1,))]
    all_states = shape((parts, rows, NST, D), bf16)
    y_loc, ends_all, *done = pl.pallas_call(
        conv_forward_kernel,
        grid=(D // LANES,),
        in_specs=[group_spec, ANY, tab_a_spec, tab_b_spec, power_spec, coup_spec, taps_spec]
        + any_one,
        out_specs=[group_spec, ANY] + any_one,
        out_shape=[shape((rows, frames, D)), all_states] + rest_out,
        scratch_shapes=[vm(SUB + frames, LANES)] + swap_scratch + rest_sems,
        input_output_aliases={7: 2} if spread_out else {},
        compiler_params=talking(3),
        name="conv_forward",
    )(u, ends, tab_a, tab_b, power, coupling, taps_f, *rest_in)

    edge_spec = pl.BlockSpec((1, PAD, D), lambda i: (i, 0, 0))
    edge_scratch = [
        vm(rows, 2, PAD, D, dtype=bf16),
        vm(PAD, D, dtype=bf16),
        dma((2, rows)),
        dma((2, rows)),
        dma((2,)),
    ]
    edge_shapes = [shape((rows, PAD, D), bf16)] * 2
    ys, gated, x2, pw, g, g_low, g_high, *done = pl.pallas_call(
        mixer_out_kernel,
        grid=(rows,),
        in_specs=[
            row_spec(frames, D),
            states_spec,
            state_spec,
            whole_spec(parts + 1, NST, D),
            flat_spec,
            row_spec(frames, D),
            small_spec,
            ANY,
            whole_spec(frames, HEADS * NST),
        ]
        + any_one,
        out_specs=[
            row_spec(frames, D),
            row_spec(frames, 2 * D),
            row_spec(frames, D),
            row_spec(frames, 2 * D),
            row_spec(frames, D),
            ANY,
            ANY,
        ]
        + any_one,
        out_shape=[
            shape((rows, frames, D), bf16),
            shape((rows, frames, 2 * D), bf16),
            shape((rows, frames, D)),
            shape((rows, frames, 2 * D), bf16),
            shape((rows, frames, D), bf16),
        ]
        + edge_shapes
        + rest_out,
        scratch_shapes=[mat(D, 2 * D), mat(D, 2 * D), vm(HEADS * NST, D), dma]
        + edge_scratch
        + rest_sems,
        input_output_aliases={9: 7} if spread_out else {},
        compiler_params=talking(4),
        name="mixer_out",
    )(y_loc, ends_all, starts, weigh_in, coupling, x1, small_params, pair, pfull, *done)
    if spread_out:
        rest = done[0].reshape(-1, BS, BS)

    kept = lambda *widths: [mat(group * frames, w) for w in widths]
    grad_shape = shape((parts * master.shape[0], BS, BS), bf16)
    layer_out, dx3, dq, grads, gain_b, d_low, d_high = pl.pallas_call(
        partial(ffb_kernel, scaling),
        grid=(rows,),
        in_specs=[
            row_spec(frames, D),
            edge_spec,
            edge_spec,
            row_spec(frames, D),
            row_spec(frames, D),
            small_spec,
            ANY,
        ],
        out_specs=[
            row_spec(frames, D),
            row_spec(frames, D),
            row_spec(frames, D),
            ANY,
            whole_spec(2, 8, D),
            ANY,
            ANY,
        ],
        out_shape=[
            shape((rows, frames, D), bf16),
            shape((rows, frames, D)),
            shape((rows, frames, D), bf16),
            grad_shape,
            shape((2, 8, D)),
        ]
        + edge_shapes,
        scratch_shapes=[
            mat(D, FF),
            mat(FF, D),
            mat(D, D),
            vm(D, FF),
            vm(D, FF),
            vm(D, D),
            vm(D // LANES, frames + 2 * PAD, LANES),
            vm(frames, D),
            vm(2 * ffn + mix, BS, BS, dtype=bf16),
        ]
        + kept(FF, FF, D, D, D, D)
        + [dma]
        + edge_scratch,
        compiler_params=talking(5),
        name="ffb",
    )(g, g_low, g_high, x2, cotangent, small_params, rest)

    dx2, dy, back_ends, grads, gain_c, kernel_grads = pl.pallas_call(
        partial(mixer_back_kernel, scaling),
        grid=(rows,),
        in_specs=[
            row_spec(frames, D),
            edge_spec,
            edge_spec,
            row_spec(frames, D),
            edge_spec,
            edge_spec,
            row_spec(frames, 2 * D),
            row_spec(frames, D),
            row_spec(frames, 2 * D),
            row_spec(frames, D),
            row_spec(frames, D),
            small_spec,
            ANY,
            whole_spec(HEADS * NST, frames),
            ANY,
        ],
        out_specs=[
            row_spec(frames, D),
            row_spec(frames, D),
            state_spec,
            ANY,
            whole_spec(8, D),
            whole_spec(16, D),
        ],
        out_shape=[
            shape((rows, frames, D)),
            shape((rows, frames, D), bf16),
            shape((rows, NST, D), bf16),
            grad_shape,
            shape((8, D)),
            shape((16, D)),
        ],
        scratch_shapes=[
            mat(D, 2 * D),
            mat(D, 2 * D),
            vm(D, 2 * D),
            vm(D, 2 * D),
            vm(D // LANES, frames + 2 * PAD, LANES),
            vm(D // LANES, frames + 2 * PAD, LANES),
            vm(frames, D),
            vm(KW, 8, D),
            vm(4 * mix, BS, BS, dtype=bf16),
        ]
        + kept(D, 2 * D, D, 2 * D)
        + [dma],
        input_output_aliases={14: 3},
        compiler_params=PARAMS,
        name="mixer_back",
    )(
        dq, d_low, d_high, g, g_low, g_high, pw, x2, gated, ys, dx3, small_params, pair,
        pfull_t, grads,
    )

    nst_spec = pl.BlockSpec((rows, NST, LANES), lambda i: (0, 0, i))
    du_loc, t_one, t_two, ends_w, back_w, lag_grads, back_all = pl.pallas_call(
        conv_back_kernel,
        grid=(D // LANES,),
        in_specs=[
            group_spec, group_spec, ANY, tab_a_spec, tab_b_spec, power_spec, coup_spec, taps_spec
        ],
        out_specs=[
            group_spec,
            coup_spec,
            coup_spec,
            nst_spec,
            nst_spec,
            pl.BlockSpec((SUB, LANES), lambda i: (0, i)),
            ANY,
        ],
        out_shape=[
            shape((rows, frames, D)),
            shape((NST, D)),
            shape((NST, D)),
            shape((rows, NST, D)),
            shape((rows, NST, D)),
            shape((SUB, D)),
            all_states,
        ],
        scratch_shapes=[
            vm(SUB + frames, LANES),
            vm(SUB + frames, LANES),
            vm(SUB, SUB, LANES),
        ]
        + swap_scratch,
        compiler_params=talking(6),
        name="conv_back",
    )(u, dy, back_ends, tab_a, tab_b, power, coupling, taps_b)

    grad_zero, grads, gain_a, sums_c = pl.pallas_call(
        partial(ffa_back_kernel, scaling),
        grid=(rows,),
        in_specs=[
            row_spec(frames, D),
            states_spec,
            states_spec,
            state_spec,
            state_spec,
            state_spec,
            state_spec,
            whole_spec(3, parts, NST, D),
            flat_spec,
            row_spec(frames, D),
            row_spec(frames, D),
            row_spec(frames, FF),
            row_spec(frames, FF),
            row_spec(frames, D),
            small_spec,
            ANY,
            whole_spec(frames, HEADS * NST),
            ANY,
        ],
        out_specs=[row_spec(frames, D), ANY, whole_spec(2, 8, D), whole_spec(4, NST, D)],
        out_shape=[
            shape((rows, frames, D)),
            grad_shape,
            shape((2, 8, D)),
            shape((4, NST, D)),
        ],
        scratch_shapes=[
            mat(D, FF),
            mat(FF, D),
            mat(D, D),
            vm(D, FF),
            vm(D, FF),
            vm(D, D),
            vm(HEADS * NST, D),
            vm(2 * ffn + mix, BS, BS, dtype=bf16),
        ]
        + kept(FF, FF, D, D, D, D)
        + [dma],
        input_output_aliases={17: 1},
        compiler_params=PARAMS,
        name="ffa_back",
    )(
        du_loc, back_all, ends_all, back_ends, ends_w, back_w, starts, weigh_back, coupling,
        x1, features, inner_a, act_a, dx2, small_params, first, mfin_t, grads,
    )

    lag_grad_c = jnp.sum(lag_decay * lag_grads[:, None, :], axis=0)
    lag_grad_r = jnp.sum(lag_decay * (lag[:, None] * lag_grads)[:, None, :], axis=0)
    d_coup = t_one + lag_grad_c + sums_c[0]
    start_back = sums_c[1] * begin_w
    d_first = d_coup * mix_all[1]
    d_second = d_coup * mix_all[0] + start_back
    d_rate = coupling * (t_two + lag_grad_r + sums_c[3])
    d_rate = d_rate + mix_all[1] * (begin * start_back + begin_w * sums_c[2])
    small_grads = [
        jnp.sum(gain_a, axis=1),
        jnp.sum(gain_c, axis=0, keepdims=True),
        jnp.sum(gain_b, axis=1),
        kernel_grads[:KW],
    ]
    stacked = jnp.concatenate(small_grads + [d_first, d_second, d_rate], axis=0) * scaling
    stacked = jnp.pad(stacked, ((0, -stacked.shape[0] % 8), (0, 0)))
    own = place * own_channels
    lanes_own = lambda v: lax.dynamic_slice_in_dim(v, own, own_channels, v.ndim - 1)
    stacked = stacked.reshape(-1, parts, own_channels).transpose(1, 0, 2)
    full_grad, owned, sums = reduce_grads(
        grads, stacked, parts, lax.axis_size("rows"), master.shape[1]
    )
    count_small = small_params.shape[0]
    small_sum = sums[:count_small]
    mix_sum = sums[count_small : count_small + 2 * NST]
    mix_sum = mix_sum.reshape(2, NST, own_channels).transpose(0, 2, 1)
    rate_sum = sums[count_small + 2 * NST : count_small + 3 * NST]
    rate_sum = jnp.sum(rate_sum.reshape(NST, own_heads, HALF), axis=2)
    decay_sum = -rate_sum.T * jnp.exp(decay_logs)
    new_small = lanes_own(small_params) - rate_small * small_sum
    new_decay = decay_logs - rate_small * decay_sum
    new_mix = state_mix - rate_small * mix_sum

    shard_w = jnp.exp(-lanes_own(rate_nc)[None] * (shard.astype(f32) * span)[:, None, None])
    start_grad = jnp.sum(lanes_own(back_all).astype(f32) * shard_w[:, None], axis=0) * lanes_own(mix_all[1])
    start_grad = start_grad.transpose(0, 2, 1)
    chosen = (state_source[None, :] == jnp.arange(rows, dtype=jnp.int32)[:, None]).astype(f32)
    grad_state = jnp.sum(chosen[:, :, None, None] * start_grad[None], axis=1)

    count, slice_rows = owned.shape[0], owned.shape[1]
    mine = lax.axis_index("rows") * slice_rows
    pick = (
        jnp.arange(slice_rows, dtype=jnp.int32)[:, None] + mine
        == jnp.arange(BS, dtype=jnp.int32)[None, :]
    ).astype(bf16)
    group = 11 if count % 11 == 0 else 1
    part_spec = pl.BlockSpec((group, slice_rows, BS), lambda i: (i, 0, 0))
    full_spec = pl.BlockSpec((group, BS, BS), lambda i: (i, 0, 0))
    new_left, new_right, new_master, new_copy, grad_blocks = pl.pallas_call(
        shampoo_kernel,
        grid=(count // group,),
        in_specs=[
            whole_spec(slice_rows, BS),
            part_spec,
            full_spec,
            part_spec,
            part_spec,
            part_spec,
            full_spec,
            part_spec,
        ],
        out_specs=[part_spec] * 5,
        out_shape=[
            shape(owned.shape),
            shape(owned.shape),
            shape(owned.shape),
            shape(owned.shape, bf16),
            shape(owned.shape),
        ],
        compiler_params=PARAMS,
        name="shampoo",
    )(pick, owned, full_grad, left_stats, right_stats, left_root, right_root, master)
    return (
        layer_out,
        grad_zero,
        grad_state,
        grad_blocks,
        new_left,
        new_right,
        new_master,
        new_copy,
        small_sum,
        new_small,
        decay_sum,
        mix_sum,
        new_decay,
        new_mix,
    )


def solution(mesh):
    return jax.shard_map(
        body,
        mesh=mesh,
        in_specs=(
            P("rows", "tm", None),
            P("rows", "tm", None),
            P("rows", "tm", None),
            P("rows"),
            P("tm", "rows", None),
            P("tm", "rows", None),
            P("tm", "rows", None),
            P("tm", "rows", None),
            P("tm", None, None),
            P(),
            P("tm", None),
            P(None, "tm", None),
        ),
        out_specs=(
            P("rows", "tm", None),
            P("rows", "tm", None),
            P("rows", "tm", None),
            P("tm", "rows", None),
            P("tm", "rows", None),
            P("tm", "rows", None),
            P("tm", "rows", None),
            P("tm", "rows", None),
            P(None, "tm"),
            P(None, "tm"),
            P("tm", None),
            P(None, "tm", None),
            P("tm", None),
            P(None, "tm", None),
        ),
        check_vma=False,
    )
```

```python
from functools import partial
import math

import jax
import jax.numpy as jnp
from jax import lax
from jax.experimental import pallas as pl
from jax.experimental.pallas import tpu as pltpu
from jax.sharding import PartitionSpec as P

D = 512
FF = 2048
NST = 32
KW = 15
BS = 256
HEADS = 8
HALF = 64
LANES = 128
SUB = 16
GROUP = 5
BOTH = 2
PAD = 8
VMEM_BYTES = 60 * 1024 * 1024

rate_blocks = 0.1
rate_small = 0.5
bf16 = jnp.bfloat16
f32 = jnp.float32


def shape(dims, dtype=f32):
    return jax.ShapeDtypeStruct(dims, dtype)


def mm(a, b):
    return jnp.dot(a, b, preferred_element_type=f32)


def mm_nt(a, b):
    return lax.dot_general(a, b, (((1,), (1,)), ((), ())), preferred_element_type=f32)


def mm_tn(a, b):
    return lax.dot_general(a, b, (((0,), (0,)), ((), ())), preferred_element_type=f32)


def sigmoid(v):
    return 0.5 * jnp.tanh(0.5 * v) + 0.5


def norm(v):
    center = v - jnp.mean(v, axis=-1, keepdims=True)
    spread = jnp.mean(center * center, axis=-1, keepdims=True)
    inv = lax.rsqrt(spread + 1e-05)
    return center * inv, inv


def norm_back(hat, inv, scale, incoming):
    scaled = incoming * scale
    mean_one = jnp.mean(scaled, axis=-1, keepdims=True)
    mean_two = jnp.mean(scaled * hat, axis=-1, keepdims=True)
    return inv * (scaled - mean_one - hat * mean_two)


def flat(ref):
    v = ref[...]
    return v.reshape(-1, v.shape[-1])


def put_rows(ref, v):
    ref[...] = v.astype(ref.dtype).reshape(ref.shape)


def fold8(v):
    return jnp.sum(v.reshape(-1, 8, v.shape[-1]), axis=0)


def load_matrices(stack, plan, sem):
    copies = []
    for first, dst in plan:
        down, across = dst.shape[0] // BS, dst.shape[1] // BS
        for i in range(down):
            for j in range(across):
                copies.append(
                    pltpu.make_async_copy(
                        stack.at[first + i * across + j],
                        dst.at[pl.ds(i * BS, BS), pl.ds(j * BS, BS)],
                        sem,
                    )
                )
    for copy in copies:
        copy.start()
    for copy in copies:
        copy.wait()


def store_blocks(plan, scaling, grads, stage, sem):
    copies = []
    for acc, first, transposed in plan:
        rows, cols = acc.shape
        down, across = (cols, rows) if transposed else (rows, cols)
        for i in range(down // BS):
            for j in range(across // BS):
                slot = len(copies)
                if transposed:
                    part = (acc[pl.ds(j * BS, BS), pl.ds(i * BS, BS)] * scaling).T
                else:
                    part = acc[pl.ds(i * BS, BS), pl.ds(j * BS, BS)] * scaling
                stage[slot] = part.astype(bf16)
                copy = pltpu.make_async_copy(
                    stage.at[slot], grads.at[first + i * (across // BS) + j], sem
                )
                copy.start()
                copies.append(copy)
    for copy in copies:
        copy.wait()


def head_mask():
    row = lax.broadcasted_iota(jnp.int32, (HEADS * NST, D), 0) // NST
    col = lax.broadcasted_iota(jnp.int32, (HEADS * NST, D), 1) // HALF
    return (row == col).astype(f32)


def spread_heads(v, mask):
    return (jnp.concatenate([v] * HEADS, axis=0) * mask).astype(bf16)


def local_states(table, v, out):
    frames = table.shape[1]
    first = lax.broadcasted_iota(jnp.int32, (NST, LANES), 1) < HALF
    for b in range(out.shape[0]):
        for g in range(D // LANES):
            here = v[b * frames : (b + 1) * frames, g * LANES : (g + 1) * LANES]
            both = mm(table[pl.ds(2 * NST * g, 2 * NST), :], here)
            picked = jnp.where(first, both[:NST], both[NST:])
            out[b, :, pl.ds(g * LANES, LANES)] = picked.astype(out.dtype)


ANY = pl.BlockSpec(memory_space=pl.ANY)
PARAMS = pltpu.CompilerParams(
    dimension_semantics=("arbitrary",), vmem_limit_bytes=VMEM_BYTES
)


def vm(*dims, dtype=f32):
    return pltpu.VMEM(dims, dtype)


def peers():
    place, row = lax.axis_index("tm"), lax.axis_index("rows")
    return place, row // 2, row % 2


def square(place):
    x, y = place % 2, place // 2
    return 2 * y + 1 - x, 2 * (1 - y) + x, 2 * (1 - y) + 1 - x


def at(place, level, core):
    return {"tm": place, "rows": level * 2 + core}


def remote(src, dst, send, recv, device):
    return pltpu.make_async_remote_copy(
        src_ref=src,
        dst_ref=dst,
        send_sem=send,
        recv_sem=recv,
        device_id=device,
        device_id_type=pl.DeviceIdType.MESH,
    )


def signal(sem, device):
    pl.semaphore_signal(sem, inc=1, device_id=device, device_id_type=pl.DeviceIdType.MESH)


def chunk_ranges(count, chunks):
    edges = [count * c // chunks for c in range(chunks + 1)]
    out = []
    for first, end in zip(edges[:-1], edges[1:]):
        middle = (first + end + 1) // 2
        out.append((first, end, middle))
    return out


class Gather:
    def __init__(self, piece, stack, sems, chunks=1):
        self.piece, self.stack, self.sems = piece, stack, sems
        self.place, self.level, self.core = peers()
        self.xp, self.yp, self.dp = square(self.place)
        self.levels = stack.shape[2]
        self.ranges = chunk_ranges(stack.shape[1], chunks)
        self.all = range(chunks)

    def own(self, c):
        first, end, unused = self.ranges[c]
        n = pl.ds(first, end - first)
        spot = self.stack.at[self.place, n, self.level, self.core]
        return pltpu.make_async_copy(self.piece.at[n], spot, self.sems["own"].at[c])

    def z(self, c, d):
        first, end, unused = self.ranges[c]
        n = pl.ds(first, end - first)
        spot = self.stack.at[self.place, n, self.level, self.core]
        send, recv = self.sems["zs"].at[c, d - 1], self.sems["zr"].at[c, d - 1]
        target = (self.level + d) % self.levels
        return remote(self.piece.at[n], spot, send, recv, at(self.place, target, self.core))

    def z_start(self, c):
        self.own(c).start()
        for d in range(1, self.levels):
            self.z(c, d).start()

    def z_arrive(self, c):
        self.own(c).wait()
        for d in range(1, self.levels):
            self.z(c, d).wait_recv()

    def z_end(self, c):
        for d in range(1, self.levels):
            self.z(c, d).wait_send()

    def part(self, name, c, i, owner, first, end, device):
        spot = self.stack.at[owner, pl.ds(first, end - first), :, self.core]
        send, recv = self.sems[name + "s"].at[c, i], self.sems[name + "r"].at[c, i]
        return remote(spot, spot, send, recv, device)

    def x(self, c, i):
        first, end, mid = self.ranges[c]
        what = ((self.place, first, mid), (self.place, mid, end), (self.yp, mid, end))[i]
        return self.part("x", c, i, *what, at(self.xp, self.level, self.core))

    def y(self, c, i):
        first, end, mid = self.ranges[c]
        what = ((self.place, mid, end), (self.place, first, mid), (self.xp, first, mid))[i]
        return self.part("y", c, i, *what, at(self.yp, self.level, self.core))

    def other(self, c, i):
        first, end, mid = self.ranges[c]
        what = (
            (self.place, first, end),
            (self.xp, first, mid),
            (self.yp, mid, end),
            (self.xp, mid, end),
            (self.yp, first, mid),
            (self.dp, first, mid),
            (self.dp, mid, end),
        )[i]
        return self.part("c", c, i, *what, at(self.place, self.level, 1 - self.core))

    def spread(self, c):
        for copy in (self.x(c, 0), self.y(c, 0), self.x(c, 1), self.y(c, 1), self.other(c, 0)):
            copy.start()

    def forward(self, c):
        self.x(c, 0).wait_recv()
        self.y(c, 2).start()
        self.y(c, 0).wait_recv()
        self.x(c, 2).start()
        self.other(c, 1).start()
        self.other(c, 2).start()
        self.x(c, 1).wait_recv()
        self.other(c, 3).start()
        self.y(c, 1).wait_recv()
        self.other(c, 4).start()

    def finish(self, c):
        self.y(c, 2).wait_recv()
        self.other(c, 5).start()
        self.x(c, 2).wait_recv()
        self.other(c, 6).start()

    def end(self, c):
        for i in range(7):
            self.other(c, i).wait_recv()
        for i in range(7):
            self.other(c, i).wait_send()
        for i in range(3):
            self.x(c, i).wait_send()
            self.y(c, i).wait_send()


Z_SEMS = ("own", "zs", "zr")
XY_SEMS = ("xs", "xr", "ys", "yr", "cs", "cr")


def gather_sems(names, levels, chunks=1):
    width = {"own": (), "z": (levels - 1,), "x": (3,), "y": (3,), "c": (7,)}
    key = lambda name: name if name == "own" else name[0]
    return [pltpu.SemaphoreType.DMA((chunks,) + width[key(name)]) for name in names]


def block_sets():
    ffn, mix = D // BS * (FF // BS), (D // BS) ** 2
    ids = lambda *ranges: [b for first, end in ranges for b in range(first, end)]
    return (
        ids((0, 2 * ffn), (4 * ffn, 4 * ffn + mix)),
        ids((4 * ffn + mix, 4 * ffn + 5 * mix)),
        ids((2 * ffn, 4 * ffn), (4 * ffn + 5 * mix, 4 * ffn + 6 * mix)),
    )


def move_runs(ids, places, count):
    runs, each = [], len(ids) // places
    for index, b in enumerate(ids):
        owner, k, v, j = b // count, b % count, index // each, index % each
        if runs:
            o0, k0, v0, j0, n0 = runs[-1]
            if (o0, v0) == (owner, v) and k0 + n0 == k:
                runs[-1] = (o0, k0, v0, j0, n0 + 1)
                continue
        runs.append((owner, k, v, j, 1))
    return runs


def greet(devices):
    barrier = pltpu.get_barrier_semaphore()
    for device in devices:
        signal(barrier, device)


def met(count):
    pl.semaphore_wait(pltpu.get_barrier_semaphore(), count)


def gather_kernel(
    master, pack, first, pair, rest, pack_all,
    rounded, piece, piece_pair, piece_rest, run_send, run_recv, pk_send, pk_recv, *sems,
):
    place, level, core = peers()
    others = square(place)
    levels = first.shape[2]
    greet([at(other, level, core) for other in others] + [at(place, level, 1 - core)])
    greet([at(place, (level + d) % levels, core) for d in range(1, levels)])
    rounded[...] = master[...].astype(bf16)
    met(3 + levels)
    moves = []
    for ids, target in zip(block_sets(), (piece, piece_pair, piece_rest)):
        for run in move_runs(ids, first.shape[0], master.shape[0]):
            moves.append((len(moves), target) + run)

    def move(index, target, owner, k, v, j, n):
        src, dst = rounded.at[pl.ds(k, n)], target.at[pl.ds(j, n)]
        if owner == v:
            return pltpu.make_async_copy(src, dst, run_send.at[index])
        return remote(src, dst, run_send.at[index], run_recv.at[index], at(v, level, core))

    def arrive(entry):
        index, target, owner, k, v, j, n = entry
        if owner == v:
            pl.when(place == v)(lambda: move(*entry).wait())
        else:
            pl.when(place == v)(lambda: move(*entry).wait_recv())

    for entry in moves:
        pl.when(place == entry[2])(lambda entry=entry: move(*entry).start())
    own_pack = pltpu.make_async_copy(pack, pack_all.at[place], pk_send.at[3])
    own_pack.start()
    packs = [
        remote(pack, pack_all.at[place], pk_send.at[d], pk_recv.at[d], at(other, level, core))
        for d, other in enumerate(others)
    ]
    for copy in packs:
        copy.start()
    for entry in moves:
        if entry[1] is piece:
            arrive(entry)
    names = Z_SEMS + XY_SEMS
    chunks = sems[0].shape[0]
    it = Gather(piece, first, dict(zip(names, sems)), chunks)
    later, sems = [], sems[len(names) :]
    for i, (what, stack) in enumerate(((piece_pair, pair), (piece_rest, rest))):
        later.append(Gather(what, stack, dict(zip(Z_SEMS, sems[3 * i : 3 * i + 3]))))
    it.z_start(0)
    for c in it.all:
        it.z_arrive(c)
        it.spread(c)
        if c == 0:
            for ahead in range(1, chunks):
                it.z_start(ahead)
            for entry in moves:
                if entry[1] is not piece:
                    arrive(entry)
        if c == chunks - 1:
            for other_set in later:
                other_set.z_start(0)
        if c >= 1:
            it.forward(c - 1)
        if c >= 2:
            it.finish(c - 2)
    it.forward(chunks - 1)
    for c in range(max(chunks - 2, 0), chunks):
        it.finish(c)
    for c in it.all:
        it.end(c)
        it.z_end(c)
    for other_set in later:
        other_set.z_arrive(0)
        other_set.z_end(0)
    for entry in moves:
        if entry[2] != entry[4]:
            pl.when(place == entry[2])(lambda entry=entry: move(*entry).wait_send())
    own_pack.wait()
    for copy in packs:
        copy.wait()


def gather_first(master, pack, parts, devices, chunks=3):
    count, slab, cols = master.shape
    levels = devices // 2
    each = [len(ids) // parts for ids in block_sets()]
    runs = sum(len(move_runs(ids, parts, count)) for ids in block_sets())
    dma = lambda *dims: pltpu.SemaphoreType.DMA(dims)
    return pl.pallas_call(
        gather_kernel,
        in_specs=[pl.BlockSpec(memory_space=pltpu.VMEM), ANY],
        out_specs=[ANY] * 4,
        out_shape=[
            shape((parts, each[0], levels, 2, slab, cols), bf16),
            shape((parts, each[1], levels, 2, slab, cols), bf16),
            shape((parts, each[2], levels, 2, slab, cols), bf16),
            shape((parts,) + pack.shape, pack.dtype),
        ],
        scratch_shapes=[
            vm(count, slab, cols, dtype=bf16),
            vm(each[0], slab, cols, dtype=bf16),
            vm(each[1], slab, cols, dtype=bf16),
            vm(each[2], slab, cols, dtype=bf16),
            dma(runs),
            dma(runs),
            dma(4),
            dma(3),
        ]
        + gather_sems(Z_SEMS + XY_SEMS, levels, chunks)
        + gather_sems(Z_SEMS, levels) * 2,
        compiler_params=pltpu.CompilerParams(
            collective_id=1, has_side_effects=True, vmem_limit_bytes=VMEM_BYTES
        ),
        name="gather_first",
    )(master, pack)


R_XY = ("load", "cs", "cr", "xs", "xr", "ys", "yr")
R_Z = ("zs", "zr")


def reduce_sems(names, chunks=1):
    width = {"x": (3,), "y": (3,), "z": (2,)}
    dims = lambda name: width.get(name[0], ())
    return [pltpu.SemaphoreType.DMA((chunks,) + dims(name)) for name in names]


def square_bufs(m, parts, levels, slab):
    vb = lambda *dims: pltpu.VMEM(dims + (slab, BS), bf16)
    return [vb(parts, m, levels)] * 2 + [vb(2, m, levels)] * 2


def level_bufs(m, slab):
    vb = lambda *dims: pltpu.VMEM(dims + (slab, BS), bf16)
    return [vb(m, 2), vb(m)]


class Reduce:
    def __init__(self, sizes, sems, grads=None, square_refs=None, red=None, level_refs=None, out=None):
        self.sems, self.grads, self.red, self.out = sems, grads, red, out
        if square_refs is not None:
            self.mine, self.came, self.from_x, self.from_y = square_refs
        if level_refs is not None:
            self.near_in, self.far_in = level_refs
        self.place, self.level, self.core = peers()
        self.xp, self.yp, self.dp = square(self.place)
        self.low, self.high = self.level % 2, self.level // 2
        self.near_by = self.level + 1 - 2 * self.low
        self.far_off = self.level + 2 - 4 * self.high
        edges = [sum(sizes[:c]) for c in range(len(sizes) + 1)]
        self.ranges = [(a, b, (a + b + 1) // 2) for a, b in zip(edges[:-1], edges[1:])]
        self.all = range(len(sizes))

    def n(self, c):
        first, end, unused = self.ranges[c]
        return pl.ds(first, end - first)

    def load(self, c):
        src = self.grads.at[:, self.n(c), :, self.core]
        return pltpu.make_async_copy(src, self.mine.at[:, self.n(c)], self.sems["load"].at[c])

    def swap(self, c):
        return remote(
            self.grads.at[:, self.n(c), :, 1 - self.core],
            self.came.at[:, self.n(c)],
            self.sems["cs"].at[c],
            self.sems["cr"].at[c],
            at(self.place, self.level, 1 - self.core),
        )

    def side(self, c, i, name, into, device, what):
        owner, slot, first, end = what
        n = pl.ds(first, end - first)
        send, recv = self.sems[name + "s"].at[c, i], self.sems[name + "r"].at[c, i]
        return remote(self.mine.at[owner, n], into.at[slot, n], send, recv, device)

    def x(self, c, i):
        first, end, mid = self.ranges[c]
        what = ((self.dp, 0, first, mid), (self.xp, 1, first, mid), (self.xp, 1, mid, end))[i]
        return self.side(c, i, "x", self.from_x, at(self.xp, self.level, self.core), what)

    def y(self, c, i):
        first, end, mid = self.ranges[c]
        what = ((self.dp, 0, mid, end), (self.yp, 1, mid, end), (self.yp, 1, first, mid))[i]
        return self.side(c, i, "y", self.from_y, at(self.yp, self.level, self.core), what)

    def add(self, owner, first, end, ref, slot):
        def one(k, carry):
            self.mine[owner, k] = self.mine[owner, k] + ref[slot, k]
            return carry

        lax.fori_loop(first, end, one, 0)

    def start(self, c):
        self.load(c).start()
        self.swap(c).start()

    def begin(self, c):
        first, end, unused = self.ranges[c]
        self.load(c).wait()
        self.swap(c).wait_recv()
        self.add(self.dp, first, end, self.came, self.dp)
        self.x(c, 0).start()
        self.y(c, 0).start()
        self.add(self.xp, first, end, self.came, self.xp)
        self.x(c, 1).start()
        self.add(self.yp, first, end, self.came, self.yp)
        self.y(c, 1).start()
        self.add(self.place, first, end, self.came, self.place)

    def second(self, c):
        first, end, mid = self.ranges[c]
        self.x(c, 0).wait_recv()
        self.add(self.yp, first, mid, self.from_x, 0)
        self.y(c, 2).start()
        self.y(c, 0).wait_recv()
        self.add(self.xp, mid, end, self.from_y, 0)
        self.x(c, 2).start()

    def combine(self, c):
        first, end, unused = self.ranges[c]
        for i in (1, 2):
            self.x(c, i).wait_recv()
            self.y(c, i).wait_recv()

        def one(k, carry):
            total = self.mine[self.place, k].astype(f32) + self.from_x[1, k].astype(f32)
            total = (total + self.from_y[1, k].astype(f32)).astype(bf16)
            self.red[k] = total.reshape(self.red.shape[1:])
            return carry

        lax.fori_loop(first, end, one, 0)

    def square_end(self, c):
        self.swap(c).wait_send()
        for i in range(3):
            self.x(c, i).wait_send()
            self.y(c, i).wait_send()

    def near(self, c):
        return remote(
            self.red.at[self.n(c), :, 1 - self.low],
            self.near_in.at[self.n(c)],
            self.sems["zs"].at[c, 0],
            self.sems["zr"].at[c, 0],
            at(self.place, self.near_by, self.core),
        )

    def far(self, c):
        return remote(
            self.near_in.at[self.n(c), 1 - self.high],
            self.far_in.at[self.n(c)],
            self.sems["zs"].at[c, 1],
            self.sems["zr"].at[c, 1],
            at(self.place, self.far_off, self.core),
        )

    def across(self, c):
        first, end, unused = self.ranges[c]
        self.near(c).wait_recv()

        def one(k, carry):
            self.near_in[k] = self.red[k, :, self.low] + self.near_in[k]
            return carry

        lax.fori_loop(first, end, one, 0)
        self.far(c).start()

    def settle(self, c):
        first, end, unused = self.ranges[c]
        self.far(c).wait_recv()

        def one(k, carry):
            self.out[k] = self.near_in[k, self.high] + self.far_in[k]
            return carry

        lax.fori_loop(first, end, one, 0)

    def levels_end(self, c):
        self.near(c).wait_send()
        self.far(c).wait_send()


def ffa_forward_kernel(feat, small, stack, mfin, *refs):
    step, last = pl.program_id(0), pl.num_programs(0) - 1
    pair = None
    if len(refs) > 9:
        refs, sems = refs[1:7] + refs[7:11], refs[11:]
        pair = Gather(None, refs[5], dict(zip(XY_SEMS, sems)))
        refs = refs[:5] + refs[6:]
    x1_o, inner_o, act_o, u_o, f_o, wi, wo, wu, sem = refs

    @pl.when(step == 0)
    def _():
        if pair is not None:
            place, level, core = peers()
            greet([at(other, level, core) for other in square(place)])
            greet([at(place, level, 1 - core)])
        ffn, mix = D // BS * (FF // BS), (D // BS) ** 2
        load_matrices(stack, ((0, wi), (ffn, wo), (2 * ffn, wu)), sem)
        if pair is not None:
            met(4)
            pair.spread(0)

    x0 = flat(feat).astype(f32)
    hat, unused = norm(x0)
    inner = mm((hat * small[0:1]).astype(bf16), wi[...])
    act = (inner * sigmoid(inner)).astype(bf16)
    put_rows(inner_o, inner)
    put_rows(act_o, act)
    x1 = x0 + 0.5 * mm(act, wo[...])
    put_rows(x1_o, x1)
    hat, unused = norm(x1)
    u = mm((hat * small[1:2]).astype(bf16), wu[...]).astype(bf16)
    put_rows(u_o, u)
    local_states(mfin, u, f_o)
    if pair is not None:
        pl.when(step == last - 1)(lambda: pair.forward(0))

        @pl.when(step == last)
        def _():
            pair.finish(0)
            pair.end(0)


def pack_heads(ref, rows):
    first = lax.broadcasted_iota(jnp.int32, (ref.shape[1], LANES), 1) < HALF
    low, high = [], []
    for p in range(rows // 2):
        a, b = ref[2 * p].astype(f32), ref[2 * p + 1].astype(f32)
        low.append(jnp.where(first, a, pltpu.roll(b, HALF, 1)).astype(bf16))
        high.append(jnp.where(first, pltpu.roll(a, HALF, 1), b).astype(bf16))
    return jnp.concatenate(low, axis=1), jnp.concatenate(high, axis=1)


def pack_params(v, rows):
    first = lax.broadcasted_iota(jnp.int32, v.shape, 1) < HALF
    rolled = pltpu.roll(v, HALF, 1)
    low = jnp.where(first, v, rolled)
    high = jnp.where(first, rolled, v)
    return (
        jnp.concatenate([low] * (rows // 2), axis=1),
        jnp.concatenate([high] * (rows // 2), axis=1),
    )


def unpack_pair(low, high, p):
    low = low[:, p * LANES : (p + 1) * LANES]
    high = high[:, p * LANES : (p + 1) * LANES]
    first = lax.broadcasted_iota(jnp.int32, low.shape, 1) < HALF
    return (
        jnp.where(first, low, pltpu.roll(high, HALF, 1)),
        jnp.where(first, pltpu.roll(low, HALF, 1), high),
    )


def swap_states(mine, whole, first_step, last_step, own_sem, send, recv, pair=None):
    place, level, core = peers()
    parts = whole.shape[0]
    others = [(place + d) % parts for d in range(1, parts)]

    def copies():
        return [
            remote(mine, whole.at[place], send.at[d], recv.at[d], at(other, level, core))
            for d, other in enumerate(others)
        ]

    own = lambda: pltpu.make_async_copy(mine, whole.at[place], own_sem)

    @pl.when(first_step)
    def _():
        barrier = pltpu.get_barrier_semaphore()
        for other in others:
            signal(barrier, at(other, level, core))
        if pair is not None:
            signal(barrier, at(place, level, 1 - core))
        own().start()

    def end():
        @pl.when(first_step)
        def _():
            met(parts - 1 + (pair is not None))
            for copy in copies():
                copy.start()
            if pair is not None:
                pair.spread(0)

        if pair is not None:
            step = pl.program_id(0)

            @pl.when(step == pl.num_programs(0) - 2)
            def _():
                pair.forward(0)

            @pl.when(last_step)
            def _():
                pair.finish(0)
                pair.end(0)

        @pl.when(last_step)
        def _():
            own().wait()
            for copy in copies():
                copy.wait()

    return end


def tile_lanes(v, width):
    return jnp.concatenate([v] * (width // LANES), axis=1)


def conv_forward_kernel(u, ends, tab_a, tab_b, power, coup, taps, *refs):
    step = pl.program_id(0)
    pair = None
    if len(refs) > 6:
        refs, sems = refs[1:7] + refs[7:8], refs[8:]
        pair = Gather(None, refs[2], dict(zip(XY_SEMS, sems)), 2)
        refs = refs[:2] + refs[3:]
    y_o, ends_all, pad, own_sem, send, recv = refs
    end_swap = swap_states(
        ends, ends_all, step == 0, step == pl.num_programs(0) - 1, own_sem, send, recv, pair
    )
    rows, frames = u.shape[0], u.shape[1]
    span = GROUP * SUB
    coup_both = pack_params(coup[...], rows)
    packed = pack_heads(u, rows)
    width = packed[0].shape[1]
    results = []
    for h in range(2):
        scale = [tile_lanes(power[h, i], width) for i in range(GROUP)]
        carry = None
        outs = []
        for g in range(frames // span):
            local = mm(tab_a[h, 0], packed[h][g * span : (g + 1) * span])
            parts = [local[i * NST : (i + 1) * NST] for i in range(GROUP)]
            if carry is None:
                states = [jnp.zeros_like(parts[0])] + parts[:-1]
                carry = parts[-1]
            else:
                states = [carry] + [parts[i] + scale[i] * carry for i in range(GROUP - 1)]
                carry = parts[-1] + scale[-1] * carry
            scaled = jnp.concatenate([v * coup_both[h] for v in states], axis=0)
            outs.append(mm(tab_b[h, 1], scaled.astype(bf16)))
        results.append(jnp.concatenate(outs, axis=0))
    for p in range(rows // 2):
        one, two = unpack_pair(results[0], results[1], p)
        y_o[2 * p] = one
        y_o[2 * p + 1] = two
    pad[0:SUB] = jnp.zeros((SUB, LANES), f32)
    chunk = frames // 5

    def one_row(i, carry):
        pad[pl.ds(SUB, frames)] = u[i].astype(f32)
        for r in range(0, frames, chunk):
            acc = y_o[i, pl.ds(r, chunk)].reshape(-1, SUB, LANES)
            for d in range(SUB):
                piece = pad[pl.ds(SUB + r - d, chunk)].reshape(-1, SUB, LANES)
                acc = acc + piece * taps[d][None]
            y_o[i, pl.ds(r, chunk)] = acc.reshape(chunk, LANES)
        return carry

    lax.fori_loop(0, rows, one_row, 0)
    end_swap()


def edge_sender(edges, low_all, high_all, zeros, send, recv, zero_sem, step, per, rest=None):
    place, level, core = peers()
    parts = lax.axis_size("tm")
    steps = edges.shape[0]
    not_first, not_last = place > 0, place < parts - 1
    after = (place + 1) % parts
    before = (place + parts - 1) % parts

    def up(i):
        return remote(
            edges.at[i, 1], low_all.at[i], send.at[0, i], recv.at[0, i], at(after, level, core)
        )

    def down(i):
        return remote(
            edges.at[i, 0], high_all.at[i], send.at[1, i], recv.at[1, i], at(before, level, core)
        )

    def blank(ref, i, k):
        return pltpu.make_async_copy(zeros, ref.at[i], zero_sem.at[k])

    @pl.when(step == 0)
    def _():
        if rest is None:
            pl.when(not_last)(lambda: greet([at(after, level, core)]))
            pl.when(not_first)(lambda: greet([at(before, level, core)]))
        else:
            greet([at(other, level, core) for other in square(place)])
            greet([at(place, level, 1 - core)])
        zeros[...] = jnp.zeros_like(zeros)

        @pl.when(place == 0)
        def _():
            for i in range(steps):
                blank(low_all, i, 0).start()

        @pl.when(place == parts - 1)
        def _():
            for i in range(steps):
                blank(high_all, i, 1).start()

    def put(v):
        @pl.when(step == 0)
        def _():
            below = (place + parts - 1) // parts
            above = (2 * parts - 2 - place) // parts
            met(below + above if rest is None else parts)
            if rest is not None:
                rest.spread(1)

        if rest is not None:
            pl.when(step == steps // per // 2)(lambda: rest.forward(1))
            pl.when(step == steps // per - 1)(lambda: rest.finish(1))

        frames = v.shape[0] // per
        for b in range(per):
            row = step * per + b
            edges[row, 0] = v[b * frames : b * frames + PAD]
            edges[row, 1] = v[(b + 1) * frames - PAD : (b + 1) * frames]
            pl.when(not_last)(lambda row=row: up(row).start())
            pl.when(not_first)(lambda row=row: down(row).start())

        @pl.when(step == steps // per - 1)
        def _():
            for i in range(steps):
                pl.when(not_last)(lambda i=i: up(i).wait_send())
                pl.when(not_first)(lambda i=i: down(i).wait_send())
                pl.when(not_first)(lambda i=i: up(i).wait_recv())
                pl.when(not_last)(lambda i=i: down(i).wait_recv())

            if rest is not None:
                rest.end(1)

            @pl.when(place == 0)
            def _():
                for i in range(steps):
                    blank(low_all, i, 0).wait()

            @pl.when(place == parts - 1)
            def _():
                for i in range(steps):
                    blank(high_all, i, 1).wait()

    return put


def mixer_out_kernel(
    y, ends_all, starts, weigh, coup, x1, small, stack, pfull, *refs
):
    step = pl.program_id(0)
    rest = None
    if len(refs) > 16:
        refs, sems = refs[1:8] + refs[8:18], refs[18:]
        rest = Gather(None, refs[7], dict(zip(XY_SEMS, sems)), 2)
        refs = refs[:7] + refs[8:]
    ys_o, gated_o, x2_o, pw_o, g_o, low_o, high_o, wo, wp, mask, sem = refs[:11]
    edges, zeros, send, recv, zero_sem = refs[11:]
    put = edge_sender(edges, low_o, high_o, zeros, send, recv, zero_sem, step, 1, rest)

    @pl.when(step == 0)
    def _():
        ffn, mix = D // BS * (FF // BS), (D // BS) ** 2
        load_matrices(stack, ((0, wo), (2 * mix, wp)), sem)
        mask[...] = head_mask()

    came = weigh[0] * ends_all[0, 0].astype(f32)
    for i in range(1, ends_all.shape[0]):
        came = came + weigh[i] * ends_all[i, 0].astype(f32)
    zin = coup[...] * came + weigh[ends_all.shape[0]] * starts[0]
    ys = (y[0] + mm(pfull[...], spread_heads(zin, mask[...]))).astype(bf16)
    ys_o[0] = ys
    gated = mm(ys, wo[...])
    gated_o[0] = gated.astype(bf16)
    x2 = x1[0] + gated[:, :D] * sigmoid(gated[:, D:])
    x2_o[0] = x2
    hat, unused = norm(x2)
    pw = mm((hat * small[2:3]).astype(bf16), wp[...])
    pw_o[0] = pw.astype(bf16)
    g = (pw[:, :D] * sigmoid(pw[:, D:])).astype(bf16)
    g_o[0] = g
    put(g)


def fill_pad(pad, low, body, high):
    frames = body.shape[0]
    for g in range(D // LANES):
        lanes = slice(g * LANES, (g + 1) * LANES)
        pad[g, 0:PAD] = low[:, lanes].astype(f32)
        pad[g, pl.ds(PAD, frames)] = body[:, lanes].astype(f32)
        pad[g, pl.ds(PAD + frames, PAD)] = high[:, lanes].astype(f32)


def ffb_kernel(
    scale, g, low, high, x2, cot, small, stack,
    out_o, dx3_o, dq_o, grads, gain_o, low_o, high_o,
    wi, wo, wq, acc_in, acc_out, acc_q, pad, q_s, stage, k_act, k_din, k_n, k_dp, k_a, k_dpq, sem,
    edges, zeros, send, recv, zero_sem,
):
    step = pl.program_id(0)
    frames = g.shape[1]
    put = edge_sender(edges, low_o, high_o, zeros, send, recv, zero_sem, step, 1)

    @pl.when(step == 0)
    def _():
        ffn, mix = D // BS * (FF // BS), (D // BS) ** 2
        load_matrices(stack, ((0, wi), (ffn, wo), (2 * ffn, wq)), sem)
        acc_in[...] = jnp.zeros_like(acc_in)
        acc_out[...] = jnp.zeros_like(acc_out)
        acc_q[...] = jnp.zeros_like(acc_q)
        gain_o[...] = jnp.zeros_like(gain_o)

    fill_pad(pad, low[0], g[0], high[0])
    chunk = frames // 5
    for c in range(D // LANES):
        lanes = slice(c * LANES, (c + 1) * LANES)
        for r in range(0, frames, chunk):
            acc = small[5:6, lanes] * pad[c, pl.ds(r + PAD - 7, chunk)]
            for j in range(1, KW):
                acc = acc + small[5 + j : 6 + j, lanes] * pad[c, pl.ds(r + j + PAD - 7, chunk)]
            q_s[pl.ds(r, chunk), lanes] = acc
    q = q_s[...]
    sig_q = sigmoid(q)
    act_q = q * sig_q
    a3 = act_q.astype(bf16)
    x3 = x2[0] + mm(a3, wq[...])
    hat3, inv3 = norm(x3)
    n3 = (hat3 * small[3:4]).astype(bf16)
    inner = mm(n3, wi[...])
    sig = sigmoid(inner)
    act = inner * sig
    b4 = act.astype(bf16)
    x4 = x3 + 0.5 * mm(b4, wo[...])
    hat4, inv4 = norm(x4)
    out_o[0] = (hat4 * small[4:5]).astype(bf16)
    c4 = cot[0].astype(f32)
    gain_o[1] += fold8(c4 * hat4)
    dx4 = norm_back(hat4, inv4, small[4:5], c4)
    dp = (0.5 * dx4).astype(bf16)
    dact = mm_nt(dp, wo[...])
    dinner = ((sig + act * (1.0 - sig)) * dact).astype(bf16)
    group = k_n.shape[0] // frames
    keep = pl.ds(pl.multiple_of(step % group * frames, frames), frames)
    k_act[keep] = b4
    k_din[keep] = dinner
    k_n[keep] = n3
    k_dp[keep] = dp
    k_a[keep] = a3
    dn3 = mm_nt(dinner, wi[...])
    gain_o[0] += fold8(dn3 * hat3)
    dx3 = dx4 + norm_back(hat3, inv3, small[3:4], dn3)
    dx3_o[0] = dx3
    dpq = dx3.astype(bf16)
    k_dpq[keep] = dpq
    da3 = mm_nt(dpq, wq[...])
    dq = ((sig_q + act_q * (1.0 - sig_q)) * da3).astype(bf16)
    dq_o[0] = dq
    put(dq)

    @pl.when(step % group == group - 1)
    def _():
        acc_out[...] += mm_tn(k_dp[...], k_act[...])
        acc_in[...] += mm_tn(k_n[...], k_din[...])
        acc_q[...] += mm_tn(k_a[...], k_dpq[...])

    @pl.when(step == pl.num_programs(0) - 1)
    def _():
        ffn, mix = D // BS * (FF // BS), (D // BS) ** 2
        plan = (
            (acc_in, 0, False),
            (acc_out, ffn, True),
            (acc_q, 2 * ffn, False),
        )
        store_blocks(plan, scale, grads, stage, sem)


def mixer_back_kernel(
    scale, dq, dlow, dhigh, g, glow, ghigh, pw, x2, gated, ys, dx3, small, stack, pfull_t, *refs
):
    step, last = pl.program_id(0), pl.num_programs(0) - 1
    frames = dq.shape[1]
    rest = None
    if len(refs) > 20:
        grads_rest, refs = refs[0], refs[1:]
        red, bufs, sems = refs[6], refs[21:25], refs[25:]
        half = (red.shape[0] + 1) // 2
        rest = Reduce((half, red.shape[0] - half), dict(zip(R_XY, sems)), grads_rest, bufs, red)
        refs = refs[:6] + refs[7:21]
    dx2_o, dy_o, gst_o, grads, gain_o, dk_o, wo, wp, acc_p, acc_o, dpad, gpad = refs[:12]
    dg_s, dk_s, stage, k_n, k_dpw, k_ys, k_dg, sem = refs[12:]

    @pl.when(step == 0)
    def _():
        ffn, mix = D // BS * (FF // BS), (D // BS) ** 2
        if rest is not None:
            greet([at(other, rest.level, rest.core) for other in (rest.xp, rest.yp, rest.dp)])
            greet([at(rest.place, rest.level, 1 - rest.core)])
        load_matrices(stack, ((0, wo), (2 * mix, wp)), sem)
        if rest is not None:
            met(4)
            for c in rest.all:
                rest.start(c)
        acc_p[...] = jnp.zeros_like(acc_p)
        acc_o[...] = jnp.zeros_like(acc_o)
        gain_o[...] = jnp.zeros_like(gain_o)
        dk_s[...] = jnp.zeros_like(dk_s)

    fill_pad(dpad, dlow[0], dq[0], dhigh[0])
    fill_pad(gpad, glow[0], g[0], ghigh[0])
    chunk = frames // 5
    for c in range(D // LANES):
        lanes = slice(c * LANES, (c + 1) * LANES)
        for r in range(0, frames, chunk):
            here = dpad[c, pl.ds(r + PAD, chunk)]
            acc = small[5:6, lanes] * dpad[c, pl.ds(r + PAD + 7, chunk)]
            for j in range(1, KW):
                acc = acc + small[5 + j : 6 + j, lanes] * dpad[c, pl.ds(r - j + PAD + 7, chunk)]
            dg_s[pl.ds(r, chunk), lanes] = acc
            for j in range(KW):
                dk_s[j, :, lanes] += fold8(here * gpad[c, pl.ds(r + j + PAD - 7, chunk)])
    dg = dg_s[...]
    value = pw[0, :, :D].astype(f32)
    gate = sigmoid(pw[0, :, D:].astype(f32))
    dvalue = (dg * gate).astype(bf16)
    dgate = (dg * value * gate * (1.0 - gate)).astype(bf16)
    dpw = jnp.concatenate([dvalue, dgate], axis=1)
    hat2, inv2 = norm(x2[0])
    n2 = (hat2 * small[2:3]).astype(bf16)
    group = k_n.shape[0] // frames
    keep = pl.ds(pl.multiple_of(step % group * frames, frames), frames)
    k_n[keep] = n2
    k_dpw[keep] = dpw
    k_ys[keep] = ys[0]
    dn2 = mm_nt(dpw, wp[...])
    gain_o[...] += fold8(dn2 * hat2)
    dx2 = dx3[0] + norm_back(hat2, inv2, small[2:3], dn2)
    dx2_o[0] = dx2
    value = gated[0, :, :D].astype(f32)
    gate = sigmoid(gated[0, :, D:].astype(f32))
    dvalue = (dx2 * gate).astype(bf16)
    dgate = (dx2 * value * gate * (1.0 - gate)).astype(bf16)
    dgated = jnp.concatenate([dvalue, dgate], axis=1)
    k_dg[keep] = dgated
    dy = mm_nt(dgated, wo[...]).astype(bf16)
    dy_o[0] = dy
    local_states(pfull_t, dy, gst_o)

    if rest is not None:
        for c in rest.all:
            pl.when(step == 0)(lambda c=c: rest.begin(c))
            pl.when(step == last - 3 + 2 * c)(lambda c=c: rest.second(c))

    @pl.when(step % group == group - 1)
    def _():
        acc_p[...] += mm_tn(k_n[...], k_dpw[...])
        acc_o[...] += mm_tn(k_ys[...], k_dg[...])

    @pl.when(step == pl.num_programs(0) - 1)
    def _():
        ffn, mix = D // BS * (FF // BS), (D // BS) ** 2
        plan = ((acc_o, 0, False), (acc_p, 2 * mix, False))
        store_blocks(plan, scale, grads, stage, sem)
        if rest is not None:
            for c in rest.all:
                rest.combine(c)
                rest.square_end(c)
        for j in range(KW):
            dk_o[j : j + 1] = jnp.sum(dk_s[j], axis=0, keepdims=True)


def conv_back_kernel(
    u, dy, back_ends, tab_a, tab_b, power, coup, taps,
    du_o, t1_o, t2_o, fp_o, gp_o, dk_o, back_all,
    upad, dpad, acc_s, own_sem, send, recv,
):
    step = pl.program_id(0)
    end_swap = swap_states(
        back_ends, back_all, step == 0, step == pl.num_programs(0) - 1, own_sem, send, recv
    )
    rows, frames = u.shape[0], u.shape[1]
    span = GROUP * SUB
    coup_both = pack_params(coup[...], rows)
    u_both = pack_heads(u, rows)
    d_both = pack_heads(dy, rows)
    width = u_both[0].shape[1]
    du, first_sum, second_sum, end_u, end_d = [], [], [], [], []
    for h in range(2):
        scale = [tile_lanes(power[h, i], width) for i in range(GROUP)]
        aged = [scale[i] * float(SUB * (i + 1)) for i in range(GROUP)]
        zero = jnp.zeros((NST, width), f32)
        carry, carry_w = zero, zero
        states, states_w = [], []
        for g in range(frames // span):
            here = u_both[h][g * span : (g + 1) * span]
            local = mm(tab_a[h, 0], here)
            local_w = mm(tab_a[h, 1], here)
            parts = [local[i * NST : (i + 1) * NST] for i in range(GROUP)]
            parts_w = [local_w[i * NST : (i + 1) * NST] for i in range(GROUP)]
            states.append([carry] + [parts[i] + scale[i] * carry for i in range(GROUP - 1)])
            states_w.append(
                [carry_w]
                + [parts_w[i] + scale[i] * carry_w + aged[i] * carry for i in range(GROUP - 1)]
            )
            carry_w = parts_w[-1] + scale[-1] * carry_w + aged[-1] * carry
            carry = parts[-1] + scale[-1] * carry
        end_u.append(carry_w)
        later, later_w = zero, zero
        one, two = zero, zero
        outs = []
        for g in reversed(range(frames // span)):
            here = d_both[h][g * span : (g + 1) * span]
            back = mm(tab_a[h, 2], here)
            back_w = mm(tab_a[h, 3], here)
            parts = [back[i * NST : (i + 1) * NST] for i in range(GROUP)]
            parts_w = [back_w[i * NST : (i + 1) * NST] for i in range(GROUP)]
            into = jnp.concatenate([v * coup_both[h] for v in parts[1:] + [later]], axis=0)
            outs.append(mm(tab_b[h, 0], into.astype(bf16)))
            for i in range(GROUP):
                one = one + parts[i] * states[g][i]
                two = two + (parts_w[i] * states[g][i] + parts[i] * states_w[g][i])
            new, new_w = parts[0], parts_w[0]
            for i in range(GROUP - 1):
                new = new + scale[i] * parts[i + 1]
                new_w = new_w + (scale[i] * parts_w[i + 1] + aged[i] * parts[i + 1])
            later_w = new_w + scale[-1] * later_w + aged[-1] * later
            later = new + scale[-1] * later
        end_d.append(later_w)
        first_sum.append(one)
        second_sum.append(two)
        du.append(jnp.concatenate(outs[::-1], axis=0))
    first = lax.broadcasted_iota(jnp.int32, (NST, LANES), 1) < HALF
    for sums, out in ((first_sum, t1_o), (second_sum, t2_o)):
        both = []
        for v in sums:
            total = v[:, :LANES]
            for p in range(1, rows // 2):
                total = total + v[:, p * LANES : (p + 1) * LANES]
            both.append(total + pltpu.roll(total, HALF, 1))
        out[...] = jnp.where(first, both[0], both[1])
    for p in range(rows // 2):
        for pair, out in ((du, du_o), (end_u, fp_o), (end_d, gp_o)):
            one, two = unpack_pair(pair[0], pair[1], p)
            out[2 * p] = one
            out[2 * p + 1] = two
    chunk = frames // 5
    upad[0:SUB] = jnp.zeros((SUB, LANES), f32)
    dpad[pl.ds(frames, SUB)] = jnp.zeros((SUB, LANES), f32)
    acc_s[...] = jnp.zeros_like(acc_s)

    def one_row(i, carry):
        upad[pl.ds(SUB, frames)] = u[i].astype(f32)
        dpad[pl.ds(0, frames)] = dy[i].astype(f32)
        for r in range(0, frames, chunk):
            acc = du_o[i, pl.ds(r, chunk)].reshape(-1, SUB, LANES)
            here = dpad[pl.ds(r, chunk)]
            for d in range(SUB):
                piece = dpad[pl.ds(r + d, chunk)].reshape(-1, SUB, LANES)
                acc = acc + piece * taps[d][None]
                product = (here * upad[pl.ds(SUB + r - d, chunk)]).reshape(-1, SUB, LANES)
                acc_s[d] += jnp.sum(product, axis=0)
            du_o[i, pl.ds(r, chunk)] = acc.reshape(chunk, LANES)
        return carry

    lax.fori_loop(0, rows, one_row, 0)
    spot = lax.broadcasted_iota(jnp.int32, (SUB, LANES), 0)
    for d in range(SUB):
        kept = jnp.where(spot >= d, acc_s[d], 0.0)
        dk_o[d : d + 1] = jnp.sum(kept, axis=0, keepdims=True)
    end_swap()


def ffa_back_kernel(
    scale, du_loc, back_all, ends_all, back_ends, ends_w, back_w, starts, weigh, coup,
    x1, feat, inner_r, act_r, dx2, small, stack, mfin_t, *refs
):
    step, last = pl.program_id(0), pl.num_programs(0) - 1
    pair = None
    if len(refs) > 19:
        grads_pair, red_in, refs = refs[0], refs[1], refs[2:]
        out_pair, out_rest = refs[4:6]
        red_rest, rest_bufs, red_pair, square_refs = refs[21], refs[22:24], refs[24], refs[25:29]
        pair_bufs, sems = refs[29:31], refs[31:]
        refs = refs[:4] + refs[6:21]
        pair = Reduce(
            out_pair.shape[:1], dict(zip(R_XY + R_Z, sems)), grads_pair, square_refs, red_pair,
            pair_bufs, out_pair,
        )
        rest = Reduce(
            out_rest.shape[:1], dict(zip(R_Z, sems[9:])), None, None, red_rest, rest_bufs, out_rest
        )
    dx0_o, grads, gain_o, sums_o, wi, wo, wu, acc_in, acc_out, acc_u = refs[:10]
    mask, stage, k_act, k_din, k_n, k_dp, k_m, k_du, sem = refs[10:]

    @pl.when(step == 0)
    def _():
        ffn, mix = D // BS * (FF // BS), (D // BS) ** 2
        if pair is not None:
            greet([at(other, pair.level, pair.core) for other in (pair.xp, pair.yp, pair.dp)])
            greet([at(pair.place, other, pair.core) for other in (pair.near_by, pair.far_off)])
            greet([at(pair.place, pair.level, 1 - pair.core)])
            red_rest[...] = red_in[...]
        load_matrices(stack, ((0, wi), (ffn, wo), (2 * ffn, wu)), sem)
        if pair is not None:
            met(6)
            pair.start(0)
            rest.near(0).start()
        mask[...] = head_mask()
        acc_in[...] = jnp.zeros_like(acc_in)
        acc_out[...] = jnp.zeros_like(acc_out)
        acc_u[...] = jnp.zeros_like(acc_u)
        gain_o[...] = jnp.zeros_like(gain_o)
        sums_o[...] = jnp.zeros_like(sums_o)

    frames = feat.shape[1]
    group = k_n.shape[0] // frames
    keep = pl.ds(pl.multiple_of(step % group * frames, frames), frames)
    parts = ends_all.shape[0]
    came, came_w, later = 0.0, 0.0, 0.0
    for i in range(parts):
        end = ends_all[i, 0].astype(f32)
        came = came + weigh[0, i] * end
        came_w = came_w + weigh[1, i] * end
        later = later + weigh[2, i] * back_all[i, 0].astype(f32)
    mine = back_ends[0].astype(f32)
    sums_o[0] += mine * came
    sums_o[1] += starts[0] * mine
    sums_o[2] += starts[0] * back_w[0]
    sums_o[3] += back_w[0] * came + mine * came_w + later * ends_w[0]
    du = (du_loc[0] + mm(mfin_t[...], spread_heads(coup[...] * later, mask[...]))).astype(bf16)
    hat1, inv1 = norm(x1[0])
    n1 = (hat1 * small[1:2]).astype(bf16)
    k_m[keep] = n1
    k_du[keep] = du
    dn1 = mm_nt(du, wu[...])
    gain_o[1] += fold8(dn1 * hat1)
    dx1 = dx2[0] + norm_back(hat1, inv1, small[1:2], dn1)
    dp = (0.5 * dx1).astype(bf16)
    dact = mm_nt(dp, wo[...])
    inner = inner_r[0].astype(f32)
    sig = sigmoid(inner)
    dinner = ((sig + inner * sig * (1.0 - sig)) * dact).astype(bf16)
    hat0, inv0 = norm(feat[0].astype(f32))
    n0 = (hat0 * small[0:1]).astype(bf16)
    k_act[keep] = act_r[0]
    k_din[keep] = dinner
    k_n[keep] = n0
    k_dp[keep] = dp
    dn0 = mm_nt(dinner, wi[...])
    gain_o[0] += fold8(dn0 * hat0)
    dx0_o[0] = dx1 + norm_back(hat0, inv0, small[0:1], dn0)

    if pair is not None:

        @pl.when(step == 0)
        def _():
            pair.begin(0)

        @pl.when(step == last - 4)
        def _():
            rest.across(0)

        @pl.when(step == last - 3)
        def _():
            pair.second(0)

        @pl.when(step == last - 2)
        def _():
            rest.settle(0)
            pair.combine(0)
            pair.near(0).start()

        @pl.when(step == last - 1)
        def _():
            pair.across(0)

    @pl.when(step % group == group - 1)
    def _():
        acc_out[...] += mm_tn(k_dp[...], k_act[...])
        acc_in[...] += mm_tn(k_n[...], k_din[...])
        acc_u[...] += mm_tn(k_m[...], k_du[...])

    @pl.when(step == pl.num_programs(0) - 1)
    def _():
        ffn, mix = D // BS * (FF // BS), (D // BS) ** 2
        plan = ((acc_in, 0, False), (acc_out, ffn, True), (acc_u, 2 * ffn, False))
        store_blocks(plan, scale, grads, stage, sem)
        if pair is not None:
            pair.settle(0)
            pair.square_end(0)
            pair.levels_end(0)
            rest.levels_end(0)


def shampoo_kernel(
    pick, owned, full, left, right, lroot, rroot, master, nl_o, nr_o, nm_o, nc_o, own_o
):
    for i in range(full.shape[0]):
        whole = full[i]
        mine = owned[i]
        own_o[i] = mine.astype(f32)
        nl_o[i] = 0.5 * left[i] + 0.5 * mm_nt(mine, whole)
        columns = mm_nt(pick[...], whole).astype(bf16)
        nr_o[i] = 0.5 * right[i] + 0.5 * mm(columns, whole)
        side = mm(lroot[i].astype(bf16), whole)
        step = mm(side.astype(bf16), rroot[i].astype(bf16))
        new = master[i] - rate_blocks * step
        nm_o[i] = new
        nc_o[i] = new.astype(bf16)


def deliveries(sizes, parts, count):
    edges = [sum(sizes[:c]) for c in range(len(sizes) + 1)]
    runs = []
    for which, ids in enumerate(block_sets()):
        for owner, k, v, j, n in move_runs(ids, parts, count):
            if which:
                runs.append((0, which, owner, k, v, j, n))
                continue
            for c, (a, b) in enumerate(zip(edges[:-1], edges[1:])):
                low, high = max(a, j), min(b, j + n)
                if low < high:
                    runs.append((c + 1, 0, owner, k + low - j, v, low, high - low))
    groups = []
    for chunk, unused, owner, k, v, j, n in sorted(runs, key=lambda run: (run[0], run[2], run[3])):
        if groups and groups[-1][:2] == (chunk, owner) and sum(groups[-1][2:]) == k:
            groups[-1] = (chunk, owner, groups[-1][2], groups[-1][3] + n)
        else:
            groups.append((chunk, owner, k, n))
    return runs, groups


def reduce_kernel(
    sizes, runs, groups, grads, share_pair, share_rest, small, full, owned_o, small_sum,
    mine, came, from_x, from_y, red, near_in, far_in, share_first, owned, s_tm, s_core, s_z,
    d_send, d_recv, a_send, a_recv, f_send, f_recv, s_send, s_recv, put_sem, *sems,
):
    it = Reduce(
        sizes, dict(zip(R_XY + R_Z, sems)), grads, (mine, came, from_x, from_y), red,
        (near_in, far_in), share_first,
    )
    place, level, core = it.place, it.level, it.core
    low, high, near, far = it.low, it.high, it.near_by, it.far_off
    diagonal = 2 * (1 - high) + 1 - low
    others = (it.xp, it.yp, it.dp)
    greet([at(other, level, core) for other in others])
    greet([at(place, other, core) for other in (near, far, diagonal)])
    greet([at(place, level, 1 - core)])
    shares = (share_first, share_pair, share_rest)

    def deliver(index):
        unused, which, owner, k, v, j, n = runs[index]
        src, dst = shares[which].at[pl.ds(j, n)], owned.at[pl.ds(k, n)]
        if owner == v:
            return pltpu.make_async_copy(src, dst, d_send.at[index])
        return remote(src, dst, d_send.at[index], d_recv.at[index], at(owner, level, core))

    def in_chunk(c):
        return [i for i, run in enumerate(runs) if run[0] == c]

    def send_out(c):
        for i in in_chunk(c):
            pl.when(place == runs[i][4])(lambda i=i: deliver(i).start())

    def come_in(c):
        for i in in_chunk(c):
            local = runs[i][2] == runs[i][4]
            done = (lambda i=i: deliver(i).wait()) if local else (lambda i=i: deliver(i).wait_recv())
            pl.when(place == runs[i][2])(done)

    def sent_out():
        for i, run in enumerate(runs):
            if run[2] != run[4]:
                pl.when(place == run[4])(lambda i=i: deliver(i).wait_send())

    def spot(g, where):
        unused, owner, k, n = groups[g]
        return full.at[pl.ds(k, n), where // 2, where % 2, core]

    def held(g):
        unused, owner, k, n = groups[g]
        return owned.at[pl.ds(k, n)]

    def put(g):
        return pltpu.make_async_copy(held(g), spot(g, level), put_sem.at[g])

    def along(g, i):
        src = spot(g, far) if i == 2 else held(g)
        dst = spot(g, far if i == 2 else level)
        target = at(place, far if i == 0 else near, core)
        return remote(src, dst, a_send.at[g, i], a_recv.at[g, i], target)

    def to_core(g, i):
        where = (level, far, near, diagonal)[i]
        src = held(g) if i == 0 else spot(g, where)
        target = at(place, level, 1 - core)
        return remote(src, spot(g, where), f_send.at[g, i], f_recv.at[g, i], target)

    def for_groups(c, act):
        for g, group in enumerate(groups):
            if c is None or group[0] == c:
                pl.when(place == group[1])(lambda g=g: act(g))

    def spread(g):
        put(g).start()
        along(g, 0).start()
        along(g, 1).start()
        to_core(g, 0).start()

    def pass_on(g):
        along(g, 0).wait_recv()
        along(g, 2).start()
        to_core(g, 1).start()
        along(g, 1).wait_recv()
        to_core(g, 2).start()

    def last(g):
        along(g, 2).wait_recv()
        to_core(g, 3).start()

    def finish(g):
        put(g).wait()
        for i in range(4):
            to_core(g, i).wait_recv()
        for i in range(4):
            to_core(g, i).wait_send()
        for i in range(3):
            along(g, i).wait_send()

    def to_place(d):
        send, recv = s_send.at[d], s_recv.at[d]
        return remote(small.at[others[d]], s_tm.at[d], send, recv, at(others[d], level, core))

    def to_sibling():
        target = at(place, level, 1 - core)
        return remote(s_core.at[0], s_core.at[1], s_send.at[3], s_recv.at[3], target)

    def to_level(d):
        target = at(place, (near, far, diagonal)[d], core)
        return remote(s_z.at[level], s_z.at[level], s_send.at[4 + d], s_recv.at[4 + d], target)

    def reduced(c):
        it.combine(c)
        it.near(c).start()

    def settled(c):
        it.settle(c)
        send_out(c + 1)

    def arrived(c):
        come_in(c + 1)
        for_groups(c + 1, spread)

    met(7)
    for c in it.all:
        it.start(c)
    send_out(0)
    for d in range(3):
        to_place(d).start()
    stages = (
        it.begin, it.second, reduced, it.across, settled, arrived,
        lambda c: for_groups(c + 1, pass_on), lambda c: for_groups(c + 1, last),
    )
    chunks = len(sizes)
    for tick in range(chunks + len(stages) - 1):
        for index, stage in enumerate(stages):
            if 0 <= tick - index < chunks:
                stage(tick - index)
        if tick == 0:
            come_in(0)
            for_groups(0, spread)
            for d in range(3):
                to_place(d).wait_recv()
            s_core[0] = small[place] + (s_tm[0] + s_tm[1]) + s_tm[2]
            to_sibling().start()
        if tick == 1:
            to_sibling().wait_recv()
            s_z[level] = s_core[0] + s_core[1]
            for d in range(3):
                to_level(d).start()
        if tick == 2:
            for_groups(0, pass_on)
        if tick == 3:
            for_groups(0, last)
    for d in range(3):
        to_level(d).wait_recv()
    small_sum[...] = (s_z[0] + s_z[1]) + (s_z[2] + s_z[3])
    owned_o[...] = owned[...]
    for_groups(None, finish)
    for c in it.all:
        it.square_end(c)
        it.levels_end(c)
    sent_out()
    for d in range(3):
        to_place(d).wait_send()
        to_level(d).wait_send()
    to_sibling().wait_send()


def reduce_grads(first, pair, rest, small, parts, devices, slab):
    levels = devices // 2
    ffn, mix = D // BS * (FF // BS), (D // BS) ** 2
    if parts != 4 or levels != 4:
        grads = [first[: 2 * ffn], rest[: 2 * ffn], first[2 * ffn :], pair, rest[2 * ffn :]]
        owned = jnp.concatenate(grads, axis=0)
        owned = lax.psum_scatter(owned, "tm", scatter_dimension=0, tiled=True)
        owned = lax.psum_scatter(owned, "rows", scatter_dimension=1, tiled=True)
        full = lax.all_gather(owned, "rows", axis=1, tiled=True)
        small = lax.psum_scatter(small, "tm", scatter_dimension=0, tiled=True)[0]
        return full, owned, lax.psum(small, "rows")
    sizes = (3, 3, 3)
    m, chunks = first.shape[1], len(sizes)
    count = sum(len(ids) for ids in block_sets()) // parts
    runs, groups = deliveries(sizes, parts, count)
    dma = lambda *dims: pltpu.SemaphoreType.DMA(dims)
    vb = lambda *dims: pltpu.VMEM(dims + (slab, BS), bf16)
    vmem = pl.BlockSpec(memory_space=pltpu.VMEM)
    part = small.shape[1:]
    full, owned, small_sum = pl.pallas_call(
        partial(reduce_kernel, sizes, runs, groups),
        in_specs=[ANY, vmem, vmem, vmem],
        out_specs=[ANY, vmem, vmem],
        out_shape=[
            shape((count, 2, 2, 2, slab, BS), bf16),
            shape((count, slab, BS), bf16),
            shape(part),
        ],
        scratch_shapes=square_bufs(m, parts, levels, slab)
        + [vb(m, 2, 2)]
        + level_bufs(m, slab)
        + [vb(m), vb(count), vm(3, *part), vm(2, *part), vm(levels, *part)]
        + [dma(len(runs)), dma(len(runs)), dma(len(groups), 3), dma(len(groups), 3)]
        + [dma(len(groups), 4), dma(len(groups), 4), dma(7), dma(7), dma(len(groups))]
        + reduce_sems(R_XY + R_Z, chunks),
        compiler_params=pltpu.CompilerParams(
            collective_id=2, has_side_effects=True, vmem_limit_bytes=VMEM_BYTES
        ),
        name="reduce_grads",
    )(first, pair, rest, small)
    return full.reshape(count, BS, BS), owned, small_sum


def row_spec(frames, width, per=1):
    return pl.BlockSpec((per, frames, width), lambda i: (i, 0, 0))


def whole_spec(*dims):
    return pl.BlockSpec(dims, lambda i: (0,) * len(dims))


def talking(number):
    return pltpu.CompilerParams(
        dimension_semantics=("arbitrary",),
        vmem_limit_bytes=VMEM_BYTES,
        collective_id=number,
        has_side_effects=True,
    )


def body(
    features,
    cotangent,
    state_bank,
    state_source,
    master,
    left_stats,
    right_stats,
    left_root,
    right_root,
    small_params,
    decay_logs,
    state_mix,
):
    rows, frames, width = features.shape
    tokens = rows * frames
    parts = lax.axis_size("tm")
    place = lax.axis_index("tm")
    scaling = 1.0 / math.sqrt(tokens * parts * lax.axis_size("rows"))
    ffn, mix = D // BS * (FF // BS), (D // BS) ** 2

    own_heads, own_channels = decay_logs.shape[0], state_mix.shape[1]
    starts_own = state_bank[state_source]
    params = jnp.concatenate(
        [decay_logs.reshape(-1), state_mix.reshape(-1), starts_own.reshape(-1)]
    )
    cut_one = own_heads * NST
    cut_two = cut_one + 2 * own_channels * NST
    cut_three = cut_two + rows * own_channels * NST
    params = jnp.pad(params, (0, -cut_three % (8 * LANES))).reshape(-1, LANES)
    devices = lax.axis_size("rows")
    levels = devices // 2
    spread_out = parts == 4
    if spread_out:
        first, pair, rest, packed = gather_first(master, params, parts, devices)
        first = first.reshape(-1, BS, BS)
        pair_out, rest_out = [shape(pair.shape, bf16)], [shape(rest.shape, bf16)]
        any_one, pair_in, rest_in = [ANY], [pair], [rest]
        pair_sems, rest_sems = gather_sems(XY_SEMS, levels), gather_sems(XY_SEMS, levels, 2)
    else:
        stack = lax.all_gather(master.astype(bf16), "rows", axis=1, tiled=True)
        stack = lax.all_gather(stack, "tm", axis=0, tiled=True)
        packed = lax.all_gather(params, "tm", axis=0)
        first, pair, rest = (stack[jnp.array(ids)] for ids in block_sets())
        pair_out = rest_out = any_one = pair_in = rest_in = pair_sems = rest_sems = []

    packed = packed.reshape(parts, -1)
    logs = packed[:, :cut_one].reshape(HEADS, NST)
    mix_all = packed[:, cut_one:cut_two].reshape(parts, 2, own_channels, NST)
    mix_all = mix_all.transpose(1, 3, 0, 2).reshape(2, NST, D)
    starts = packed[:, cut_two:cut_three].reshape(parts, rows, own_channels, NST)
    starts = starts.transpose(1, 3, 0, 2).reshape(rows, NST, D)

    rates = jnp.exp(logs)
    rate_nc = jnp.repeat(rates.T, HALF, axis=1)
    coupling = mix_all[0] * mix_all[1]
    state_row = jnp.arange(GROUP * NST, dtype=jnp.int32)
    part_of = state_row // NST
    rate_row = jnp.tile(rates, (1, GROUP))[:, :, None]
    inner_t = jnp.arange(GROUP * SUB, dtype=jnp.int32)
    age = SUB * (part_of + 1)[:, None] - 1 - inner_t[None, :]
    age_f = jnp.maximum(age, 0).astype(f32)
    tab_in = jnp.where(age >= 0, jnp.exp(-rate_row * age_f), 0.0)
    since = (inner_t % SUB + 1).astype(f32)
    inside = (inner_t // SUB)[None, :] == part_of[:, None]
    tab_out = jnp.where(inside, jnp.exp(-rate_row * since), 0.0)
    tab_a = jnp.stack([tab_in, tab_in * age_f, tab_out, tab_out * since], axis=1).astype(bf16)
    tab_b = jnp.stack([tab_in, tab_out], axis=1).astype(bf16).transpose(0, 1, 3, 2)
    steps_of = SUB * jnp.arange(1, GROUP + 1, dtype=f32)
    power = jnp.exp(-rates[:, None, :, None] * steps_of[None, :, None, None])
    power = jnp.broadcast_to(power, (HEADS, GROUP, NST, LANES))
    time = jnp.arange(frames, dtype=jnp.int32)
    flat_rates = rates.reshape(-1)
    next_t = (time + 1).astype(f32)
    left_t = (frames - 1 - time).astype(f32)
    pfull = jnp.exp(-flat_rates[None, :] * next_t[:, None]).astype(bf16)
    pfull_t = jnp.exp(-flat_rates[:, None] * next_t[None, :]).astype(bf16)
    mfin = jnp.exp(-flat_rates[:, None] * left_t[None, :]).astype(bf16)
    mfin_t = jnp.exp(-flat_rates[None, :] * left_t[:, None]).astype(bf16)
    lag = jnp.arange(SUB, dtype=f32)
    lag_decay = jnp.exp(-rate_nc[None] * lag[:, None, None])
    kernel_lags = jnp.sum(coupling[None] * lag_decay, axis=1)
    slot = jnp.arange(SUB, dtype=jnp.int32)
    taps_f = jnp.where(slot[:, None, None] <= slot[None, :, None], kernel_lags[:, None, :], 0.0)
    taps_b = jnp.where(
        slot[:, None, None] + slot[None, :, None] < SUB, kernel_lags[:, None, :], 0.0
    )

    span = float(frames)
    shard = jnp.arange(parts, dtype=jnp.int32)

    def passing(apart):
        length = jnp.maximum(apart, 0).astype(f32)[:, None, None] * span
        weight = jnp.where(
            (apart >= 0)[:, None, None], jnp.exp(-rate_nc[None] * length), 0.0
        )
        return weight, weight * length

    behind_w, behind_l = passing(place - 1 - shard)
    ahead_w, unused = passing(shard - place - 1)
    begin = place.astype(f32) * span
    begin_w = jnp.exp(-rate_nc * begin)
    weigh_in = jnp.concatenate([behind_w, (mix_all[1] * begin_w)[None]], axis=0)
    weigh_back = jnp.stack([behind_w, behind_l, ahead_w], axis=0)

    mat = lambda r, c: vm(r, c, dtype=bf16)
    dma = pltpu.SemaphoreType.DMA
    group = 3 if rows % 3 == 0 else 1
    small_spec = whole_spec(*small_params.shape)
    state_spec = pl.BlockSpec((1, NST, D), lambda i: (i, 0, 0))
    states_spec = pl.BlockSpec((parts, 1, NST, D), lambda i: (0, i, 0, 0))
    flat_spec = whole_spec(NST, D)
    x1, inner_a, act_a, u, ends, *done = pl.pallas_call(
        ffa_forward_kernel,
        grid=(rows // BOTH,),
        in_specs=[row_spec(frames, D, BOTH), small_spec, ANY, whole_spec(HEADS * NST, frames)]
        + any_one,
        out_specs=[
            row_spec(frames, D, BOTH),
            row_spec(frames, FF, BOTH),
            row_spec(frames, FF, BOTH),
            row_spec(frames, D, BOTH),
            pl.BlockSpec((BOTH, NST, D), lambda i: (i, 0, 0)),
        ]
        + any_one,
        out_shape=[
            shape((rows, frames, D)),
            shape((rows, frames, FF), bf16),
            shape((rows, frames, FF), bf16),
            shape((rows, frames, D), bf16),
            shape((rows, NST, D), bf16),
        ]
        + pair_out,
        scratch_shapes=[mat(D, FF), mat(FF, D), mat(D, D), dma] + pair_sems,
        input_output_aliases={4: 5} if spread_out else {},
        compiler_params=talking(7) if spread_out else PARAMS,
        name="ffa_forward",
    )(features, small_params, first, mfin, *pair_in)
    if spread_out:
        pair = done[0].reshape(-1, BS, BS)

    group_spec = pl.BlockSpec((rows, frames, LANES), lambda i: (0, 0, i))
    tab_a_spec = pl.BlockSpec((2,) + tab_a.shape[1:], lambda i: (i, 0, 0, 0))
    tab_b_spec = pl.BlockSpec((2,) + tab_b.shape[1:], lambda i: (i, 0, 0, 0))
    power_spec = pl.BlockSpec((2,) + power.shape[1:], lambda i: (i, 0, 0, 0))
    coup_spec = pl.BlockSpec((NST, LANES), lambda i: (0, i))
    taps_spec = pl.BlockSpec((SUB, SUB, LANES), lambda i: (0, 0, i))
    swap_scratch = [dma, dma((parts - 1,)), dma((parts - 1,))]
    all_states = shape((parts, rows, NST, D), bf16)
    y_loc, ends_all, *done = pl.pallas_call(
        conv_forward_kernel,
        grid=(D // LANES,),
        in_specs=[group_spec, ANY, tab_a_spec, tab_b_spec, power_spec, coup_spec, taps_spec]
        + any_one,
        out_specs=[group_spec, ANY] + any_one,
        out_shape=[shape((rows, frames, D)), all_states] + rest_out,
        scratch_shapes=[vm(SUB + frames, LANES)] + swap_scratch + rest_sems,
        input_output_aliases={7: 2} if spread_out else {},
        compiler_params=talking(3),
        name="conv_forward",
    )(u, ends, tab_a, tab_b, power, coupling, taps_f, *rest_in)

    edge_spec = pl.BlockSpec((1, PAD, D), lambda i: (i, 0, 0))
    edge_scratch = [
        vm(rows, 2, PAD, D, dtype=bf16),
        vm(PAD, D, dtype=bf16),
        dma((2, rows)),
        dma((2, rows)),
        dma((2,)),
    ]
    edge_shapes = [shape((rows, PAD, D), bf16)] * 2
    ys, gated, x2, pw, g, g_low, g_high, *done = pl.pallas_call(
        mixer_out_kernel,
        grid=(rows,),
        in_specs=[
            row_spec(frames, D),
            states_spec,
            state_spec,
            whole_spec(parts + 1, NST, D),
            flat_spec,
            row_spec(frames, D),
            small_spec,
            ANY,
            whole_spec(frames, HEADS * NST),
        ]
        + any_one,
        out_specs=[
            row_spec(frames, D),
            row_spec(frames, 2 * D),
            row_spec(frames, D),
            row_spec(frames, 2 * D),
            row_spec(frames, D),
            ANY,
            ANY,
        ]
        + any_one,
        out_shape=[
            shape((rows, frames, D), bf16),
            shape((rows, frames, 2 * D), bf16),
            shape((rows, frames, D)),
            shape((rows, frames, 2 * D), bf16),
            shape((rows, frames, D), bf16),
        ]
        + edge_shapes
        + rest_out,
        scratch_shapes=[mat(D, 2 * D), mat(D, 2 * D), vm(HEADS * NST, D), dma]
        + edge_scratch
        + rest_sems,
        input_output_aliases={9: 7} if spread_out else {},
        compiler_params=talking(4),
        name="mixer_out",
    )(y_loc, ends_all, starts, weigh_in, coupling, x1, small_params, pair, pfull, *done)
    if spread_out:
        rest = done[0].reshape(-1, BS, BS)

    kept = lambda *widths: [mat(group * frames, w) for w in widths]
    slab = master.shape[1]
    spread_back = spread_out and levels == 4
    sizes = [len(ids) // parts for ids in block_sets()]
    if spread_back:
        grad_shapes = [shape((parts, n, levels, 2, slab, BS), bf16) for n in sizes]
        flat_shapes = [shape((parts * n, BS, BS), bf16) for n in sizes]
    else:
        flat_shapes = [shape((len(ids), BS, BS), bf16) for ids in block_sets()]
    unflat = lambda v, k: v.reshape(grad_shapes[k].shape) if spread_back else v
    layer_out, dx3, dq, grads_rest, gain_b, d_low, d_high = pl.pallas_call(
        partial(ffb_kernel, scaling),
        grid=(rows,),
        in_specs=[
            row_spec(frames, D),
            edge_spec,
            edge_spec,
            row_spec(frames, D),
            row_spec(frames, D),
            small_spec,
            ANY,
        ],
        out_specs=[
            row_spec(frames, D),
            row_spec(frames, D),
            row_spec(frames, D),
            ANY,
            whole_spec(2, 8, D),
            ANY,
            ANY,
        ],
        out_shape=[
            shape((rows, frames, D), bf16),
            shape((rows, frames, D)),
            shape((rows, frames, D), bf16),
            flat_shapes[2],
            shape((2, 8, D)),
        ]
        + edge_shapes,
        scratch_shapes=[
            mat(D, FF),
            mat(FF, D),
            mat(D, D),
            vm(D, FF),
            vm(D, FF),
            vm(D, D),
            vm(D // LANES, frames + 2 * PAD, LANES),
            vm(frames, D),
            vm(2 * ffn + mix, BS, BS, dtype=bf16),
        ]
        + kept(FF, FF, D, D, D, D)
        + [dma]
        + edge_scratch,
        compiler_params=talking(5),
        name="ffb",
    )(g, g_low, g_high, x2, cotangent, small_params, rest)

    dx2, dy, back_ends, grads_pair, gain_c, kernel_grads, *red_rest = pl.pallas_call(
        partial(mixer_back_kernel, scaling),
        grid=(rows,),
        in_specs=[
            row_spec(frames, D),
            edge_spec,
            edge_spec,
            row_spec(frames, D),
            edge_spec,
            edge_spec,
            row_spec(frames, 2 * D),
            row_spec(frames, D),
            row_spec(frames, 2 * D),
            row_spec(frames, D),
            row_spec(frames, D),
            small_spec,
            ANY,
            whole_spec(HEADS * NST, frames),
        ]
        + [ANY] * spread_back,
        out_specs=[
            row_spec(frames, D),
            row_spec(frames, D),
            state_spec,
            ANY,
            whole_spec(8, D),
            whole_spec(16, D),
        ]
        + [whole_spec(sizes[2], 2, 2, slab, BS)] * spread_back,
        out_shape=[
            shape((rows, frames, D)),
            shape((rows, frames, D), bf16),
            shape((rows, NST, D), bf16),
            flat_shapes[1],
            shape((8, D)),
            shape((16, D)),
        ]
        + [shape((sizes[2], 2, 2, slab, BS), bf16)] * spread_back,
        scratch_shapes=[
            mat(D, 2 * D),
            mat(D, 2 * D),
            vm(D, 2 * D),
            vm(D, 2 * D),
            vm(D // LANES, frames + 2 * PAD, LANES),
            vm(D // LANES, frames + 2 * PAD, LANES),
            vm(frames, D),
            vm(KW, 8, D),
            vm(4 * mix, BS, BS, dtype=bf16),
        ]
        + kept(D, 2 * D, D, 2 * D)
        + [dma]
        + (square_bufs(sizes[2], parts, levels, slab) + reduce_sems(R_XY, 2)) * spread_back,
        compiler_params=talking(8) if spread_back else PARAMS,
        name="mixer_back",
    )(
        dq, d_low, d_high, g, g_low, g_high, pw, x2, gated, ys, dx3, small_params, pair,
        pfull_t, *[unflat(grads_rest, 2)] * spread_back,
    )

    nst_spec = pl.BlockSpec((rows, NST, LANES), lambda i: (0, 0, i))
    du_loc, t_one, t_two, ends_w, back_w, lag_grads, back_all = pl.pallas_call(
        conv_back_kernel,
        grid=(D // LANES,),
        in_specs=[
            group_spec, group_spec, ANY, tab_a_spec, tab_b_spec, power_spec, coup_spec, taps_spec
        ],
        out_specs=[
            group_spec,
            coup_spec,
            coup_spec,
            nst_spec,
            nst_spec,
            pl.BlockSpec((SUB, LANES), lambda i: (0, i)),
            ANY,
        ],
        out_shape=[
            shape((rows, frames, D)),
            shape((NST, D)),
            shape((NST, D)),
            shape((rows, NST, D)),
            shape((rows, NST, D)),
            shape((SUB, D)),
            all_states,
        ],
        scratch_shapes=[
            vm(SUB + frames, LANES),
            vm(SUB + frames, LANES),
            vm(SUB, SUB, LANES),
        ]
        + swap_scratch,
        compiler_params=talking(6),
        name="conv_back",
    )(u, dy, back_ends, tab_a, tab_b, power, coupling, taps_b)

    grad_zero, grads_first, gain_a, sums_c, *shares = pl.pallas_call(
        partial(ffa_back_kernel, scaling),
        grid=(rows,),
        in_specs=[
            row_spec(frames, D),
            states_spec,
            states_spec,
            state_spec,
            state_spec,
            state_spec,
            state_spec,
            whole_spec(3, parts, NST, D),
            flat_spec,
            row_spec(frames, D),
            row_spec(frames, D),
            row_spec(frames, FF),
            row_spec(frames, FF),
            row_spec(frames, D),
            small_spec,
            ANY,
            whole_spec(frames, HEADS * NST),
        ]
        + [ANY, whole_spec(sizes[2], 2, 2, slab, BS)] * spread_back,
        out_specs=[row_spec(frames, D), ANY, whole_spec(2, 8, D), whole_spec(4, NST, D)]
        + [whole_spec(n, slab, BS) for n in sizes[1:]] * spread_back,
        out_shape=[
            shape((rows, frames, D)),
            flat_shapes[0],
            shape((2, 8, D)),
            shape((4, NST, D)),
        ]
        + [shape((n, slab, BS), bf16) for n in sizes[1:]] * spread_back,
        scratch_shapes=[
            mat(D, FF),
            mat(FF, D),
            mat(D, D),
            vm(D, FF),
            vm(D, FF),
            vm(D, D),
            vm(HEADS * NST, D),
            vm(2 * ffn + mix, BS, BS, dtype=bf16),
        ]
        + kept(FF, FF, D, D, D, D)
        + [dma]
        + (
            [vm(sizes[2], 2, 2, slab, BS, dtype=bf16)]
            + level_bufs(sizes[2], slab)
            + [vm(sizes[1], 2, 2, slab, BS, dtype=bf16)]
            + square_bufs(sizes[1], parts, levels, slab)
            + level_bufs(sizes[1], slab)
            + reduce_sems(R_XY + R_Z + R_Z)
        )
        * spread_back,
        compiler_params=talking(9) if spread_back else PARAMS,
        name="ffa_back",
    )(
        du_loc, back_all, ends_all, back_ends, ends_w, back_w, starts, weigh_back, coupling,
        x1, features, inner_a, act_a, dx2, small_params, first, mfin_t,
        *([unflat(grads_pair, 1)] + red_rest) * spread_back,
    )

    lag_grad_c = jnp.sum(lag_decay * lag_grads[:, None, :], axis=0)
    lag_grad_r = jnp.sum(lag_decay * (lag[:, None] * lag_grads)[:, None, :], axis=0)
    d_coup = t_one + lag_grad_c + sums_c[0]
    start_back = sums_c[1] * begin_w
    d_first = d_coup * mix_all[1]
    d_second = d_coup * mix_all[0] + start_back
    d_rate = coupling * (t_two + lag_grad_r + sums_c[3])
    d_rate = d_rate + mix_all[1] * (begin * start_back + begin_w * sums_c[2])
    small_grads = [
        jnp.sum(gain_a, axis=1),
        jnp.sum(gain_c, axis=0, keepdims=True),
        jnp.sum(gain_b, axis=1),
        kernel_grads[:KW],
    ]
    stacked = jnp.concatenate(small_grads + [d_first, d_second, d_rate], axis=0) * scaling
    stacked = jnp.pad(stacked, ((0, -stacked.shape[0] % 8), (0, 0)))
    own = place * own_channels
    lanes_own = lambda v: lax.dynamic_slice_in_dim(v, own, own_channels, v.ndim - 1)
    stacked = stacked.reshape(-1, parts, own_channels).transpose(1, 0, 2)
    full_grad, owned, sums = reduce_grads(
        unflat(grads_first, 0),
        *(shares if spread_back else (grads_pair, grads_rest)),
        stacked,
        parts,
        devices,
        slab,
    )
    count_small = small_params.shape[0]
    small_sum = sums[:count_small]
    mix_sum = sums[count_small : count_small + 2 * NST]
    mix_sum = mix_sum.reshape(2, NST, own_channels).transpose(0, 2, 1)
    rate_sum = sums[count_small + 2 * NST : count_small + 3 * NST]
    rate_sum = jnp.sum(rate_sum.reshape(NST, own_heads, HALF), axis=2)
    decay_sum = -rate_sum.T * jnp.exp(decay_logs)
    new_small = lanes_own(small_params) - rate_small * small_sum
    new_decay = decay_logs - rate_small * decay_sum
    new_mix = state_mix - rate_small * mix_sum

    shard_w = jnp.exp(-lanes_own(rate_nc)[None] * (shard.astype(f32) * span)[:, None, None])
    start_grad = jnp.sum(lanes_own(back_all).astype(f32) * shard_w[:, None], axis=0) * lanes_own(mix_all[1])
    start_grad = start_grad.transpose(0, 2, 1)
    chosen = (state_source[None, :] == jnp.arange(rows, dtype=jnp.int32)[:, None]).astype(f32)
    grad_state = jnp.sum(chosen[:, :, None, None] * start_grad[None], axis=1)

    count, slice_rows = owned.shape[0], owned.shape[1]
    mine = lax.axis_index("rows") * slice_rows
    pick = (
        jnp.arange(slice_rows, dtype=jnp.int32)[:, None] + mine
        == jnp.arange(BS, dtype=jnp.int32)[None, :]
    ).astype(bf16)
    group = 11 if count % 11 == 0 else 1
    part_spec = pl.BlockSpec((group, slice_rows, BS), lambda i: (i, 0, 0))
    full_spec = pl.BlockSpec((group, BS, BS), lambda i: (i, 0, 0))
    new_left, new_right, new_master, new_copy, grad_blocks = pl.pallas_call(
        shampoo_kernel,
        grid=(count // group,),
        in_specs=[
            whole_spec(slice_rows, BS),
            part_spec,
            full_spec,
            part_spec,
            part_spec,
            part_spec,
            full_spec,
            part_spec,
        ],
        out_specs=[part_spec] * 5,
        out_shape=[
            shape(owned.shape),
            shape(owned.shape),
            shape(owned.shape),
            shape(owned.shape, bf16),
            shape(owned.shape),
        ],
        compiler_params=PARAMS,
        name="shampoo",
    )(pick, owned, full_grad, left_stats, right_stats, left_root, right_root, master)
    return (
        layer_out,
        grad_zero,
        grad_state,
        grad_blocks,
        new_left,
        new_right,
        new_master,
        new_copy,
        small_sum,
        new_small,
        decay_sum,
        mix_sum,
        new_decay,
        new_mix,
    )


def solution(mesh):
    return jax.shard_map(
        body,
        mesh=mesh,
        in_specs=(
            P("rows", "tm", None),
            P("rows", "tm", None),
            P("rows", "tm", None),
            P("rows"),
            P("tm", "rows", None),
            P("tm", "rows", None),
            P("tm", "rows", None),
            P("tm", "rows", None),
            P("tm", None, None),
            P(),
            P("tm", None),
            P(None, "tm", None),
        ),
        out_specs=(
            P("rows", "tm", None),
            P("rows", "tm", None),
            P("rows", "tm", None),
            P("tm", "rows", None),
            P("tm", "rows", None),
            P("tm", "rows", None),
            P("tm", "rows", None),
            P("tm", "rows", None),
            P(None, "tm"),
            P(None, "tm"),
            P("tm", None),
            P(None, "tm", None),
            P("tm", None),
            P(None, "tm", None),
        ),
        check_vma=False,
    )
```

```python
from functools import partial
import math

import jax
import jax.numpy as jnp
from jax import lax
from jax.experimental import pallas as pl
from jax.experimental.pallas import tpu as pltpu
from jax.sharding import PartitionSpec as P

D = 512
FF = 2048
NST = 32
KW = 15
BS = 256
HEADS = 8
HALF = 64
LANES = 128
SUB = 16
GROUP = 5
BOTH = 2
PAD = 8
VMEM_BYTES = 60 * 1024 * 1024

rate_blocks = 0.1
rate_small = 0.5
bf16 = jnp.bfloat16
f32 = jnp.float32


def shape(dims, dtype=f32):
    return jax.ShapeDtypeStruct(dims, dtype)


def mm(a, b):
    return jnp.dot(a, b, preferred_element_type=f32)


def mm_nt(a, b):
    return lax.dot_general(a, b, (((1,), (1,)), ((), ())), preferred_element_type=f32)


def mm_tn(a, b):
    return lax.dot_general(a, b, (((0,), (0,)), ((), ())), preferred_element_type=f32)


def sigmoid(v):
    return 0.5 * jnp.tanh(0.5 * v) + 0.5


def norm(v):
    center = v - jnp.mean(v, axis=-1, keepdims=True)
    spread = jnp.mean(center * center, axis=-1, keepdims=True)
    inv = lax.rsqrt(spread + 1e-05)
    return center * inv, inv


def norm_back(hat, inv, scale, incoming):
    scaled = incoming * scale
    mean_one = jnp.mean(scaled, axis=-1, keepdims=True)
    mean_two = jnp.mean(scaled * hat, axis=-1, keepdims=True)
    return inv * (scaled - mean_one - hat * mean_two)


def flat(ref):
    v = ref[...]
    return v.reshape(-1, v.shape[-1])


def put_rows(ref, v):
    ref[...] = v.astype(ref.dtype).reshape(ref.shape)


def fold8(v):
    return jnp.sum(v.reshape(-1, 8, v.shape[-1]), axis=0)


def load_matrices(stack, plan, sem):
    copies = []
    for first, dst in plan:
        down, across = dst.shape[0] // BS, dst.shape[1] // BS
        for i in range(down):
            for j in range(across):
                copies.append(
                    pltpu.make_async_copy(
                        stack.at[first + i * across + j],
                        dst.at[pl.ds(i * BS, BS), pl.ds(j * BS, BS)],
                        sem,
                    )
                )
    for copy in copies:
        copy.start()
    for copy in copies:
        copy.wait()


def store_blocks(plan, scaling, grads, stage, sem):
    copies = []
    for acc, first, transposed in plan:
        rows, cols = acc.shape
        down, across = (cols, rows) if transposed else (rows, cols)
        for i in range(down // BS):
            for j in range(across // BS):
                slot = len(copies)
                if transposed:
                    part = (acc[pl.ds(j * BS, BS), pl.ds(i * BS, BS)] * scaling).T
                else:
                    part = acc[pl.ds(i * BS, BS), pl.ds(j * BS, BS)] * scaling
                stage[slot] = part.astype(bf16)
                copy = pltpu.make_async_copy(
                    stage.at[slot], grads.at[first + i * (across // BS) + j], sem
                )
                copy.start()
                copies.append(copy)
    for copy in copies:
        copy.wait()


def head_mask():
    row = lax.broadcasted_iota(jnp.int32, (HEADS * NST, D), 0) // NST
    col = lax.broadcasted_iota(jnp.int32, (HEADS * NST, D), 1) // HALF
    return (row == col).astype(f32)


def spread_heads(v, mask):
    return (jnp.concatenate([v] * HEADS, axis=0) * mask).astype(bf16)


def join_lanes(ref):
    return jnp.concatenate([ref[i] for i in range(ref.shape[0])], axis=1)


def rate_rows(logs):
    own = logs.shape[2] // HALF
    places = range(logs.shape[0])
    return [jnp.exp(logs[p, j : j + 1, 0:NST]) for p in places for j in range(own)]


def as_column(row):
    down = lax.broadcasted_iota(jnp.int32, (NST, NST), 0)
    across = lax.broadcasted_iota(jnp.int32, (NST, NST), 1)
    return jnp.sum(jnp.where(down == across, row, 0.0), axis=1, keepdims=True)


def channel_rates(logs):
    first = lax.broadcasted_iota(jnp.int32, (NST, LANES), 1) < HALF
    columns = [as_column(row) for row in rate_rows(logs)]
    pairs = zip(columns[0::2], columns[1::2])
    return jnp.concatenate([jnp.where(first, a, b) for a, b in pairs], axis=1)


def frame_decay(logs, table, to_end):
    frames = table.shape[0]
    rates = jnp.concatenate(rate_rows(logs), axis=1)
    time = lax.broadcasted_iota(jnp.int32, table.shape, 0)
    length = frames - 1 - time if to_end else time + 1
    table[...] = jnp.exp(-rates * length.astype(f32)).astype(bf16)


def passing(rates, apart, frames):
    length = (apart * frames).astype(f32)
    weight = jnp.where(apart >= 0, jnp.exp(-rates * jnp.maximum(length, 0.0)), 0.0)
    return weight, weight * length


def local_states(table, v, out):
    frames = table.shape[0]
    first = lax.broadcasted_iota(jnp.int32, (NST, LANES), 1) < HALF
    for b in range(out.shape[0]):
        for q in range(D // (2 * LANES)):
            here = v[b * frames : (b + 1) * frames, 2 * q * LANES : 2 * (q + 1) * LANES]
            four = mm_tn(table[:, q * LANES : (q + 1) * LANES], here)
            for i in range(2):
                both = four[2 * i * NST : 2 * (i + 1) * NST, i * LANES : (i + 1) * LANES]
                picked = jnp.where(first, both[:NST], both[NST:])
                out[b, :, pl.ds((2 * q + i) * LANES, LANES)] = picked.astype(out.dtype)


def chunk_tables(row):
    column = as_column(row)
    span = GROUP * SUB
    time = lax.broadcasted_iota(jnp.int32, (NST, span), 1)
    since = (time % SUB + 1).astype(f32)
    into, into_w, out, out_w, power = [], [], [], [], []
    for i in range(GROUP):
        age = SUB * (i + 1) - 1 - time
        age_f = jnp.maximum(age, 0).astype(f32)
        value = jnp.where(age >= 0, jnp.exp(-column * age_f), 0.0)
        into.append(value)
        into_w.append(value * age_f)
        value = jnp.where(time // SUB == i, jnp.exp(-column * since), 0.0)
        out.append(value)
        out_w.append(value * since)
        power.append(jnp.exp(-column * float(SUB * (i + 1))))
    join = lambda parts: jnp.concatenate(parts, axis=0).astype(bf16)
    return join(into), join(into_w), join(out), join(out_w), power


def lag_taps(rates, coup, taps, backward):
    place = lax.broadcasted_iota(jnp.int32, (SUB, LANES), 0)
    for d in range(SUB):
        lag = jnp.sum(coup * jnp.exp(-rates * float(d)), axis=0, keepdims=True)
        inside = place + d < SUB if backward else place >= d
        taps[d] = jnp.where(inside, lag, 0.0)


ANY = pl.BlockSpec(memory_space=pl.ANY)
PARAMS = pltpu.CompilerParams(
    dimension_semantics=("arbitrary",), vmem_limit_bytes=VMEM_BYTES
)


def vm(*dims, dtype=f32):
    return pltpu.VMEM(dims, dtype)


def peers():
    place, row = lax.axis_index("tm"), lax.axis_index("rows")
    return place, row // 2, row % 2


def square(place):
    x, y = place % 2, place // 2
    return 2 * y + 1 - x, 2 * (1 - y) + x, 2 * (1 - y) + 1 - x


def at(place, level, core):
    return {"tm": place, "rows": level * 2 + core}


def remote(src, dst, send, recv, device):
    return pltpu.make_async_remote_copy(
        src_ref=src,
        dst_ref=dst,
        send_sem=send,
        recv_sem=recv,
        device_id=device,
        device_id_type=pl.DeviceIdType.MESH,
    )


def signal(sem, device):
    pl.semaphore_signal(sem, inc=1, device_id=device, device_id_type=pl.DeviceIdType.MESH)


def chunk_ranges(count, chunks):
    edges = [count * c // chunks for c in range(chunks + 1)]
    out = []
    for first, end in zip(edges[:-1], edges[1:]):
        middle = (first + end + 1) // 2
        out.append((first, end, middle))
    return out


class Gather:
    def __init__(self, piece, stack, sems, chunks=1):
        self.piece, self.stack, self.sems = piece, stack, sems
        self.place, self.level, self.core = peers()
        self.xp, self.yp, self.dp = square(self.place)
        self.levels = stack.shape[2]
        self.ranges = chunk_ranges(stack.shape[1], chunks)
        self.all = range(chunks)

    def own(self, c):
        first, end, unused = self.ranges[c]
        n = pl.ds(first, end - first)
        spot = self.stack.at[self.place, n, self.level, self.core]
        return pltpu.make_async_copy(self.piece.at[n], spot, self.sems["own"].at[c])

    def z(self, c, d):
        first, end, unused = self.ranges[c]
        n = pl.ds(first, end - first)
        spot = self.stack.at[self.place, n, self.level, self.core]
        send, recv = self.sems["zs"].at[c, d - 1], self.sems["zr"].at[c, d - 1]
        target = (self.level + d) % self.levels
        return remote(self.piece.at[n], spot, send, recv, at(self.place, target, self.core))

    def z_start(self, c):
        self.own(c).start()
        for d in range(1, self.levels):
            self.z(c, d).start()

    def z_arrive(self, c):
        self.own(c).wait()
        for d in range(1, self.levels):
            self.z(c, d).wait_recv()

    def z_end(self, c):
        for d in range(1, self.levels):
            self.z(c, d).wait_send()

    def part(self, name, c, i, owner, first, end, device):
        spot = self.stack.at[owner, pl.ds(first, end - first), :, self.core]
        send, recv = self.sems[name + "s"].at[c, i], self.sems[name + "r"].at[c, i]
        return remote(spot, spot, send, recv, device)

    def x(self, c, i):
        first, end, mid = self.ranges[c]
        what = ((self.place, first, mid), (self.place, mid, end), (self.yp, mid, end))[i]
        return self.part("x", c, i, *what, at(self.xp, self.level, self.core))

    def y(self, c, i):
        first, end, mid = self.ranges[c]
        what = ((self.place, mid, end), (self.place, first, mid), (self.xp, first, mid))[i]
        return self.part("y", c, i, *what, at(self.yp, self.level, self.core))

    def other(self, c, i):
        first, end, mid = self.ranges[c]
        what = (
            (self.place, first, end),
            (self.xp, first, mid),
            (self.yp, mid, end),
            (self.xp, mid, end),
            (self.yp, first, mid),
            (self.dp, first, mid),
            (self.dp, mid, end),
        )[i]
        return self.part("c", c, i, *what, at(self.place, self.level, 1 - self.core))

    def spread(self, c):
        for copy in (self.x(c, 0), self.y(c, 0), self.x(c, 1), self.y(c, 1), self.other(c, 0)):
            copy.start()

    def forward(self, c):
        self.x(c, 0).wait_recv()
        self.y(c, 2).start()
        self.y(c, 0).wait_recv()
        self.x(c, 2).start()
        self.other(c, 1).start()
        self.other(c, 2).start()
        self.x(c, 1).wait_recv()
        self.other(c, 3).start()
        self.y(c, 1).wait_recv()
        self.other(c, 4).start()

    def finish(self, c):
        self.y(c, 2).wait_recv()
        self.other(c, 5).start()
        self.x(c, 2).wait_recv()
        self.other(c, 6).start()

    def end(self, c):
        for i in range(7):
            self.other(c, i).wait_recv()
        for i in range(7):
            self.other(c, i).wait_send()
        for i in range(3):
            self.x(c, i).wait_send()
            self.y(c, i).wait_send()


Z_SEMS = ("own", "zs", "zr")
XY_SEMS = ("xs", "xr", "ys", "yr", "cs", "cr")


def gather_sems(names, levels, chunks=1):
    width = {"own": (), "z": (levels - 1,), "x": (3,), "y": (3,), "c": (7,)}
    key = lambda name: name if name == "own" else name[0]
    return [pltpu.SemaphoreType.DMA((chunks,) + width[key(name)]) for name in names]


def block_sets():
    ffn, mix = D // BS * (FF // BS), (D // BS) ** 2
    ids = lambda *ranges: [b for first, end in ranges for b in range(first, end)]
    return (
        ids((0, 2 * ffn), (4 * ffn, 4 * ffn + mix)),
        ids((4 * ffn + mix, 4 * ffn + 5 * mix)),
        ids((2 * ffn, 4 * ffn), (4 * ffn + 5 * mix, 4 * ffn + 6 * mix)),
    )


def move_runs(ids, places, count):
    runs, each = [], len(ids) // places
    for index, b in enumerate(ids):
        owner, k, v, j = b // count, b % count, index // each, index % each
        if runs:
            o0, k0, v0, j0, n0 = runs[-1]
            if (o0, v0) == (owner, v) and k0 + n0 == k:
                runs[-1] = (o0, k0, v0, j0, n0 + 1)
                continue
        runs.append((owner, k, v, j, 1))
    return runs


def greet(devices):
    barrier = pltpu.get_barrier_semaphore()
    for device in devices:
        signal(barrier, device)


def met(count):
    pl.semaphore_wait(pltpu.get_barrier_semaphore(), count)


def gather_kernel(
    source, master, bank, mix_terms, logs, first, pair, rest, pack_all,
    pack, rounded, piece, piece_pair, piece_rest, run_send, run_recv, pk_send, pk_recv, *sems,
):
    place, level, core = peers()
    others = square(place)
    levels = first.shape[2]
    greet([at(other, level, core) for other in others] + [at(place, level, 1 - core)])
    greet([at(place, (level + d) % levels, core) for d in range(1, levels)])
    rounded[...] = master[...].astype(bf16)
    count = bank.shape[0]
    for i in range(count):
        pack[i * NST : (i + 1) * NST] = bank[source[i]]
    for i in range(2):
        pack[(count + i) * NST : (count + i + 1) * NST] = mix_terms[i]
    pack[(count + 2) * NST :] = jnp.zeros((8, pack.shape[1]), f32)
    pack[(count + 2) * NST : (count + 2) * NST + logs.shape[0], 0:NST] = logs[...]
    met(3 + levels)
    moves = []
    for ids, target in zip(block_sets(), (piece, piece_pair, piece_rest)):
        for run in move_runs(ids, first.shape[0], master.shape[0]):
            moves.append((len(moves), target) + run)

    def move(index, target, owner, k, v, j, n):
        src, dst = rounded.at[pl.ds(k, n)], target.at[pl.ds(j, n)]
        if owner == v:
            return pltpu.make_async_copy(src, dst, run_send.at[index])
        return remote(src, dst, run_send.at[index], run_recv.at[index], at(v, level, core))

    def arrive(entry):
        index, target, owner, k, v, j, n = entry
        if owner == v:
            pl.when(place == v)(lambda: move(*entry).wait())
        else:
            pl.when(place == v)(lambda: move(*entry).wait_recv())

    for entry in moves:
        pl.when(place == entry[2])(lambda entry=entry: move(*entry).start())
    own_pack = pltpu.make_async_copy(pack, pack_all.at[place], pk_send.at[3])
    own_pack.start()
    packs = [
        remote(pack, pack_all.at[place], pk_send.at[d], pk_recv.at[d], at(other, level, core))
        for d, other in enumerate(others)
    ]
    for copy in packs:
        copy.start()
    for entry in moves:
        if entry[1] is piece:
            arrive(entry)
    names = Z_SEMS + XY_SEMS
    chunks = sems[0].shape[0]
    it = Gather(piece, first, dict(zip(names, sems)), chunks)
    later, sems = [], sems[len(names) :]
    for i, (what, stack) in enumerate(((piece_pair, pair), (piece_rest, rest))):
        later.append(Gather(what, stack, dict(zip(Z_SEMS, sems[3 * i : 3 * i + 3]))))
    it.z_start(0)
    for c in it.all:
        it.z_arrive(c)
        it.spread(c)
        if c == 0:
            for ahead in range(1, chunks):
                it.z_start(ahead)
            for entry in moves:
                if entry[1] is not piece:
                    arrive(entry)
        if c == chunks - 1:
            for other_set in later:
                other_set.z_start(0)
        if c >= 1:
            it.forward(c - 1)
        if c >= 2:
            it.finish(c - 2)
    it.forward(chunks - 1)
    for c in range(max(chunks - 2, 0), chunks):
        it.finish(c)
    for c in it.all:
        it.end(c)
        it.z_end(c)
    for other_set in later:
        other_set.z_arrive(0)
        other_set.z_end(0)
    for entry in moves:
        if entry[2] != entry[4]:
            pl.when(place == entry[2])(lambda entry=entry: move(*entry).wait_send())
    own_pack.wait()
    for copy in packs:
        copy.wait()


def gather_first(master, bank, mix_terms, logs, source, parts, devices, chunks=3):
    count, slab, cols = master.shape
    levels = devices // 2
    each = [len(ids) // parts for ids in block_sets()]
    runs = sum(len(move_runs(ids, parts, count)) for ids in block_sets())
    dma = lambda *dims: pltpu.SemaphoreType.DMA(dims)
    pack = ((bank.shape[0] + 2) * NST + 8, bank.shape[2])
    return pl.pallas_call(
        gather_kernel,
        in_specs=[pl.BlockSpec(memory_space=pltpu.SMEM)]
        + [pl.BlockSpec(memory_space=pltpu.VMEM)] * 4,
        out_specs=[ANY] * 4,
        out_shape=[
            shape((parts, each[0], levels, 2, slab, cols), bf16),
            shape((parts, each[1], levels, 2, slab, cols), bf16),
            shape((parts, each[2], levels, 2, slab, cols), bf16),
            shape((parts,) + pack),
        ],
        scratch_shapes=[
            vm(*pack),
            vm(count, slab, cols, dtype=bf16),
            vm(each[0], slab, cols, dtype=bf16),
            vm(each[1], slab, cols, dtype=bf16),
            vm(each[2], slab, cols, dtype=bf16),
            dma(runs),
            dma(runs),
            dma(4),
            dma(3),
        ]
        + gather_sems(Z_SEMS + XY_SEMS, levels, chunks)
        + gather_sems(Z_SEMS, levels) * 2,
        compiler_params=pltpu.CompilerParams(
            collective_id=1, has_side_effects=True, vmem_limit_bytes=VMEM_BYTES
        ),
        name="gather_first",
    )(source, master, bank, mix_terms, logs)


R_XY = ("load", "cs", "cr", "xs", "xr", "ys", "yr")
R_Z = ("zs", "zr")


def reduce_sems(names, chunks=1):
    width = {"x": (3,), "y": (3,), "z": (2,)}
    dims = lambda name: width.get(name[0], ())
    return [pltpu.SemaphoreType.DMA((chunks,) + dims(name)) for name in names]


def square_bufs(m, parts, levels, slab):
    vb = lambda *dims: pltpu.VMEM(dims + (slab, BS), bf16)
    return [vb(parts, m, levels)] * 2 + [vb(2, m, levels)] * 2


def level_bufs(m, slab):
    vb = lambda *dims: pltpu.VMEM(dims + (slab, BS), bf16)
    return [vb(m, 2), vb(m)]


class Reduce:
    def __init__(self, sizes, sems, grads=None, square_refs=None, red=None, level_refs=None, out=None):
        self.sems, self.grads, self.red, self.out = sems, grads, red, out
        if square_refs is not None:
            self.mine, self.came, self.from_x, self.from_y = square_refs
        if level_refs is not None:
            self.near_in, self.far_in = level_refs
        self.place, self.level, self.core = peers()
        self.xp, self.yp, self.dp = square(self.place)
        self.low, self.high = self.level % 2, self.level // 2
        self.near_by = self.level + 1 - 2 * self.low
        self.far_off = self.level + 2 - 4 * self.high
        edges = [sum(sizes[:c]) for c in range(len(sizes) + 1)]
        self.ranges = [(a, b, (a + b + 1) // 2) for a, b in zip(edges[:-1], edges[1:])]
        self.all = range(len(sizes))

    def n(self, c):
        first, end, unused = self.ranges[c]
        return pl.ds(first, end - first)

    def load(self, c):
        src = self.grads.at[:, self.n(c), :, self.core]
        return pltpu.make_async_copy(src, self.mine.at[:, self.n(c)], self.sems["load"].at[c])

    def swap(self, c):
        return remote(
            self.grads.at[:, self.n(c), :, 1 - self.core],
            self.came.at[:, self.n(c)],
            self.sems["cs"].at[c],
            self.sems["cr"].at[c],
            at(self.place, self.level, 1 - self.core),
        )

    def side(self, c, i, name, into, device, what):
        owner, slot, first, end = what
        n = pl.ds(first, end - first)
        send, recv = self.sems[name + "s"].at[c, i], self.sems[name + "r"].at[c, i]
        return remote(self.mine.at[owner, n], into.at[slot, n], send, recv, device)

    def x(self, c, i):
        first, end, mid = self.ranges[c]
        what = ((self.dp, 0, first, mid), (self.xp, 1, first, mid), (self.xp, 1, mid, end))[i]
        return self.side(c, i, "x", self.from_x, at(self.xp, self.level, self.core), what)

    def y(self, c, i):
        first, end, mid = self.ranges[c]
        what = ((self.dp, 0, mid, end), (self.yp, 1, mid, end), (self.yp, 1, first, mid))[i]
        return self.side(c, i, "y", self.from_y, at(self.yp, self.level, self.core), what)

    def add(self, owner, first, end, ref, slot):
        def one(k, carry):
            self.mine[owner, k] = self.mine[owner, k] + ref[slot, k]
            return carry

        lax.fori_loop(first, end, one, 0)

    def start(self, c):
        self.load(c).start()
        self.swap(c).start()

    def begin(self, c):
        first, end, unused = self.ranges[c]
        self.load(c).wait()
        self.swap(c).wait_recv()
        self.add(self.dp, first, end, self.came, self.dp)
        self.x(c, 0).start()
        self.y(c, 0).start()
        self.add(self.xp, first, end, self.came, self.xp)
        self.x(c, 1).start()
        self.add(self.yp, first, end, self.came, self.yp)
        self.y(c, 1).start()
        self.add(self.place, first, end, self.came, self.place)

    def second(self, c):
        first, end, mid = self.ranges[c]
        self.x(c, 0).wait_recv()
        self.add(self.yp, first, mid, self.from_x, 0)
        self.y(c, 2).start()
        self.y(c, 0).wait_recv()
        self.add(self.xp, mid, end, self.from_y, 0)
        self.x(c, 2).start()

    def combine(self, c):
        first, end, unused = self.ranges[c]
        for i in (1, 2):
            self.x(c, i).wait_recv()
            self.y(c, i).wait_recv()

        def one(k, carry):
            total = self.mine[self.place, k].astype(f32) + self.from_x[1, k].astype(f32)
            total = (total + self.from_y[1, k].astype(f32)).astype(bf16)
            self.red[k] = total.reshape(self.red.shape[1:])
            return carry

        lax.fori_loop(first, end, one, 0)

    def square_end(self, c):
        self.swap(c).wait_send()
        for i in range(3):
            self.x(c, i).wait_send()
            self.y(c, i).wait_send()

    def near(self, c):
        return remote(
            self.red.at[self.n(c), :, 1 - self.low],
            self.near_in.at[self.n(c)],
            self.sems["zs"].at[c, 0],
            self.sems["zr"].at[c, 0],
            at(self.place, self.near_by, self.core),
        )

    def far(self, c):
        return remote(
            self.near_in.at[self.n(c), 1 - self.high],
            self.far_in.at[self.n(c)],
            self.sems["zs"].at[c, 1],
            self.sems["zr"].at[c, 1],
            at(self.place, self.far_off, self.core),
        )

    def across(self, c):
        first, end, unused = self.ranges[c]
        self.near(c).wait_recv()

        def one(k, carry):
            self.near_in[k] = self.red[k, :, self.low] + self.near_in[k]
            return carry

        lax.fori_loop(first, end, one, 0)
        self.far(c).start()

    def settle(self, c):
        first, end, unused = self.ranges[c]
        self.far(c).wait_recv()

        def one(k, carry):
            self.out[k] = self.near_in[k, self.high] + self.far_in[k]
            return carry

        lax.fori_loop(first, end, one, 0)

    def levels_end(self, c):
        self.near(c).wait_send()
        self.far(c).wait_send()


def ffa_forward_kernel(feat, small, stack, logs, *refs):
    step, last = pl.program_id(0), pl.num_programs(0) - 1
    pair = None
    if len(refs) > 10:
        refs, sems = refs[1:12], refs[12:]
        pair = Gather(None, refs[5], dict(zip(XY_SEMS, sems)))
        refs = refs[:5] + refs[6:]
    x1_o, inner_o, act_o, u_o, f_o, wi, wo, wu, table, sem = refs

    @pl.when(step == 0)
    def _():
        if pair is not None:
            place, level, core = peers()
            greet([at(other, level, core) for other in square(place)])
            greet([at(place, level, 1 - core)])
        ffn, mix = D // BS * (FF // BS), (D // BS) ** 2
        load_matrices(stack, ((0, wi), (ffn, wo), (2 * ffn, wu)), sem)
        if pair is not None:
            met(4)
            pair.spread(0)
        frame_decay(logs, table, True)

    x0 = flat(feat).astype(f32)
    hat, unused = norm(x0)
    inner = mm((hat * small[0:1]).astype(bf16), wi[...])
    act = (inner * sigmoid(inner)).astype(bf16)
    put_rows(inner_o, inner)
    put_rows(act_o, act)
    x1 = x0 + 0.5 * mm(act, wo[...])
    put_rows(x1_o, x1)
    hat, unused = norm(x1)
    u = mm((hat * small[1:2]).astype(bf16), wu[...]).astype(bf16)
    put_rows(u_o, u)
    local_states(table, u, f_o)
    if pair is not None:
        pl.when(step == last - 1)(lambda: pair.forward(0))

        @pl.when(step == last)
        def _():
            pair.finish(0)
            pair.end(0)


def pack_heads(ref, rows):
    first = lax.broadcasted_iota(jnp.int32, (ref.shape[1], LANES), 1) < HALF
    low, high = [], []
    for p in range(rows // 2):
        a, b = ref[2 * p].astype(f32), ref[2 * p + 1].astype(f32)
        low.append(jnp.where(first, a, pltpu.roll(b, HALF, 1)).astype(bf16))
        high.append(jnp.where(first, pltpu.roll(a, HALF, 1), b).astype(bf16))
    return jnp.concatenate(low, axis=1), jnp.concatenate(high, axis=1)


def pack_params(v, rows):
    first = lax.broadcasted_iota(jnp.int32, v.shape, 1) < HALF
    rolled = pltpu.roll(v, HALF, 1)
    low = jnp.where(first, v, rolled)
    high = jnp.where(first, rolled, v)
    return (
        jnp.concatenate([low] * (rows // 2), axis=1),
        jnp.concatenate([high] * (rows // 2), axis=1),
    )


def unpack_pair(low, high, p):
    low = low[:, p * LANES : (p + 1) * LANES]
    high = high[:, p * LANES : (p + 1) * LANES]
    first = lax.broadcasted_iota(jnp.int32, low.shape, 1) < HALF
    return (
        jnp.where(first, low, pltpu.roll(high, HALF, 1)),
        jnp.where(first, pltpu.roll(low, HALF, 1), high),
    )


def swap_states(mine, whole, first_step, last_step, own_sem, send, recv, rest=None):
    place, level, core = peers()
    parts = whole.shape[0]
    others = [(place + d) % parts for d in range(1, parts)]

    def copies():
        return [
            remote(mine, whole.at[place], send.at[d], recv.at[d], at(other, level, core))
            for d, other in enumerate(others)
        ]

    own = lambda: pltpu.make_async_copy(mine, whole.at[place], own_sem)

    @pl.when(first_step)
    def _():
        greet([at(other, level, core) for other in others])
        if rest is not None:
            greet([at(place, level, 1 - core)])
        own().start()

    def begin():
        @pl.when(first_step)
        def _():
            met(parts - 1 + (rest is not None))
            for copy in copies():
                copy.start()
            if rest is not None:
                rest.spread(0)

    def end():
        if rest is not None:
            pl.when(pl.program_id(0) == pl.num_programs(0) - 2)(lambda: rest.forward(0))

        @pl.when(last_step)
        def _():
            if rest is not None:
                rest.finish(0)
                rest.end(0)
            own().wait()
            for copy in copies():
                copy.wait()

    return begin, end


def tile_lanes(v, width):
    return jnp.concatenate([v] * (width // LANES), axis=1)


def conv_forward_kernel(u, ends, logs, mix_one, mix_two, *refs):
    step = pl.program_id(0)
    pair = None
    if len(refs) > 7:
        refs, sems = refs[1:9], refs[9:]
        pair = Gather(None, refs[2], dict(zip(XY_SEMS, sems)), 2)
        refs = refs[:2] + refs[3:]
    y_o, ends_all, pad, taps, own_sem, send, recv = refs
    begin_swap, end_swap = swap_states(
        ends, ends_all, step == 0, step == pl.num_programs(0) - 1, own_sem, send, recv, pair
    )
    rows, frames = u.shape[0], u.shape[1]
    span = GROUP * SUB
    coup = join_lanes(mix_one) * join_lanes(mix_two)
    lag_taps(channel_rates(logs), coup, taps, False)
    coup_both = pack_params(coup, rows)
    heads = rate_rows(logs)
    packed = pack_heads(u, rows)
    width = packed[0].shape[1]
    begin_swap()
    results = []
    for h in range(2):
        into, unused, out, unused, power = chunk_tables(heads[h])
        scale = [jnp.broadcast_to(v, (NST, width)) for v in power]
        carry = None
        outs = []
        for g in range(frames // span):
            local = mm(into, packed[h][g * span : (g + 1) * span])
            parts = [local[i * NST : (i + 1) * NST] for i in range(GROUP)]
            if carry is None:
                states = [jnp.zeros_like(parts[0])] + parts[:-1]
                carry = parts[-1]
            else:
                states = [carry] + [parts[i] + scale[i] * carry for i in range(GROUP - 1)]
                carry = parts[-1] + scale[-1] * carry
            scaled = jnp.concatenate([v * coup_both[h] for v in states], axis=0)
            outs.append(mm_tn(out, scaled.astype(bf16)))
        results.append(jnp.concatenate(outs, axis=0))
    for p in range(rows // 2):
        one, two = unpack_pair(results[0], results[1], p)
        y_o[2 * p] = one
        y_o[2 * p + 1] = two
    pad[0:SUB] = jnp.zeros((SUB, LANES), f32)
    chunk = frames // 5

    def one_row(i, carry):
        pad[pl.ds(SUB, frames)] = u[i].astype(f32)
        for r in range(0, frames, chunk):
            acc = y_o[i, pl.ds(r, chunk)].reshape(-1, SUB, LANES)
            for d in range(SUB):
                piece = pad[pl.ds(SUB + r - d, chunk)].reshape(-1, SUB, LANES)
                acc = acc + piece * taps[d][None]
            y_o[i, pl.ds(r, chunk)] = acc.reshape(chunk, LANES)
        return carry

    lax.fori_loop(0, rows, one_row, 0)
    end_swap()


def edge_sender(edges, low_all, high_all, zeros, send, recv, zero_sem, step, per, rest=None):
    place, level, core = peers()
    parts = lax.axis_size("tm")
    steps = edges.shape[0]
    not_first, not_last = place > 0, place < parts - 1
    after = (place + 1) % parts
    before = (place + parts - 1) % parts

    def up(i):
        return remote(
            edges.at[i, 1], low_all.at[i], send.at[0, i], recv.at[0, i], at(after, level, core)
        )

    def down(i):
        return remote(
            edges.at[i, 0], high_all.at[i], send.at[1, i], recv.at[1, i], at(before, level, core)
        )

    def blank(ref, i, k):
        return pltpu.make_async_copy(zeros, ref.at[i], zero_sem.at[k])

    @pl.when(step == 0)
    def _():
        if rest is None:
            pl.when(not_last)(lambda: greet([at(after, level, core)]))
            pl.when(not_first)(lambda: greet([at(before, level, core)]))
        zeros[...] = jnp.zeros_like(zeros)

        @pl.when(place == 0)
        def _():
            for i in range(steps):
                blank(low_all, i, 0).start()

        @pl.when(place == parts - 1)
        def _():
            for i in range(steps):
                blank(high_all, i, 1).start()

    def put(v):
        @pl.when(step == 0)
        def _():
            below = (place + parts - 1) // parts
            above = (2 * parts - 2 - place) // parts
            if rest is None:
                met(below + above)

        if rest is not None:
            pl.when(step == steps // per // 2)(lambda: rest.forward(1))
            pl.when(step == steps // per - 1)(lambda: rest.finish(1))

        frames = v.shape[0] // per
        for b in range(per):
            row = step * per + b
            edges[row, 0] = v[b * frames : b * frames + PAD]
            edges[row, 1] = v[(b + 1) * frames - PAD : (b + 1) * frames]
            pl.when(not_last)(lambda row=row: up(row).start())
            pl.when(not_first)(lambda row=row: down(row).start())

        @pl.when(step == steps // per - 1)
        def _():
            for i in range(steps):
                pl.when(not_last)(lambda i=i: up(i).wait_send())
                pl.when(not_first)(lambda i=i: down(i).wait_send())
                pl.when(not_first)(lambda i=i: up(i).wait_recv())
                pl.when(not_last)(lambda i=i: down(i).wait_recv())

            if rest is not None:
                rest.end(1)

            @pl.when(place == 0)
            def _():
                for i in range(steps):
                    blank(low_all, i, 0).wait()

            @pl.when(place == parts - 1)
            def _():
                for i in range(steps):
                    blank(high_all, i, 1).wait()

    return put


def mixer_out_kernel(
    y, ends_all, starts, mix_one, mix_two, logs, x1, small, stack, *refs
):
    step = pl.program_id(0)
    rest = None
    if len(refs) > 19:
        refs, sems = refs[1:21], refs[21:]
        rest = Gather(None, refs[7], dict(zip(XY_SEMS, sems)), 2)
        refs = refs[:7] + refs[8:]
    ys_o, gated_o, x2_o, pw_o, g_o, low_o, high_o, wo, wp, mask, sem = refs[:11]
    table, weigh, coup, edges, zeros, send, recv, zero_sem = refs[11:]
    parts = ends_all.shape[0]
    put = edge_sender(edges, low_o, high_o, zeros, send, recv, zero_sem, step, 1, rest)

    @pl.when(step == 0)
    def _():
        ffn, mix = D // BS * (FF // BS), (D // BS) ** 2
        if rest is not None:
            greet([at(other, rest.level, rest.core) for other in (rest.xp, rest.yp, rest.dp)])
            greet([at(rest.place, rest.level, 1 - rest.core)])
        load_matrices(stack, ((0, wo), (2 * mix, wp)), sem)
        if rest is not None:
            met(4)
            rest.spread(1)
        mask[...] = head_mask()
        place = lax.axis_index("tm")
        frames = table.shape[0]
        frame_decay(logs, table, False)
        rates = channel_rates(logs)
        for i in range(parts):
            weigh[i], unused = passing(rates, place - 1 - i, frames)
        two = join_lanes(mix_two)
        weigh[parts] = two * passing(rates, place, frames)[0]
        coup[...] = join_lanes(mix_one) * two

    came = weigh[0] * ends_all[0, 0].astype(f32)
    for i in range(1, parts):
        came = came + weigh[i] * ends_all[i, 0].astype(f32)
    zin = coup[...] * came + weigh[parts] * join_lanes(starts)
    ys = (y[0] + mm(table[...], spread_heads(zin, mask[...]))).astype(bf16)
    ys_o[0] = ys
    gated = mm(ys, wo[...])
    gated_o[0] = gated.astype(bf16)
    x2 = x1[0] + gated[:, :D] * sigmoid(gated[:, D:])
    x2_o[0] = x2
    hat, unused = norm(x2)
    pw = mm((hat * small[2:3]).astype(bf16), wp[...])
    pw_o[0] = pw.astype(bf16)
    g = (pw[:, :D] * sigmoid(pw[:, D:])).astype(bf16)
    g_o[0] = g
    put(g)


def fill_pad(pad, low, body, high):
    frames = body.shape[0]
    for g in range(D // LANES):
        lanes = slice(g * LANES, (g + 1) * LANES)
        pad[g, 0:PAD] = low[:, lanes].astype(f32)
        pad[g, pl.ds(PAD, frames)] = body[:, lanes].astype(f32)
        pad[g, pl.ds(PAD + frames, PAD)] = high[:, lanes].astype(f32)


def ffb_kernel(
    scale, g, low, high, x2, cot, small, stack,
    out_o, dx3_o, dq_o, grads, gain_o, low_o, high_o,
    wi, wo, wq, acc_in, acc_out, acc_q, pad, q_s, stage, k_act, k_din, k_n, k_dp, k_a, k_dpq, sem,
    edges, zeros, send, recv, zero_sem,
):
    step = pl.program_id(0)
    frames = g.shape[1]
    put = edge_sender(edges, low_o, high_o, zeros, send, recv, zero_sem, step, 1)

    @pl.when(step == 0)
    def _():
        ffn, mix = D // BS * (FF // BS), (D // BS) ** 2
        load_matrices(stack, ((0, wi), (ffn, wo), (2 * ffn, wq)), sem)
        acc_in[...] = jnp.zeros_like(acc_in)
        acc_out[...] = jnp.zeros_like(acc_out)
        acc_q[...] = jnp.zeros_like(acc_q)
        gain_o[...] = jnp.zeros_like(gain_o)

    fill_pad(pad, low[0], g[0], high[0])
    chunk = frames // 5
    for c in range(D // LANES):
        lanes = slice(c * LANES, (c + 1) * LANES)
        for r in range(0, frames, chunk):
            acc = small[5:6, lanes] * pad[c, pl.ds(r + PAD - 7, chunk)]
            for j in range(1, KW):
                acc = acc + small[5 + j : 6 + j, lanes] * pad[c, pl.ds(r + j + PAD - 7, chunk)]
            q_s[pl.ds(r, chunk), lanes] = acc
    q = q_s[...]
    sig_q = sigmoid(q)
    act_q = q * sig_q
    a3 = act_q.astype(bf16)
    x3 = x2[0] + mm(a3, wq[...])
    hat3, inv3 = norm(x3)
    n3 = (hat3 * small[3:4]).astype(bf16)
    inner = mm(n3, wi[...])
    sig = sigmoid(inner)
    act = inner * sig
    b4 = act.astype(bf16)
    x4 = x3 + 0.5 * mm(b4, wo[...])
    hat4, inv4 = norm(x4)
    out_o[0] = (hat4 * small[4:5]).astype(bf16)
    c4 = cot[0].astype(f32)
    gain_o[1] += fold8(c4 * hat4)
    dx4 = norm_back(hat4, inv4, small[4:5], c4)
    dp = (0.5 * dx4).astype(bf16)
    dact = mm_nt(dp, wo[...])
    dinner = ((sig + act * (1.0 - sig)) * dact).astype(bf16)
    group = k_n.shape[0] // frames
    keep = pl.ds(pl.multiple_of(step % group * frames, frames), frames)
    k_act[keep] = b4
    k_din[keep] = dinner
    k_n[keep] = n3
    k_dp[keep] = dp
    k_a[keep] = a3
    dn3 = mm_nt(dinner, wi[...])
    gain_o[0] += fold8(dn3 * hat3)
    dx3 = dx4 + norm_back(hat3, inv3, small[3:4], dn3)
    dx3_o[0] = dx3
    dpq = dx3.astype(bf16)
    k_dpq[keep] = dpq
    da3 = mm_nt(dpq, wq[...])
    dq = ((sig_q + act_q * (1.0 - sig_q)) * da3).astype(bf16)
    dq_o[0] = dq
    put(dq)

    @pl.when(step % group == group - 1)
    def _():
        acc_out[...] += mm_tn(k_dp[...], k_act[...])
        acc_in[...] += mm_tn(k_n[...], k_din[...])
        acc_q[...] += mm_tn(k_a[...], k_dpq[...])

    @pl.when(step == pl.num_programs(0) - 1)
    def _():
        ffn, mix = D // BS * (FF // BS), (D // BS) ** 2
        plan = (
            (acc_in, 0, False),
            (acc_out, ffn, True),
            (acc_q, 2 * ffn, False),
        )
        store_blocks(plan, scale, grads, stage, sem)


def mixer_back_kernel(
    scale, dq, dlow, dhigh, g, glow, ghigh, pw, x2, gated, ys, dx3, small, stack, logs, *refs
):
    step, last = pl.program_id(0), pl.num_programs(0) - 1
    frames = dq.shape[1]
    rest = None
    if len(refs) > 21:
        grads_rest, refs = refs[0], refs[1:]
        red, bufs, sems = refs[6], refs[22:26], refs[26:]
        half = (red.shape[0] + 1) // 2
        rest = Reduce((half, red.shape[0] - half), dict(zip(R_XY, sems)), grads_rest, bufs, red)
        refs = refs[:6] + refs[7:22]
    dx2_o, dy_o, gst_o, grads, gain_o, dk_o, wo, wp, acc_p, acc_o, dpad, gpad = refs[:12]
    dg_s, dk_s, stage, k_n, k_dpw, k_ys, k_dg, table, sem = refs[12:]

    @pl.when(step == 0)
    def _():
        ffn, mix = D // BS * (FF // BS), (D // BS) ** 2
        if rest is not None:
            greet([at(other, rest.level, rest.core) for other in (rest.xp, rest.yp, rest.dp)])
            greet([at(rest.place, rest.level, 1 - rest.core)])
        load_matrices(stack, ((0, wo), (2 * mix, wp)), sem)
        if rest is not None:
            met(4)
            for c in rest.all:
                rest.start(c)
        frame_decay(logs, table, False)
        acc_p[...] = jnp.zeros_like(acc_p)
        acc_o[...] = jnp.zeros_like(acc_o)
        gain_o[...] = jnp.zeros_like(gain_o)
        dk_s[...] = jnp.zeros_like(dk_s)

    fill_pad(dpad, dlow[0], dq[0], dhigh[0])
    fill_pad(gpad, glow[0], g[0], ghigh[0])
    chunk = frames // 5
    for c in range(D // LANES):
        lanes = slice(c * LANES, (c + 1) * LANES)
        for r in range(0, frames, chunk):
            here = dpad[c, pl.ds(r + PAD, chunk)]
            acc = small[5:6, lanes] * dpad[c, pl.ds(r + PAD + 7, chunk)]
            for j in range(1, KW):
                acc = acc + small[5 + j : 6 + j, lanes] * dpad[c, pl.ds(r - j + PAD + 7, chunk)]
            dg_s[pl.ds(r, chunk), lanes] = acc
            for j in range(KW):
                dk_s[j, :, lanes] += fold8(here * gpad[c, pl.ds(r + j + PAD - 7, chunk)])
    dg = dg_s[...]
    value = pw[0, :, :D].astype(f32)
    gate = sigmoid(pw[0, :, D:].astype(f32))
    dvalue = (dg * gate).astype(bf16)
    dgate = (dg * value * gate * (1.0 - gate)).astype(bf16)
    dpw = jnp.concatenate([dvalue, dgate], axis=1)
    hat2, inv2 = norm(x2[0])
    n2 = (hat2 * small[2:3]).astype(bf16)
    group = k_n.shape[0] // frames
    keep = pl.ds(pl.multiple_of(step % group * frames, frames), frames)
    k_n[keep] = n2
    k_dpw[keep] = dpw
    k_ys[keep] = ys[0]
    dn2 = mm_nt(dpw, wp[...])
    gain_o[...] += fold8(dn2 * hat2)
    dx2 = dx3[0] + norm_back(hat2, inv2, small[2:3], dn2)
    dx2_o[0] = dx2
    value = gated[0, :, :D].astype(f32)
    gate = sigmoid(gated[0, :, D:].astype(f32))
    dvalue = (dx2 * gate).astype(bf16)
    dgate = (dx2 * value * gate * (1.0 - gate)).astype(bf16)
    dgated = jnp.concatenate([dvalue, dgate], axis=1)
    k_dg[keep] = dgated
    dy = mm_nt(dgated, wo[...]).astype(bf16)
    dy_o[0] = dy
    local_states(table, dy, gst_o)

    if rest is not None:
        for c in rest.all:
            pl.when(step == 0)(lambda c=c: rest.begin(c))
            pl.when(step == last - 3 + 2 * c)(lambda c=c: rest.second(c))

    @pl.when(step % group == group - 1)
    def _():
        acc_p[...] += mm_tn(k_n[...], k_dpw[...])
        acc_o[...] += mm_tn(k_ys[...], k_dg[...])

    @pl.when(step == pl.num_programs(0) - 1)
    def _():
        ffn, mix = D // BS * (FF // BS), (D // BS) ** 2
        plan = ((acc_o, 0, False), (acc_p, 2 * mix, False))
        store_blocks(plan, scale, grads, stage, sem)
        if rest is not None:
            for c in rest.all:
                rest.combine(c)
                rest.square_end(c)
        for j in range(KW):
            dk_o[j : j + 1] = jnp.sum(dk_s[j], axis=0, keepdims=True)


def conv_back_kernel(
    u, dy, back_ends, logs, mix_one, mix_two,
    du_o, t1_o, t2_o, fp_o, gp_o, back_all,
    upad, dpad, acc_s, taps, own_sem, send, recv,
):
    step = pl.program_id(0)
    begin_swap, end_swap = swap_states(
        back_ends, back_all, step == 0, step == pl.num_programs(0) - 1, own_sem, send, recv
    )
    rows, frames = u.shape[0], u.shape[1]
    span = GROUP * SUB
    coup = join_lanes(mix_one) * join_lanes(mix_two)
    rates = channel_rates(logs)
    lag_taps(rates, coup, taps, True)
    coup_both = pack_params(coup, rows)
    heads = rate_rows(logs)
    u_both = pack_heads(u, rows)
    d_both = pack_heads(dy, rows)
    width = u_both[0].shape[1]
    du, first_sum, second_sum, end_u, end_d = [], [], [], [], []
    for h in range(2):
        into, into_w, out, out_w, power = chunk_tables(heads[h])
        scale = [jnp.broadcast_to(v, (NST, width)) for v in power]
        aged = [scale[i] * float(SUB * (i + 1)) for i in range(GROUP)]
        zero = jnp.zeros((NST, width), f32)
        carry, carry_w = zero, zero
        states, states_w = [], []
        for g in range(frames // span):
            here = u_both[h][g * span : (g + 1) * span]
            local = mm(into, here)
            local_w = mm(into_w, here)
            parts = [local[i * NST : (i + 1) * NST] for i in range(GROUP)]
            parts_w = [local_w[i * NST : (i + 1) * NST] for i in range(GROUP)]
            states.append([carry] + [parts[i] + scale[i] * carry for i in range(GROUP - 1)])
            states_w.append(
                [carry_w]
                + [parts_w[i] + scale[i] * carry_w + aged[i] * carry for i in range(GROUP - 1)]
            )
            carry_w = parts_w[-1] + scale[-1] * carry_w + aged[-1] * carry
            carry = parts[-1] + scale[-1] * carry
        end_u.append(carry_w)
        later, later_w = zero, zero
        one, two = zero, zero
        outs = []
        for g in reversed(range(frames // span)):
            here = d_both[h][g * span : (g + 1) * span]
            back = mm(out, here)
            back_w = mm(out_w, here)
            parts = [back[i * NST : (i + 1) * NST] for i in range(GROUP)]
            parts_w = [back_w[i * NST : (i + 1) * NST] for i in range(GROUP)]
            grads = jnp.concatenate([v * coup_both[h] for v in parts[1:] + [later]], axis=0)
            outs.append(mm_tn(into, grads.astype(bf16)))
            for i in range(GROUP):
                one = one + parts[i] * states[g][i]
                two = two + (parts_w[i] * states[g][i] + parts[i] * states_w[g][i])
            new, new_w = parts[0], parts_w[0]
            for i in range(GROUP - 1):
                new = new + scale[i] * parts[i + 1]
                new_w = new_w + (scale[i] * parts_w[i + 1] + aged[i] * parts[i + 1])
            later_w = new_w + scale[-1] * later_w + aged[-1] * later
            later = new + scale[-1] * later
        end_d.append(later_w)
        first_sum.append(one)
        second_sum.append(two)
        du.append(jnp.concatenate(outs[::-1], axis=0))
    first = lax.broadcasted_iota(jnp.int32, (NST, LANES), 1) < HALF
    for sums, out in ((first_sum, t1_o), (second_sum, t2_o)):
        both = []
        for v in sums:
            total = v[:, :LANES]
            for p in range(1, rows // 2):
                total = total + v[:, p * LANES : (p + 1) * LANES]
            both.append(total + pltpu.roll(total, HALF, 1))
        out[...] = jnp.where(first, both[0], both[1])
    for p in range(rows // 2):
        for pair, out in ((du, du_o), (end_u, fp_o), (end_d, gp_o)):
            one, two = unpack_pair(pair[0], pair[1], p)
            out[2 * p] = one
            out[2 * p + 1] = two
    chunk = frames // 5
    upad[0:SUB] = jnp.zeros((SUB, LANES), f32)
    dpad[pl.ds(frames, SUB)] = jnp.zeros((SUB, LANES), f32)
    acc_s[...] = jnp.zeros_like(acc_s)

    def one_row(i, carry):
        upad[pl.ds(SUB, frames)] = u[i].astype(f32)
        dpad[pl.ds(0, frames)] = dy[i].astype(f32)
        for r in range(0, frames, chunk):
            acc = du_o[i, pl.ds(r, chunk)].reshape(-1, SUB, LANES)
            here = dpad[pl.ds(r, chunk)]
            for d in range(SUB):
                piece = dpad[pl.ds(r + d, chunk)].reshape(-1, SUB, LANES)
                acc = acc + piece * taps[d][None]
                product = (here * upad[pl.ds(SUB + r - d, chunk)]).reshape(-1, SUB, LANES)
                acc_s[d] += jnp.sum(product, axis=0)
            du_o[i, pl.ds(r, chunk)] = acc.reshape(chunk, LANES)
        return carry

    lax.fori_loop(0, rows, one_row, 0)
    spot = lax.broadcasted_iota(jnp.int32, (SUB, LANES), 0)
    one, two = t1_o[...], t2_o[...]
    for d in range(SUB):
        kept = jnp.where(spot >= d, acc_s[d], 0.0)
        grad = jnp.exp(-rates * float(d)) * jnp.sum(kept, axis=0, keepdims=True)
        one = one + grad
        two = two + float(d) * grad
    t1_o[...] = one
    t2_o[...] = two
    begin_swap()
    end_swap()


def ffa_back_kernel(
    scale, du_loc, back_all, ends_all, back_ends, ends_w, back_w, starts, mix_one, mix_two, logs,
    t_one, t_two, gain_b, gain_c, kernel_grads,
    x1, feat, inner_r, act_r, dx2, small, stack, *refs
):
    step, last = pl.program_id(0), pl.num_programs(0) - 1
    pair = None
    if len(refs) > 23:
        grads_pair, red_in, refs = refs[0], refs[1], refs[2:]
        out_pair, out_rest = refs[3:5]
        red_rest, rest_bufs, red_pair, square_refs = refs[25], refs[26:28], refs[28], refs[29:33]
        pair_bufs, sems = refs[33:35], refs[35:]
        refs = refs[:3] + refs[5:25]
        pair = Reduce(
            out_pair.shape[:1], dict(zip(R_XY + R_Z, sems)), grads_pair, square_refs, red_pair,
            pair_bufs, out_pair,
        )
        rest = Reduce(
            out_rest.shape[:1], dict(zip(R_Z, sems[9:])), None, None, red_rest, rest_bufs, out_rest
        )
    dx0_o, grads, small_o, wi, wo, wu, acc_in, acc_out, acc_u = refs[:9]
    mask, stage, k_act, k_din, k_n, k_dp, k_m, k_du, sem = refs[9:18]
    gain_o, sums_o, table, weigh, coup = refs[18:]
    place, parts = lax.axis_index("tm"), ends_all.shape[0]

    @pl.when(step == 0)
    def _():
        ffn, mix = D // BS * (FF // BS), (D // BS) ** 2
        if pair is not None:
            greet([at(other, pair.level, pair.core) for other in (pair.xp, pair.yp, pair.dp)])
            greet([at(pair.place, other, pair.core) for other in (pair.near_by, pair.far_off)])
            greet([at(pair.place, pair.level, 1 - pair.core)])
            red_rest[...] = red_in[...]
        load_matrices(stack, ((0, wi), (ffn, wo), (2 * ffn, wu)), sem)
        if pair is not None:
            met(6)
            pair.start(0)
            rest.near(0).start()
        mask[...] = head_mask()
        frames = table.shape[0]
        frame_decay(logs, table, True)
        rates = channel_rates(logs)
        for i in range(parts):
            weigh[0, i], weigh[1, i] = passing(rates, place - 1 - i, frames)
            weigh[2, i], unused = passing(rates, i - place - 1, frames)
        coup[...] = join_lanes(mix_one) * join_lanes(mix_two)
        acc_in[...] = jnp.zeros_like(acc_in)
        acc_out[...] = jnp.zeros_like(acc_out)
        acc_u[...] = jnp.zeros_like(acc_u)
        gain_o[...] = jnp.zeros_like(gain_o)
        sums_o[...] = jnp.zeros_like(sums_o)

    frames = feat.shape[1]
    group = k_n.shape[0] // frames
    keep = pl.ds(pl.multiple_of(step % group * frames, frames), frames)
    came, came_w, later = 0.0, 0.0, 0.0
    for i in range(parts):
        end = ends_all[i, 0].astype(f32)
        came = came + weigh[0, i] * end
        came_w = came_w + weigh[1, i] * end
        later = later + weigh[2, i] * back_all[i, 0].astype(f32)
    mine = back_ends[0].astype(f32)
    start = join_lanes(starts)
    sums_o[0] += mine * came
    sums_o[1] += start * mine
    sums_o[2] += start * back_w[0]
    sums_o[3] += back_w[0] * came + mine * came_w + later * ends_w[0]
    du = (du_loc[0] + mm(table[...], spread_heads(coup[...] * later, mask[...]))).astype(bf16)
    hat1, inv1 = norm(x1[0])
    n1 = (hat1 * small[1:2]).astype(bf16)
    k_m[keep] = n1
    k_du[keep] = du
    dn1 = mm_nt(du, wu[...])
    gain_o[1] += fold8(dn1 * hat1)
    dx1 = dx2[0] + norm_back(hat1, inv1, small[1:2], dn1)
    dp = (0.5 * dx1).astype(bf16)
    dact = mm_nt(dp, wo[...])
    inner = inner_r[0].astype(f32)
    sig = sigmoid(inner)
    dinner = ((sig + inner * sig * (1.0 - sig)) * dact).astype(bf16)
    hat0, inv0 = norm(feat[0].astype(f32))
    n0 = (hat0 * small[0:1]).astype(bf16)
    k_act[keep] = act_r[0]
    k_din[keep] = dinner
    k_n[keep] = n0
    k_dp[keep] = dp
    dn0 = mm_nt(dinner, wi[...])
    gain_o[0] += fold8(dn0 * hat0)
    dx0_o[0] = dx1 + norm_back(hat0, inv0, small[0:1], dn0)

    if pair is not None:

        @pl.when(step == 0)
        def _():
            pair.begin(0)

        @pl.when(step == last - 4)
        def _():
            rest.across(0)

        @pl.when(step == last - 3)
        def _():
            pair.second(0)

        @pl.when(step == last - 2)
        def _():
            rest.settle(0)
            pair.combine(0)
            pair.near(0).start()

        @pl.when(step == last - 1)
        def _():
            pair.across(0)

    @pl.when(step % group == group - 1)
    def _():
        acc_out[...] += mm_tn(k_dp[...], k_act[...])
        acc_in[...] += mm_tn(k_n[...], k_din[...])
        acc_u[...] += mm_tn(k_m[...], k_du[...])

    @pl.when(step == pl.num_programs(0) - 1)
    def _():
        ffn, mix = D // BS * (FF // BS), (D // BS) ** 2
        one, two = join_lanes(mix_one), join_lanes(mix_two)
        begin = (place * frames).astype(f32)
        begin_w = jnp.exp(-channel_rates(logs) * begin)
        d_coup = t_one[...] + sums_o[0]
        start_back = sums_o[1] * begin_w
        d_rate = coup[...] * (t_two[...] + sums_o[3])
        d_rate = d_rate + two * (begin * start_back + begin_w * sums_o[2])
        total = lambda v: jnp.sum(v, axis=0, keepdims=True)
        gains = [total(gain_o[0]), total(gain_o[1]), total(gain_c[...])]
        gains += [total(gain_b[0]), total(gain_b[1]), kernel_grads[0:KW]]
        entries = gains + [d_coup * two, d_coup * one + start_back, d_rate]
        own = small_o.shape[2]
        small_o[...] = jnp.zeros_like(small_o)
        row = 0
        for entry in entries:
            count = entry.shape[0]
            if count == NST:
                row = -(-row // 8) * 8
            for p in range(parts):
                small_o[p, row : row + count] = entry[:, p * own : (p + 1) * own] * scale
            row += count
        plan = ((acc_in, 0, False), (acc_out, ffn, True), (acc_u, 2 * ffn, False))
        store_blocks(plan, scale, grads, stage, sem)
        if pair is not None:
            pair.settle(0)
            pair.square_end(0)
            pair.levels_end(0)
            rest.levels_end(0)


def shampoo_kernel(
    frames, source, owned, full, left, right, lroot, rroot, master, sums, small, logs, mix_terms,
    back_all, result, slope, nl_o, nr_o, nm_o, nc_o, own_o,
    small_o, new_small_o, decay_o, mix_o, new_decay_o, new_mix_o, state_o, result_o, slope_o,
):
    step = pl.program_id(0)
    result_o[...] = result[...]
    slope_o[...] = slope[...]

    @pl.when(step == 0)
    def _():
        place = lax.axis_index("tm")
        parts, rows, width = back_all.shape[0], back_all.shape[1], state_o.shape[2]
        columns = [as_column(jnp.exp(logs[j : j + 1])) for j in range(logs.shape[0])]
        over = [jnp.broadcast_to(column, (NST, HALF)) for column in columns]
        rates = jnp.concatenate(over, axis=1)
        decays = [jnp.exp(-rates * float(frames * i)) * mix_terms[1] for i in range(parts)]
        grads = []
        for r in range(rows):
            grad = 0.0
            for p in range(parts):
                total = 0.0
                for i in range(parts):
                    part = back_all[i, r, :, p * width : (p + 1) * width].astype(f32)
                    total = total + part * decays[i]
                grad = grad + jnp.where(place == p, total, 0.0)
            grads.append(grad)
        for r in range(rows):
            total = 0.0
            for i in range(rows):
                total = total + jnp.where(source[i] == r, grads[i], 0.0)
            state_o[r] = total

    @pl.when(step == 0)
    def _():
        count = small_o.shape[0]
        grad = sums[0:count]
        small_o[...] = grad
        width = small_o.shape[1]
        own_small = 0.0
        for p in range(small.shape[1] // width):
            part = small[:, p * width : (p + 1) * width]
            own_small = own_small + jnp.where(lax.axis_index("tm") == p, part, 0.0)
        new_small_o[...] = own_small - rate_small * grad
        row = -(-count // 8) * 8
        for i in range(2):
            grad = sums[row + i * NST : row + (i + 1) * NST]
            mix_o[i] = grad
            new_mix_o[i] = mix_terms[i] - rate_small * grad
        by_channel = sums[row + 2 * NST : row + 3 * NST].T
        for j in range(logs.shape[0]):
            here = jnp.sum(by_channel[j * HALF : (j + 1) * HALF], axis=0, keepdims=True)
            grad = -here * jnp.exp(logs[j : j + 1])
            decay_o[j : j + 1] = grad
            new_decay_o[j : j + 1] = logs[j : j + 1] - rate_small * grad

    slab = owned.shape[1]
    down = lax.broadcasted_iota(jnp.int32, (slab, BS), 0) + lax.axis_index("rows") * slab
    pick = (down == lax.broadcasted_iota(jnp.int32, (slab, BS), 1)).astype(f32).astype(bf16)
    for i in range(full.shape[0]):
        whole = full[i]
        mine = owned[i]
        own_o[i] = mine.astype(f32)
        nl_o[i] = 0.5 * left[i] + 0.5 * mm_nt(mine, whole)
        columns = mm_nt(pick, whole).astype(bf16)
        nr_o[i] = 0.5 * right[i] + 0.5 * mm(columns, whole)
        side = mm(lroot[i].astype(bf16), whole)
        step = mm(side.astype(bf16), rroot[i].astype(bf16))
        new = master[i] - rate_blocks * step
        nm_o[i] = new
        nc_o[i] = new.astype(bf16)


def deliveries(sizes, parts, count):
    edges = [sum(sizes[:c]) for c in range(len(sizes) + 1)]
    runs = []
    for which, ids in enumerate(block_sets()):
        for owner, k, v, j, n in move_runs(ids, parts, count):
            if which:
                runs.append((0, which, owner, k, v, j, n))
                continue
            for c, (a, b) in enumerate(zip(edges[:-1], edges[1:])):
                low, high = max(a, j), min(b, j + n)
                if low < high:
                    runs.append((c + 1, 0, owner, k + low - j, v, low, high - low))
    groups = []
    for chunk, unused, owner, k, v, j, n in sorted(runs, key=lambda run: (run[0], run[2], run[3])):
        if groups and groups[-1][:2] == (chunk, owner) and sum(groups[-1][2:]) == k:
            groups[-1] = (chunk, owner, groups[-1][2], groups[-1][3] + n)
        else:
            groups.append((chunk, owner, k, n))
    return runs, groups


def reduce_kernel(
    sizes, runs, groups, grads, share_pair, share_rest, small, full, owned_o, small_sum,
    mine, came, from_x, from_y, red, near_in, far_in, share_first, owned, s_tm, s_core, s_z,
    d_send, d_recv, a_send, a_recv, f_send, f_recv, s_send, s_recv, put_sem, *sems,
):
    it = Reduce(
        sizes, dict(zip(R_XY + R_Z, sems)), grads, (mine, came, from_x, from_y), red,
        (near_in, far_in), share_first,
    )
    place, level, core = it.place, it.level, it.core
    low, high, near, far = it.low, it.high, it.near_by, it.far_off
    diagonal = 2 * (1 - high) + 1 - low
    others = (it.xp, it.yp, it.dp)
    greet([at(other, level, core) for other in others])
    greet([at(place, other, core) for other in (near, far, diagonal)])
    greet([at(place, level, 1 - core)])
    shares = (share_first, share_pair, share_rest)

    def deliver(index):
        unused, which, owner, k, v, j, n = runs[index]
        src, dst = shares[which].at[pl.ds(j, n)], owned.at[pl.ds(k, n)]
        if owner == v:
            return pltpu.make_async_copy(src, dst, d_send.at[index])
        return remote(src, dst, d_send.at[index], d_recv.at[index], at(owner, level, core))

    def in_chunk(c):
        return [i for i, run in enumerate(runs) if run[0] == c]

    def send_out(c):
        for i in in_chunk(c):
            pl.when(place == runs[i][4])(lambda i=i: deliver(i).start())

    def come_in(c):
        for i in in_chunk(c):
            local = runs[i][2] == runs[i][4]
            done = (lambda i=i: deliver(i).wait()) if local else (lambda i=i: deliver(i).wait_recv())
            pl.when(place == runs[i][2])(done)

    def sent_out():
        for i, run in enumerate(runs):
            if run[2] != run[4]:
                pl.when(place == run[4])(lambda i=i: deliver(i).wait_send())

    def spot(g, where):
        unused, owner, k, n = groups[g]
        return full.at[pl.ds(k, n), where // 2, where % 2, core]

    def held(g):
        unused, owner, k, n = groups[g]
        return owned.at[pl.ds(k, n)]

    def put(g):
        return pltpu.make_async_copy(held(g), spot(g, level), put_sem.at[g])

    def along(g, i):
        src = spot(g, far) if i == 2 else held(g)
        dst = spot(g, far if i == 2 else level)
        target = at(place, far if i == 0 else near, core)
        return remote(src, dst, a_send.at[g, i], a_recv.at[g, i], target)

    def to_core(g, i):
        where = (level, far, near, diagonal)[i]
        src = held(g) if i == 0 else spot(g, where)
        target = at(place, level, 1 - core)
        return remote(src, spot(g, where), f_send.at[g, i], f_recv.at[g, i], target)

    def for_groups(c, act):
        for g, group in enumerate(groups):
            if c is None or group[0] == c:
                pl.when(place == group[1])(lambda g=g: act(g))

    def spread(g):
        put(g).start()
        along(g, 0).start()
        along(g, 1).start()
        to_core(g, 0).start()

    def pass_on(g):
        along(g, 0).wait_recv()
        along(g, 2).start()
        to_core(g, 1).start()
        along(g, 1).wait_recv()
        to_core(g, 2).start()

    def last(g):
        along(g, 2).wait_recv()
        to_core(g, 3).start()

    def finish(g):
        put(g).wait()
        for i in range(4):
            to_core(g, i).wait_recv()
        for i in range(4):
            to_core(g, i).wait_send()
        for i in range(3):
            along(g, i).wait_send()

    def to_place(d):
        send, recv = s_send.at[d], s_recv.at[d]
        return remote(small.at[others[d]], s_tm.at[d], send, recv, at(others[d], level, core))

    def to_sibling():
        target = at(place, level, 1 - core)
        return remote(s_core.at[0], s_core.at[1], s_send.at[3], s_recv.at[3], target)

    def to_level(d):
        target = at(place, (near, far, diagonal)[d], core)
        return remote(s_z.at[level], s_z.at[level], s_send.at[4 + d], s_recv.at[4 + d], target)

    def reduced(c):
        it.combine(c)
        it.near(c).start()

    def settled(c):
        it.settle(c)
        send_out(c + 1)

    def arrived(c):
        come_in(c + 1)
        for_groups(c + 1, spread)

    met(7)
    for c in it.all:
        it.start(c)
    send_out(0)
    for d in range(3):
        to_place(d).start()
    stages = (
        it.begin, it.second, reduced, it.across, settled, arrived,
        lambda c: for_groups(c + 1, pass_on), lambda c: for_groups(c + 1, last),
    )
    chunks = len(sizes)
    for tick in range(chunks + len(stages) - 1):
        for index, stage in enumerate(stages):
            if 0 <= tick - index < chunks:
                stage(tick - index)
        if tick == 0:
            come_in(0)
            for_groups(0, spread)
            for d in range(3):
                to_place(d).wait_recv()
            s_core[0] = small[place] + (s_tm[0] + s_tm[1]) + s_tm[2]
            to_sibling().start()
        if tick == 1:
            to_sibling().wait_recv()
            s_z[level] = s_core[0] + s_core[1]
            for d in range(3):
                to_level(d).start()
        if tick == 2:
            for_groups(0, pass_on)
        if tick == 3:
            for_groups(0, last)
    for d in range(3):
        to_level(d).wait_recv()
    small_sum[...] = (s_z[0] + s_z[1]) + (s_z[2] + s_z[3])
    owned_o[...] = owned[...]
    for_groups(None, finish)
    for c in it.all:
        it.square_end(c)
        it.levels_end(c)
    sent_out()
    for d in range(3):
        to_place(d).wait_send()
        to_level(d).wait_send()
    to_sibling().wait_send()


def reduce_grads(first, pair, rest, small, parts, devices, slab):
    levels = devices // 2
    ffn, mix = D // BS * (FF // BS), (D // BS) ** 2
    if parts != 4 or levels != 4:
        grads = [first[: 2 * ffn], rest[: 2 * ffn], first[2 * ffn :], pair, rest[2 * ffn :]]
        owned = jnp.concatenate(grads, axis=0)
        owned = lax.psum_scatter(owned, "tm", scatter_dimension=0, tiled=True)
        owned = lax.psum_scatter(owned, "rows", scatter_dimension=1, tiled=True)
        full = lax.all_gather(owned, "rows", axis=1, tiled=True)
        small = lax.psum_scatter(small, "tm", scatter_dimension=0, tiled=True)[0]
        return full, owned, lax.psum(small, "rows")
    sizes = (3, 3, 3)
    m, chunks = first.shape[1], len(sizes)
    count = sum(len(ids) for ids in block_sets()) // parts
    runs, groups = deliveries(sizes, parts, count)
    dma = lambda *dims: pltpu.SemaphoreType.DMA(dims)
    vb = lambda *dims: pltpu.VMEM(dims + (slab, BS), bf16)
    vmem = pl.BlockSpec(memory_space=pltpu.VMEM)
    part = small.shape[1:]
    full, owned, small_sum = pl.pallas_call(
        partial(reduce_kernel, sizes, runs, groups),
        in_specs=[ANY, vmem, vmem, vmem],
        out_specs=[ANY, vmem, vmem],
        out_shape=[
            shape((count, 2, 2, 2, slab, BS), bf16),
            shape((count, slab, BS), bf16),
            shape(part),
        ],
        scratch_shapes=square_bufs(m, parts, levels, slab)
        + [vb(m, 2, 2)]
        + level_bufs(m, slab)
        + [vb(m), vb(count), vm(3, *part), vm(2, *part), vm(levels, *part)]
        + [dma(len(runs)), dma(len(runs)), dma(len(groups), 3), dma(len(groups), 3)]
        + [dma(len(groups), 4), dma(len(groups), 4), dma(7), dma(7), dma(len(groups))]
        + reduce_sems(R_XY + R_Z, chunks),
        compiler_params=pltpu.CompilerParams(
            collective_id=2, has_side_effects=True, vmem_limit_bytes=VMEM_BYTES
        ),
        name="reduce_grads",
    )(first, pair, rest, small)
    return full.reshape(count, BS, BS), owned, small_sum


def row_spec(frames, width, per=1):
    return pl.BlockSpec((per, frames, width), lambda i: (i, 0, 0))


def whole_spec(*dims):
    return pl.BlockSpec(dims, lambda i: (0,) * len(dims))


def talking(number):
    return pltpu.CompilerParams(
        dimension_semantics=("arbitrary",),
        vmem_limit_bytes=VMEM_BYTES,
        collective_id=number,
        has_side_effects=True,
    )


def body(
    features,
    cotangent,
    state_bank,
    state_source,
    master,
    left_stats,
    right_stats,
    left_root,
    right_root,
    small_params,
    decay_logs,
    state_mix,
):
    rows, frames, width = features.shape
    tokens = rows * frames
    parts = lax.axis_size("tm")
    place = lax.axis_index("tm")
    scaling = 1.0 / math.sqrt(tokens * parts * lax.axis_size("rows"))
    ffn, mix = D // BS * (FF // BS), (D // BS) ** 2

    own_heads, own_channels = decay_logs.shape[0], state_mix.shape[1]
    mix_t = state_mix.transpose(0, 2, 1)
    bank_t = state_bank.transpose(0, 2, 1)
    devices = lax.axis_size("rows")
    levels = devices // 2
    spread_out = parts == 4
    if spread_out:
        first, pair, rest, packed = gather_first(
            master, bank_t, mix_t, decay_logs, state_source, parts, devices
        )
        first = first.reshape(-1, BS, BS)
        pair_out, rest_out = [shape(pair.shape, bf16)], [shape(rest.shape, bf16)]
        any_one, pair_in, rest_in = [ANY], [pair], [rest]
        pair_sems, rest_sems = gather_sems(XY_SEMS, levels), gather_sems(XY_SEMS, levels, 2)
    else:
        stack = lax.all_gather(master.astype(bf16), "rows", axis=1, tiled=True)
        stack = lax.all_gather(stack, "tm", axis=0, tiled=True)
        logs_own = jnp.pad(decay_logs, ((0, 8 - own_heads), (0, own_channels - NST)))
        params = [bank_t[state_source].reshape(-1, own_channels), mix_t.reshape(-1, own_channels)]
        packed = lax.all_gather(jnp.concatenate(params + [logs_own], axis=0), "tm", axis=0)
        first, pair, rest = (stack[jnp.array(ids)] for ids in block_sets())
        pair_out = rest_out = any_one = pair_in = rest_in = pair_sems = rest_sems = []

    mix_row = rows
    logs_row = (rows + 2) * NST // 8
    per_group = LANES // own_channels
    wide = lambda at_row: pl.BlockSpec((parts, NST, own_channels), lambda i: (0, at_row, 0))
    narrow = lambda at_row: pl.BlockSpec((per_group, NST, own_channels), lambda i: (i, at_row, 0))
    starts_spec = pl.BlockSpec((parts, NST, own_channels), lambda i: (0, i, 0))
    logs_spec = pl.BlockSpec((parts, 8, own_channels), lambda i: (0, logs_row, 0))
    logs_part = pl.BlockSpec((per_group, 8, own_channels), lambda i: (i, logs_row, 0))
    all_params = [wide(mix_row), wide(mix_row + 1), logs_spec]
    part_params = [logs_part, narrow(mix_row), narrow(mix_row + 1)]

    mat = lambda r, c: vm(r, c, dtype=bf16)
    dma = pltpu.SemaphoreType.DMA
    group = 3 if rows % 3 == 0 else 1
    small_spec = whole_spec(*small_params.shape)
    state_spec = pl.BlockSpec((1, NST, D), lambda i: (i, 0, 0))
    states_spec = pl.BlockSpec((parts, 1, NST, D), lambda i: (0, i, 0, 0))
    flat_spec = whole_spec(NST, D)
    x1, inner_a, act_a, u, ends, *done = pl.pallas_call(
        ffa_forward_kernel,
        grid=(rows // BOTH,),
        in_specs=[row_spec(frames, D, BOTH), small_spec, ANY, logs_spec]
        + any_one,
        out_specs=[
            row_spec(frames, D, BOTH),
            row_spec(frames, FF, BOTH),
            row_spec(frames, FF, BOTH),
            row_spec(frames, D, BOTH),
            pl.BlockSpec((BOTH, NST, D), lambda i: (i, 0, 0)),
        ]
        + any_one,
        out_shape=[
            shape((rows, frames, D)),
            shape((rows, frames, FF), bf16),
            shape((rows, frames, FF), bf16),
            shape((rows, frames, D), bf16),
            shape((rows, NST, D), bf16),
        ]
        + pair_out,
        scratch_shapes=[mat(D, FF), mat(FF, D), mat(D, D), mat(frames, HEADS * NST), dma] + pair_sems,
        input_output_aliases={4: 5} if spread_out else {},
        compiler_params=talking(7) if spread_out else PARAMS,
        name="ffa_forward",
    )(features, small_params, first, packed, *pair_in)
    if spread_out:
        pair = done[0].reshape(-1, BS, BS)

    group_spec = pl.BlockSpec((rows, frames, LANES), lambda i: (0, 0, i))
    coup_spec = pl.BlockSpec((NST, LANES), lambda i: (0, i))
    swap_scratch = [dma, dma((parts - 1,)), dma((parts - 1,))]
    all_states = shape((parts, rows, NST, D), bf16)
    y_loc, ends_all, *done = pl.pallas_call(
        conv_forward_kernel,
        grid=(D // LANES,),
        in_specs=[group_spec, ANY] + part_params
        + any_one,
        out_specs=[group_spec, ANY] + any_one,
        out_shape=[shape((rows, frames, D)), all_states] + rest_out,
        scratch_shapes=[vm(SUB + frames, LANES), vm(SUB, SUB, LANES)] + swap_scratch + rest_sems,
        input_output_aliases={5: 2} if spread_out else {},
        compiler_params=talking(3),
        name="conv_forward",
    )(u, ends, packed, packed, packed, *rest_in)

    edge_spec = pl.BlockSpec((1, PAD, D), lambda i: (i, 0, 0))
    edge_scratch = [
        vm(rows, 2, PAD, D, dtype=bf16),
        vm(PAD, D, dtype=bf16),
        dma((2, rows)),
        dma((2, rows)),
        dma((2,)),
    ]
    edge_shapes = [shape((rows, PAD, D), bf16)] * 2
    ys, gated, x2, pw, g, g_low, g_high, *done = pl.pallas_call(
        mixer_out_kernel,
        grid=(rows,),
        in_specs=[
            row_spec(frames, D),
            states_spec,
            starts_spec,
        ]
        + all_params
        + [row_spec(frames, D), small_spec, ANY]
        + any_one,
        out_specs=[
            row_spec(frames, D),
            row_spec(frames, 2 * D),
            row_spec(frames, D),
            row_spec(frames, 2 * D),
            row_spec(frames, D),
            ANY,
            ANY,
        ]
        + any_one,
        out_shape=[
            shape((rows, frames, D), bf16),
            shape((rows, frames, 2 * D), bf16),
            shape((rows, frames, D)),
            shape((rows, frames, 2 * D), bf16),
            shape((rows, frames, D), bf16),
        ]
        + edge_shapes
        + rest_out,
        scratch_shapes=[mat(D, 2 * D), mat(D, 2 * D), vm(HEADS * NST, D), dma]
        + [mat(frames, HEADS * NST), vm(parts + 1, NST, D), vm(NST, D)]
        + edge_scratch
        + rest_sems,
        input_output_aliases={9: 7} if spread_out else {},
        compiler_params=talking(4),
        name="mixer_out",
    )(y_loc, ends_all, packed, packed, packed, packed, x1, small_params, pair, *done)
    if spread_out:
        rest = done[0].reshape(-1, BS, BS)

    kept = lambda *widths: [mat(group * frames, w) for w in widths]
    slab = master.shape[1]
    spread_back = spread_out and levels == 4
    sizes = [len(ids) // parts for ids in block_sets()]
    if spread_back:
        grad_shapes = [shape((parts, n, levels, 2, slab, BS), bf16) for n in sizes]
        flat_shapes = [shape((parts * n, BS, BS), bf16) for n in sizes]
    else:
        flat_shapes = [shape((len(ids), BS, BS), bf16) for ids in block_sets()]
    unflat = lambda v, k: v.reshape(grad_shapes[k].shape) if spread_back else v
    layer_out, dx3, dq, grads_rest, gain_b, d_low, d_high = pl.pallas_call(
        partial(ffb_kernel, scaling),
        grid=(rows,),
        in_specs=[
            row_spec(frames, D),
            edge_spec,
            edge_spec,
            row_spec(frames, D),
            row_spec(frames, D),
            small_spec,
            ANY,
        ],
        out_specs=[
            row_spec(frames, D),
            row_spec(frames, D),
            row_spec(frames, D),
            ANY,
            whole_spec(2, 8, D),
            ANY,
            ANY,
        ],
        out_shape=[
            shape((rows, frames, D), bf16),
            shape((rows, frames, D)),
            shape((rows, frames, D), bf16),
            flat_shapes[2],
            shape((2, 8, D)),
        ]
        + edge_shapes,
        scratch_shapes=[
            mat(D, FF),
            mat(FF, D),
            mat(D, D),
            vm(D, FF),
            vm(D, FF),
            vm(D, D),
            vm(D // LANES, frames + 2 * PAD, LANES),
            vm(frames, D),
            vm(2 * ffn + mix, BS, BS, dtype=bf16),
        ]
        + kept(FF, FF, D, D, D, D)
        + [dma]
        + edge_scratch,
        compiler_params=talking(5),
        name="ffb",
    )(g, g_low, g_high, x2, cotangent, small_params, rest)

    dx2, dy, back_ends, grads_pair, gain_c, kernel_grads, *red_rest = pl.pallas_call(
        partial(mixer_back_kernel, scaling),
        grid=(rows,),
        in_specs=[
            row_spec(frames, D),
            edge_spec,
            edge_spec,
            row_spec(frames, D),
            edge_spec,
            edge_spec,
            row_spec(frames, 2 * D),
            row_spec(frames, D),
            row_spec(frames, 2 * D),
            row_spec(frames, D),
            row_spec(frames, D),
            small_spec,
            ANY,
            logs_spec,
        ]
        + [ANY] * spread_back,
        out_specs=[
            row_spec(frames, D),
            row_spec(frames, D),
            state_spec,
            ANY,
            whole_spec(8, D),
            whole_spec(16, D),
        ]
        + [whole_spec(sizes[2], 2, 2, slab, BS)] * spread_back,
        out_shape=[
            shape((rows, frames, D)),
            shape((rows, frames, D), bf16),
            shape((rows, NST, D), bf16),
            flat_shapes[1],
            shape((8, D)),
            shape((16, D)),
        ]
        + [shape((sizes[2], 2, 2, slab, BS), bf16)] * spread_back,
        scratch_shapes=[
            mat(D, 2 * D),
            mat(D, 2 * D),
            vm(D, 2 * D),
            vm(D, 2 * D),
            vm(D // LANES, frames + 2 * PAD, LANES),
            vm(D // LANES, frames + 2 * PAD, LANES),
            vm(frames, D),
            vm(KW, 8, D),
            vm(4 * mix, BS, BS, dtype=bf16),
        ]
        + kept(D, 2 * D, D, 2 * D)
        + [mat(frames, HEADS * NST), dma]
        + (square_bufs(sizes[2], parts, levels, slab) + reduce_sems(R_XY, 2)) * spread_back,
        compiler_params=talking(8) if spread_back else PARAMS,
        name="mixer_back",
    )(
        dq, d_low, d_high, g, g_low, g_high, pw, x2, gated, ys, dx3, small_params, pair,
        packed, *[unflat(grads_rest, 2)] * spread_back,
    )

    nst_spec = pl.BlockSpec((rows, NST, LANES), lambda i: (0, 0, i))
    du_loc, t_one, t_two, ends_w, back_w, back_all = pl.pallas_call(
        conv_back_kernel,
        grid=(D // LANES,),
        in_specs=[group_spec, group_spec, ANY] + part_params,
        out_specs=[
            group_spec,
            coup_spec,
            coup_spec,
            nst_spec,
            nst_spec,
            ANY,
        ],
        out_shape=[
            shape((rows, frames, D)),
            shape((NST, D)),
            shape((NST, D)),
            shape((rows, NST, D)),
            shape((rows, NST, D)),
            all_states,
        ],
        scratch_shapes=[
            vm(SUB + frames, LANES),
            vm(SUB + frames, LANES),
            vm(SUB, SUB, LANES),
            vm(SUB, SUB, LANES),
        ]
        + swap_scratch,
        compiler_params=talking(6),
        name="conv_back",
    )(u, dy, back_ends, packed, packed, packed)

    small_rows = -(-small_params.shape[0] // 8) * 8 + 3 * NST
    grad_zero, grads_first, small_all, *shares = pl.pallas_call(
        partial(ffa_back_kernel, scaling),
        grid=(rows,),
        in_specs=[
            row_spec(frames, D),
            states_spec,
            states_spec,
            state_spec,
            state_spec,
            state_spec,
            starts_spec,
        ]
        + all_params
        + [
            flat_spec,
            flat_spec,
            whole_spec(2, 8, D),
            whole_spec(8, D),
            whole_spec(16, D),
            row_spec(frames, D),
            row_spec(frames, D),
            row_spec(frames, FF),
            row_spec(frames, FF),
            row_spec(frames, D),
            small_spec,
            ANY,
        ]
        + [ANY, whole_spec(sizes[2], 2, 2, slab, BS)] * spread_back,
        out_specs=[row_spec(frames, D), ANY, whole_spec(parts, small_rows, own_channels)]
        + [whole_spec(n, slab, BS) for n in sizes[1:]] * spread_back,
        out_shape=[
            shape((rows, frames, D)),
            flat_shapes[0],
            shape((parts, small_rows, own_channels)),
        ]
        + [shape((n, slab, BS), bf16) for n in sizes[1:]] * spread_back,
        scratch_shapes=[
            mat(D, FF),
            mat(FF, D),
            mat(D, D),
            vm(D, FF),
            vm(D, FF),
            vm(D, D),
            vm(HEADS * NST, D),
            vm(2 * ffn + mix, BS, BS, dtype=bf16),
        ]
        + kept(FF, FF, D, D, D, D)
        + [dma, vm(2, 8, D), vm(4, NST, D), mat(frames, HEADS * NST)]
        + [vm(3, parts, NST, D), vm(NST, D)]
        + (
            [vm(sizes[2], 2, 2, slab, BS, dtype=bf16)]
            + level_bufs(sizes[2], slab)
            + [vm(sizes[1], 2, 2, slab, BS, dtype=bf16)]
            + square_bufs(sizes[1], parts, levels, slab)
            + level_bufs(sizes[1], slab)
            + reduce_sems(R_XY + R_Z + R_Z)
        )
        * spread_back,
        compiler_params=talking(9) if spread_back else PARAMS,
        name="ffa_back",
    )(
        du_loc, back_all, ends_all, back_ends, ends_w, back_w, packed, packed, packed, packed,
        t_one, t_two, gain_b, gain_c, kernel_grads,
        x1, features, inner_a, act_a, dx2, small_params, first,
        *([unflat(grads_pair, 1)] + red_rest) * spread_back,
    )

    full_grad, owned, sums = reduce_grads(
        unflat(grads_first, 0),
        *(shares if spread_back else (grads_pair, grads_rest)),
        small_all,
        parts,
        devices,
        slab,
    )
    count, slice_rows = owned.shape[0], owned.shape[1]
    group = 11 if count % 11 == 0 else 1
    part_spec = pl.BlockSpec((group, slice_rows, BS), lambda i: (i, 0, 0))
    full_spec = pl.BlockSpec((group, BS, BS), lambda i: (i, 0, 0))
    small_shape = (small_params.shape[0], own_channels)
    carry_spec = row_spec(frames, D, rows * group // count)
    small_outs = [small_shape, small_shape, decay_logs.shape, mix_t.shape]
    small_outs += [decay_logs.shape, mix_t.shape, bank_t.shape]
    new_left, new_right, new_master, new_copy, grad_blocks, *others = pl.pallas_call(
        partial(shampoo_kernel, frames),
        grid=(count // group,),
        in_specs=[
            pl.BlockSpec(memory_space=pltpu.SMEM),
            part_spec,
            full_spec,
            part_spec,
            part_spec,
            part_spec,
            full_spec,
            part_spec,
            whole_spec(*sums.shape),
            whole_spec(*small_params.shape),
            whole_spec(*decay_logs.shape),
            whole_spec(*mix_t.shape),
            whole_spec(*back_all.shape),
            carry_spec,
            carry_spec,
        ],
        out_specs=[part_spec] * 5 + [whole_spec(*dims) for dims in small_outs]
        + [carry_spec] * 2,
        out_shape=[
            shape(owned.shape),
            shape(owned.shape),
            shape(owned.shape),
            shape(owned.shape, bf16),
            shape(owned.shape),
        ]
        + [shape(dims) for dims in small_outs]
        + [shape(layer_out.shape, bf16), shape(grad_zero.shape)],
        compiler_params=PARAMS,
        name="shampoo",
    )(
        state_source, owned, full_grad, left_stats, right_stats, left_root, right_root, master,
        sums, small_params, decay_logs, mix_t, back_all, layer_out, grad_zero,
    )
    *small_results, grad_state, layer_out, grad_zero = others
    for i in (3, 5):
        small_results[i] = small_results[i].transpose(0, 2, 1)
    grad_state = grad_state.transpose(0, 2, 1)
    return (
        layer_out,
        grad_zero,
        grad_state,
        grad_blocks,
        new_left,
        new_right,
        new_master,
        new_copy,
        *small_results,
    )


def solution(mesh):
    return jax.shard_map(
        body,
        mesh=mesh,
        in_specs=(
            P("rows", "tm", None),
            P("rows", "tm", None),
            P("rows", "tm", None),
            P("rows"),
            P("tm", "rows", None),
            P("tm", "rows", None),
            P("tm", "rows", None),
            P("tm", "rows", None),
            P("tm", None, None),
            P(),
            P("tm", None),
            P(None, "tm", None),
        ),
        out_specs=(
            P("rows", "tm", None),
            P("rows", "tm", None),
            P("rows", "tm", None),
            P("tm", "rows", None),
            P("tm", "rows", None),
            P("tm", "rows", None),
            P("tm", "rows", None),
            P("tm", "rows", None),
            P(None, "tm"),
            P(None, "tm"),
            P("tm", None),
            P(None, "tm", None),
            P("tm", None),
            P(None, "tm", None),
        ),
        check_vma=False,
    )
```

```python
from functools import partial
import math

import jax
import jax.numpy as jnp
from jax import lax
from jax.experimental import pallas as pl
from jax.experimental.pallas import tpu as pltpu
from jax.sharding import PartitionSpec as P

D = 512
FF = 2048
NST = 32
KW = 15
BS = 256
HEADS = 8
HALF = 64
LANES = 128
SUB = 16
GROUP = 5
BOTH = 2
PAD = 8
VMEM_BYTES = 60 * 1024 * 1024

rate_blocks = 0.1
rate_small = 0.5
bf16 = jnp.bfloat16
f32 = jnp.float32


def shape(dims, dtype=f32):
    return jax.ShapeDtypeStruct(dims, dtype)


def mm(a, b):
    return jnp.dot(a, b, preferred_element_type=f32)


def mm_nt(a, b):
    return lax.dot_general(a, b, (((1,), (1,)), ((), ())), preferred_element_type=f32)


def mm_tn(a, b):
    return lax.dot_general(a, b, (((0,), (0,)), ((), ())), preferred_element_type=f32)


def sigmoid(v):
    return 0.5 * jnp.tanh(0.5 * v) + 0.5


def norm(v):
    center = v - jnp.mean(v, axis=-1, keepdims=True)
    spread = jnp.mean(center * center, axis=-1, keepdims=True)
    inv = lax.rsqrt(spread + 1e-05)
    return center * inv, inv


def norm_back(hat, inv, scale, incoming):
    scaled = incoming * scale
    mean_one = jnp.mean(scaled, axis=-1, keepdims=True)
    mean_two = jnp.mean(scaled * hat, axis=-1, keepdims=True)
    return inv * (scaled - mean_one - hat * mean_two)


def flat(ref):
    v = ref[...]
    return v.reshape(-1, v.shape[-1])


def put_rows(ref, v):
    ref[...] = v.astype(ref.dtype).reshape(ref.shape)


def fold8(v):
    return jnp.sum(v.reshape(-1, 8, v.shape[-1]), axis=0)


class Matrices:
    def __init__(self, stack, plan, sem):
        self.copies = []
        for index, (first, dst) in enumerate(plan):
            across = dst.shape[1] // BS
            spots = [(i, j) for i in range(dst.shape[0] // BS) for j in range(across)]
            self.copies.append(
                [
                    pltpu.make_async_copy(
                        stack.at[first + i * across + j],
                        dst.at[pl.ds(i * BS, BS), pl.ds(j * BS, BS)],
                        sem.at[index],
                    )
                    for i, j in spots
                ]
            )

    def start(self):
        for copies in self.copies:
            for copy in copies:
                copy.start()

    def wait(self, index):
        for copy in self.copies[index]:
            copy.wait()


def store_blocks(plan, scaling, grads, stage, sem):
    copies = []
    for acc, first, transposed in plan:
        rows, cols = acc.shape
        down, across = (cols, rows) if transposed else (rows, cols)
        for i in range(down // BS):
            for j in range(across // BS):
                slot = len(copies)
                if transposed:
                    part = (acc[pl.ds(j * BS, BS), pl.ds(i * BS, BS)] * scaling).T
                else:
                    part = acc[pl.ds(i * BS, BS), pl.ds(j * BS, BS)] * scaling
                stage[slot] = part.astype(bf16)
                copy = pltpu.make_async_copy(
                    stage.at[slot], grads.at[first + i * (across // BS) + j], sem
                )
                copy.start()
                copies.append(copy)
    for copy in copies:
        copy.wait()


def head_mask():
    row = lax.broadcasted_iota(jnp.int32, (HEADS * NST, D), 0) // NST
    col = lax.broadcasted_iota(jnp.int32, (HEADS * NST, D), 1) // HALF
    return (row == col).astype(f32)


def spread_heads(v, mask):
    return (jnp.concatenate([v] * HEADS, axis=0) * mask).astype(bf16)


def join_lanes(ref):
    return jnp.concatenate([ref[i] for i in range(ref.shape[0])], axis=1)


def rate_rows(logs):
    own = logs.shape[2] // HALF
    places = range(logs.shape[0])
    return [jnp.exp(logs[p, j : j + 1, 0:NST]) for p in places for j in range(own)]


def as_column(row):
    down = lax.broadcasted_iota(jnp.int32, (NST, NST), 0)
    across = lax.broadcasted_iota(jnp.int32, (NST, NST), 1)
    return jnp.sum(jnp.where(down == across, row, 0.0), axis=1, keepdims=True)


def channel_rates(logs):
    first = lax.broadcasted_iota(jnp.int32, (NST, LANES), 1) < HALF
    columns = [as_column(row) for row in rate_rows(logs)]
    pairs = zip(columns[0::2], columns[1::2])
    return jnp.concatenate([jnp.where(first, a, b) for a, b in pairs], axis=1)


def frame_decay(logs, table, to_end):
    frames = table.shape[0]
    rates = jnp.concatenate(rate_rows(logs), axis=1)
    time = lax.broadcasted_iota(jnp.int32, table.shape, 0)
    length = frames - 1 - time if to_end else time + 1
    table[...] = jnp.exp(-rates * length.astype(f32)).astype(bf16)


def passing(rates, apart, frames):
    length = (apart * frames).astype(f32)
    weight = jnp.where(apart >= 0, jnp.exp(-rates * jnp.maximum(length, 0.0)), 0.0)
    return weight, weight * length


def local_states(table, v, out):
    frames = table.shape[0]
    first = lax.broadcasted_iota(jnp.int32, (NST, LANES), 1) < HALF
    for b in range(out.shape[0]):
        for q in range(D // (2 * LANES)):
            here = v[b * frames : (b + 1) * frames, 2 * q * LANES : 2 * (q + 1) * LANES]
            four = mm_tn(table[:, q * LANES : (q + 1) * LANES], here)
            for i in range(2):
                both = four[2 * i * NST : 2 * (i + 1) * NST, i * LANES : (i + 1) * LANES]
                picked = jnp.where(first, both[:NST], both[NST:])
                out[b, :, pl.ds((2 * q + i) * LANES, LANES)] = picked.astype(out.dtype)


def chunk_tables(row):
    column = as_column(row)
    span = GROUP * SUB
    time = lax.broadcasted_iota(jnp.int32, (NST, span), 1)
    since = (time % SUB + 1).astype(f32)
    into, into_w, out, out_w, power = [], [], [], [], []
    for i in range(GROUP):
        age = SUB * (i + 1) - 1 - time
        age_f = jnp.maximum(age, 0).astype(f32)
        value = jnp.where(age >= 0, jnp.exp(-column * age_f), 0.0)
        into.append(value)
        into_w.append(value * age_f)
        value = jnp.where(time // SUB == i, jnp.exp(-column * since), 0.0)
        out.append(value)
        out_w.append(value * since)
        power.append(jnp.exp(-column * float(SUB * (i + 1))))
    join = lambda parts: jnp.concatenate(parts, axis=0).astype(bf16)
    return join(into), join(into_w), join(out), join(out_w), power


def lag_taps(rates, coup, taps, backward):
    place = lax.broadcasted_iota(jnp.int32, (SUB, LANES), 0)
    for d in range(SUB):
        lag = jnp.sum(coup * jnp.exp(-rates * float(d)), axis=0, keepdims=True)
        inside = place + d < SUB if backward else place >= d
        taps[d] = jnp.where(inside, lag, 0.0)


ANY = pl.BlockSpec(memory_space=pl.ANY)
PARAMS = pltpu.CompilerParams(
    dimension_semantics=("arbitrary",), vmem_limit_bytes=VMEM_BYTES
)


def vm(*dims, dtype=f32):
    return pltpu.VMEM(dims, dtype)


def peers():
    place, row = lax.axis_index("tm"), lax.axis_index("rows")
    return place, row // 2, row % 2


def square(place):
    x, y = place % 2, place // 2
    return 2 * y + 1 - x, 2 * (1 - y) + x, 2 * (1 - y) + 1 - x


def at(place, level, core):
    return {"tm": place, "rows": level * 2 + core}


def remote(src, dst, send, recv, device):
    return pltpu.make_async_remote_copy(
        src_ref=src,
        dst_ref=dst,
        send_sem=send,
        recv_sem=recv,
        device_id=device,
        device_id_type=pl.DeviceIdType.MESH,
    )


def signal(sem, device):
    pl.semaphore_signal(sem, inc=1, device_id=device, device_id_type=pl.DeviceIdType.MESH)


def chunk_ranges(count, chunks):
    edges = [count * c // chunks for c in range(chunks + 1)]
    out = []
    for first, end in zip(edges[:-1], edges[1:]):
        middle = (first + end + 1) // 2
        out.append((first, end, middle))
    return out


class Gather:
    def __init__(self, piece, stack, sems, chunks=1):
        self.piece, self.stack, self.sems = piece, stack, sems
        self.place, self.level, self.core = peers()
        self.xp, self.yp, self.dp = square(self.place)
        self.levels = stack.shape[2]
        self.ranges = chunk_ranges(stack.shape[1], chunks)
        self.all = range(chunks)

    def own(self, c):
        first, end, unused = self.ranges[c]
        n = pl.ds(first, end - first)
        spot = self.stack.at[self.place, n, self.level, self.core]
        return pltpu.make_async_copy(self.piece.at[n], spot, self.sems["own"].at[c])

    def z(self, c, d):
        first, end, unused = self.ranges[c]
        n = pl.ds(first, end - first)
        spot = self.stack.at[self.place, n, self.level, self.core]
        send, recv = self.sems["zs"].at[c, d - 1], self.sems["zr"].at[c, d - 1]
        target = (self.level + d) % self.levels
        return remote(self.piece.at[n], spot, send, recv, at(self.place, target, self.core))

    def z_start(self, c):
        self.own(c).start()
        for d in range(1, self.levels):
            self.z(c, d).start()

    def z_arrive(self, c):
        self.own(c).wait()
        for d in range(1, self.levels):
            self.z(c, d).wait_recv()

    def z_end(self, c):
        for d in range(1, self.levels):
            self.z(c, d).wait_send()

    def part(self, name, c, i, owner, first, end, device):
        spot = self.stack.at[owner, pl.ds(first, end - first), :, self.core]
        send, recv = self.sems[name + "s"].at[c, i], self.sems[name + "r"].at[c, i]
        return remote(spot, spot, send, recv, device)

    def x(self, c, i):
        first, end, mid = self.ranges[c]
        what = ((self.place, first, mid), (self.place, mid, end), (self.yp, mid, end))[i]
        return self.part("x", c, i, *what, at(self.xp, self.level, self.core))

    def y(self, c, i):
        first, end, mid = self.ranges[c]
        what = ((self.place, mid, end), (self.place, first, mid), (self.xp, first, mid))[i]
        return self.part("y", c, i, *what, at(self.yp, self.level, self.core))

    def other(self, c, i):
        first, end, mid = self.ranges[c]
        what = (
            (self.place, first, end),
            (self.xp, first, mid),
            (self.yp, mid, end),
            (self.xp, mid, end),
            (self.yp, first, mid),
            (self.dp, first, mid),
            (self.dp, mid, end),
        )[i]
        return self.part("c", c, i, *what, at(self.place, self.level, 1 - self.core))

    def spread(self, c):
        for copy in (self.x(c, 0), self.y(c, 0), self.x(c, 1), self.y(c, 1), self.other(c, 0)):
            copy.start()

    def forward(self, c):
        self.x(c, 0).wait_recv()
        self.y(c, 2).start()
        self.y(c, 0).wait_recv()
        self.x(c, 2).start()
        self.other(c, 1).start()
        self.other(c, 2).start()
        self.x(c, 1).wait_recv()
        self.other(c, 3).start()
        self.y(c, 1).wait_recv()
        self.other(c, 4).start()

    def finish(self, c):
        self.y(c, 2).wait_recv()
        self.other(c, 5).start()
        self.x(c, 2).wait_recv()
        self.other(c, 6).start()

    def end(self, c):
        for i in range(7):
            self.other(c, i).wait_recv()
        for i in range(7):
            self.other(c, i).wait_send()
        for i in range(3):
            self.x(c, i).wait_send()
            self.y(c, i).wait_send()


Z_SEMS = ("own", "zs", "zr")
XY_SEMS = ("xs", "xr", "ys", "yr", "cs", "cr")


def gather_sems(names, levels, chunks=1):
    width = {"own": (), "z": (levels - 1,), "x": (3,), "y": (3,), "c": (7,)}
    key = lambda name: name if name == "own" else name[0]
    return [pltpu.SemaphoreType.DMA((chunks,) + width[key(name)]) for name in names]


def block_sets():
    ffn, mix = D // BS * (FF // BS), (D // BS) ** 2
    ids = lambda *ranges: [b for first, end in ranges for b in range(first, end)]
    return (
        ids((0, 2 * ffn), (4 * ffn, 4 * ffn + mix)),
        ids((4 * ffn + mix, 4 * ffn + 5 * mix)),
        ids((2 * ffn, 4 * ffn), (4 * ffn + 5 * mix, 4 * ffn + 6 * mix)),
    )


def move_runs(ids, places, count):
    runs, each = [], len(ids) // places
    for index, b in enumerate(ids):
        owner, k, v, j = b // count, b % count, index // each, index % each
        if runs:
            o0, k0, v0, j0, n0 = runs[-1]
            if (o0, v0) == (owner, v) and k0 + n0 == k:
                runs[-1] = (o0, k0, v0, j0, n0 + 1)
                continue
        runs.append((owner, k, v, j, 1))
    return runs


def greet(devices):
    barrier = pltpu.get_barrier_semaphore()
    for device in devices:
        signal(barrier, device)


def met(count):
    pl.semaphore_wait(pltpu.get_barrier_semaphore(), count)


def gather_kernel(
    source, master, bank, mix_terms, logs, first, pair, rest, pack_all,
    pack, rounded, piece, piece_pair, piece_rest, run_send, run_recv, pk_send, pk_recv, *sems,
):
    place, level, core = peers()
    others = square(place)
    levels = first.shape[2]
    greet([at(other, level, core) for other in others] + [at(place, level, 1 - core)])
    greet([at(place, (level + d) % levels, core) for d in range(1, levels)])
    rounded[...] = master[...].astype(bf16)
    count = bank.shape[0]
    for i in range(count):
        pack[i * NST : (i + 1) * NST] = bank[source[i]]
    for i in range(2):
        pack[(count + i) * NST : (count + i + 1) * NST] = mix_terms[i]
    pack[(count + 2) * NST :] = jnp.zeros((8, pack.shape[1]), f32)
    pack[(count + 2) * NST : (count + 2) * NST + logs.shape[0], 0:NST] = logs[...]
    met(3 + levels)
    moves = []
    for ids, target in zip(block_sets(), (piece, piece_pair, piece_rest)):
        for run in move_runs(ids, first.shape[0], master.shape[0]):
            moves.append((len(moves), target) + run)

    def move(index, target, owner, k, v, j, n):
        src, dst = rounded.at[pl.ds(k, n)], target.at[pl.ds(j, n)]
        if owner == v:
            return pltpu.make_async_copy(src, dst, run_send.at[index])
        return remote(src, dst, run_send.at[index], run_recv.at[index], at(v, level, core))

    def arrive(entry):
        index, target, owner, k, v, j, n = entry
        if owner == v:
            pl.when(place == v)(lambda: move(*entry).wait())
        else:
            pl.when(place == v)(lambda: move(*entry).wait_recv())

    for entry in moves:
        pl.when(place == entry[2])(lambda entry=entry: move(*entry).start())
    own_pack = pltpu.make_async_copy(pack, pack_all.at[place], pk_send.at[3])
    own_pack.start()
    packs = [
        remote(pack, pack_all.at[place], pk_send.at[d], pk_recv.at[d], at(other, level, core))
        for d, other in enumerate(others)
    ]
    for copy in packs:
        copy.start()
    for entry in moves:
        if entry[1] is piece:
            arrive(entry)
    names = Z_SEMS + XY_SEMS
    chunks = sems[0].shape[0]
    it = Gather(piece, first, dict(zip(names, sems)), chunks)
    later, sems = [], sems[len(names) :]
    for i, (what, stack) in enumerate(((piece_pair, pair), (piece_rest, rest))):
        later.append(Gather(what, stack, dict(zip(Z_SEMS, sems[3 * i : 3 * i + 3]))))
    it.z_start(0)
    for c in it.all:
        it.z_arrive(c)
        it.spread(c)
        if c == 0:
            for ahead in range(1, chunks):
                it.z_start(ahead)
            for entry in moves:
                if entry[1] is not piece:
                    arrive(entry)
        if c == chunks - 1:
            for other_set in later:
                other_set.z_start(0)
        if c >= 1:
            it.forward(c - 1)
        if c >= 2:
            it.finish(c - 2)
    it.forward(chunks - 1)
    for c in range(max(chunks - 2, 0), chunks):
        it.finish(c)
    for c in it.all:
        it.end(c)
        it.z_end(c)
    for other_set in later:
        other_set.z_arrive(0)
        other_set.z_end(0)
    for entry in moves:
        if entry[2] != entry[4]:
            pl.when(place == entry[2])(lambda entry=entry: move(*entry).wait_send())
    own_pack.wait()
    for copy in packs:
        copy.wait()


def gather_first(master, bank, mix_terms, logs, source, parts, devices, chunks=3):
    count, slab, cols = master.shape
    levels = devices // 2
    each = [len(ids) // parts for ids in block_sets()]
    runs = sum(len(move_runs(ids, parts, count)) for ids in block_sets())
    dma = lambda *dims: pltpu.SemaphoreType.DMA(dims)
    pack = ((bank.shape[0] + 2) * NST + 8, bank.shape[2])
    return pl.pallas_call(
        gather_kernel,
        in_specs=[pl.BlockSpec(memory_space=pltpu.SMEM)]
        + [pl.BlockSpec(memory_space=pltpu.VMEM)] * 4,
        out_specs=[ANY] * 4,
        out_shape=[
            shape((parts, each[0], levels, 2, slab, cols), bf16),
            shape((parts, each[1], levels, 2, slab, cols), bf16),
            shape((parts, each[2], levels, 2, slab, cols), bf16),
            shape((parts,) + pack),
        ],
        scratch_shapes=[
            vm(*pack),
            vm(count, slab, cols, dtype=bf16),
            vm(each[0], slab, cols, dtype=bf16),
            vm(each[1], slab, cols, dtype=bf16),
            vm(each[2], slab, cols, dtype=bf16),
            dma(runs),
            dma(runs),
            dma(4),
            dma(3),
        ]
        + gather_sems(Z_SEMS + XY_SEMS, levels, chunks)
        + gather_sems(Z_SEMS, levels) * 2,
        compiler_params=pltpu.CompilerParams(
            collective_id=1, has_side_effects=True, vmem_limit_bytes=VMEM_BYTES
        ),
        name="gather_first",
    )(source, master, bank, mix_terms, logs)


R_XY = ("load", "cs", "cr", "xs", "xr", "ys", "yr")
R_Z = ("zs", "zr")


def reduce_sems(names, chunks=1):
    width = {"x": (3,), "y": (3,), "z": (2,)}
    dims = lambda name: width.get(name[0], ())
    return [pltpu.SemaphoreType.DMA((chunks,) + dims(name)) for name in names]


def square_bufs(m, parts, levels, slab):
    vb = lambda *dims: pltpu.VMEM(dims + (slab, BS), bf16)
    return [vb(parts, m, levels)] * 2 + [vb(2, m, levels)] * 2


def level_bufs(m, slab):
    vb = lambda *dims: pltpu.VMEM(dims + (slab, BS), bf16)
    return [vb(m, 2), vb(m)]


class Reduce:
    def __init__(self, sizes, sems, grads=None, square_refs=None, red=None, level_refs=None, out=None):
        self.sems, self.grads, self.red, self.out = sems, grads, red, out
        if square_refs is not None:
            self.mine, self.came, self.from_x, self.from_y = square_refs
        if level_refs is not None:
            self.near_in, self.far_in = level_refs
        self.place, self.level, self.core = peers()
        self.xp, self.yp, self.dp = square(self.place)
        self.low, self.high = self.level % 2, self.level // 2
        self.near_by = self.level + 1 - 2 * self.low
        self.far_off = self.level + 2 - 4 * self.high
        edges = [sum(sizes[:c]) for c in range(len(sizes) + 1)]
        self.ranges = [(a, b, (a + b + 1) // 2) for a, b in zip(edges[:-1], edges[1:])]
        self.all = range(len(sizes))

    def n(self, c):
        first, end, unused = self.ranges[c]
        return pl.ds(first, end - first)

    def load(self, c):
        src = self.grads.at[:, self.n(c), :, self.core]
        return pltpu.make_async_copy(src, self.mine.at[:, self.n(c)], self.sems["load"].at[c])

    def swap(self, c):
        return remote(
            self.grads.at[:, self.n(c), :, 1 - self.core],
            self.came.at[:, self.n(c)],
            self.sems["cs"].at[c],
            self.sems["cr"].at[c],
            at(self.place, self.level, 1 - self.core),
        )

    def side(self, c, i, name, into, device, what):
        owner, slot, first, end = what
        n = pl.ds(first, end - first)
        send, recv = self.sems[name + "s"].at[c, i], self.sems[name + "r"].at[c, i]
        return remote(self.mine.at[owner, n], into.at[slot, n], send, recv, device)

    def x(self, c, i):
        first, end, mid = self.ranges[c]
        what = ((self.dp, 0, first, mid), (self.xp, 1, first, mid), (self.xp, 1, mid, end))[i]
        return self.side(c, i, "x", self.from_x, at(self.xp, self.level, self.core), what)

    def y(self, c, i):
        first, end, mid = self.ranges[c]
        what = ((self.dp, 0, mid, end), (self.yp, 1, mid, end), (self.yp, 1, first, mid))[i]
        return self.side(c, i, "y", self.from_y, at(self.yp, self.level, self.core), what)

    def add(self, owner, first, end, ref, slot):
        def one(k, carry):
            self.mine[owner, k] = self.mine[owner, k] + ref[slot, k]
            return carry

        lax.fori_loop(first, end, one, 0)

    def start(self, c):
        self.load(c).start()
        self.swap(c).start()

    def begin(self, c):
        first, end, unused = self.ranges[c]
        self.load(c).wait()
        self.swap(c).wait_recv()
        self.add(self.dp, first, end, self.came, self.dp)
        self.x(c, 0).start()
        self.y(c, 0).start()
        self.add(self.xp, first, end, self.came, self.xp)
        self.x(c, 1).start()
        self.add(self.yp, first, end, self.came, self.yp)
        self.y(c, 1).start()
        self.add(self.place, first, end, self.came, self.place)

    def second(self, c):
        first, end, mid = self.ranges[c]
        self.x(c, 0).wait_recv()
        self.add(self.yp, first, mid, self.from_x, 0)
        self.y(c, 2).start()
        self.y(c, 0).wait_recv()
        self.add(self.xp, mid, end, self.from_y, 0)
        self.x(c, 2).start()

    def combine(self, c):
        first, end, unused = self.ranges[c]
        for i in (1, 2):
            self.x(c, i).wait_recv()
            self.y(c, i).wait_recv()

        def one(k, carry):
            total = self.mine[self.place, k].astype(f32) + self.from_x[1, k].astype(f32)
            total = (total + self.from_y[1, k].astype(f32)).astype(bf16)
            self.red[k] = total.reshape(self.red.shape[1:])
            return carry

        lax.fori_loop(first, end, one, 0)

    def square_end(self, c):
        self.swap(c).wait_send()
        for i in range(3):
            self.x(c, i).wait_send()
            self.y(c, i).wait_send()

    def near(self, c):
        return remote(
            self.red.at[self.n(c), :, 1 - self.low],
            self.near_in.at[self.n(c)],
            self.sems["zs"].at[c, 0],
            self.sems["zr"].at[c, 0],
            at(self.place, self.near_by, self.core),
        )

    def far(self, c):
        return remote(
            self.near_in.at[self.n(c), 1 - self.high],
            self.far_in.at[self.n(c)],
            self.sems["zs"].at[c, 1],
            self.sems["zr"].at[c, 1],
            at(self.place, self.far_off, self.core),
        )

    def across(self, c):
        first, end, unused = self.ranges[c]
        self.near(c).wait_recv()

        def one(k, carry):
            self.near_in[k] = self.red[k, :, self.low] + self.near_in[k]
            return carry

        lax.fori_loop(first, end, one, 0)
        self.far(c).start()

    def settle(self, c):
        first, end, unused = self.ranges[c]
        self.far(c).wait_recv()

        def one(k, carry):
            self.out[k] = self.near_in[k, self.high] + self.far_in[k]
            return carry

        lax.fori_loop(first, end, one, 0)

    def direct(self, c, i):
        high = (self.high, 1 - self.high, 1 - self.high)[i]
        low = (1 - self.low, self.low, 1 - self.low)[i]
        diagonal = 2 * (1 - self.high) + 1 - self.low
        target = (self.near_by, self.far_off, diagonal)[i]
        return remote(
            self.red.at[self.n(c), high, low],
            self.direct_in.at[i, self.n(c)],
            self.sems["zs"].at[c, i],
            self.sems["zr"].at[c, i],
            at(self.place, target, self.core),
        )

    def settle_direct(self, c):
        first, end, unused = self.ranges[c]
        for i in range(3):
            self.direct(c, i).wait_recv()

        def one(k, carry):
            total = self.red[k, self.high, self.low].astype(f32)
            for i in range(3):
                total = total + self.direct_in[i, k].astype(f32)
            self.out[k] = total.astype(bf16)
            return carry

        lax.fori_loop(first, end, one, 0)

    def levels_end(self, c):
        self.near(c).wait_send()
        self.far(c).wait_send()


def ffa_forward_kernel(feat, small, stack, logs, *refs):
    step, last = pl.program_id(0), pl.num_programs(0) - 1
    pair = None
    if len(refs) > 10:
        refs, sems = refs[1:12], refs[12:]
        pair = Gather(None, refs[5], dict(zip(XY_SEMS, sems)))
        refs = refs[:5] + refs[6:]
    x1_o, inner_o, act_o, u_o, f_o, wi, wo, wu, table, sem = refs

    @pl.when(step == 0)
    def _():
        if pair is not None:
            place, level, core = peers()
            greet([at(other, level, core) for other in square(place)])
            greet([at(place, level, 1 - core)])
        ffn, mix = D // BS * (FF // BS), (D // BS) ** 2
        weights = Matrices(stack, ((0, wi), (ffn, wo), (2 * ffn, wu)), sem)
        weights.start()
        if pair is not None:
            met(4)
            pair.spread(0)
        frame_decay(logs, table, True)
        for index in range(3):
            weights.wait(index)

    x0 = flat(feat).astype(f32)
    hat, unused = norm(x0)
    inner = mm((hat * small[0:1]).astype(bf16), wi[...])
    act = (inner * sigmoid(inner)).astype(bf16)
    put_rows(inner_o, inner)
    put_rows(act_o, act)
    x1 = x0 + 0.5 * mm(act, wo[...])
    put_rows(x1_o, x1)
    hat, unused = norm(x1)
    u = mm((hat * small[1:2]).astype(bf16), wu[...]).astype(bf16)
    put_rows(u_o, u)
    local_states(table, u, f_o)
    if pair is not None:
        pl.when(step == last - 1)(lambda: pair.forward(0))

        @pl.when(step == last)
        def _():
            pair.finish(0)
            pair.end(0)


def pack_heads(ref, rows):
    first = lax.broadcasted_iota(jnp.int32, (ref.shape[1], LANES), 1) < HALF
    low, high = [], []
    for p in range(rows // 2):
        a, b = ref[2 * p].astype(f32), ref[2 * p + 1].astype(f32)
        low.append(jnp.where(first, a, pltpu.roll(b, HALF, 1)).astype(bf16))
        high.append(jnp.where(first, pltpu.roll(a, HALF, 1), b).astype(bf16))
    return jnp.concatenate(low, axis=1), jnp.concatenate(high, axis=1)


def pack_params(v, rows):
    first = lax.broadcasted_iota(jnp.int32, v.shape, 1) < HALF
    rolled = pltpu.roll(v, HALF, 1)
    low = jnp.where(first, v, rolled)
    high = jnp.where(first, rolled, v)
    return (
        jnp.concatenate([low] * (rows // 2), axis=1),
        jnp.concatenate([high] * (rows // 2), axis=1),
    )


def unpack_pair(low, high, p):
    low = low[:, p * LANES : (p + 1) * LANES]
    high = high[:, p * LANES : (p + 1) * LANES]
    first = lax.broadcasted_iota(jnp.int32, low.shape, 1) < HALF
    return (
        jnp.where(first, low, pltpu.roll(high, HALF, 1)),
        jnp.where(first, pltpu.roll(low, HALF, 1), high),
    )


def swap_states(mine, whole, first_step, last_step, own_sem, send, recv, rest=None):
    place, level, core = peers()
    parts = whole.shape[0]
    others = [(place + d) % parts for d in range(1, parts)]

    def copies():
        return [
            remote(mine, whole.at[place], send.at[d], recv.at[d], at(other, level, core))
            for d, other in enumerate(others)
        ]

    own = lambda: pltpu.make_async_copy(mine, whole.at[place], own_sem)

    @pl.when(first_step)
    def _():
        greet([at(other, level, core) for other in others])
        if rest is not None:
            greet([at(place, level, 1 - core)])
        own().start()

    def begin():
        @pl.when(first_step)
        def _():
            met(parts - 1 + (rest is not None))
            for copy in copies():
                copy.start()
            if rest is not None:
                rest.spread(0)

    def end():
        if rest is not None:
            pl.when(pl.program_id(0) == pl.num_programs(0) - 2)(lambda: rest.forward(0))

        @pl.when(last_step)
        def _():
            if rest is not None:
                rest.finish(0)
                rest.end(0)
            own().wait()
            for copy in copies():
                copy.wait()

    return begin, end


def tile_lanes(v, width):
    return jnp.concatenate([v] * (width // LANES), axis=1)


def conv_forward_kernel(u, ends, logs, mix_one, mix_two, *refs):
    step = pl.program_id(0)
    pair = None
    if len(refs) > 7:
        refs, sems = refs[1:9], refs[9:]
        pair = Gather(None, refs[2], dict(zip(XY_SEMS, sems)), 2)
        refs = refs[:2] + refs[3:]
    y_o, ends_all, pad, taps, own_sem, send, recv = refs
    begin_swap, end_swap = swap_states(
        ends, ends_all, step == 0, step == pl.num_programs(0) - 1, own_sem, send, recv, pair
    )
    rows, frames = u.shape[0], u.shape[1]
    span = GROUP * SUB
    coup = join_lanes(mix_one) * join_lanes(mix_two)
    lag_taps(channel_rates(logs), coup, taps, False)
    coup_both = pack_params(coup, rows)
    heads = rate_rows(logs)
    packed = pack_heads(u, rows)
    width = packed[0].shape[1]
    begin_swap()
    results = []
    for h in range(2):
        into, unused, out, unused, power = chunk_tables(heads[h])
        scale = [jnp.broadcast_to(v, (NST, width)) for v in power]
        carry = None
        outs = []
        for g in range(frames // span):
            local = mm(into, packed[h][g * span : (g + 1) * span])
            parts = [local[i * NST : (i + 1) * NST] for i in range(GROUP)]
            if carry is None:
                states = [jnp.zeros_like(parts[0])] + parts[:-1]
                carry = parts[-1]
            else:
                states = [carry] + [parts[i] + scale[i] * carry for i in range(GROUP - 1)]
                carry = parts[-1] + scale[-1] * carry
            scaled = jnp.concatenate([v * coup_both[h] for v in states], axis=0)
            outs.append(mm_tn(out, scaled.astype(bf16)))
        results.append(jnp.concatenate(outs, axis=0))
    for p in range(rows // 2):
        one, two = unpack_pair(results[0], results[1], p)
        y_o[2 * p] = one
        y_o[2 * p + 1] = two
    pad[0:SUB] = jnp.zeros((SUB, LANES), f32)
    chunk = frames // 5

    def one_row(i, carry):
        pad[pl.ds(SUB, frames)] = u[i].astype(f32)
        for r in range(0, frames, chunk):
            acc = y_o[i, pl.ds(r, chunk)].reshape(-1, SUB, LANES)
            for d in range(SUB):
                piece = pad[pl.ds(SUB + r - d, chunk)].reshape(-1, SUB, LANES)
                acc = acc + piece * taps[d][None]
            y_o[i, pl.ds(r, chunk)] = acc.reshape(chunk, LANES)
        return carry

    lax.fori_loop(0, rows, one_row, 0)
    end_swap()


def edge_sender(edges, low_all, high_all, zeros, send, recv, zero_sem, step, per, rest=None):
    place, level, core = peers()
    parts = lax.axis_size("tm")
    steps = edges.shape[0]
    not_first, not_last = place > 0, place < parts - 1
    after = (place + 1) % parts
    before = (place + parts - 1) % parts

    def up(i):
        return remote(
            edges.at[i, 1], low_all.at[i], send.at[0, i], recv.at[0, i], at(after, level, core)
        )

    def down(i):
        return remote(
            edges.at[i, 0], high_all.at[i], send.at[1, i], recv.at[1, i], at(before, level, core)
        )

    def blank(ref, i, k):
        return pltpu.make_async_copy(zeros, ref.at[i], zero_sem.at[k])

    @pl.when(step == 0)
    def _():
        if rest is None:
            pl.when(not_last)(lambda: greet([at(after, level, core)]))
            pl.when(not_first)(lambda: greet([at(before, level, core)]))
        zeros[...] = jnp.zeros_like(zeros)

        @pl.when(place == 0)
        def _():
            for i in range(steps):
                blank(low_all, i, 0).start()

        @pl.when(place == parts - 1)
        def _():
            for i in range(steps):
                blank(high_all, i, 1).start()

    def put(v):
        @pl.when(step == 0)
        def _():
            below = (place + parts - 1) // parts
            above = (2 * parts - 2 - place) // parts
            if rest is None:
                met(below + above)

        if rest is not None:
            pl.when(step == steps // per // 2)(lambda: rest.forward(1))
            pl.when(step == steps // per - 1)(lambda: rest.finish(1))

        frames = v.shape[0] // per
        for b in range(per):
            row = step * per + b
            edges[row, 0] = v[b * frames : b * frames + PAD]
            edges[row, 1] = v[(b + 1) * frames - PAD : (b + 1) * frames]
            pl.when(not_last)(lambda row=row: up(row).start())
            pl.when(not_first)(lambda row=row: down(row).start())

        @pl.when(step == steps // per - 1)
        def _():
            for i in range(steps):
                pl.when(not_last)(lambda i=i: up(i).wait_send())
                pl.when(not_first)(lambda i=i: down(i).wait_send())
                pl.when(not_first)(lambda i=i: up(i).wait_recv())
                pl.when(not_last)(lambda i=i: down(i).wait_recv())

            if rest is not None:
                rest.end(1)

            @pl.when(place == 0)
            def _():
                for i in range(steps):
                    blank(low_all, i, 0).wait()

            @pl.when(place == parts - 1)
            def _():
                for i in range(steps):
                    blank(high_all, i, 1).wait()

    return put


def mixer_out_kernel(
    y, ends_all, starts, mix_one, mix_two, logs, x1, small, stack, *refs
):
    step = pl.program_id(0)
    rest = None
    if len(refs) > 19:
        refs, sems = refs[1:21], refs[21:]
        rest = Gather(None, refs[7], dict(zip(XY_SEMS, sems)), 2)
        refs = refs[:7] + refs[8:]
    ys_o, gated_o, x2_o, pw_o, g_o, low_o, high_o, wo, wp, mask, sem = refs[:11]
    table, weigh, coup, edges, zeros, send, recv, zero_sem = refs[11:]
    parts = ends_all.shape[0]
    put = edge_sender(edges, low_o, high_o, zeros, send, recv, zero_sem, step, 1, rest)

    @pl.when(step == 0)
    def _():
        ffn, mix = D // BS * (FF // BS), (D // BS) ** 2
        if rest is not None:
            greet([at(other, rest.level, rest.core) for other in (rest.xp, rest.yp, rest.dp)])
            greet([at(rest.place, rest.level, 1 - rest.core)])
        weights = Matrices(stack, ((0, wo), (2 * mix, wp)), sem)
        weights.start()
        if rest is not None:
            met(4)
            rest.spread(1)
        mask[...] = head_mask()
        place = lax.axis_index("tm")
        frames = table.shape[0]
        frame_decay(logs, table, False)
        rates = channel_rates(logs)
        for i in range(parts):
            weigh[i], unused = passing(rates, place - 1 - i, frames)
        two = join_lanes(mix_two)
        weigh[parts] = two * passing(rates, place, frames)[0]
        coup[...] = join_lanes(mix_one) * two
        for index in range(2):
            weights.wait(index)

    came = weigh[0] * ends_all[0, 0].astype(f32)
    for i in range(1, parts):
        came = came + weigh[i] * ends_all[i, 0].astype(f32)
    zin = coup[...] * came + weigh[parts] * join_lanes(starts)
    ys = (y[0] + mm(table[...], spread_heads(zin, mask[...]))).astype(bf16)
    ys_o[0] = ys
    gated = mm(ys, wo[...])
    gated_o[0] = gated.astype(bf16)
    x2 = x1[0] + gated[:, :D] * sigmoid(gated[:, D:])
    x2_o[0] = x2
    hat, unused = norm(x2)
    pw = mm((hat * small[2:3]).astype(bf16), wp[...])
    pw_o[0] = pw.astype(bf16)
    g = (pw[:, :D] * sigmoid(pw[:, D:])).astype(bf16)
    g_o[0] = g
    put(g)


def fill_pad(pad, low, body, high):
    frames = body.shape[0]
    for g in range(D // LANES):
        lanes = slice(g * LANES, (g + 1) * LANES)
        pad[g, 0:PAD] = low[:, lanes].astype(f32)
        pad[g, pl.ds(PAD, frames)] = body[:, lanes].astype(f32)
        pad[g, pl.ds(PAD + frames, PAD)] = high[:, lanes].astype(f32)


def ffb_kernel(
    scale, g, low, high, x2, cot, small, stack,
    out_o, dx3_o, dq_o, grads, gain_o, low_o, high_o,
    wi, wo, wq, acc_in, acc_out, acc_q, pad, q_s, stage, k_act, k_din, k_n, k_dp, k_a, k_dpq, sem,
    edges, zeros, send, recv, zero_sem,
):
    step = pl.program_id(0)
    frames = g.shape[1]
    put = edge_sender(edges, low_o, high_o, zeros, send, recv, zero_sem, step, 1)

    ffn, mix = D // BS * (FF // BS), (D // BS) ** 2
    weights = Matrices(stack, ((2 * ffn, wq), (0, wi), (ffn, wo)), sem)

    def ready(*which):
        @pl.when(step == 0)
        def _():
            for index in which:
                weights.wait(index)

    @pl.when(step == 0)
    def _():
        weights.start()
        acc_in[...] = jnp.zeros_like(acc_in)
        acc_out[...] = jnp.zeros_like(acc_out)
        acc_q[...] = jnp.zeros_like(acc_q)
        gain_o[...] = jnp.zeros_like(gain_o)

    fill_pad(pad, low[0], g[0], high[0])
    chunk = frames // 5
    for c in range(D // LANES):
        lanes = slice(c * LANES, (c + 1) * LANES)
        for r in range(0, frames, chunk):
            acc = small[5:6, lanes] * pad[c, pl.ds(r + PAD - 7, chunk)]
            for j in range(1, KW):
                acc = acc + small[5 + j : 6 + j, lanes] * pad[c, pl.ds(r + j + PAD - 7, chunk)]
            q_s[pl.ds(r, chunk), lanes] = acc
    ready(0, 1, 2)
    q = q_s[...]
    sig_q = sigmoid(q)
    act_q = q * sig_q
    a3 = act_q.astype(bf16)
    x3 = x2[0] + mm(a3, wq[...])
    hat3, inv3 = norm(x3)
    n3 = (hat3 * small[3:4]).astype(bf16)
    inner = mm(n3, wi[...])
    sig = sigmoid(inner)
    act = inner * sig
    b4 = act.astype(bf16)
    x4 = x3 + 0.5 * mm(b4, wo[...])
    hat4, inv4 = norm(x4)
    out_o[0] = (hat4 * small[4:5]).astype(bf16)
    c4 = cot[0].astype(f32)
    gain_o[1] += fold8(c4 * hat4)
    dx4 = norm_back(hat4, inv4, small[4:5], c4)
    dp = (0.5 * dx4).astype(bf16)
    dact = mm_nt(dp, wo[...])
    dinner = ((sig + act * (1.0 - sig)) * dact).astype(bf16)
    group = k_n.shape[0] // frames
    keep = pl.ds(pl.multiple_of(step % group * frames, frames), frames)
    k_act[keep] = b4
    k_din[keep] = dinner
    k_n[keep] = n3
    k_dp[keep] = dp
    k_a[keep] = a3
    dn3 = mm_nt(dinner, wi[...])
    gain_o[0] += fold8(dn3 * hat3)
    dx3 = dx4 + norm_back(hat3, inv3, small[3:4], dn3)
    dx3_o[0] = dx3
    dpq = dx3.astype(bf16)
    k_dpq[keep] = dpq
    da3 = mm_nt(dpq, wq[...])
    dq = ((sig_q + act_q * (1.0 - sig_q)) * da3).astype(bf16)
    dq_o[0] = dq
    put(dq)

    @pl.when(step % group == group - 1)
    def _():
        acc_out[...] += mm_tn(k_dp[...], k_act[...])
        acc_in[...] += mm_tn(k_n[...], k_din[...])
        acc_q[...] += mm_tn(k_a[...], k_dpq[...])

    @pl.when(step == pl.num_programs(0) - 1)
    def _():
        ffn, mix = D // BS * (FF // BS), (D // BS) ** 2
        plan = (
            (acc_in, 0, False),
            (acc_out, ffn, True),
            (acc_q, 2 * ffn, False),
        )
        store_blocks(plan, scale, grads, stage, sem.at[0])


def mixer_back_kernel(
    scale, dq, dlow, dhigh, g, glow, ghigh, pw, x2, gated, ys, dx3, small, stack, logs, *refs
):
    step, last = pl.program_id(0), pl.num_programs(0) - 1
    frames = dq.shape[1]
    rest = None
    if len(refs) > 21:
        grads_rest, refs = refs[0], refs[1:]
        red, bufs, sems = refs[6], refs[22:26], refs[26:]
        half = (red.shape[0] + 1) // 2
        rest = Reduce((half, red.shape[0] - half), dict(zip(R_XY, sems)), grads_rest, bufs, red)
        refs = refs[:6] + refs[7:22]
    dx2_o, dy_o, gst_o, grads, gain_o, dk_o, wo, wp, acc_p, acc_o, dpad, gpad = refs[:12]
    dg_s, dk_s, stage, k_n, k_dpw, k_ys, k_dg, table, sem = refs[12:]

    @pl.when(step == 0)
    def _():
        ffn, mix = D // BS * (FF // BS), (D // BS) ** 2
        if rest is not None:
            greet([at(other, rest.level, rest.core) for other in (rest.xp, rest.yp, rest.dp)])
            greet([at(rest.place, rest.level, 1 - rest.core)])
        weights = Matrices(stack, ((0, wo), (2 * mix, wp)), sem)
        weights.start()
        if rest is not None:
            met(4)
            for c in rest.all:
                rest.start(c)
        frame_decay(logs, table, False)
        acc_p[...] = jnp.zeros_like(acc_p)
        acc_o[...] = jnp.zeros_like(acc_o)
        gain_o[...] = jnp.zeros_like(gain_o)
        dk_s[...] = jnp.zeros_like(dk_s)
        for index in range(2):
            weights.wait(index)

    fill_pad(dpad, dlow[0], dq[0], dhigh[0])
    fill_pad(gpad, glow[0], g[0], ghigh[0])
    chunk = frames // 5
    for c in range(D // LANES):
        lanes = slice(c * LANES, (c + 1) * LANES)
        for r in range(0, frames, chunk):
            here = dpad[c, pl.ds(r + PAD, chunk)]
            acc = small[5:6, lanes] * dpad[c, pl.ds(r + PAD + 7, chunk)]
            for j in range(1, KW):
                acc = acc + small[5 + j : 6 + j, lanes] * dpad[c, pl.ds(r - j + PAD + 7, chunk)]
            dg_s[pl.ds(r, chunk), lanes] = acc
            for j in range(KW):
                dk_s[j, :, lanes] += fold8(here * gpad[c, pl.ds(r + j + PAD - 7, chunk)])
    dg = dg_s[...]
    value = pw[0, :, :D].astype(f32)
    gate = sigmoid(pw[0, :, D:].astype(f32))
    dvalue = (dg * gate).astype(bf16)
    dgate = (dg * value * gate * (1.0 - gate)).astype(bf16)
    dpw = jnp.concatenate([dvalue, dgate], axis=1)
    hat2, inv2 = norm(x2[0])
    n2 = (hat2 * small[2:3]).astype(bf16)
    group = k_n.shape[0] // frames
    keep = pl.ds(pl.multiple_of(step % group * frames, frames), frames)
    k_n[keep] = n2
    k_dpw[keep] = dpw
    k_ys[keep] = ys[0]
    dn2 = mm_nt(dpw, wp[...])
    gain_o[...] += fold8(dn2 * hat2)
    dx2 = dx3[0] + norm_back(hat2, inv2, small[2:3], dn2)
    dx2_o[0] = dx2
    value = gated[0, :, :D].astype(f32)
    gate = sigmoid(gated[0, :, D:].astype(f32))
    dvalue = (dx2 * gate).astype(bf16)
    dgate = (dx2 * value * gate * (1.0 - gate)).astype(bf16)
    dgated = jnp.concatenate([dvalue, dgate], axis=1)
    k_dg[keep] = dgated
    dy = mm_nt(dgated, wo[...]).astype(bf16)
    dy_o[0] = dy
    local_states(table, dy, gst_o)

    if rest is not None:
        for c in rest.all:
            pl.when(step == 0)(lambda c=c: rest.begin(c))
            pl.when(step == last - 3 + 2 * c)(lambda c=c: rest.second(c))

    @pl.when(step % group == group - 1)
    def _():
        acc_p[...] += mm_tn(k_n[...], k_dpw[...])
        acc_o[...] += mm_tn(k_ys[...], k_dg[...])

    @pl.when(step == pl.num_programs(0) - 1)
    def _():
        ffn, mix = D // BS * (FF // BS), (D // BS) ** 2
        plan = ((acc_o, 0, False), (acc_p, 2 * mix, False))
        store_blocks(plan, scale, grads, stage, sem.at[0])
        if rest is not None:
            for c in rest.all:
                rest.combine(c)
                rest.square_end(c)
        for j in range(KW):
            dk_o[j : j + 1] = jnp.sum(dk_s[j], axis=0, keepdims=True)


def conv_back_kernel(
    u, dy, back_ends, logs, mix_one, mix_two,
    du_o, t1_o, t2_o, fp_o, gp_o, back_all,
    upad, dpad, acc_s, taps, own_sem, send, recv,
):
    step = pl.program_id(0)
    begin_swap, end_swap = swap_states(
        back_ends, back_all, step == 0, step == pl.num_programs(0) - 1, own_sem, send, recv
    )
    rows, frames = u.shape[0], u.shape[1]
    span = GROUP * SUB
    coup = join_lanes(mix_one) * join_lanes(mix_two)
    rates = channel_rates(logs)
    lag_taps(rates, coup, taps, True)
    coup_both = pack_params(coup, rows)
    heads = rate_rows(logs)
    u_both = pack_heads(u, rows)
    d_both = pack_heads(dy, rows)
    width = u_both[0].shape[1]
    du, first_sum, second_sum, end_u, end_d = [], [], [], [], []
    for h in range(2):
        into, into_w, out, out_w, power = chunk_tables(heads[h])
        scale = [jnp.broadcast_to(v, (NST, width)) for v in power]
        aged = [scale[i] * float(SUB * (i + 1)) for i in range(GROUP)]
        zero = jnp.zeros((NST, width), f32)
        carry, carry_w = zero, zero
        states, states_w = [], []
        for g in range(frames // span):
            here = u_both[h][g * span : (g + 1) * span]
            local = mm(into, here)
            local_w = mm(into_w, here)
            parts = [local[i * NST : (i + 1) * NST] for i in range(GROUP)]
            parts_w = [local_w[i * NST : (i + 1) * NST] for i in range(GROUP)]
            states.append([carry] + [parts[i] + scale[i] * carry for i in range(GROUP - 1)])
            states_w.append(
                [carry_w]
                + [parts_w[i] + scale[i] * carry_w + aged[i] * carry for i in range(GROUP - 1)]
            )
            carry_w = parts_w[-1] + scale[-1] * carry_w + aged[-1] * carry
            carry = parts[-1] + scale[-1] * carry
        end_u.append(carry_w)
        later, later_w = zero, zero
        one, two = zero, zero
        outs = []
        for g in reversed(range(frames // span)):
            here = d_both[h][g * span : (g + 1) * span]
            back = mm(out, here)
            back_w = mm(out_w, here)
            parts = [back[i * NST : (i + 1) * NST] for i in range(GROUP)]
            parts_w = [back_w[i * NST : (i + 1) * NST] for i in range(GROUP)]
            grads = jnp.concatenate([v * coup_both[h] for v in parts[1:] + [later]], axis=0)
            outs.append(mm_tn(into, grads.astype(bf16)))
            for i in range(GROUP):
                one = one + parts[i] * states[g][i]
                two = two + (parts_w[i] * states[g][i] + parts[i] * states_w[g][i])
            new, new_w = parts[0], parts_w[0]
            for i in range(GROUP - 1):
                new = new + scale[i] * parts[i + 1]
                new_w = new_w + (scale[i] * parts_w[i + 1] + aged[i] * parts[i + 1])
            later_w = new_w + scale[-1] * later_w + aged[-1] * later
            later = new + scale[-1] * later
        end_d.append(later_w)
        first_sum.append(one)
        second_sum.append(two)
        du.append(jnp.concatenate(outs[::-1], axis=0))
    first = lax.broadcasted_iota(jnp.int32, (NST, LANES), 1) < HALF
    for sums, out in ((first_sum, t1_o), (second_sum, t2_o)):
        both = []
        for v in sums:
            total = v[:, :LANES]
            for p in range(1, rows // 2):
                total = total + v[:, p * LANES : (p + 1) * LANES]
            both.append(total + pltpu.roll(total, HALF, 1))
        out[...] = jnp.where(first, both[0], both[1])
    for p in range(rows // 2):
        for pair, out in ((du, du_o), (end_u, fp_o), (end_d, gp_o)):
            one, two = unpack_pair(pair[0], pair[1], p)
            out[2 * p] = one
            out[2 * p + 1] = two
    chunk = frames // 5
    upad[0:SUB] = jnp.zeros((SUB, LANES), f32)
    dpad[pl.ds(frames, SUB)] = jnp.zeros((SUB, LANES), f32)
    acc_s[...] = jnp.zeros_like(acc_s)

    def one_row(i, carry):
        upad[pl.ds(SUB, frames)] = u[i].astype(f32)
        dpad[pl.ds(0, frames)] = dy[i].astype(f32)
        for r in range(0, frames, chunk):
            acc = du_o[i, pl.ds(r, chunk)].reshape(-1, SUB, LANES)
            here = dpad[pl.ds(r, chunk)]
            for d in range(SUB):
                piece = dpad[pl.ds(r + d, chunk)].reshape(-1, SUB, LANES)
                acc = acc + piece * taps[d][None]
                product = (here * upad[pl.ds(SUB + r - d, chunk)]).reshape(-1, SUB, LANES)
                acc_s[d] += jnp.sum(product, axis=0)
            du_o[i, pl.ds(r, chunk)] = acc.reshape(chunk, LANES)
        return carry

    lax.fori_loop(0, rows, one_row, 0)
    spot = lax.broadcasted_iota(jnp.int32, (SUB, LANES), 0)
    one, two = t1_o[...], t2_o[...]
    for d in range(SUB):
        kept = jnp.where(spot >= d, acc_s[d], 0.0)
        grad = jnp.exp(-rates * float(d)) * jnp.sum(kept, axis=0, keepdims=True)
        one = one + grad
        two = two + float(d) * grad
    t1_o[...] = one
    t2_o[...] = two
    begin_swap()
    end_swap()


def ffa_back_kernel(
    scale, du_loc, back_all, ends_all, back_ends, ends_w, back_w, starts, mix_one, mix_two, logs,
    t_one, t_two, gain_b, gain_c, kernel_grads,
    x1, feat, inner_r, act_r, dx2, small, stack, *refs
):
    step, last = pl.program_id(0), pl.num_programs(0) - 1
    pair = None
    if len(refs) > 23:
        grads_pair, red_in, refs = refs[0], refs[1], refs[2:]
        out_pair, out_rest = refs[3:5]
        red_rest, rest_bufs, red_pair, square_refs = refs[25], refs[26:28], refs[28], refs[29:33]
        pair_bufs, sems = refs[33:35], refs[35:]
        refs = refs[:3] + refs[5:25]
        pair = Reduce(
            out_pair.shape[:1], dict(zip(R_XY + R_Z, sems)), grads_pair, square_refs, red_pair,
            pair_bufs, out_pair,
        )
        rest = Reduce(
            out_rest.shape[:1], dict(zip(R_Z, sems[9:])), None, None, red_rest, rest_bufs, out_rest
        )
    dx0_o, grads, small_o, wi, wo, wu, acc_in, acc_out, acc_u = refs[:9]
    mask, stage, k_act, k_din, k_n, k_dp, k_m, k_du, sem = refs[9:18]
    gain_o, sums_o, table, weigh, coup = refs[18:]
    place, parts = lax.axis_index("tm"), ends_all.shape[0]

    ffn, mix = D // BS * (FF // BS), (D // BS) ** 2
    weights = Matrices(stack, ((2 * ffn, wu), (ffn, wo), (0, wi)), sem)

    @pl.when(step == 0)
    def _():
        if pair is not None:
            greet([at(other, pair.level, pair.core) for other in (pair.xp, pair.yp, pair.dp)])
            greet([at(pair.place, other, pair.core) for other in (pair.near_by, pair.far_off)])
            greet([at(pair.place, pair.level, 1 - pair.core)])
            red_rest[...] = red_in[...]
        weights.start()
        if pair is not None:
            met(6)
            pair.start(0)
            rest.near(0).start()
        mask[...] = head_mask()
        frames = table.shape[0]
        frame_decay(logs, table, True)
        rates = channel_rates(logs)
        for i in range(parts):
            weigh[0, i], weigh[1, i] = passing(rates, place - 1 - i, frames)
            weigh[2, i], unused = passing(rates, i - place - 1, frames)
        coup[...] = join_lanes(mix_one) * join_lanes(mix_two)
        acc_in[...] = jnp.zeros_like(acc_in)
        acc_out[...] = jnp.zeros_like(acc_out)
        acc_u[...] = jnp.zeros_like(acc_u)
        gain_o[...] = jnp.zeros_like(gain_o)
        sums_o[...] = jnp.zeros_like(sums_o)
        for index in range(3):
            weights.wait(index)

    frames = feat.shape[1]
    group = k_n.shape[0] // frames
    keep = pl.ds(pl.multiple_of(step % group * frames, frames), frames)
    came, came_w, later = 0.0, 0.0, 0.0
    for i in range(parts):
        end = ends_all[i, 0].astype(f32)
        came = came + weigh[0, i] * end
        came_w = came_w + weigh[1, i] * end
        later = later + weigh[2, i] * back_all[i, 0].astype(f32)
    mine = back_ends[0].astype(f32)
    start = join_lanes(starts)
    sums_o[0] += mine * came
    sums_o[1] += start * mine
    sums_o[2] += start * back_w[0]
    sums_o[3] += back_w[0] * came + mine * came_w + later * ends_w[0]
    du = (du_loc[0] + mm(table[...], spread_heads(coup[...] * later, mask[...]))).astype(bf16)
    hat1, inv1 = norm(x1[0])
    n1 = (hat1 * small[1:2]).astype(bf16)
    k_m[keep] = n1
    k_du[keep] = du
    dn1 = mm_nt(du, wu[...])
    gain_o[1] += fold8(dn1 * hat1)
    dx1 = dx2[0] + norm_back(hat1, inv1, small[1:2], dn1)
    dp = (0.5 * dx1).astype(bf16)
    dact = mm_nt(dp, wo[...])
    inner = inner_r[0].astype(f32)
    sig = sigmoid(inner)
    dinner = ((sig + inner * sig * (1.0 - sig)) * dact).astype(bf16)
    hat0, inv0 = norm(feat[0].astype(f32))
    n0 = (hat0 * small[0:1]).astype(bf16)
    k_act[keep] = act_r[0]
    k_din[keep] = dinner
    k_n[keep] = n0
    k_dp[keep] = dp
    dn0 = mm_nt(dinner, wi[...])
    gain_o[0] += fold8(dn0 * hat0)
    dx0_o[0] = dx1 + norm_back(hat0, inv0, small[0:1], dn0)

    if pair is not None:

        @pl.when(step == 0)
        def _():
            pair.begin(0)

        @pl.when(step == last - 4)
        def _():
            rest.across(0)

        @pl.when(step == last - 3)
        def _():
            pair.second(0)

        @pl.when(step == last - 2)
        def _():
            rest.settle(0)
            pair.combine(0)
            pair.near(0).start()

        @pl.when(step == last - 1)
        def _():
            pair.across(0)

    @pl.when(step % group == group - 1)
    def _():
        acc_out[...] += mm_tn(k_dp[...], k_act[...])
        acc_in[...] += mm_tn(k_n[...], k_din[...])
        acc_u[...] += mm_tn(k_m[...], k_du[...])

    @pl.when(step == pl.num_programs(0) - 1)
    def _():
        ffn, mix = D // BS * (FF // BS), (D // BS) ** 2
        one, two = join_lanes(mix_one), join_lanes(mix_two)
        begin = (place * frames).astype(f32)
        begin_w = jnp.exp(-channel_rates(logs) * begin)
        d_coup = t_one[...] + sums_o[0]
        start_back = sums_o[1] * begin_w
        d_rate = coup[...] * (t_two[...] + sums_o[3])
        d_rate = d_rate + two * (begin * start_back + begin_w * sums_o[2])
        total = lambda v: jnp.sum(v, axis=0, keepdims=True)
        gains = [total(gain_o[0]), total(gain_o[1]), total(gain_c[...])]
        gains += [total(gain_b[0]), total(gain_b[1]), kernel_grads[0:KW]]
        entries = gains + [d_coup * two, d_coup * one + start_back, d_rate]
        own = small_o.shape[2]
        small_o[...] = jnp.zeros_like(small_o)
        row = 0
        for entry in entries:
            count = entry.shape[0]
            if count == NST:
                row = -(-row // 8) * 8
            for p in range(parts):
                small_o[p, row : row + count] = entry[:, p * own : (p + 1) * own] * scale
            row += count
        plan = ((acc_in, 0, False), (acc_out, ffn, True), (acc_u, 2 * ffn, False))
        store_blocks(plan, scale, grads, stage, sem.at[0])
        if pair is not None:
            pair.settle(0)
            pair.square_end(0)
            pair.levels_end(0)
            rest.levels_end(0)


def shampoo_kernel(
    frames, source, owned, full, left, right, lroot, rroot, master, sums, small, logs, mix_terms,
    back_all, result, slope, nl_o, nr_o, nm_o, nc_o, own_o,
    small_o, new_small_o, decay_o, mix_o, new_decay_o, new_mix_o, state_o, result_o, slope_o,
):
    step = pl.program_id(0)
    result_o[...] = result[...]
    slope_o[...] = slope[...]

    @pl.when(step == 0)
    def _():
        place = lax.axis_index("tm")
        parts, rows, width = back_all.shape[0], back_all.shape[1], state_o.shape[2]
        columns = [as_column(jnp.exp(logs[j : j + 1])) for j in range(logs.shape[0])]
        over = [jnp.broadcast_to(column, (NST, HALF)) for column in columns]
        rates = jnp.concatenate(over, axis=1)
        decays = [jnp.exp(-rates * float(frames * i)) * mix_terms[1] for i in range(parts)]
        grads = []
        for r in range(rows):
            grad = 0.0
            for p in range(parts):
                total = 0.0
                for i in range(parts):
                    part = back_all[i, r, :, p * width : (p + 1) * width].astype(f32)
                    total = total + part * decays[i]
                grad = grad + jnp.where(place == p, total, 0.0)
            grads.append(grad)
        for r in range(rows):
            total = 0.0
            for i in range(rows):
                total = total + jnp.where(source[i] == r, grads[i], 0.0)
            state_o[r] = total

    @pl.when(step == 0)
    def _():
        count = small_o.shape[0]
        grad = sums[0:count]
        small_o[...] = grad
        width = small_o.shape[1]
        own_small = 0.0
        for p in range(small.shape[1] // width):
            part = small[:, p * width : (p + 1) * width]
            own_small = own_small + jnp.where(lax.axis_index("tm") == p, part, 0.0)
        new_small_o[...] = own_small - rate_small * grad
        row = -(-count // 8) * 8
        for i in range(2):
            grad = sums[row + i * NST : row + (i + 1) * NST]
            mix_o[i] = grad
            new_mix_o[i] = mix_terms[i] - rate_small * grad
        by_channel = sums[row + 2 * NST : row + 3 * NST].T
        for j in range(logs.shape[0]):
            here = jnp.sum(by_channel[j * HALF : (j + 1) * HALF], axis=0, keepdims=True)
            grad = -here * jnp.exp(logs[j : j + 1])
            decay_o[j : j + 1] = grad
            new_decay_o[j : j + 1] = logs[j : j + 1] - rate_small * grad

    slab = owned.shape[1]
    down = lax.broadcasted_iota(jnp.int32, (slab, BS), 0) + lax.axis_index("rows") * slab
    pick = (down == lax.broadcasted_iota(jnp.int32, (slab, BS), 1)).astype(f32).astype(bf16)
    for i in range(full.shape[0]):
        whole = full[i]
        mine = owned[i]
        own_o[i] = mine.astype(f32)
        pair = mm_nt(jnp.concatenate([mine, pick], axis=0), whole)
        nl_o[i] = 0.5 * left[i] + 0.5 * pair[:slab]
        pair = jnp.concatenate([pair[slab:], lroot[i]], axis=0).astype(bf16)
        pair = mm(pair, whole)
        nr_o[i] = 0.5 * right[i] + 0.5 * pair[:slab]
        side = pair[slab:]
        step = mm(side.astype(bf16), rroot[i].astype(bf16))
        new = master[i] - rate_blocks * step
        nm_o[i] = new
        nc_o[i] = new.astype(bf16)


def deliveries(sizes, parts, count):
    edges = [sum(sizes[:c]) for c in range(len(sizes) + 1)]
    runs = []
    for which, ids in enumerate(block_sets()):
        for owner, k, v, j, n in move_runs(ids, parts, count):
            if which:
                runs.append((0, which, owner, k, v, j, n))
                continue
            for c, (a, b) in enumerate(zip(edges[:-1], edges[1:])):
                low, high = max(a, j), min(b, j + n)
                if low < high:
                    runs.append((c + 1, 0, owner, k + low - j, v, low, high - low))
    groups = []
    for chunk, unused, owner, k, v, j, n in sorted(runs, key=lambda run: (run[0], run[2], run[3])):
        if groups and groups[-1][:2] == (chunk, owner) and sum(groups[-1][2:]) == k:
            groups[-1] = (chunk, owner, groups[-1][2], groups[-1][3] + n)
        else:
            groups.append((chunk, owner, k, n))
    return runs, groups


def reduce_kernel(
    sizes, runs, groups, grads, share_pair, share_rest, small, full, owned_o, small_sum,
    mine, came, from_x, from_y, red, direct_in, share_first, owned, s_tm, s_core, s_z,
    d_send, d_recv, a_send, a_recv, f_send, f_recv, s_send, s_recv, put_sem, *sems,
):
    it = Reduce(
        sizes, dict(zip(R_XY + R_Z, sems)), grads, (mine, came, from_x, from_y), red, None, share_first
    )
    it.direct_in = direct_in
    place, level, core = it.place, it.level, it.core
    low, high, near, far = it.low, it.high, it.near_by, it.far_off
    diagonal = 2 * (1 - high) + 1 - low
    others = (it.xp, it.yp, it.dp)
    greet([at(other, level, core) for other in others])
    greet([at(place, other, core) for other in (near, far, diagonal)])
    greet([at(place, level, 1 - core)])
    shares = (share_first, share_pair, share_rest)

    def deliver(index):
        unused, which, owner, k, v, j, n = runs[index]
        src, dst = shares[which].at[pl.ds(j, n)], owned.at[pl.ds(k, n)]
        if owner == v:
            return pltpu.make_async_copy(src, dst, d_send.at[index])
        return remote(src, dst, d_send.at[index], d_recv.at[index], at(owner, level, core))

    def in_chunk(c):
        return [i for i, run in enumerate(runs) if run[0] == c]

    def send_out(c):
        for i in in_chunk(c):
            pl.when(place == runs[i][4])(lambda i=i: deliver(i).start())

    def come_in(c):
        for i in in_chunk(c):
            local = runs[i][2] == runs[i][4]
            done = (lambda i=i: deliver(i).wait()) if local else (lambda i=i: deliver(i).wait_recv())
            pl.when(place == runs[i][2])(done)

    def sent_out():
        for i, run in enumerate(runs):
            if run[2] != run[4]:
                pl.when(place == run[4])(lambda i=i: deliver(i).wait_send())

    def spot(g, where):
        unused, owner, k, n = groups[g]
        return full.at[pl.ds(k, n), where // 2, where % 2, core]

    def held(g):
        unused, owner, k, n = groups[g]
        return owned.at[pl.ds(k, n)]

    def put(g):
        return pltpu.make_async_copy(held(g), spot(g, level), put_sem.at[g])

    def at_once(g):
        return groups[g][0] == len(sizes)

    def along(g, i):
        passed = i == 2 and not at_once(g)
        src = spot(g, far) if passed else held(g)
        dst = spot(g, far if passed else level)
        target = (far, near, near if passed else diagonal)[i]
        target = at(place, target, core)
        return remote(src, dst, a_send.at[g, i], a_recv.at[g, i], target)

    def to_core(g, i):
        where = (level, far, near, diagonal)[i]
        src = held(g) if i == 0 else spot(g, where)
        target = at(place, level, 1 - core)
        return remote(src, spot(g, where), f_send.at[g, i], f_recv.at[g, i], target)

    def for_groups(c, act):
        for g, group in enumerate(groups):
            if c is None or group[0] == c:
                pl.when(place == group[1])(lambda g=g: act(g))

    def spread(g):
        put(g).start()
        along(g, 0).start()
        along(g, 1).start()
        if at_once(g):
            along(g, 2).start()
        to_core(g, 0).start()

    def pass_on(g):
        along(g, 0).wait_recv()
        if not at_once(g):
            along(g, 2).start()
        to_core(g, 1).start()
        along(g, 1).wait_recv()
        to_core(g, 2).start()
        if at_once(g):
            along(g, 2).wait_recv()
            to_core(g, 3).start()

    def last(g):
        if not at_once(g):
            along(g, 2).wait_recv()
            to_core(g, 3).start()

    def finish(g):
        put(g).wait()
        for i in range(4):
            to_core(g, i).wait_recv()
        for i in range(4):
            to_core(g, i).wait_send()
        for i in range(3):
            along(g, i).wait_send()

    def to_place(d):
        send, recv = s_send.at[d], s_recv.at[d]
        return remote(small.at[others[d]], s_tm.at[d], send, recv, at(others[d], level, core))

    def to_sibling():
        target = at(place, level, 1 - core)
        return remote(s_core.at[0], s_core.at[1], s_send.at[3], s_recv.at[3], target)

    def to_level(d):
        target = at(place, (near, far, diagonal)[d], core)
        return remote(s_z.at[level], s_z.at[level], s_send.at[4 + d], s_recv.at[4 + d], target)

    def reduced(c):
        it.combine(c)
        for i in range(3):
            it.direct(c, i).start()

    def settled(c):
        it.settle_direct(c)
        send_out(c + 1)

    def arrived(c):
        come_in(c + 1)
        for_groups(c + 1, spread)

    met(7)
    for c in it.all:
        it.start(c)
    send_out(0)
    for d in range(3):
        to_place(d).start()
    stages = (
        it.begin, it.second, reduced, settled, arrived,
        lambda c: for_groups(c + 1, pass_on), lambda c: for_groups(c + 1, last),
    )
    chunks = len(sizes)
    for tick in range(chunks + len(stages) - 1):
        for index, stage in enumerate(stages):
            if 0 <= tick - index < chunks:
                stage(tick - index)
        if tick == 0:
            come_in(0)
            for_groups(0, spread)
            for d in range(3):
                to_place(d).wait_recv()
            s_core[0] = small[place] + (s_tm[0] + s_tm[1]) + s_tm[2]
            to_sibling().start()
        if tick == 1:
            to_sibling().wait_recv()
            s_z[level] = s_core[0] + s_core[1]
            for d in range(3):
                to_level(d).start()
        if tick == 2:
            for_groups(0, pass_on)
        if tick == 3:
            for_groups(0, last)
    for d in range(3):
        to_level(d).wait_recv()
    small_sum[...] = (s_z[0] + s_z[1]) + (s_z[2] + s_z[3])
    owned_o[...] = owned[...]
    for_groups(None, finish)
    for c in it.all:
        it.square_end(c)
        for i in range(3):
            it.direct(c, i).wait_send()
    sent_out()
    for d in range(3):
        to_place(d).wait_send()
        to_level(d).wait_send()
    to_sibling().wait_send()


def reduce_grads(first, pair, rest, small, parts, devices, slab):
    levels = devices // 2
    ffn, mix = D // BS * (FF // BS), (D // BS) ** 2
    if parts != 4 or levels != 4:
        grads = [first[: 2 * ffn], rest[: 2 * ffn], first[2 * ffn :], pair, rest[2 * ffn :]]
        owned = jnp.concatenate(grads, axis=0)
        owned = lax.psum_scatter(owned, "tm", scatter_dimension=0, tiled=True)
        owned = lax.psum_scatter(owned, "rows", scatter_dimension=1, tiled=True)
        full = lax.all_gather(owned, "rows", axis=1, tiled=True)
        small = lax.psum_scatter(small, "tm", scatter_dimension=0, tiled=True)[0]
        return full, owned, lax.psum(small, "rows")
    sizes = (3, 3, 3)
    m, chunks = first.shape[1], len(sizes)
    count = sum(len(ids) for ids in block_sets()) // parts
    runs, groups = deliveries(sizes, parts, count)
    dma = lambda *dims: pltpu.SemaphoreType.DMA(dims)
    vb = lambda *dims: pltpu.VMEM(dims + (slab, BS), bf16)
    vmem = pl.BlockSpec(memory_space=pltpu.VMEM)
    part = small.shape[1:]
    full, owned, small_sum = pl.pallas_call(
        partial(reduce_kernel, sizes, runs, groups),
        in_specs=[ANY, vmem, vmem, vmem],
        out_specs=[ANY, vmem, vmem],
        out_shape=[
            shape((count, 2, 2, 2, slab, BS), bf16),
            shape((count, slab, BS), bf16),
            shape(part),
        ],
        scratch_shapes=square_bufs(m, parts, levels, slab)
        + [vb(m, 2, 2), vb(3, m), vb(m), vb(count), vm(3, *part), vm(2, *part), vm(levels, *part)]
        + [dma(len(runs)), dma(len(runs)), dma(len(groups), 3), dma(len(groups), 3)]
        + [dma(len(groups), 4), dma(len(groups), 4), dma(7), dma(7), dma(len(groups))]
        + reduce_sems(R_XY, chunks)
        + [dma(chunks, 3)] * 2,
        compiler_params=pltpu.CompilerParams(
            collective_id=2, has_side_effects=True, vmem_limit_bytes=VMEM_BYTES
        ),
        name="reduce_grads",
    )(first, pair, rest, small)
    return full.reshape(count, BS, BS), owned, small_sum


def row_spec(frames, width, per=1):
    return pl.BlockSpec((per, frames, width), lambda i: (i, 0, 0))


def whole_spec(*dims):
    return pl.BlockSpec(dims, lambda i: (0,) * len(dims))


def talking(number):
    return pltpu.CompilerParams(
        dimension_semantics=("arbitrary",),
        vmem_limit_bytes=VMEM_BYTES,
        collective_id=number,
        has_side_effects=True,
    )


def body(
    features,
    cotangent,
    state_bank,
    state_source,
    master,
    left_stats,
    right_stats,
    left_root,
    right_root,
    small_params,
    decay_logs,
    state_mix,
):
    rows, frames, width = features.shape
    tokens = rows * frames
    parts = lax.axis_size("tm")
    place = lax.axis_index("tm")
    scaling = 1.0 / math.sqrt(tokens * parts * lax.axis_size("rows"))
    ffn, mix = D // BS * (FF // BS), (D // BS) ** 2

    own_heads, own_channels = decay_logs.shape[0], state_mix.shape[1]
    mix_t = state_mix.transpose(0, 2, 1)
    bank_t = state_bank.transpose(0, 2, 1)
    devices = lax.axis_size("rows")
    levels = devices // 2
    spread_out = parts == 4
    if spread_out:
        first, pair, rest, packed = gather_first(
            master, bank_t, mix_t, decay_logs, state_source, parts, devices
        )
        first = first.reshape(-1, BS, BS)
        pair_out, rest_out = [shape(pair.shape, bf16)], [shape(rest.shape, bf16)]
        any_one, pair_in, rest_in = [ANY], [pair], [rest]
        pair_sems, rest_sems = gather_sems(XY_SEMS, levels), gather_sems(XY_SEMS, levels, 2)
    else:
        stack = lax.all_gather(master.astype(bf16), "rows", axis=1, tiled=True)
        stack = lax.all_gather(stack, "tm", axis=0, tiled=True)
        logs_own = jnp.pad(decay_logs, ((0, 8 - own_heads), (0, own_channels - NST)))
        params = [bank_t[state_source].reshape(-1, own_channels), mix_t.reshape(-1, own_channels)]
        packed = lax.all_gather(jnp.concatenate(params + [logs_own], axis=0), "tm", axis=0)
        first, pair, rest = (stack[jnp.array(ids)] for ids in block_sets())
        pair_out = rest_out = any_one = pair_in = rest_in = pair_sems = rest_sems = []

    mix_row = rows
    logs_row = (rows + 2) * NST // 8
    per_group = LANES // own_channels
    wide = lambda at_row: pl.BlockSpec((parts, NST, own_channels), lambda i: (0, at_row, 0))
    narrow = lambda at_row: pl.BlockSpec((per_group, NST, own_channels), lambda i: (i, at_row, 0))
    starts_spec = pl.BlockSpec((parts, NST, own_channels), lambda i: (0, i, 0))
    logs_spec = pl.BlockSpec((parts, 8, own_channels), lambda i: (0, logs_row, 0))
    logs_part = pl.BlockSpec((per_group, 8, own_channels), lambda i: (i, logs_row, 0))
    all_params = [wide(mix_row), wide(mix_row + 1), logs_spec]
    part_params = [logs_part, narrow(mix_row), narrow(mix_row + 1)]

    mat = lambda r, c: vm(r, c, dtype=bf16)
    dma = pltpu.SemaphoreType.DMA
    group = 3 if rows % 3 == 0 else 1
    small_spec = whole_spec(*small_params.shape)
    state_spec = pl.BlockSpec((1, NST, D), lambda i: (i, 0, 0))
    states_spec = pl.BlockSpec((parts, 1, NST, D), lambda i: (0, i, 0, 0))
    flat_spec = whole_spec(NST, D)
    x1, inner_a, act_a, u, ends, *done = pl.pallas_call(
        ffa_forward_kernel,
        grid=(rows // BOTH,),
        in_specs=[row_spec(frames, D, BOTH), small_spec, ANY, logs_spec]
        + any_one,
        out_specs=[
            row_spec(frames, D, BOTH),
            row_spec(frames, FF, BOTH),
            row_spec(frames, FF, BOTH),
            row_spec(frames, D, BOTH),
            pl.BlockSpec((BOTH, NST, D), lambda i: (i, 0, 0)),
        ]
        + any_one,
        out_shape=[
            shape((rows, frames, D)),
            shape((rows, frames, FF), bf16),
            shape((rows, frames, FF), bf16),
            shape((rows, frames, D), bf16),
            shape((rows, NST, D), bf16),
        ]
        + pair_out,
        scratch_shapes=[mat(D, FF), mat(FF, D), mat(D, D), mat(frames, HEADS * NST), dma((3,))] + pair_sems,
        input_output_aliases={4: 5} if spread_out else {},
        compiler_params=talking(7) if spread_out else PARAMS,
        name="ffa_forward",
    )(features, small_params, first, packed, *pair_in)
    if spread_out:
        pair = done[0].reshape(-1, BS, BS)

    group_spec = pl.BlockSpec((rows, frames, LANES), lambda i: (0, 0, i))
    coup_spec = pl.BlockSpec((NST, LANES), lambda i: (0, i))
    swap_scratch = [dma, dma((parts - 1,)), dma((parts - 1,))]
    all_states = shape((parts, rows, NST, D), bf16)
    y_loc, ends_all, *done = pl.pallas_call(
        conv_forward_kernel,
        grid=(D // LANES,),
        in_specs=[group_spec, ANY] + part_params
        + any_one,
        out_specs=[group_spec, ANY] + any_one,
        out_shape=[shape((rows, frames, D)), all_states] + rest_out,
        scratch_shapes=[vm(SUB + frames, LANES), vm(SUB, SUB, LANES)] + swap_scratch + rest_sems,
        input_output_aliases={5: 2} if spread_out else {},
        compiler_params=talking(3),
        name="conv_forward",
    )(u, ends, packed, packed, packed, *rest_in)

    edge_spec = pl.BlockSpec((1, PAD, D), lambda i: (i, 0, 0))
    edge_scratch = [
        vm(rows, 2, PAD, D, dtype=bf16),
        vm(PAD, D, dtype=bf16),
        dma((2, rows)),
        dma((2, rows)),
        dma((2,)),
    ]
    edge_shapes = [shape((rows, PAD, D), bf16)] * 2
    ys, gated, x2, pw, g, g_low, g_high, *done = pl.pallas_call(
        mixer_out_kernel,
        grid=(rows,),
        in_specs=[
            row_spec(frames, D),
            states_spec,
            starts_spec,
        ]
        + all_params
        + [row_spec(frames, D), small_spec, ANY]
        + any_one,
        out_specs=[
            row_spec(frames, D),
            row_spec(frames, 2 * D),
            row_spec(frames, D),
            row_spec(frames, 2 * D),
            row_spec(frames, D),
            ANY,
            ANY,
        ]
        + any_one,
        out_shape=[
            shape((rows, frames, D), bf16),
            shape((rows, frames, 2 * D), bf16),
            shape((rows, frames, D)),
            shape((rows, frames, 2 * D), bf16),
            shape((rows, frames, D), bf16),
        ]
        + edge_shapes
        + rest_out,
        scratch_shapes=[mat(D, 2 * D), mat(D, 2 * D), vm(HEADS * NST, D), dma((3,))]
        + [mat(frames, HEADS * NST), vm(parts + 1, NST, D), vm(NST, D)]
        + edge_scratch
        + rest_sems,
        input_output_aliases={9: 7} if spread_out else {},
        compiler_params=talking(4),
        name="mixer_out",
    )(y_loc, ends_all, packed, packed, packed, packed, x1, small_params, pair, *done)
    if spread_out:
        rest = done[0].reshape(-1, BS, BS)

    kept = lambda *widths: [mat(group * frames, w) for w in widths]
    slab = master.shape[1]
    spread_back = spread_out and levels == 4
    sizes = [len(ids) // parts for ids in block_sets()]
    if spread_back:
        grad_shapes = [shape((parts, n, levels, 2, slab, BS), bf16) for n in sizes]
        flat_shapes = [shape((parts * n, BS, BS), bf16) for n in sizes]
    else:
        flat_shapes = [shape((len(ids), BS, BS), bf16) for ids in block_sets()]
    unflat = lambda v, k: v.reshape(grad_shapes[k].shape) if spread_back else v
    layer_out, dx3, dq, grads_rest, gain_b, d_low, d_high = pl.pallas_call(
        partial(ffb_kernel, scaling),
        grid=(rows,),
        in_specs=[
            row_spec(frames, D),
            edge_spec,
            edge_spec,
            row_spec(frames, D),
            row_spec(frames, D),
            small_spec,
            ANY,
        ],
        out_specs=[
            row_spec(frames, D),
            row_spec(frames, D),
            row_spec(frames, D),
            ANY,
            whole_spec(2, 8, D),
            ANY,
            ANY,
        ],
        out_shape=[
            shape((rows, frames, D), bf16),
            shape((rows, frames, D)),
            shape((rows, frames, D), bf16),
            flat_shapes[2],
            shape((2, 8, D)),
        ]
        + edge_shapes,
        scratch_shapes=[
            mat(D, FF),
            mat(FF, D),
            mat(D, D),
            vm(D, FF),
            vm(D, FF),
            vm(D, D),
            vm(D // LANES, frames + 2 * PAD, LANES),
            vm(frames, D),
            vm(2 * ffn + mix, BS, BS, dtype=bf16),
        ]
        + kept(FF, FF, D, D, D, D)
        + [dma((3,))]
        + edge_scratch,
        compiler_params=talking(5),
        name="ffb",
    )(g, g_low, g_high, x2, cotangent, small_params, rest)

    dx2, dy, back_ends, grads_pair, gain_c, kernel_grads, *red_rest = pl.pallas_call(
        partial(mixer_back_kernel, scaling),
        grid=(rows,),
        in_specs=[
            row_spec(frames, D),
            edge_spec,
            edge_spec,
            row_spec(frames, D),
            edge_spec,
            edge_spec,
            row_spec(frames, 2 * D),
            row_spec(frames, D),
            row_spec(frames, 2 * D),
            row_spec(frames, D),
            row_spec(frames, D),
            small_spec,
            ANY,
            logs_spec,
        ]
        + [ANY] * spread_back,
        out_specs=[
            row_spec(frames, D),
            row_spec(frames, D),
            state_spec,
            ANY,
            whole_spec(8, D),
            whole_spec(16, D),
        ]
        + [whole_spec(sizes[2], 2, 2, slab, BS)] * spread_back,
        out_shape=[
            shape((rows, frames, D)),
            shape((rows, frames, D), bf16),
            shape((rows, NST, D), bf16),
            flat_shapes[1],
            shape((8, D)),
            shape((16, D)),
        ]
        + [shape((sizes[2], 2, 2, slab, BS), bf16)] * spread_back,
        scratch_shapes=[
            mat(D, 2 * D),
            mat(D, 2 * D),
            vm(D, 2 * D),
            vm(D, 2 * D),
            vm(D // LANES, frames + 2 * PAD, LANES),
            vm(D // LANES, frames + 2 * PAD, LANES),
            vm(frames, D),
            vm(KW, 8, D),
            vm(4 * mix, BS, BS, dtype=bf16),
        ]
        + kept(D, 2 * D, D, 2 * D)
        + [mat(frames, HEADS * NST), dma((3,))]
        + (square_bufs(sizes[2], parts, levels, slab) + reduce_sems(R_XY, 2)) * spread_back,
        compiler_params=talking(8) if spread_back else PARAMS,
        name="mixer_back",
    )(
        dq, d_low, d_high, g, g_low, g_high, pw, x2, gated, ys, dx3, small_params, pair,
        packed, *[unflat(grads_rest, 2)] * spread_back,
    )

    nst_spec = pl.BlockSpec((rows, NST, LANES), lambda i: (0, 0, i))
    du_loc, t_one, t_two, ends_w, back_w, back_all = pl.pallas_call(
        conv_back_kernel,
        grid=(D // LANES,),
        in_specs=[group_spec, group_spec, ANY] + part_params,
        out_specs=[
            group_spec,
            coup_spec,
            coup_spec,
            nst_spec,
            nst_spec,
            ANY,
        ],
        out_shape=[
            shape((rows, frames, D)),
            shape((NST, D)),
            shape((NST, D)),
            shape((rows, NST, D)),
            shape((rows, NST, D)),
            all_states,
        ],
        scratch_shapes=[
            vm(SUB + frames, LANES),
            vm(SUB + frames, LANES),
            vm(SUB, SUB, LANES),
            vm(SUB, SUB, LANES),
        ]
        + swap_scratch,
        compiler_params=talking(6),
        name="conv_back",
    )(u, dy, back_ends, packed, packed, packed)

    small_rows = -(-small_params.shape[0] // 8) * 8 + 3 * NST
    grad_zero, grads_first, small_all, *shares = pl.pallas_call(
        partial(ffa_back_kernel, scaling),
        grid=(rows,),
        in_specs=[
            row_spec(frames, D),
            states_spec,
            states_spec,
            state_spec,
            state_spec,
            state_spec,
            starts_spec,
        ]
        + all_params
        + [
            flat_spec,
            flat_spec,
            whole_spec(2, 8, D),
            whole_spec(8, D),
            whole_spec(16, D),
            row_spec(frames, D),
            row_spec(frames, D),
            row_spec(frames, FF),
            row_spec(frames, FF),
            row_spec(frames, D),
            small_spec,
            ANY,
        ]
        + [ANY, whole_spec(sizes[2], 2, 2, slab, BS)] * spread_back,
        out_specs=[row_spec(frames, D), ANY, whole_spec(parts, small_rows, own_channels)]
        + [whole_spec(n, slab, BS) for n in sizes[1:]] * spread_back,
        out_shape=[
            shape((rows, frames, D)),
            flat_shapes[0],
            shape((parts, small_rows, own_channels)),
        ]
        + [shape((n, slab, BS), bf16) for n in sizes[1:]] * spread_back,
        scratch_shapes=[
            mat(D, FF),
            mat(FF, D),
            mat(D, D),
            vm(D, FF),
            vm(D, FF),
            vm(D, D),
            vm(HEADS * NST, D),
            vm(2 * ffn + mix, BS, BS, dtype=bf16),
        ]
        + kept(FF, FF, D, D, D, D)
        + [dma((3,)), vm(2, 8, D), vm(4, NST, D), mat(frames, HEADS * NST)]
        + [vm(3, parts, NST, D), vm(NST, D)]
        + (
            [vm(sizes[2], 2, 2, slab, BS, dtype=bf16)]
            + level_bufs(sizes[2], slab)
            + [vm(sizes[1], 2, 2, slab, BS, dtype=bf16)]
            + square_bufs(sizes[1], parts, levels, slab)
            + level_bufs(sizes[1], slab)
            + reduce_sems(R_XY + R_Z + R_Z)
        )
        * spread_back,
        compiler_params=talking(9) if spread_back else PARAMS,
        name="ffa_back",
    )(
        du_loc, back_all, ends_all, back_ends, ends_w, back_w, packed, packed, packed, packed,
        t_one, t_two, gain_b, gain_c, kernel_grads,
        x1, features, inner_a, act_a, dx2, small_params, first,
        *([unflat(grads_pair, 1)] + red_rest) * spread_back,
    )

    full_grad, owned, sums = reduce_grads(
        unflat(grads_first, 0),
        *(shares if spread_back else (grads_pair, grads_rest)),
        small_all,
        parts,
        devices,
        slab,
    )
    count, slice_rows = owned.shape[0], owned.shape[1]
    group = 11 if count % 11 == 0 else 1
    part_spec = pl.BlockSpec((group, slice_rows, BS), lambda i: (i, 0, 0))
    full_spec = pl.BlockSpec((group, BS, BS), lambda i: (i, 0, 0))
    small_shape = (small_params.shape[0], own_channels)
    carry_spec = row_spec(frames, D, rows * group // count)
    small_outs = [small_shape, small_shape, decay_logs.shape, mix_t.shape]
    small_outs += [decay_logs.shape, mix_t.shape, bank_t.shape]
    new_left, new_right, new_master, new_copy, grad_blocks, *others = pl.pallas_call(
        partial(shampoo_kernel, frames),
        grid=(count // group,),
        in_specs=[
            pl.BlockSpec(memory_space=pltpu.SMEM),
            part_spec,
            full_spec,
            part_spec,
            part_spec,
            part_spec,
            full_spec,
            part_spec,
            whole_spec(*sums.shape),
            whole_spec(*small_params.shape),
            whole_spec(*decay_logs.shape),
            whole_spec(*mix_t.shape),
            whole_spec(*back_all.shape),
            carry_spec,
            carry_spec,
        ],
        out_specs=[part_spec] * 5 + [whole_spec(*dims) for dims in small_outs]
        + [carry_spec] * 2,
        out_shape=[
            shape(owned.shape),
            shape(owned.shape),
            shape(owned.shape),
            shape(owned.shape, bf16),
            shape(owned.shape),
        ]
        + [shape(dims) for dims in small_outs]
        + [shape(layer_out.shape, bf16), shape(grad_zero.shape)],
        compiler_params=PARAMS,
        name="shampoo",
    )(
        state_source, owned, full_grad, left_stats, right_stats, left_root, right_root, master,
        sums, small_params, decay_logs, mix_t, back_all, layer_out, grad_zero,
    )
    *small_results, grad_state, layer_out, grad_zero = others
    for i in (3, 5):
        small_results[i] = small_results[i].transpose(0, 2, 1)
    grad_state = grad_state.transpose(0, 2, 1)
    return (
        layer_out,
        grad_zero,
        grad_state,
        grad_blocks,
        new_left,
        new_right,
        new_master,
        new_copy,
        *small_results,
    )


def solution(mesh):
    return jax.shard_map(
        body,
        mesh=mesh,
        in_specs=(
            P("rows", "tm", None),
            P("rows", "tm", None),
            P("rows", "tm", None),
            P("rows"),
            P("tm", "rows", None),
            P("tm", "rows", None),
            P("tm", "rows", None),
            P("tm", "rows", None),
            P("tm", None, None),
            P(),
            P("tm", None),
            P(None, "tm", None),
        ),
        out_specs=(
            P("rows", "tm", None),
            P("rows", "tm", None),
            P("rows", "tm", None),
            P("tm", "rows", None),
            P("tm", "rows", None),
            P("tm", "rows", None),
            P("tm", "rows", None),
            P("tm", "rows", None),
            P(None, "tm"),
            P(None, "tm"),
            P("tm", None),
            P(None, "tm", None),
            P("tm", None),
            P(None, "tm", None),
        ),
        check_vma=False,
    )
```

```python
from functools import partial
import math

import jax
import jax.numpy as jnp
from jax import lax
from jax.experimental import pallas as pl
from jax.experimental.pallas import tpu as pltpu
from jax.sharding import PartitionSpec as P

D = 512
FF = 2048
NST = 32
KW = 15
BS = 256
HEADS = 8
HALF = 64
LANES = 128
SUB = 16
GROUP = 5
BOTH = 2
PAD = 8
VMEM_BYTES = 60 * 1024 * 1024

rate_blocks = 0.1
rate_small = 0.5
bf16 = jnp.bfloat16
f32 = jnp.float32


def shape(dims, dtype=f32):
    return jax.ShapeDtypeStruct(dims, dtype)


def mm(a, b):
    return jnp.dot(a, b, preferred_element_type=f32)


def mm_nt(a, b):
    return lax.dot_general(a, b, (((1,), (1,)), ((), ())), preferred_element_type=f32)


def mm_tn(a, b):
    return lax.dot_general(a, b, (((0,), (0,)), ((), ())), preferred_element_type=f32)


def sigmoid(v):
    return 0.5 * jnp.tanh(0.5 * v) + 0.5


def norm(v):
    center = v - jnp.mean(v, axis=-1, keepdims=True)
    spread = jnp.mean(center * center, axis=-1, keepdims=True)
    inv = lax.rsqrt(spread + 1e-05)
    return center * inv, inv


def norm_back(hat, inv, scale, incoming):
    scaled = incoming * scale
    mean_one = jnp.mean(scaled, axis=-1, keepdims=True)
    mean_two = jnp.mean(scaled * hat, axis=-1, keepdims=True)
    return inv * (scaled - mean_one - hat * mean_two)


def flat(ref):
    v = ref[...]
    return v.reshape(-1, v.shape[-1])


def put_rows(ref, v):
    ref[...] = v.astype(ref.dtype).reshape(ref.shape)


def fold8(v):
    return jnp.sum(v.reshape(-1, 8, v.shape[-1]), axis=0)


class Matrices:
    def __init__(self, stack, plan, sem):
        self.copies = []
        for index, (first, dst) in enumerate(plan):
            across = dst.shape[1] // BS
            spots = [(i, j) for i in range(dst.shape[0] // BS) for j in range(across)]
            self.copies.append(
                [
                    pltpu.make_async_copy(
                        stack.at[first + i * across + j],
                        dst.at[pl.ds(i * BS, BS), pl.ds(j * BS, BS)],
                        sem.at[index],
                    )
                    for i, j in spots
                ]
            )

    def start(self):
        for copies in self.copies:
            for copy in copies:
                copy.start()

    def wait(self, index):
        for copy in self.copies[index]:
            copy.wait()


def store_blocks(plan, scaling, grads, stage, sem):
    copies = []
    for acc, first, transposed in plan:
        rows, cols = acc.shape
        down, across = (cols, rows) if transposed else (rows, cols)
        for i in range(down // BS):
            for j in range(across // BS):
                slot = len(copies)
                if transposed:
                    part = (acc[pl.ds(j * BS, BS), pl.ds(i * BS, BS)] * scaling).T
                else:
                    part = acc[pl.ds(i * BS, BS), pl.ds(j * BS, BS)] * scaling
                stage[slot] = part.astype(bf16)
                copy = pltpu.make_async_copy(
                    stage.at[slot], grads.at[first + i * (across // BS) + j], sem
                )
                copy.start()
                copies.append(copy)
    for copy in copies:
        copy.wait()


def head_mask():
    row = lax.broadcasted_iota(jnp.int32, (HEADS * NST, D), 0) // NST
    col = lax.broadcasted_iota(jnp.int32, (HEADS * NST, D), 1) // HALF
    return (row == col).astype(f32)


def spread_heads(v, mask):
    return (jnp.concatenate([v] * HEADS, axis=0) * mask).astype(bf16)


def join_lanes(ref):
    return jnp.concatenate([ref[i] for i in range(ref.shape[0])], axis=1)


def rate_rows(logs):
    own = logs.shape[2] // HALF
    places = range(logs.shape[0])
    return [jnp.exp(logs[p, j : j + 1, 0:NST]) for p in places for j in range(own)]


def as_column(row):
    down = lax.broadcasted_iota(jnp.int32, (NST, NST), 0)
    across = lax.broadcasted_iota(jnp.int32, (NST, NST), 1)
    return jnp.sum(jnp.where(down == across, row, 0.0), axis=1, keepdims=True)


def channel_rates(logs):
    first = lax.broadcasted_iota(jnp.int32, (NST, LANES), 1) < HALF
    columns = [as_column(row) for row in rate_rows(logs)]
    pairs = zip(columns[0::2], columns[1::2])
    return jnp.concatenate([jnp.where(first, a, b) for a, b in pairs], axis=1)


def frame_decay(logs, table, to_end):
    frames = table.shape[0]
    rates = jnp.concatenate(rate_rows(logs), axis=1)
    time = lax.broadcasted_iota(jnp.int32, table.shape, 0)
    length = frames - 1 - time if to_end else time + 1
    table[...] = jnp.exp(-rates * length.astype(f32)).astype(bf16)


def passing(rates, apart, frames):
    length = (apart * frames).astype(f32)
    weight = jnp.where(apart >= 0, jnp.exp(-rates * jnp.maximum(length, 0.0)), 0.0)
    return weight, weight * length


def local_states(table, v, out):
    frames = table.shape[0]
    first = lax.broadcasted_iota(jnp.int32, (NST, LANES), 1) < HALF
    for b in range(out.shape[0]):
        for q in range(D // (2 * LANES)):
            here = v[b * frames : (b + 1) * frames, 2 * q * LANES : 2 * (q + 1) * LANES]
            four = mm_tn(table[:, q * LANES : (q + 1) * LANES], here)
            for i in range(2):
                both = four[2 * i * NST : 2 * (i + 1) * NST, i * LANES : (i + 1) * LANES]
                picked = jnp.where(first, both[:NST], both[NST:])
                out[b, :, pl.ds((2 * q + i) * LANES, LANES)] = picked.astype(out.dtype)


def chunk_tables(row):
    column = as_column(row)
    span = GROUP * SUB
    time = lax.broadcasted_iota(jnp.int32, (NST, span), 1)
    since = (time % SUB + 1).astype(f32)
    into, into_w, out, out_w, power = [], [], [], [], []
    for i in range(GROUP):
        age = SUB * (i + 1) - 1 - time
        age_f = jnp.maximum(age, 0).astype(f32)
        value = jnp.where(age >= 0, jnp.exp(-column * age_f), 0.0)
        into.append(value)
        into_w.append(value * age_f)
        value = jnp.where(time // SUB == i, jnp.exp(-column * since), 0.0)
        out.append(value)
        out_w.append(value * since)
        power.append(jnp.exp(-column * float(SUB * (i + 1))))
    join = lambda parts: jnp.concatenate(parts, axis=0).astype(bf16)
    return join(into), join(into_w), join(out), join(out_w), power


def lag_taps(rates, coup, taps, backward):
    place = lax.broadcasted_iota(jnp.int32, (SUB, LANES), 0)
    for d in range(SUB):
        lag = jnp.sum(coup * jnp.exp(-rates * float(d)), axis=0, keepdims=True)
        inside = place + d < SUB if backward else place >= d
        taps[d] = jnp.where(inside, lag, 0.0)


ANY = pl.BlockSpec(memory_space=pl.ANY)
PARAMS = pltpu.CompilerParams(
    dimension_semantics=("arbitrary",), vmem_limit_bytes=VMEM_BYTES
)


def vm(*dims, dtype=f32):
    return pltpu.VMEM(dims, dtype)


def peers():
    place, row = lax.axis_index("tm"), lax.axis_index("rows")
    return place, row // 2, row % 2


def square(place):
    x, y = place % 2, place // 2
    return 2 * y + 1 - x, 2 * (1 - y) + x, 2 * (1 - y) + 1 - x


def at(place, level, core):
    return {"tm": place, "rows": level * 2 + core}


def remote(src, dst, send, recv, device):
    return pltpu.make_async_remote_copy(
        src_ref=src,
        dst_ref=dst,
        send_sem=send,
        recv_sem=recv,
        device_id=device,
        device_id_type=pl.DeviceIdType.MESH,
    )


def signal(sem, device):
    pl.semaphore_signal(sem, inc=1, device_id=device, device_id_type=pl.DeviceIdType.MESH)


def chunk_ranges(count, chunks):
    edges = [count * c // chunks for c in range(chunks + 1)]
    out = []
    for first, end in zip(edges[:-1], edges[1:]):
        middle = (first + end + 1) // 2
        out.append((first, end, middle))
    return out


class Gather:
    def __init__(self, piece, stack, sems, chunks=1):
        self.piece, self.stack, self.sems = piece, stack, sems
        self.place, self.level, self.core = peers()
        self.xp, self.yp, self.dp = square(self.place)
        self.levels = stack.shape[2]
        self.ranges = chunk_ranges(stack.shape[1], chunks)
        self.all = range(chunks)

    def own(self, c):
        first, end, unused = self.ranges[c]
        n = pl.ds(first, end - first)
        spot = self.stack.at[self.place, n, self.level, self.core]
        return pltpu.make_async_copy(self.piece.at[n], spot, self.sems["own"].at[c])

    def z(self, c, d):
        first, end, unused = self.ranges[c]
        n = pl.ds(first, end - first)
        spot = self.stack.at[self.place, n, self.level, self.core]
        send, recv = self.sems["zs"].at[c, d - 1], self.sems["zr"].at[c, d - 1]
        target = (self.level + d) % self.levels
        return remote(self.piece.at[n], spot, send, recv, at(self.place, target, self.core))

    def z_start(self, c):
        self.own(c).start()
        for d in range(1, self.levels):
            self.z(c, d).start()

    def z_arrive(self, c):
        self.own(c).wait()
        for d in range(1, self.levels):
            self.z(c, d).wait_recv()

    def z_end(self, c):
        for d in range(1, self.levels):
            self.z(c, d).wait_send()

    def part(self, name, c, i, owner, first, end, device):
        spot = self.stack.at[owner, pl.ds(first, end - first), :, self.core]
        send, recv = self.sems[name + "s"].at[c, i], self.sems[name + "r"].at[c, i]
        return remote(spot, spot, send, recv, device)

    def x(self, c, i):
        first, end, mid = self.ranges[c]
        what = ((self.place, first, mid), (self.place, mid, end), (self.yp, mid, end))[i]
        return self.part("x", c, i, *what, at(self.xp, self.level, self.core))

    def y(self, c, i):
        first, end, mid = self.ranges[c]
        what = ((self.place, mid, end), (self.place, first, mid), (self.xp, first, mid))[i]
        return self.part("y", c, i, *what, at(self.yp, self.level, self.core))

    def other(self, c, i):
        first, end, mid = self.ranges[c]
        what = (
            (self.place, first, end),
            (self.xp, first, mid),
            (self.yp, mid, end),
            (self.xp, mid, end),
            (self.yp, first, mid),
            (self.dp, first, mid),
            (self.dp, mid, end),
        )[i]
        return self.part("c", c, i, *what, at(self.place, self.level, 1 - self.core))

    def spread(self, c):
        for copy in (self.x(c, 0), self.y(c, 0), self.x(c, 1), self.y(c, 1), self.other(c, 0)):
            copy.start()

    def forward(self, c):
        self.x(c, 0).wait_recv()
        self.y(c, 2).start()
        self.y(c, 0).wait_recv()
        self.x(c, 2).start()
        self.other(c, 1).start()
        self.other(c, 2).start()
        self.x(c, 1).wait_recv()
        self.other(c, 3).start()
        self.y(c, 1).wait_recv()
        self.other(c, 4).start()

    def finish(self, c):
        self.y(c, 2).wait_recv()
        self.other(c, 5).start()
        self.x(c, 2).wait_recv()
        self.other(c, 6).start()

    def end(self, c):
        for i in range(7):
            self.other(c, i).wait_recv()
        for i in range(7):
            self.other(c, i).wait_send()
        for i in range(3):
            self.x(c, i).wait_send()
            self.y(c, i).wait_send()


Z_SEMS = ("own", "zs", "zr")
XY_SEMS = ("xs", "xr", "ys", "yr", "cs", "cr")


def gather_sems(names, levels, chunks=1):
    width = {"own": (), "z": (levels - 1,), "x": (3,), "y": (3,), "c": (7,)}
    key = lambda name: name if name == "own" else name[0]
    return [pltpu.SemaphoreType.DMA((chunks,) + width[key(name)]) for name in names]


def block_sets():
    ffn, mix = D // BS * (FF // BS), (D // BS) ** 2
    ids = lambda *ranges: [b for first, end in ranges for b in range(first, end)]
    return (
        ids((0, 2 * ffn), (4 * ffn, 4 * ffn + mix)),
        ids((4 * ffn + mix, 4 * ffn + 5 * mix)),
        ids((2 * ffn, 4 * ffn), (4 * ffn + 5 * mix, 4 * ffn + 6 * mix)),
    )


def move_runs(ids, places, count):
    runs, each = [], len(ids) // places
    for index, b in enumerate(ids):
        owner, k, v, j = b // count, b % count, index // each, index % each
        if runs:
            o0, k0, v0, j0, n0 = runs[-1]
            if (o0, v0) == (owner, v) and k0 + n0 == k:
                runs[-1] = (o0, k0, v0, j0, n0 + 1)
                continue
        runs.append((owner, k, v, j, 1))
    return runs


def greet(devices):
    barrier = pltpu.get_barrier_semaphore()
    for device in devices:
        signal(barrier, device)


def met(count):
    pl.semaphore_wait(pltpu.get_barrier_semaphore(), count)


def gather_kernel(
    source, master, bank, mix_terms, logs, first, pair, rest, pack_all,
    pack, rounded, piece, piece_pair, piece_rest, run_send, run_recv, pk_send, pk_recv, *sems,
):
    place, level, core = peers()
    others = square(place)
    levels = first.shape[2]
    greet([at(other, level, core) for other in others] + [at(place, level, 1 - core)])
    greet([at(place, (level + d) % levels, core) for d in range(1, levels)])
    rounded[...] = master[...].astype(bf16)
    count = bank.shape[0]
    for i in range(count):
        pack[i * NST : (i + 1) * NST] = bank[source[i]]
    for i in range(2):
        pack[(count + i) * NST : (count + i + 1) * NST] = mix_terms[i]
    pack[(count + 2) * NST :] = jnp.zeros((8, pack.shape[1]), f32)
    pack[(count + 2) * NST : (count + 2) * NST + logs.shape[0], 0:NST] = logs[...]
    met(3 + levels)
    moves = []
    for ids, target in zip(block_sets(), (piece, piece_pair, piece_rest)):
        for run in move_runs(ids, first.shape[0], master.shape[0]):
            moves.append((len(moves), target) + run)

    def move(index, target, owner, k, v, j, n):
        src, dst = rounded.at[pl.ds(k, n)], target.at[pl.ds(j, n)]
        if owner == v:
            return pltpu.make_async_copy(src, dst, run_send.at[index])
        return remote(src, dst, run_send.at[index], run_recv.at[index], at(v, level, core))

    def arrive(entry):
        index, target, owner, k, v, j, n = entry
        if owner == v:
            pl.when(place == v)(lambda: move(*entry).wait())
        else:
            pl.when(place == v)(lambda: move(*entry).wait_recv())

    for entry in moves:
        pl.when(place == entry[2])(lambda entry=entry: move(*entry).start())
    own_pack = pltpu.make_async_copy(pack, pack_all.at[place], pk_send.at[3])
    own_pack.start()
    packs = [
        remote(pack, pack_all.at[place], pk_send.at[d], pk_recv.at[d], at(other, level, core))
        for d, other in enumerate(others)
    ]
    for copy in packs:
        copy.start()
    for entry in moves:
        if entry[1] is piece:
            arrive(entry)
    names = Z_SEMS + XY_SEMS
    chunks = sems[0].shape[0]
    it = Gather(piece, first, dict(zip(names, sems)), chunks)
    later, sems = [], sems[len(names) :]
    for i, (what, stack) in enumerate(((piece_pair, pair), (piece_rest, rest))):
        later.append(Gather(what, stack, dict(zip(Z_SEMS, sems[3 * i : 3 * i + 3]))))
    it.z_start(0)
    for c in it.all:
        it.z_arrive(c)
        it.spread(c)
        if c == 0:
            for ahead in range(1, chunks):
                it.z_start(ahead)
            for entry in moves:
                if entry[1] is not piece:
                    arrive(entry)
        if c == chunks - 1:
            for other_set in later:
                other_set.z_start(0)
        if c >= 1:
            it.forward(c - 1)
        if c >= 2:
            it.finish(c - 2)
    it.forward(chunks - 1)
    for c in range(max(chunks - 2, 0), chunks):
        it.finish(c)
    for c in it.all:
        it.end(c)
        it.z_end(c)
    for other_set in later:
        other_set.z_arrive(0)
        other_set.z_end(0)
    for entry in moves:
        if entry[2] != entry[4]:
            pl.when(place == entry[2])(lambda entry=entry: move(*entry).wait_send())
    own_pack.wait()
    for copy in packs:
        copy.wait()


def gather_first(master, bank, mix_terms, logs, source, parts, devices, chunks=3):
    count, slab, cols = master.shape
    levels = devices // 2
    each = [len(ids) // parts for ids in block_sets()]
    runs = sum(len(move_runs(ids, parts, count)) for ids in block_sets())
    dma = lambda *dims: pltpu.SemaphoreType.DMA(dims)
    pack = ((bank.shape[0] + 2) * NST + 8, bank.shape[2])
    return pl.pallas_call(
        gather_kernel,
        in_specs=[pl.BlockSpec(memory_space=pltpu.SMEM)]
        + [pl.BlockSpec(memory_space=pltpu.VMEM)] * 4,
        out_specs=[ANY] * 4,
        out_shape=[
            shape((parts, each[0], levels, 2, slab, cols), bf16),
            shape((parts, each[1], levels, 2, slab, cols), bf16),
            shape((parts, each[2], levels, 2, slab, cols), bf16),
            shape((parts,) + pack),
        ],
        scratch_shapes=[
            vm(*pack),
            vm(count, slab, cols, dtype=bf16),
            vm(each[0], slab, cols, dtype=bf16),
            vm(each[1], slab, cols, dtype=bf16),
            vm(each[2], slab, cols, dtype=bf16),
            dma(runs),
            dma(runs),
            dma(4),
            dma(3),
        ]
        + gather_sems(Z_SEMS + XY_SEMS, levels, chunks)
        + gather_sems(Z_SEMS, levels) * 2,
        compiler_params=pltpu.CompilerParams(
            collective_id=1, has_side_effects=True, vmem_limit_bytes=VMEM_BYTES
        ),
        name="gather_first",
    )(source, master, bank, mix_terms, logs)


R_XY = ("load", "cs", "cr", "xs", "xr", "ys", "yr")
R_Z = ("zs", "zr")


def reduce_sems(names, chunks=1):
    width = {"x": (3,), "y": (3,), "z": (3,)}
    dims = lambda name: width.get(name[0], ())
    return [pltpu.SemaphoreType.DMA((chunks,) + dims(name)) for name in names]


def square_bufs(m, parts, levels, slab):
    vb = lambda *dims: pltpu.VMEM(dims + (slab, BS), bf16)
    return [vb(parts, m, levels)] * 2 + [vb(2, m, levels)] * 2


def level_bufs(m, slab):
    vb = lambda *dims: pltpu.VMEM(dims + (slab, BS), bf16)
    return [vb(m, 2), vb(m)]


class Reduce:
    def __init__(self, sizes, sems, grads=None, square_refs=None, red=None, level_refs=None, out=None):
        self.sems, self.grads, self.red, self.out = sems, grads, red, out
        if square_refs is not None:
            self.mine, self.came, self.from_x, self.from_y = square_refs
        if level_refs is not None:
            self.near_in, self.far_in = level_refs
        self.place, self.level, self.core = peers()
        self.xp, self.yp, self.dp = square(self.place)
        self.low, self.high = self.level % 2, self.level // 2
        self.near_by = self.level + 1 - 2 * self.low
        self.far_off = self.level + 2 - 4 * self.high
        edges = [sum(sizes[:c]) for c in range(len(sizes) + 1)]
        self.ranges = [(a, b, (a + b + 1) // 2) for a, b in zip(edges[:-1], edges[1:])]
        self.all = range(len(sizes))

    def n(self, c):
        first, end, unused = self.ranges[c]
        return pl.ds(first, end - first)

    def load(self, c):
        src = self.grads.at[:, self.n(c), :, self.core]
        return pltpu.make_async_copy(src, self.mine.at[:, self.n(c)], self.sems["load"].at[c])

    def swap(self, c):
        return remote(
            self.grads.at[:, self.n(c), :, 1 - self.core],
            self.came.at[:, self.n(c)],
            self.sems["cs"].at[c],
            self.sems["cr"].at[c],
            at(self.place, self.level, 1 - self.core),
        )

    def side(self, c, i, name, into, device, what):
        owner, slot, first, end = what
        n = pl.ds(first, end - first)
        send, recv = self.sems[name + "s"].at[c, i], self.sems[name + "r"].at[c, i]
        return remote(self.mine.at[owner, n], into.at[slot, n], send, recv, device)

    def x(self, c, i):
        first, end, mid = self.ranges[c]
        what = ((self.dp, 0, first, mid), (self.xp, 1, first, mid), (self.xp, 1, mid, end))[i]
        return self.side(c, i, "x", self.from_x, at(self.xp, self.level, self.core), what)

    def y(self, c, i):
        first, end, mid = self.ranges[c]
        what = ((self.dp, 0, mid, end), (self.yp, 1, mid, end), (self.yp, 1, first, mid))[i]
        return self.side(c, i, "y", self.from_y, at(self.yp, self.level, self.core), what)

    def add(self, owner, first, end, ref, slot):
        def one(k, carry):
            self.mine[owner, k] = self.mine[owner, k] + ref[slot, k]
            return carry

        lax.fori_loop(first, end, one, 0)

    def start(self, c):
        self.load(c).start()
        self.swap(c).start()

    def begin(self, c):
        first, end, unused = self.ranges[c]
        self.load(c).wait()
        self.swap(c).wait_recv()
        self.add(self.dp, first, end, self.came, self.dp)
        self.x(c, 0).start()
        self.y(c, 0).start()
        self.add(self.xp, first, end, self.came, self.xp)
        self.x(c, 1).start()
        self.add(self.yp, first, end, self.came, self.yp)
        self.y(c, 1).start()
        self.add(self.place, first, end, self.came, self.place)

    def second(self, c):
        first, end, mid = self.ranges[c]
        self.x(c, 0).wait_recv()
        self.add(self.yp, first, mid, self.from_x, 0)
        self.y(c, 2).start()
        self.y(c, 0).wait_recv()
        self.add(self.xp, mid, end, self.from_y, 0)
        self.x(c, 2).start()

    def combine(self, c):
        first, end, unused = self.ranges[c]
        for i in (1, 2):
            self.x(c, i).wait_recv()
            self.y(c, i).wait_recv()

        def one(k, carry):
            total = self.mine[self.place, k].astype(f32) + self.from_x[1, k].astype(f32)
            total = (total + self.from_y[1, k].astype(f32)).astype(bf16)
            self.red[k] = total.reshape(self.red.shape[1:])
            return carry

        lax.fori_loop(first, end, one, 0)

    def square_end(self, c):
        self.swap(c).wait_send()
        for i in range(3):
            self.x(c, i).wait_send()
            self.y(c, i).wait_send()

    def near(self, c):
        return remote(
            self.red.at[self.n(c), :, 1 - self.low],
            self.near_in.at[self.n(c)],
            self.sems["zs"].at[c, 0],
            self.sems["zr"].at[c, 0],
            at(self.place, self.near_by, self.core),
        )

    def far(self, c):
        return remote(
            self.near_in.at[self.n(c), 1 - self.high],
            self.far_in.at[self.n(c)],
            self.sems["zs"].at[c, 1],
            self.sems["zr"].at[c, 1],
            at(self.place, self.far_off, self.core),
        )

    def across(self, c):
        first, end, unused = self.ranges[c]
        self.near(c).wait_recv()

        def one(k, carry):
            self.near_in[k] = self.red[k, :, self.low] + self.near_in[k]
            return carry

        lax.fori_loop(first, end, one, 0)
        self.far(c).start()

    def settle(self, c):
        first, end, unused = self.ranges[c]
        self.far(c).wait_recv()

        def one(k, carry):
            self.out[k] = self.near_in[k, self.high] + self.far_in[k]
            return carry

        lax.fori_loop(first, end, one, 0)

    def direct(self, c, i):
        high = (self.high, 1 - self.high, 1 - self.high)[i]
        low = (1 - self.low, self.low, 1 - self.low)[i]
        diagonal = 2 * (1 - self.high) + 1 - self.low
        target = (self.near_by, self.far_off, diagonal)[i]
        return remote(
            self.red.at[self.n(c), high, low],
            self.direct_in.at[i, self.n(c)],
            self.sems["zs"].at[c, i],
            self.sems["zr"].at[c, i],
            at(self.place, target, self.core),
        )

    def settle_direct(self, c):
        first, end, unused = self.ranges[c]
        for i in range(3):
            self.direct(c, i).wait_recv()

        def one(k, carry):
            total = self.red[k, self.high, self.low].astype(f32)
            for i in range(3):
                total = total + self.direct_in[i, k].astype(f32)
            self.out[k] = total.astype(bf16)
            return carry

        lax.fori_loop(first, end, one, 0)

    def levels_end(self, c):
        self.near(c).wait_send()
        self.far(c).wait_send()


def ffa_forward_kernel(feat, small, stack, logs, *refs):
    step, last = pl.program_id(0), pl.num_programs(0) - 1
    pair = None
    if len(refs) > 10:
        refs, sems = refs[1:12], refs[12:]
        pair = Gather(None, refs[5], dict(zip(XY_SEMS, sems)))
        refs = refs[:5] + refs[6:]
    x1_o, inner_o, act_o, u_o, f_o, wi, wo, wu, table, sem = refs

    @pl.when(step == 0)
    def _():
        if pair is not None:
            place, level, core = peers()
            greet([at(other, level, core) for other in square(place)])
            greet([at(place, level, 1 - core)])
        ffn, mix = D // BS * (FF // BS), (D // BS) ** 2
        weights = Matrices(stack, ((0, wi), (ffn, wo), (2 * ffn, wu)), sem)
        weights.start()
        if pair is not None:
            met(4)
            pair.spread(0)
        frame_decay(logs, table, True)
        for index in range(3):
            weights.wait(index)

    x0 = flat(feat).astype(f32)
    hat, unused = norm(x0)
    inner = mm((hat * small[0:1]).astype(bf16), wi[...])
    act = (inner * sigmoid(inner)).astype(bf16)
    put_rows(inner_o, inner)
    put_rows(act_o, act)
    x1 = x0 + 0.5 * mm(act, wo[...])
    put_rows(x1_o, x1)
    hat, unused = norm(x1)
    u = mm((hat * small[1:2]).astype(bf16), wu[...]).astype(bf16)
    put_rows(u_o, u)
    local_states(table, u, f_o)
    if pair is not None:
        pl.when(step == last - 1)(lambda: pair.forward(0))

        @pl.when(step == last)
        def _():
            pair.finish(0)
            pair.end(0)


def pack_heads(ref, rows):
    first = lax.broadcasted_iota(jnp.int32, (ref.shape[1], LANES), 1) < HALF
    low, high = [], []
    for p in range(rows // 2):
        a, b = ref[2 * p].astype(f32), ref[2 * p + 1].astype(f32)
        low.append(jnp.where(first, a, pltpu.roll(b, HALF, 1)).astype(bf16))
        high.append(jnp.where(first, pltpu.roll(a, HALF, 1), b).astype(bf16))
    return jnp.concatenate(low, axis=1), jnp.concatenate(high, axis=1)


def pack_params(v, rows):
    first = lax.broadcasted_iota(jnp.int32, v.shape, 1) < HALF
    rolled = pltpu.roll(v, HALF, 1)
    low = jnp.where(first, v, rolled)
    high = jnp.where(first, rolled, v)
    return (
        jnp.concatenate([low] * (rows // 2), axis=1),
        jnp.concatenate([high] * (rows // 2), axis=1),
    )


def unpack_pair(low, high, p):
    low = low[:, p * LANES : (p + 1) * LANES]
    high = high[:, p * LANES : (p + 1) * LANES]
    first = lax.broadcasted_iota(jnp.int32, low.shape, 1) < HALF
    return (
        jnp.where(first, low, pltpu.roll(high, HALF, 1)),
        jnp.where(first, pltpu.roll(low, HALF, 1), high),
    )


def swap_states(mine, whole, first_step, last_step, own_sem, send, recv, rest=None):
    place, level, core = peers()
    parts = whole.shape[0]
    others = [(place + d) % parts for d in range(1, parts)]

    def copies():
        return [
            remote(mine, whole.at[place], send.at[d], recv.at[d], at(other, level, core))
            for d, other in enumerate(others)
        ]

    own = lambda: pltpu.make_async_copy(mine, whole.at[place], own_sem)

    @pl.when(first_step)
    def _():
        greet([at(other, level, core) for other in others])
        if rest is not None:
            greet([at(place, level, 1 - core)])
        own().start()

    def begin():
        @pl.when(first_step)
        def _():
            met(parts - 1 + (rest is not None))
            for copy in copies():
                copy.start()
            if rest is not None:
                rest.spread(0)

    def end():
        if rest is not None:
            pl.when(pl.program_id(0) == pl.num_programs(0) - 2)(lambda: rest.forward(0))

        @pl.when(last_step)
        def _():
            if rest is not None:
                rest.finish(0)
                rest.end(0)
            own().wait()
            for copy in copies():
                copy.wait()

    return begin, end


def tile_lanes(v, width):
    return jnp.concatenate([v] * (width // LANES), axis=1)


def conv_forward_kernel(u, ends, logs, mix_one, mix_two, *refs):
    step = pl.program_id(0)
    pair = None
    if len(refs) > 7:
        refs, sems = refs[1:9], refs[9:]
        pair = Gather(None, refs[2], dict(zip(XY_SEMS, sems)), 2)
        refs = refs[:2] + refs[3:]
    y_o, ends_all, pad, taps, own_sem, send, recv = refs
    begin_swap, end_swap = swap_states(
        ends, ends_all, step == 0, step == pl.num_programs(0) - 1, own_sem, send, recv, pair
    )
    rows, frames = u.shape[0], u.shape[1]
    span = GROUP * SUB
    coup = join_lanes(mix_one) * join_lanes(mix_two)
    lag_taps(channel_rates(logs), coup, taps, False)
    coup_both = pack_params(coup, rows)
    heads = rate_rows(logs)
    packed = pack_heads(u, rows)
    width = packed[0].shape[1]
    begin_swap()
    results = []
    for h in range(2):
        into, unused, out, unused, power = chunk_tables(heads[h])
        scale = [jnp.broadcast_to(v, (NST, width)) for v in power]
        carry = None
        outs = []
        for g in range(frames // span):
            local = mm(into, packed[h][g * span : (g + 1) * span])
            parts = [local[i * NST : (i + 1) * NST] for i in range(GROUP)]
            if carry is None:
                states = [jnp.zeros_like(parts[0])] + parts[:-1]
                carry = parts[-1]
            else:
                states = [carry] + [parts[i] + scale[i] * carry for i in range(GROUP - 1)]
                carry = parts[-1] + scale[-1] * carry
            scaled = jnp.concatenate([v * coup_both[h] for v in states], axis=0)
            outs.append(mm_tn(out, scaled.astype(bf16)))
        results.append(jnp.concatenate(outs, axis=0))
    for p in range(rows // 2):
        one, two = unpack_pair(results[0], results[1], p)
        y_o[2 * p] = one
        y_o[2 * p + 1] = two
    pad[0:SUB] = jnp.zeros((SUB, LANES), f32)
    chunk = frames // 5

    def one_row(i, carry):
        pad[pl.ds(SUB, frames)] = u[i].astype(f32)
        for r in range(0, frames, chunk):
            acc = y_o[i, pl.ds(r, chunk)].reshape(-1, SUB, LANES)
            for d in range(SUB):
                piece = pad[pl.ds(SUB + r - d, chunk)].reshape(-1, SUB, LANES)
                acc = acc + piece * taps[d][None]
            y_o[i, pl.ds(r, chunk)] = acc.reshape(chunk, LANES)
        return carry

    lax.fori_loop(0, rows, one_row, 0)
    end_swap()


def edge_sender(edges, low_all, high_all, zeros, send, recv, zero_sem, step, per, rest=None):
    place, level, core = peers()
    parts = lax.axis_size("tm")
    steps = edges.shape[0]
    not_first, not_last = place > 0, place < parts - 1
    after = (place + 1) % parts
    before = (place + parts - 1) % parts

    def up(i):
        return remote(
            edges.at[i, 1], low_all.at[i], send.at[0, i], recv.at[0, i], at(after, level, core)
        )

    def down(i):
        return remote(
            edges.at[i, 0], high_all.at[i], send.at[1, i], recv.at[1, i], at(before, level, core)
        )

    def blank(ref, i, k):
        return pltpu.make_async_copy(zeros, ref.at[i], zero_sem.at[k])

    @pl.when(step == 0)
    def _():
        if rest is None:
            pl.when(not_last)(lambda: greet([at(after, level, core)]))
            pl.when(not_first)(lambda: greet([at(before, level, core)]))
        zeros[...] = jnp.zeros_like(zeros)

        @pl.when(place == 0)
        def _():
            for i in range(steps):
                blank(low_all, i, 0).start()

        @pl.when(place == parts - 1)
        def _():
            for i in range(steps):
                blank(high_all, i, 1).start()

    def put(v):
        @pl.when(step == 0)
        def _():
            below = (place + parts - 1) // parts
            above = (2 * parts - 2 - place) // parts
            if rest is None:
                met(below + above)

        if rest is not None:
            pl.when(step == steps // per // 2)(lambda: rest.forward(1))
            pl.when(step == steps // per - 1)(lambda: rest.finish(1))

        frames = v.shape[0] // per
        for b in range(per):
            row = step * per + b
            edges[row, 0] = v[b * frames : b * frames + PAD]
            edges[row, 1] = v[(b + 1) * frames - PAD : (b + 1) * frames]
            pl.when(not_last)(lambda row=row: up(row).start())
            pl.when(not_first)(lambda row=row: down(row).start())

        @pl.when(step == steps // per - 1)
        def _():
            for i in range(steps):
                pl.when(not_last)(lambda i=i: up(i).wait_send())
                pl.when(not_first)(lambda i=i: down(i).wait_send())
                pl.when(not_first)(lambda i=i: up(i).wait_recv())
                pl.when(not_last)(lambda i=i: down(i).wait_recv())

            if rest is not None:
                rest.end(1)

            @pl.when(place == 0)
            def _():
                for i in range(steps):
                    blank(low_all, i, 0).wait()

            @pl.when(place == parts - 1)
            def _():
                for i in range(steps):
                    blank(high_all, i, 1).wait()

    return put


def mixer_out_kernel(
    y, ends_all, starts, mix_one, mix_two, logs, x1, small, stack, *refs
):
    step = pl.program_id(0)
    rest = None
    if len(refs) > 19:
        refs, sems = refs[1:21], refs[21:]
        rest = Gather(None, refs[7], dict(zip(XY_SEMS, sems)), 2)
        refs = refs[:7] + refs[8:]
    ys_o, gated_o, x2_o, pw_o, g_o, low_o, high_o, wo, wp, mask, sem = refs[:11]
    table, weigh, coup, edges, zeros, send, recv, zero_sem = refs[11:]
    parts = ends_all.shape[0]
    put = edge_sender(edges, low_o, high_o, zeros, send, recv, zero_sem, step, 1, rest)

    @pl.when(step == 0)
    def _():
        ffn, mix = D // BS * (FF // BS), (D // BS) ** 2
        if rest is not None:
            greet([at(other, rest.level, rest.core) for other in (rest.xp, rest.yp, rest.dp)])
            greet([at(rest.place, rest.level, 1 - rest.core)])
        weights = Matrices(stack, ((0, wo), (2 * mix, wp)), sem)
        weights.start()
        if rest is not None:
            met(4)
            rest.spread(1)
        mask[...] = head_mask()
        place = lax.axis_index("tm")
        frames = table.shape[0]
        frame_decay(logs, table, False)
        rates = channel_rates(logs)
        for i in range(parts):
            weigh[i], unused = passing(rates, place - 1 - i, frames)
        two = join_lanes(mix_two)
        weigh[parts] = two * passing(rates, place, frames)[0]
        coup[...] = join_lanes(mix_one) * two
        for index in range(2):
            weights.wait(index)

    came = weigh[0] * ends_all[0, 0].astype(f32)
    for i in range(1, parts):
        came = came + weigh[i] * ends_all[i, 0].astype(f32)
    zin = coup[...] * came + weigh[parts] * join_lanes(starts)
    ys = (y[0] + mm(table[...], spread_heads(zin, mask[...]))).astype(bf16)
    ys_o[0] = ys
    gated = mm(ys, wo[...])
    gated_o[0] = gated.astype(bf16)
    x2 = x1[0] + gated[:, :D] * sigmoid(gated[:, D:])
    x2_o[0] = x2
    hat, unused = norm(x2)
    pw = mm((hat * small[2:3]).astype(bf16), wp[...])
    pw_o[0] = pw.astype(bf16)
    g = (pw[:, :D] * sigmoid(pw[:, D:])).astype(bf16)
    g_o[0] = g
    put(g)


def fill_pad(pad, low, body, high):
    frames = body.shape[0]
    for g in range(D // LANES):
        lanes = slice(g * LANES, (g + 1) * LANES)
        pad[g, 0:PAD] = low[:, lanes].astype(f32)
        pad[g, pl.ds(PAD, frames)] = body[:, lanes].astype(f32)
        pad[g, pl.ds(PAD + frames, PAD)] = high[:, lanes].astype(f32)


def ffb_kernel(
    scale, g, low, high, x2, cot, small, stack,
    out_o, dx3_o, dq_o, grads, gain_o, low_o, high_o,
    wi, wo, wq, acc_in, acc_out, acc_q, pad, q_s, stage, k_act, k_din, k_n, k_dp, k_a, k_dpq, sem,
    edges, zeros, send, recv, zero_sem,
):
    step = pl.program_id(0)
    frames = g.shape[1]
    put = edge_sender(edges, low_o, high_o, zeros, send, recv, zero_sem, step, 1)

    ffn, mix = D // BS * (FF // BS), (D // BS) ** 2
    weights = Matrices(stack, ((2 * ffn, wq), (0, wi), (ffn, wo)), sem)

    def ready(*which):
        @pl.when(step == 0)
        def _():
            for index in which:
                weights.wait(index)

    @pl.when(step == 0)
    def _():
        weights.start()
        acc_in[...] = jnp.zeros_like(acc_in)
        acc_out[...] = jnp.zeros_like(acc_out)
        acc_q[...] = jnp.zeros_like(acc_q)
        gain_o[...] = jnp.zeros_like(gain_o)

    fill_pad(pad, low[0], g[0], high[0])
    chunk = frames // 5
    for c in range(D // LANES):
        lanes = slice(c * LANES, (c + 1) * LANES)
        for r in range(0, frames, chunk):
            acc = small[5:6, lanes] * pad[c, pl.ds(r + PAD - 7, chunk)]
            for j in range(1, KW):
                acc = acc + small[5 + j : 6 + j, lanes] * pad[c, pl.ds(r + j + PAD - 7, chunk)]
            q_s[pl.ds(r, chunk), lanes] = acc
    ready(0, 1, 2)
    q = q_s[...]
    sig_q = sigmoid(q)
    act_q = q * sig_q
    a3 = act_q.astype(bf16)
    x3 = x2[0] + mm(a3, wq[...])
    hat3, inv3 = norm(x3)
    n3 = (hat3 * small[3:4]).astype(bf16)
    inner = mm(n3, wi[...])
    sig = sigmoid(inner)
    act = inner * sig
    b4 = act.astype(bf16)
    x4 = x3 + 0.5 * mm(b4, wo[...])
    hat4, inv4 = norm(x4)
    out_o[0] = (hat4 * small[4:5]).astype(bf16)
    c4 = cot[0].astype(f32)
    gain_o[1] += fold8(c4 * hat4)
    dx4 = norm_back(hat4, inv4, small[4:5], c4)
    dp = (0.5 * dx4).astype(bf16)
    dact = mm_nt(dp, wo[...])
    dinner = ((sig + act * (1.0 - sig)) * dact).astype(bf16)
    group = k_n.shape[0] // frames
    keep = pl.ds(pl.multiple_of(step % group * frames, frames), frames)
    k_act[keep] = b4
    k_din[keep] = dinner
    k_n[keep] = n3
    k_dp[keep] = dp
    k_a[keep] = a3
    dn3 = mm_nt(dinner, wi[...])
    gain_o[0] += fold8(dn3 * hat3)
    dx3 = dx4 + norm_back(hat3, inv3, small[3:4], dn3)
    dx3_o[0] = dx3
    dpq = dx3.astype(bf16)
    k_dpq[keep] = dpq
    da3 = mm_nt(dpq, wq[...])
    dq = ((sig_q + act_q * (1.0 - sig_q)) * da3).astype(bf16)
    dq_o[0] = dq
    put(dq)

    @pl.when(step % group == group - 1)
    def _():
        acc_out[...] += mm_tn(k_dp[...], k_act[...])
        acc_in[...] += mm_tn(k_n[...], k_din[...])
        acc_q[...] += mm_tn(k_a[...], k_dpq[...])

    @pl.when(step == pl.num_programs(0) - 1)
    def _():
        ffn, mix = D // BS * (FF // BS), (D // BS) ** 2
        plan = (
            (acc_in, 0, False),
            (acc_out, ffn, True),
            (acc_q, 2 * ffn, False),
        )
        store_blocks(plan, scale, grads, stage, sem.at[0])


def mixer_back_kernel(
    scale, dq, dlow, dhigh, g, glow, ghigh, pw, x2, gated, ys, dx3, small, stack, logs, *refs
):
    step, last = pl.program_id(0), pl.num_programs(0) - 1
    frames = dq.shape[1]
    rest = None
    if len(refs) > 21:
        grads_rest, refs = refs[0], refs[1:]
        red, bufs, sems = refs[6], refs[22:26], refs[26:]
        half = (red.shape[0] + 1) // 2
        rest = Reduce((half, red.shape[0] - half), dict(zip(R_XY, sems)), grads_rest, bufs, red)
        refs = refs[:6] + refs[7:22]
    dx2_o, dy_o, gst_o, grads, gain_o, dk_o, wo, wp, acc_p, acc_o, dpad, gpad = refs[:12]
    dg_s, dk_s, stage, k_n, k_dpw, k_ys, k_dg, table, sem = refs[12:]

    @pl.when(step == 0)
    def _():
        ffn, mix = D // BS * (FF // BS), (D // BS) ** 2
        if rest is not None:
            greet([at(other, rest.level, rest.core) for other in (rest.xp, rest.yp, rest.dp)])
            greet([at(rest.place, rest.level, 1 - rest.core)])
        weights = Matrices(stack, ((0, wo), (2 * mix, wp)), sem)
        weights.start()
        if rest is not None:
            met(4)
            for c in rest.all:
                rest.start(c)
        frame_decay(logs, table, False)
        acc_p[...] = jnp.zeros_like(acc_p)
        acc_o[...] = jnp.zeros_like(acc_o)
        gain_o[...] = jnp.zeros_like(gain_o)
        dk_s[...] = jnp.zeros_like(dk_s)
        for index in range(2):
            weights.wait(index)

    fill_pad(dpad, dlow[0], dq[0], dhigh[0])
    fill_pad(gpad, glow[0], g[0], ghigh[0])
    chunk = frames // 5
    for c in range(D // LANES):
        lanes = slice(c * LANES, (c + 1) * LANES)
        for r in range(0, frames, chunk):
            here = dpad[c, pl.ds(r + PAD, chunk)]
            acc = small[5:6, lanes] * dpad[c, pl.ds(r + PAD + 7, chunk)]
            for j in range(1, KW):
                acc = acc + small[5 + j : 6 + j, lanes] * dpad[c, pl.ds(r - j + PAD + 7, chunk)]
            dg_s[pl.ds(r, chunk), lanes] = acc
            for j in range(KW):
                dk_s[j, :, lanes] += fold8(here * gpad[c, pl.ds(r + j + PAD - 7, chunk)])
    dg = dg_s[...]
    value = pw[0, :, :D].astype(f32)
    gate = sigmoid(pw[0, :, D:].astype(f32))
    dvalue = (dg * gate).astype(bf16)
    dgate = (dg * value * gate * (1.0 - gate)).astype(bf16)
    dpw = jnp.concatenate([dvalue, dgate], axis=1)
    hat2, inv2 = norm(x2[0])
    n2 = (hat2 * small[2:3]).astype(bf16)
    group = k_n.shape[0] // frames
    keep = pl.ds(pl.multiple_of(step % group * frames, frames), frames)
    k_n[keep] = n2
    k_dpw[keep] = dpw
    k_ys[keep] = ys[0]
    dn2 = mm_nt(dpw, wp[...])
    gain_o[...] += fold8(dn2 * hat2)
    dx2 = dx3[0] + norm_back(hat2, inv2, small[2:3], dn2)
    dx2_o[0] = dx2
    value = gated[0, :, :D].astype(f32)
    gate = sigmoid(gated[0, :, D:].astype(f32))
    dvalue = (dx2 * gate).astype(bf16)
    dgate = (dx2 * value * gate * (1.0 - gate)).astype(bf16)
    dgated = jnp.concatenate([dvalue, dgate], axis=1)
    k_dg[keep] = dgated
    dy = mm_nt(dgated, wo[...]).astype(bf16)
    dy_o[0] = dy
    local_states(table, dy, gst_o)

    if rest is not None:
        for c in rest.all:
            pl.when(step == 0)(lambda c=c: rest.begin(c))
            pl.when(step == last - 3 + 2 * c)(lambda c=c: rest.second(c))

    @pl.when(step % group == group - 1)
    def _():
        acc_p[...] += mm_tn(k_n[...], k_dpw[...])
        acc_o[...] += mm_tn(k_ys[...], k_dg[...])

    @pl.when(step == pl.num_programs(0) - 1)
    def _():
        ffn, mix = D // BS * (FF // BS), (D // BS) ** 2
        plan = ((acc_o, 0, False), (acc_p, 2 * mix, False))
        store_blocks(plan, scale, grads, stage, sem.at[0])
        if rest is not None:
            for c in rest.all:
                rest.combine(c)
                rest.square_end(c)
        for j in range(KW):
            dk_o[j : j + 1] = jnp.sum(dk_s[j], axis=0, keepdims=True)


def conv_back_kernel(
    u, dy, back_ends, logs, mix_one, mix_two,
    du_o, t1_o, t2_o, fp_o, gp_o, back_all,
    upad, dpad, acc_s, taps, own_sem, send, recv,
):
    step = pl.program_id(0)
    begin_swap, end_swap = swap_states(
        back_ends, back_all, step == 0, step == pl.num_programs(0) - 1, own_sem, send, recv
    )
    rows, frames = u.shape[0], u.shape[1]
    span = GROUP * SUB
    coup = join_lanes(mix_one) * join_lanes(mix_two)
    rates = channel_rates(logs)
    lag_taps(rates, coup, taps, True)
    coup_both = pack_params(coup, rows)
    heads = rate_rows(logs)
    u_both = pack_heads(u, rows)
    d_both = pack_heads(dy, rows)
    width = u_both[0].shape[1]
    du, first_sum, second_sum, end_u, end_d = [], [], [], [], []
    for h in range(2):
        into, into_w, out, out_w, power = chunk_tables(heads[h])
        scale = [jnp.broadcast_to(v, (NST, width)) for v in power]
        aged = [scale[i] * float(SUB * (i + 1)) for i in range(GROUP)]
        zero = jnp.zeros((NST, width), f32)
        carry, carry_w = zero, zero
        states, states_w = [], []
        for g in range(frames // span):
            here = u_both[h][g * span : (g + 1) * span]
            local = mm(into, here)
            local_w = mm(into_w, here)
            parts = [local[i * NST : (i + 1) * NST] for i in range(GROUP)]
            parts_w = [local_w[i * NST : (i + 1) * NST] for i in range(GROUP)]
            states.append([carry] + [parts[i] + scale[i] * carry for i in range(GROUP - 1)])
            states_w.append(
                [carry_w]
                + [parts_w[i] + scale[i] * carry_w + aged[i] * carry for i in range(GROUP - 1)]
            )
            carry_w = parts_w[-1] + scale[-1] * carry_w + aged[-1] * carry
            carry = parts[-1] + scale[-1] * carry
        end_u.append(carry_w)
        later, later_w = zero, zero
        one, two = zero, zero
        outs = []
        for g in reversed(range(frames // span)):
            here = d_both[h][g * span : (g + 1) * span]
            back = mm(out, here)
            back_w = mm(out_w, here)
            parts = [back[i * NST : (i + 1) * NST] for i in range(GROUP)]
            parts_w = [back_w[i * NST : (i + 1) * NST] for i in range(GROUP)]
            grads = jnp.concatenate([v * coup_both[h] for v in parts[1:] + [later]], axis=0)
            outs.append(mm_tn(into, grads.astype(bf16)))
            for i in range(GROUP):
                one = one + parts[i] * states[g][i]
                two = two + (parts_w[i] * states[g][i] + parts[i] * states_w[g][i])
            new, new_w = parts[0], parts_w[0]
            for i in range(GROUP - 1):
                new = new + scale[i] * parts[i + 1]
                new_w = new_w + (scale[i] * parts_w[i + 1] + aged[i] * parts[i + 1])
            later_w = new_w + scale[-1] * later_w + aged[-1] * later
            later = new + scale[-1] * later
        end_d.append(later_w)
        first_sum.append(one)
        second_sum.append(two)
        du.append(jnp.concatenate(outs[::-1], axis=0))
    first = lax.broadcasted_iota(jnp.int32, (NST, LANES), 1) < HALF
    for sums, out in ((first_sum, t1_o), (second_sum, t2_o)):
        both = []
        for v in sums:
            total = v[:, :LANES]
            for p in range(1, rows // 2):
                total = total + v[:, p * LANES : (p + 1) * LANES]
            both.append(total + pltpu.roll(total, HALF, 1))
        out[...] = jnp.where(first, both[0], both[1])
    for p in range(rows // 2):
        for pair, out in ((du, du_o), (end_u, fp_o), (end_d, gp_o)):
            one, two = unpack_pair(pair[0], pair[1], p)
            out[2 * p] = one
            out[2 * p + 1] = two
    chunk = frames // 5
    upad[0:SUB] = jnp.zeros((SUB, LANES), f32)
    dpad[pl.ds(frames, SUB)] = jnp.zeros((SUB, LANES), f32)
    acc_s[...] = jnp.zeros_like(acc_s)

    def one_row(i, carry):
        upad[pl.ds(SUB, frames)] = u[i].astype(f32)
        dpad[pl.ds(0, frames)] = dy[i].astype(f32)
        for r in range(0, frames, chunk):
            acc = du_o[i, pl.ds(r, chunk)].reshape(-1, SUB, LANES)
            here = dpad[pl.ds(r, chunk)]
            for d in range(SUB):
                piece = dpad[pl.ds(r + d, chunk)].reshape(-1, SUB, LANES)
                acc = acc + piece * taps[d][None]
                product = (here * upad[pl.ds(SUB + r - d, chunk)]).reshape(-1, SUB, LANES)
                acc_s[d] += jnp.sum(product, axis=0)
            du_o[i, pl.ds(r, chunk)] = acc.reshape(chunk, LANES)
        return carry

    lax.fori_loop(0, rows, one_row, 0)
    spot = lax.broadcasted_iota(jnp.int32, (SUB, LANES), 0)
    one, two = t1_o[...], t2_o[...]
    for d in range(SUB):
        kept = jnp.where(spot >= d, acc_s[d], 0.0)
        grad = jnp.exp(-rates * float(d)) * jnp.sum(kept, axis=0, keepdims=True)
        one = one + grad
        two = two + float(d) * grad
    t1_o[...] = one
    t2_o[...] = two
    begin_swap()
    end_swap()


def ffa_back_kernel(
    scale, du_loc, back_all, ends_all, back_ends, ends_w, back_w, starts, mix_one, mix_two, logs,
    t_one, t_two, gain_b, gain_c, kernel_grads,
    x1, feat, inner_r, act_r, dx2, small, stack, *refs
):
    step, last = pl.program_id(0), pl.num_programs(0) - 1
    pair = None
    if len(refs) > 23:
        grads_pair, red_in, refs = refs[0], refs[1], refs[2:]
        out_pair, out_rest = refs[3:5]
        red_rest, rest_bufs, red_pair, square_refs = refs[25], refs[26:28], refs[28], refs[29:33]
        pair_bufs, sems = refs[33:35], refs[35:]
        refs = refs[:3] + refs[5:25]
        pair = Reduce(
            out_pair.shape[:1], dict(zip(R_XY + R_Z, sems)), grads_pair, square_refs, red_pair,
            pair_bufs, out_pair,
        )
        pair.direct_in = pair_bufs[0]
        rest = Reduce(
            out_rest.shape[:1], dict(zip(R_Z, sems[9:])), None, None, red_rest, rest_bufs, out_rest
        )
    dx0_o, grads, small_o, wi, wo, wu, acc_in, acc_out, acc_u = refs[:9]
    mask, stage, k_act, k_din, k_n, k_dp, k_m, k_du, sem = refs[9:18]
    gain_o, sums_o, table, weigh, coup = refs[18:]
    place, parts = lax.axis_index("tm"), ends_all.shape[0]

    ffn, mix = D // BS * (FF // BS), (D // BS) ** 2
    weights = Matrices(stack, ((2 * ffn, wu), (ffn, wo), (0, wi)), sem)

    @pl.when(step == 0)
    def _():
        if pair is not None:
            greet([at(other, pair.level, pair.core) for other in (pair.xp, pair.yp, pair.dp)])
            diagonal = 2 * (1 - pair.high) + 1 - pair.low
            levels = (pair.near_by, pair.far_off, diagonal)
            greet([at(pair.place, other, pair.core) for other in levels])
            greet([at(pair.place, pair.level, 1 - pair.core)])
            red_rest[...] = red_in[...]
        weights.start()
        if pair is not None:
            met(7)
            pair.start(0)
            rest.near(0).start()
        mask[...] = head_mask()
        frames = table.shape[0]
        frame_decay(logs, table, True)
        rates = channel_rates(logs)
        for i in range(parts):
            weigh[0, i], weigh[1, i] = passing(rates, place - 1 - i, frames)
            weigh[2, i], unused = passing(rates, i - place - 1, frames)
        coup[...] = join_lanes(mix_one) * join_lanes(mix_two)
        acc_in[...] = jnp.zeros_like(acc_in)
        acc_out[...] = jnp.zeros_like(acc_out)
        acc_u[...] = jnp.zeros_like(acc_u)
        gain_o[...] = jnp.zeros_like(gain_o)
        sums_o[...] = jnp.zeros_like(sums_o)
        for index in range(3):
            weights.wait(index)

    frames = feat.shape[1]
    group = k_n.shape[0] // frames
    keep = pl.ds(pl.multiple_of(step % group * frames, frames), frames)
    came, came_w, later = 0.0, 0.0, 0.0
    for i in range(parts):
        end = ends_all[i, 0].astype(f32)
        came = came + weigh[0, i] * end
        came_w = came_w + weigh[1, i] * end
        later = later + weigh[2, i] * back_all[i, 0].astype(f32)
    mine = back_ends[0].astype(f32)
    start = join_lanes(starts)
    sums_o[0] += mine * came
    sums_o[1] += start * mine
    sums_o[2] += start * back_w[0]
    sums_o[3] += back_w[0] * came + mine * came_w + later * ends_w[0]
    du = (du_loc[0] + mm(table[...], spread_heads(coup[...] * later, mask[...]))).astype(bf16)
    hat1, inv1 = norm(x1[0])
    n1 = (hat1 * small[1:2]).astype(bf16)
    k_m[keep] = n1
    k_du[keep] = du
    dn1 = mm_nt(du, wu[...])
    gain_o[1] += fold8(dn1 * hat1)
    dx1 = dx2[0] + norm_back(hat1, inv1, small[1:2], dn1)
    dp = (0.5 * dx1).astype(bf16)
    dact = mm_nt(dp, wo[...])
    inner = inner_r[0].astype(f32)
    sig = sigmoid(inner)
    dinner = ((sig + inner * sig * (1.0 - sig)) * dact).astype(bf16)
    hat0, inv0 = norm(feat[0].astype(f32))
    n0 = (hat0 * small[0:1]).astype(bf16)
    k_act[keep] = act_r[0]
    k_din[keep] = dinner
    k_n[keep] = n0
    k_dp[keep] = dp
    dn0 = mm_nt(dinner, wi[...])
    gain_o[0] += fold8(dn0 * hat0)
    dx0_o[0] = dx1 + norm_back(hat0, inv0, small[0:1], dn0)

    if pair is not None:

        @pl.when(step == 0)
        def _():
            pair.begin(0)

        @pl.when(step == last - 4)
        def _():
            rest.across(0)

        @pl.when(step == last - 3)
        def _():
            pair.second(0)

        @pl.when(step == last - 2)
        def _():
            rest.settle(0)
            pair.combine(0)
            for i in range(3):
                pair.direct(0, i).start()

    @pl.when(step % group == group - 1)
    def _():
        acc_out[...] += mm_tn(k_dp[...], k_act[...])
        acc_in[...] += mm_tn(k_n[...], k_din[...])
        acc_u[...] += mm_tn(k_m[...], k_du[...])

    @pl.when(step == pl.num_programs(0) - 1)
    def _():
        ffn, mix = D // BS * (FF // BS), (D // BS) ** 2
        one, two = join_lanes(mix_one), join_lanes(mix_two)
        begin = (place * frames).astype(f32)
        begin_w = jnp.exp(-channel_rates(logs) * begin)
        d_coup = t_one[...] + sums_o[0]
        start_back = sums_o[1] * begin_w
        d_rate = coup[...] * (t_two[...] + sums_o[3])
        d_rate = d_rate + two * (begin * start_back + begin_w * sums_o[2])
        total = lambda v: jnp.sum(v, axis=0, keepdims=True)
        gains = [total(gain_o[0]), total(gain_o[1]), total(gain_c[...])]
        gains += [total(gain_b[0]), total(gain_b[1]), kernel_grads[0:KW]]
        entries = gains + [d_coup * two, d_coup * one + start_back, d_rate]
        own = small_o.shape[2]
        small_o[...] = jnp.zeros_like(small_o)
        row = 0
        for entry in entries:
            count = entry.shape[0]
            if count == NST:
                row = -(-row // 8) * 8
            for p in range(parts):
                small_o[p, row : row + count] = entry[:, p * own : (p + 1) * own] * scale
            row += count
        plan = ((acc_in, 0, False), (acc_out, ffn, True), (acc_u, 2 * ffn, False))
        store_blocks(plan, scale, grads, stage, sem.at[0])
        if pair is not None:
            pair.settle_direct(0)
            pair.square_end(0)
            for i in range(3):
                pair.direct(0, i).wait_send()
            rest.levels_end(0)


def shampoo_kernel(
    frames, source, owned, full, left, right, lroot, rroot, master, sums, small, logs, mix_terms,
    back_all, result, slope, nl_o, nr_o, nm_o, nc_o, own_o,
    small_o, new_small_o, decay_o, mix_o, new_decay_o, new_mix_o, state_o, result_o, slope_o,
):
    step = pl.program_id(0)
    result_o[...] = result[...]
    slope_o[...] = slope[...]

    @pl.when(step == 0)
    def _():
        place = lax.axis_index("tm")
        parts, rows, width = back_all.shape[0], back_all.shape[1], state_o.shape[2]
        columns = [as_column(jnp.exp(logs[j : j + 1])) for j in range(logs.shape[0])]
        over = [jnp.broadcast_to(column, (NST, HALF)) for column in columns]
        rates = jnp.concatenate(over, axis=1)
        decays = [jnp.exp(-rates * float(frames * i)) * mix_terms[1] for i in range(parts)]
        grads = []
        for r in range(rows):
            grad = 0.0
            for p in range(parts):
                total = 0.0
                for i in range(parts):
                    part = back_all[i, r, :, p * width : (p + 1) * width].astype(f32)
                    total = total + part * decays[i]
                grad = grad + jnp.where(place == p, total, 0.0)
            grads.append(grad)
        for r in range(rows):
            total = 0.0
            for i in range(rows):
                total = total + jnp.where(source[i] == r, grads[i], 0.0)
            state_o[r] = total

    @pl.when(step == 0)
    def _():
        count = small_o.shape[0]
        grad = sums[0:count]
        small_o[...] = grad
        width = small_o.shape[1]
        own_small = 0.0
        for p in range(small.shape[1] // width):
            part = small[:, p * width : (p + 1) * width]
            own_small = own_small + jnp.where(lax.axis_index("tm") == p, part, 0.0)
        new_small_o[...] = own_small - rate_small * grad
        row = -(-count // 8) * 8
        for i in range(2):
            grad = sums[row + i * NST : row + (i + 1) * NST]
            mix_o[i] = grad
            new_mix_o[i] = mix_terms[i] - rate_small * grad
        by_channel = sums[row + 2 * NST : row + 3 * NST].T
        for j in range(logs.shape[0]):
            here = jnp.sum(by_channel[j * HALF : (j + 1) * HALF], axis=0, keepdims=True)
            grad = -here * jnp.exp(logs[j : j + 1])
            decay_o[j : j + 1] = grad
            new_decay_o[j : j + 1] = logs[j : j + 1] - rate_small * grad

    slab = owned.shape[1]
    down = lax.broadcasted_iota(jnp.int32, (slab, BS), 0) + lax.axis_index("rows") * slab
    pick = (down == lax.broadcasted_iota(jnp.int32, (slab, BS), 1)).astype(f32).astype(bf16)
    for i in range(full.shape[0]):
        whole = full[i]
        mine = owned[i]
        own_o[i] = mine.astype(f32)
        pair = mm_nt(jnp.concatenate([mine, pick], axis=0), whole)
        nl_o[i] = 0.5 * left[i] + 0.5 * pair[:slab]
        pair = jnp.concatenate([pair[slab:], lroot[i]], axis=0).astype(bf16)
        pair = mm(pair, whole)
        nr_o[i] = 0.5 * right[i] + 0.5 * pair[:slab]
        side = pair[slab:]
        step = mm(side.astype(bf16), rroot[i].astype(bf16))
        new = master[i] - rate_blocks * step
        nm_o[i] = new
        nc_o[i] = new.astype(bf16)


def deliveries(sizes, parts, count):
    edges = [sum(sizes[:c]) for c in range(len(sizes) + 1)]
    runs = []
    for which, ids in enumerate(block_sets()):
        for owner, k, v, j, n in move_runs(ids, parts, count):
            if which:
                runs.append((0, which, owner, k, v, j, n))
                continue
            for c, (a, b) in enumerate(zip(edges[:-1], edges[1:])):
                low, high = max(a, j), min(b, j + n)
                if low < high:
                    runs.append((c + 1, 0, owner, k + low - j, v, low, high - low))
    groups = []
    for chunk, unused, owner, k, v, j, n in sorted(runs, key=lambda run: (run[0], run[2], run[3])):
        if groups and groups[-1][:2] == (chunk, owner) and sum(groups[-1][2:]) == k:
            groups[-1] = (chunk, owner, groups[-1][2], groups[-1][3] + n)
        else:
            groups.append((chunk, owner, k, n))
    return runs, groups


def reduce_kernel(
    sizes, runs, groups, grads, share_pair, share_rest, small, full, owned_o, small_sum,
    mine, came, from_x, from_y, red, direct_in, share_first, owned, s_tm, s_core, s_z,
    d_send, d_recv, a_send, a_recv, f_send, f_recv, s_send, s_recv, put_sem, *sems,
):
    it = Reduce(
        sizes, dict(zip(R_XY + R_Z, sems)), grads, (mine, came, from_x, from_y), red, None, share_first
    )
    it.direct_in = direct_in
    place, level, core = it.place, it.level, it.core
    low, high, near, far = it.low, it.high, it.near_by, it.far_off
    diagonal = 2 * (1 - high) + 1 - low
    others = (it.xp, it.yp, it.dp)
    greet([at(other, level, core) for other in others])
    greet([at(place, other, core) for other in (near, far, diagonal)])
    greet([at(place, level, 1 - core)])
    shares = (share_first, share_pair, share_rest)

    def deliver(index):
        unused, which, owner, k, v, j, n = runs[index]
        src, dst = shares[which].at[pl.ds(j, n)], owned.at[pl.ds(k, n)]
        if owner == v:
            return pltpu.make_async_copy(src, dst, d_send.at[index])
        return remote(src, dst, d_send.at[index], d_recv.at[index], at(owner, level, core))

    def in_chunk(c):
        return [i for i, run in enumerate(runs) if run[0] == c]

    def send_out(c):
        for i in in_chunk(c):
            pl.when(place == runs[i][4])(lambda i=i: deliver(i).start())

    def come_in(c):
        for i in in_chunk(c):
            local = runs[i][2] == runs[i][4]
            done = (lambda i=i: deliver(i).wait()) if local else (lambda i=i: deliver(i).wait_recv())
            pl.when(place == runs[i][2])(done)

    def sent_out():
        for i, run in enumerate(runs):
            if run[2] != run[4]:
                pl.when(place == run[4])(lambda i=i: deliver(i).wait_send())

    def spot(g, where):
        unused, owner, k, n = groups[g]
        return full.at[pl.ds(k, n), where // 2, where % 2, core]

    def held(g):
        unused, owner, k, n = groups[g]
        return owned.at[pl.ds(k, n)]

    def put(g):
        return pltpu.make_async_copy(held(g), spot(g, level), put_sem.at[g])

    def at_once(g):
        return groups[g][0] == len(sizes)

    def along(g, i):
        passed = i == 2 and not at_once(g)
        src = spot(g, far) if passed else held(g)
        dst = spot(g, far if passed else level)
        target = (far, near, near if passed else diagonal)[i]
        target = at(place, target, core)
        return remote(src, dst, a_send.at[g, i], a_recv.at[g, i], target)

    def to_core(g, i):
        where = (level, far, near, diagonal)[i]
        src = held(g) if i == 0 else spot(g, where)
        target = at(place, level, 1 - core)
        return remote(src, spot(g, where), f_send.at[g, i], f_recv.at[g, i], target)

    def for_groups(c, act):
        for g, group in enumerate(groups):
            if c is None or group[0] == c:
                pl.when(place == group[1])(lambda g=g: act(g))

    def spread(g):
        put(g).start()
        along(g, 0).start()
        along(g, 1).start()
        if at_once(g):
            along(g, 2).start()
        to_core(g, 0).start()

    def pass_on(g):
        along(g, 0).wait_recv()
        if not at_once(g):
            along(g, 2).start()
        to_core(g, 1).start()
        along(g, 1).wait_recv()
        to_core(g, 2).start()
        if at_once(g):
            along(g, 2).wait_recv()
            to_core(g, 3).start()

    def last(g):
        if not at_once(g):
            along(g, 2).wait_recv()
            to_core(g, 3).start()

    def finish(g):
        put(g).wait()
        for i in range(4):
            to_core(g, i).wait_recv()
        for i in range(4):
            to_core(g, i).wait_send()
        for i in range(3):
            along(g, i).wait_send()

    def to_place(d):
        send, recv = s_send.at[d], s_recv.at[d]
        return remote(small.at[others[d]], s_tm.at[d], send, recv, at(others[d], level, core))

    def to_sibling():
        target = at(place, level, 1 - core)
        return remote(s_core.at[0], s_core.at[1], s_send.at[3], s_recv.at[3], target)

    def to_level(d):
        target = at(place, (near, far, diagonal)[d], core)
        return remote(s_z.at[level], s_z.at[level], s_send.at[4 + d], s_recv.at[4 + d], target)

    def reduced(c):
        it.combine(c)
        for i in range(3):
            it.direct(c, i).start()

    def settled(c):
        it.settle_direct(c)
        send_out(c + 1)

    def arrived(c):
        come_in(c + 1)
        for_groups(c + 1, spread)

    met(7)
    for c in it.all:
        it.start(c)
    send_out(0)
    for d in range(3):
        to_place(d).start()
    stages = (
        it.begin, it.second, reduced, settled, arrived,
        lambda c: for_groups(c + 1, pass_on), lambda c: for_groups(c + 1, last),
    )
    chunks = len(sizes)
    for tick in range(chunks + len(stages) - 1):
        for index, stage in enumerate(stages):
            if 0 <= tick - index < chunks:
                stage(tick - index)
        if tick == 0:
            come_in(0)
            for_groups(0, spread)
            for d in range(3):
                to_place(d).wait_recv()
            s_core[0] = small[place] + (s_tm[0] + s_tm[1]) + s_tm[2]
            to_sibling().start()
        if tick == 1:
            to_sibling().wait_recv()
            s_z[level] = s_core[0] + s_core[1]
            for d in range(3):
                to_level(d).start()
        if tick == 2:
            for_groups(0, pass_on)
        if tick == 3:
            for_groups(0, last)
    for d in range(3):
        to_level(d).wait_recv()
    small_sum[...] = (s_z[0] + s_z[1]) + (s_z[2] + s_z[3])
    owned_o[...] = owned[...]
    for_groups(None, finish)
    for c in it.all:
        it.square_end(c)
        for i in range(3):
            it.direct(c, i).wait_send()
    sent_out()
    for d in range(3):
        to_place(d).wait_send()
        to_level(d).wait_send()
    to_sibling().wait_send()


def reduce_grads(first, pair, rest, small, parts, devices, slab):
    levels = devices // 2
    ffn, mix = D // BS * (FF // BS), (D // BS) ** 2
    if parts != 4 or levels != 4:
        grads = [first[: 2 * ffn], rest[: 2 * ffn], first[2 * ffn :], pair, rest[2 * ffn :]]
        owned = jnp.concatenate(grads, axis=0)
        owned = lax.psum_scatter(owned, "tm", scatter_dimension=0, tiled=True)
        owned = lax.psum_scatter(owned, "rows", scatter_dimension=1, tiled=True)
        full = lax.all_gather(owned, "rows", axis=1, tiled=True)
        small = lax.psum_scatter(small, "tm", scatter_dimension=0, tiled=True)[0]
        return full, owned, lax.psum(small, "rows")
    sizes = (4, 3, 2)
    m, chunks = first.shape[1], len(sizes)
    count = sum(len(ids) for ids in block_sets()) // parts
    runs, groups = deliveries(sizes, parts, count)
    dma = lambda *dims: pltpu.SemaphoreType.DMA(dims)
    vb = lambda *dims: pltpu.VMEM(dims + (slab, BS), bf16)
    vmem = pl.BlockSpec(memory_space=pltpu.VMEM)
    part = small.shape[1:]
    full, owned, small_sum = pl.pallas_call(
        partial(reduce_kernel, sizes, runs, groups),
        in_specs=[ANY, vmem, vmem, vmem],
        out_specs=[ANY, vmem, vmem],
        out_shape=[
            shape((count, 2, 2, 2, slab, BS), bf16),
            shape((count, slab, BS), bf16),
            shape(part),
        ],
        scratch_shapes=square_bufs(m, parts, levels, slab)
        + [vb(m, 2, 2), vb(3, m), vb(m), vb(count), vm(3, *part), vm(2, *part), vm(levels, *part)]
        + [dma(len(runs)), dma(len(runs)), dma(len(groups), 3), dma(len(groups), 3)]
        + [dma(len(groups), 4), dma(len(groups), 4), dma(7), dma(7), dma(len(groups))]
        + reduce_sems(R_XY, chunks)
        + [dma(chunks, 3)] * 2,
        compiler_params=pltpu.CompilerParams(
            collective_id=2, has_side_effects=True, vmem_limit_bytes=VMEM_BYTES
        ),
        name="reduce_grads",
    )(first, pair, rest, small)
    return full.reshape(count, BS, BS), owned, small_sum


def row_spec(frames, width, per=1):
    return pl.BlockSpec((per, frames, width), lambda i: (i, 0, 0))


def whole_spec(*dims):
    return pl.BlockSpec(dims, lambda i: (0,) * len(dims))


def talking(number):
    return pltpu.CompilerParams(
        dimension_semantics=("arbitrary",),
        vmem_limit_bytes=VMEM_BYTES,
        collective_id=number,
        has_side_effects=True,
    )


def body(
    features,
    cotangent,
    state_bank,
    state_source,
    master,
    left_stats,
    right_stats,
    left_root,
    right_root,
    small_params,
    decay_logs,
    state_mix,
):
    rows, frames, width = features.shape
    tokens = rows * frames
    parts = lax.axis_size("tm")
    place = lax.axis_index("tm")
    scaling = 1.0 / math.sqrt(tokens * parts * lax.axis_size("rows"))
    ffn, mix = D // BS * (FF // BS), (D // BS) ** 2

    own_heads, own_channels = decay_logs.shape[0], state_mix.shape[1]
    mix_t = state_mix.transpose(0, 2, 1)
    bank_t = state_bank.transpose(0, 2, 1)
    devices = lax.axis_size("rows")
    levels = devices // 2
    spread_out = parts == 4
    if spread_out:
        first, pair, rest, packed = gather_first(
            master, bank_t, mix_t, decay_logs, state_source, parts, devices
        )
        first = first.reshape(-1, BS, BS)
        pair_out, rest_out = [shape(pair.shape, bf16)], [shape(rest.shape, bf16)]
        any_one, pair_in, rest_in = [ANY], [pair], [rest]
        pair_sems, rest_sems = gather_sems(XY_SEMS, levels), gather_sems(XY_SEMS, levels, 2)
    else:
        stack = lax.all_gather(master.astype(bf16), "rows", axis=1, tiled=True)
        stack = lax.all_gather(stack, "tm", axis=0, tiled=True)
        logs_own = jnp.pad(decay_logs, ((0, 8 - own_heads), (0, own_channels - NST)))
        params = [bank_t[state_source].reshape(-1, own_channels), mix_t.reshape(-1, own_channels)]
        packed = lax.all_gather(jnp.concatenate(params + [logs_own], axis=0), "tm", axis=0)
        first, pair, rest = (stack[jnp.array(ids)] for ids in block_sets())
        pair_out = rest_out = any_one = pair_in = rest_in = pair_sems = rest_sems = []

    mix_row = rows
    logs_row = (rows + 2) * NST // 8
    per_group = LANES // own_channels
    wide = lambda at_row: pl.BlockSpec((parts, NST, own_channels), lambda i: (0, at_row, 0))
    narrow = lambda at_row: pl.BlockSpec((per_group, NST, own_channels), lambda i: (i, at_row, 0))
    starts_spec = pl.BlockSpec((parts, NST, own_channels), lambda i: (0, i, 0))
    logs_spec = pl.BlockSpec((parts, 8, own_channels), lambda i: (0, logs_row, 0))
    logs_part = pl.BlockSpec((per_group, 8, own_channels), lambda i: (i, logs_row, 0))
    all_params = [wide(mix_row), wide(mix_row + 1), logs_spec]
    part_params = [logs_part, narrow(mix_row), narrow(mix_row + 1)]

    mat = lambda r, c: vm(r, c, dtype=bf16)
    dma = pltpu.SemaphoreType.DMA
    group = 3 if rows % 3 == 0 else 1
    small_spec = whole_spec(*small_params.shape)
    state_spec = pl.BlockSpec((1, NST, D), lambda i: (i, 0, 0))
    states_spec = pl.BlockSpec((parts, 1, NST, D), lambda i: (0, i, 0, 0))
    flat_spec = whole_spec(NST, D)
    x1, inner_a, act_a, u, ends, *done = pl.pallas_call(
        ffa_forward_kernel,
        grid=(rows // BOTH,),
        in_specs=[row_spec(frames, D, BOTH), small_spec, ANY, logs_spec]
        + any_one,
        out_specs=[
            row_spec(frames, D, BOTH),
            row_spec(frames, FF, BOTH),
            row_spec(frames, FF, BOTH),
            row_spec(frames, D, BOTH),
            pl.BlockSpec((BOTH, NST, D), lambda i: (i, 0, 0)),
        ]
        + any_one,
        out_shape=[
            shape((rows, frames, D)),
            shape((rows, frames, FF), bf16),
            shape((rows, frames, FF), bf16),
            shape((rows, frames, D), bf16),
            shape((rows, NST, D), bf16),
        ]
        + pair_out,
        scratch_shapes=[mat(D, FF), mat(FF, D), mat(D, D), mat(frames, HEADS * NST), dma((3,))] + pair_sems,
        input_output_aliases={4: 5} if spread_out else {},
        compiler_params=talking(7) if spread_out else PARAMS,
        name="ffa_forward",
    )(features, small_params, first, packed, *pair_in)
    if spread_out:
        pair = done[0].reshape(-1, BS, BS)

    group_spec = pl.BlockSpec((rows, frames, LANES), lambda i: (0, 0, i))
    coup_spec = pl.BlockSpec((NST, LANES), lambda i: (0, i))
    swap_scratch = [dma, dma((parts - 1,)), dma((parts - 1,))]
    all_states = shape((parts, rows, NST, D), bf16)
    y_loc, ends_all, *done = pl.pallas_call(
        conv_forward_kernel,
        grid=(D // LANES,),
        in_specs=[group_spec, ANY] + part_params
        + any_one,
        out_specs=[group_spec, ANY] + any_one,
        out_shape=[shape((rows, frames, D)), all_states] + rest_out,
        scratch_shapes=[vm(SUB + frames, LANES), vm(SUB, SUB, LANES)] + swap_scratch + rest_sems,
        input_output_aliases={5: 2} if spread_out else {},
        compiler_params=talking(3),
        name="conv_forward",
    )(u, ends, packed, packed, packed, *rest_in)

    edge_spec = pl.BlockSpec((1, PAD, D), lambda i: (i, 0, 0))
    edge_scratch = [
        vm(rows, 2, PAD, D, dtype=bf16),
        vm(PAD, D, dtype=bf16),
        dma((2, rows)),
        dma((2, rows)),
        dma((2,)),
    ]
    edge_shapes = [shape((rows, PAD, D), bf16)] * 2
    ys, gated, x2, pw, g, g_low, g_high, *done = pl.pallas_call(
        mixer_out_kernel,
        grid=(rows,),
        in_specs=[
            row_spec(frames, D),
            states_spec,
            starts_spec,
        ]
        + all_params
        + [row_spec(frames, D), small_spec, ANY]
        + any_one,
        out_specs=[
            row_spec(frames, D),
            row_spec(frames, 2 * D),
            row_spec(frames, D),
            row_spec(frames, 2 * D),
            row_spec(frames, D),
            ANY,
            ANY,
        ]
        + any_one,
        out_shape=[
            shape((rows, frames, D), bf16),
            shape((rows, frames, 2 * D), bf16),
            shape((rows, frames, D)),
            shape((rows, frames, 2 * D), bf16),
            shape((rows, frames, D), bf16),
        ]
        + edge_shapes
        + rest_out,
        scratch_shapes=[mat(D, 2 * D), mat(D, 2 * D), vm(HEADS * NST, D), dma((3,))]
        + [mat(frames, HEADS * NST), vm(parts + 1, NST, D), vm(NST, D)]
        + edge_scratch
        + rest_sems,
        input_output_aliases={9: 7} if spread_out else {},
        compiler_params=talking(4),
        name="mixer_out",
    )(y_loc, ends_all, packed, packed, packed, packed, x1, small_params, pair, *done)
    if spread_out:
        rest = done[0].reshape(-1, BS, BS)

    kept = lambda *widths: [mat(group * frames, w) for w in widths]
    slab = master.shape[1]
    spread_back = spread_out and levels == 4
    sizes = [len(ids) // parts for ids in block_sets()]
    if spread_back:
        grad_shapes = [shape((parts, n, levels, 2, slab, BS), bf16) for n in sizes]
        flat_shapes = [shape((parts * n, BS, BS), bf16) for n in sizes]
    else:
        flat_shapes = [shape((len(ids), BS, BS), bf16) for ids in block_sets()]
    unflat = lambda v, k: v.reshape(grad_shapes[k].shape) if spread_back else v
    layer_out, dx3, dq, grads_rest, gain_b, d_low, d_high = pl.pallas_call(
        partial(ffb_kernel, scaling),
        grid=(rows,),
        in_specs=[
            row_spec(frames, D),
            edge_spec,
            edge_spec,
            row_spec(frames, D),
            row_spec(frames, D),
            small_spec,
            ANY,
        ],
        out_specs=[
            row_spec(frames, D),
            row_spec(frames, D),
            row_spec(frames, D),
            ANY,
            whole_spec(2, 8, D),
            ANY,
            ANY,
        ],
        out_shape=[
            shape((rows, frames, D), bf16),
            shape((rows, frames, D)),
            shape((rows, frames, D), bf16),
            flat_shapes[2],
            shape((2, 8, D)),
        ]
        + edge_shapes,
        scratch_shapes=[
            mat(D, FF),
            mat(FF, D),
            mat(D, D),
            vm(D, FF),
            vm(D, FF),
            vm(D, D),
            vm(D // LANES, frames + 2 * PAD, LANES),
            vm(frames, D),
            vm(2 * ffn + mix, BS, BS, dtype=bf16),
        ]
        + kept(FF, FF, D, D, D, D)
        + [dma((3,))]
        + edge_scratch,
        compiler_params=talking(5),
        name="ffb",
    )(g, g_low, g_high, x2, cotangent, small_params, rest)

    dx2, dy, back_ends, grads_pair, gain_c, kernel_grads, *red_rest = pl.pallas_call(
        partial(mixer_back_kernel, scaling),
        grid=(rows,),
        in_specs=[
            row_spec(frames, D),
            edge_spec,
            edge_spec,
            row_spec(frames, D),
            edge_spec,
            edge_spec,
            row_spec(frames, 2 * D),
            row_spec(frames, D),
            row_spec(frames, 2 * D),
            row_spec(frames, D),
            row_spec(frames, D),
            small_spec,
            ANY,
            logs_spec,
        ]
        + [ANY] * spread_back,
        out_specs=[
            row_spec(frames, D),
            row_spec(frames, D),
            state_spec,
            ANY,
            whole_spec(8, D),
            whole_spec(16, D),
        ]
        + [whole_spec(sizes[2], 2, 2, slab, BS)] * spread_back,
        out_shape=[
            shape((rows, frames, D)),
            shape((rows, frames, D), bf16),
            shape((rows, NST, D), bf16),
            flat_shapes[1],
            shape((8, D)),
            shape((16, D)),
        ]
        + [shape((sizes[2], 2, 2, slab, BS), bf16)] * spread_back,
        scratch_shapes=[
            mat(D, 2 * D),
            mat(D, 2 * D),
            vm(D, 2 * D),
            vm(D, 2 * D),
            vm(D // LANES, frames + 2 * PAD, LANES),
            vm(D // LANES, frames + 2 * PAD, LANES),
            vm(frames, D),
            vm(KW, 8, D),
            vm(4 * mix, BS, BS, dtype=bf16),
        ]
        + kept(D, 2 * D, D, 2 * D)
        + [mat(frames, HEADS * NST), dma((3,))]
        + (square_bufs(sizes[2], parts, levels, slab) + reduce_sems(R_XY, 2)) * spread_back,
        compiler_params=talking(8) if spread_back else PARAMS,
        name="mixer_back",
    )(
        dq, d_low, d_high, g, g_low, g_high, pw, x2, gated, ys, dx3, small_params, pair,
        packed, *[unflat(grads_rest, 2)] * spread_back,
    )

    nst_spec = pl.BlockSpec((rows, NST, LANES), lambda i: (0, 0, i))
    du_loc, t_one, t_two, ends_w, back_w, back_all = pl.pallas_call(
        conv_back_kernel,
        grid=(D // LANES,),
        in_specs=[group_spec, group_spec, ANY] + part_params,
        out_specs=[
            group_spec,
            coup_spec,
            coup_spec,
            nst_spec,
            nst_spec,
            ANY,
        ],
        out_shape=[
            shape((rows, frames, D)),
            shape((NST, D)),
            shape((NST, D)),
            shape((rows, NST, D)),
            shape((rows, NST, D)),
            all_states,
        ],
        scratch_shapes=[
            vm(SUB + frames, LANES),
            vm(SUB + frames, LANES),
            vm(SUB, SUB, LANES),
            vm(SUB, SUB, LANES),
        ]
        + swap_scratch,
        compiler_params=talking(6),
        name="conv_back",
    )(u, dy, back_ends, packed, packed, packed)

    small_rows = -(-small_params.shape[0] // 8) * 8 + 3 * NST
    grad_zero, grads_first, small_all, *shares = pl.pallas_call(
        partial(ffa_back_kernel, scaling),
        grid=(rows,),
        in_specs=[
            row_spec(frames, D),
            states_spec,
            states_spec,
            state_spec,
            state_spec,
            state_spec,
            starts_spec,
        ]
        + all_params
        + [
            flat_spec,
            flat_spec,
            whole_spec(2, 8, D),
            whole_spec(8, D),
            whole_spec(16, D),
            row_spec(frames, D),
            row_spec(frames, D),
            row_spec(frames, FF),
            row_spec(frames, FF),
            row_spec(frames, D),
            small_spec,
            ANY,
        ]
        + [ANY, whole_spec(sizes[2], 2, 2, slab, BS)] * spread_back,
        out_specs=[row_spec(frames, D), ANY, whole_spec(parts, small_rows, own_channels)]
        + [whole_spec(n, slab, BS) for n in sizes[1:]] * spread_back,
        out_shape=[
            shape((rows, frames, D)),
            flat_shapes[0],
            shape((parts, small_rows, own_channels)),
        ]
        + [shape((n, slab, BS), bf16) for n in sizes[1:]] * spread_back,
        scratch_shapes=[
            mat(D, FF),
            mat(FF, D),
            mat(D, D),
            vm(D, FF),
            vm(D, FF),
            vm(D, D),
            vm(HEADS * NST, D),
            vm(2 * ffn + mix, BS, BS, dtype=bf16),
        ]
        + kept(FF, FF, D, D, D, D)
        + [dma((3,)), vm(2, 8, D), vm(4, NST, D), mat(frames, HEADS * NST)]
        + [vm(3, parts, NST, D), vm(NST, D)]
        + (
            [vm(sizes[2], 2, 2, slab, BS, dtype=bf16)]
            + level_bufs(sizes[2], slab)
            + [vm(sizes[1], 2, 2, slab, BS, dtype=bf16)]
            + square_bufs(sizes[1], parts, levels, slab)
            + [vm(3, sizes[1], slab, BS, dtype=bf16), vm(sizes[1], slab, BS, dtype=bf16)]
            + reduce_sems(R_XY + R_Z + R_Z)
        )
        * spread_back,
        compiler_params=talking(9) if spread_back else PARAMS,
        name="ffa_back",
    )(
        du_loc, back_all, ends_all, back_ends, ends_w, back_w, packed, packed, packed, packed,
        t_one, t_two, gain_b, gain_c, kernel_grads,
        x1, features, inner_a, act_a, dx2, small_params, first,
        *([unflat(grads_pair, 1)] + red_rest) * spread_back,
    )

    full_grad, owned, sums = reduce_grads(
        unflat(grads_first, 0),
        *(shares if spread_back else (grads_pair, grads_rest)),
        small_all,
        parts,
        devices,
        slab,
    )
    count, slice_rows = owned.shape[0], owned.shape[1]
    group = 11 if count % 11 == 0 else 1
    part_spec = pl.BlockSpec((group, slice_rows, BS), lambda i: (i, 0, 0))
    full_spec = pl.BlockSpec((group, BS, BS), lambda i: (i, 0, 0))
    small_shape = (small_params.shape[0], own_channels)
    carry_spec = row_spec(frames, D, rows * group // count)
    small_outs = [small_shape, small_shape, decay_logs.shape, mix_t.shape]
    small_outs += [decay_logs.shape, mix_t.shape, bank_t.shape]
    new_left, new_right, new_master, new_copy, grad_blocks, *others = pl.pallas_call(
        partial(shampoo_kernel, frames),
        grid=(count // group,),
        in_specs=[
            pl.BlockSpec(memory_space=pltpu.SMEM),
            part_spec,
            full_spec,
            part_spec,
            part_spec,
            part_spec,
            full_spec,
            part_spec,
            whole_spec(*sums.shape),
            whole_spec(*small_params.shape),
            whole_spec(*decay_logs.shape),
            whole_spec(*mix_t.shape),
            whole_spec(*back_all.shape),
            carry_spec,
            carry_spec,
        ],
        out_specs=[part_spec] * 5 + [whole_spec(*dims) for dims in small_outs]
        + [carry_spec] * 2,
        out_shape=[
            shape(owned.shape),
            shape(owned.shape),
            shape(owned.shape),
            shape(owned.shape, bf16),
            shape(owned.shape),
        ]
        + [shape(dims) for dims in small_outs]
        + [shape(layer_out.shape, bf16), shape(grad_zero.shape)],
        compiler_params=PARAMS,
        name="shampoo",
    )(
        state_source, owned, full_grad, left_stats, right_stats, left_root, right_root, master,
        sums, small_params, decay_logs, mix_t, back_all, layer_out, grad_zero,
    )
    *small_results, grad_state, layer_out, grad_zero = others
    for i in (3, 5):
        small_results[i] = small_results[i].transpose(0, 2, 1)
    grad_state = grad_state.transpose(0, 2, 1)
    return (
        layer_out,
        grad_zero,
        grad_state,
        grad_blocks,
        new_left,
        new_right,
        new_master,
        new_copy,
        *small_results,
    )


def solution(mesh):
    return jax.shard_map(
        body,
        mesh=mesh,
        in_specs=(
            P("rows", "tm", None),
            P("rows", "tm", None),
            P("rows", "tm", None),
            P("rows"),
            P("tm", "rows", None),
            P("tm", "rows", None),
            P("tm", "rows", None),
            P("tm", "rows", None),
            P("tm", None, None),
            P(),
            P("tm", None),
            P(None, "tm", None),
        ),
        out_specs=(
            P("rows", "tm", None),
            P("rows", "tm", None),
            P("rows", "tm", None),
            P("tm", "rows", None),
            P("tm", "rows", None),
            P("tm", "rows", None),
            P("tm", "rows", None),
            P("tm", "rows", None),
            P(None, "tm"),
            P(None, "tm"),
            P("tm", None),
            P(None, "tm", None),
            P("tm", None),
            P(None, "tm", None),
        ),
        check_vma=False,
    )
```
